32 devices in a mesh: fsdp: 16 (over z, x, core), tp: 2 (over y).
Axes of the slice: x: 2, y: 2, z: 4, core: 2. Of those that a mesh axis runs over, the one named last changes fastest.
Arguments:
- hidden: bfloat16 [16384, 768], P(('fsdp', 'tp')), may hold values from -6 to 6
- prev_logits: float32 [16384, 12], P(('fsdp', 'tp')), may hold values from -4 to 4
- routes: int32 [16384, 2], P(('fsdp', 'tp')), may hold values from 0 to 11, as said below
- slot_rank: int32 [16384, 2], P(('fsdp', 'tp')), may hold values from 0 to 191, as said below
- dropped: int32 [16384, 2], P(('fsdp', 'tp')), may hold values from 0 to 1, as said below
- cotangent: bfloat16 [16384, 768], P(('fsdp', 'tp')), may hold values from -6 to 6
- attn_norm: bfloat16 [768], P(('fsdp', 'tp')), may hold values from 0.5 to 1.5
- ffn_norm: bfloat16 [768], P(('fsdp', 'tp')), may hold values from 0.5 to 1.5
- w_qkv: bfloat16 [768, 3, 768], P('fsdp', None, 'tp'), may hold values from -0.21875 to 0.21875
- w_attn_out: bfloat16 [768, 768], P('fsdp', 'tp'), may hold values from -0.875 to 0.875
- w_router: bfloat16 [768, 12], P(('fsdp', 'tp')), may hold values from -0.109375 to 0.109375
- w_const_gate: bfloat16 [768, 4], P(('fsdp', 'tp')), may hold values from -0.21875 to 0.21875
- w_const_value: bfloat16 [768, 2], P(('fsdp', 'tp')), may hold values from -5 to 5
- w_expert_in: bfloat16 [8, 768, 2, 2048], P(None, 'fsdp', None, 'tp'), may hold values from -0.21875 to 0.21875
- w_expert_out: bfloat16 [8, 768, 2048], P(None, 'fsdp', 'tp'), may hold values from -0.25 to 0.25
Outputs:
- output: bfloat16 [16384, 768], P(('fsdp', 'tp'))
- grad_hidden: float32 [16384, 768], P(('fsdp', 'tp'))
- grad_attn_norm: float32 [768], P(('fsdp', 'tp'))
- grad_ffn_norm: float32 [768], P(('fsdp', 'tp'))
- grad_qkv: float32 [768, 3, 768], P('fsdp', None, 'tp')
- grad_attn_out: float32 [768, 768], P('fsdp', 'tp')
- grad_router: float32 [768, 12], P(('fsdp', 'tp'))
- grad_const_gate: float32 [768, 4], P(('fsdp', 'tp'))
- grad_const_value: float32 [768, 2], P(('fsdp', 'tp'))
- grad_expert_in: float32 [8, 768, 2, 2048], P(None, 'fsdp', None, 'tp')
- grad_expert_out: float32 [8, 768, 2048], P(None, 'fsdp', 'tp')
The draws below stay inside these ranges and needn't reach their ends.
Inputs may be any that keep to these rules, and one draw needn't show every extreme that they name: `routes`: each token names two different experts; experts 0 to 7 are feed-forward, 8 the zero expert, 9 the copy expert, 10 and 11 the constant ones. `slot_rank`: for a kept pair to a feed-forward expert: the number of earlier pairs of its sequence kept by the same expert (tokens in order, a token's first expert before its second), so that kept pairs of one expert fill slots 0 upward without gaps; 0 for all other pairs. `dropped`: 1 exactly for pairs to a feed-forward expert that come after 192 earlier pairs of their sequence to that expert.
All inputs are finite; a program needn't handle non-finite values.
Results may differ from the reference program's by a relative error of at most 0.018.
Values may be sent and summed in bfloat16 or wider, within the bound.
A program may use at most 256 MiB of HBM per device.

```python
import jax
import jax.numpy as jnp
from jax import lax

D = 768
HEADS = 12
HD = 64
FF = 2048
EXP = 8
BLOCK = 256
NE = 12
SEQ = 1024
CAP = 192
TOKENS = 16384


def routing_tables(key):
    base_key = jax.random.fold_in(key, 17)
    key_busy, key_favour, key_score = jax.random.split(base_key, 3)
    groups = TOKENS // SEQ
    busy_expert = jax.random.randint(key_busy, (groups,), 0, EXP)
    favour = jax.random.randint(key_favour, (groups, NE), 0, 300)
    favour = favour + 500 * (jnp.arange(NE)[None, :] == busy_expert[:, None]).astype(jnp.int32)
    scores = jax.random.randint(key_score, (groups, SEQ, NE), 0, 1000) + favour[:, None, :]
    scores = scores * 16 + jnp.arange(NE).astype(jnp.int32)[None, None, :]
    unused, chosen = lax.top_k(scores, 2)
    chosen = chosen.astype(jnp.int32)
    flat_pairs = chosen.reshape(groups, SEQ * 2)
    onehot = (flat_pairs[:, :, None] == jnp.arange(NE)[None, None, :]).astype(jnp.int32)
    earlier = jnp.cumsum(onehot, axis=1) - onehot
    placed = jnp.sum(earlier * onehot, axis=2)
    feed_forward = flat_pairs < EXP
    overflow = feed_forward & (placed >= CAP)
    slot_value = jnp.where(feed_forward & (placed < CAP), placed, 0)
    return (chosen.reshape(TOKENS, 2), slot_value.astype(jnp.int32).reshape(TOKENS, 2), overflow.astype(jnp.int32).reshape(TOKENS, 2))


def draw_routes(key, part):
    return routing_tables(key)[0]


def draw_slot_rank(key, part):
    return routing_tables(key)[1]


def draw_dropped(key, part):
    return routing_tables(key)[2]


def block_levels(stream_key, shape, cuts, smallest, top_value):
    level = 1.0
    for position, blocks in cuts:
        steps = jax.random.uniform(jax.random.fold_in(jax.random.fold_in(stream_key, 6), position), (blocks,), jnp.float32, smallest / len(cuts), top_value / len(cuts))
        level = level * jnp.repeat(jnp.exp(steps), shape[position] // blocks).reshape((-1,) + (1,) * (len(shape) - 1 - position))
    return level


def scatter_about(key, dims, scale, most, shards=(), held_as=jnp.bfloat16):
    loudness = block_levels(key, dims, shards, -0.22, 0.18) if shards else 1.0
    values = jax.random.normal(key, dims, jnp.float32) * scale * loudness
    return jnp.minimum(jnp.maximum(values, -most), most).astype(held_as)


def setup_inputs(seed: int = 0) -> dict:
    key_list = jax.random.split(jax.random.key(seed), 16)
    return {
        "hidden": scatter_about(key_list[0], (TOKENS, D), 1.0, 6.0, ((0, 32),)),
        "prev_logits": scatter_about(key_list[1], (TOKENS, NE), 0.5, 4.0, ((0, 32),), jnp.float32),
        "routes": draw_routes(jax.random.fold_in(key_list[15], 71), 0),
        "slot_rank": draw_slot_rank(jax.random.fold_in(key_list[15], 71), 0),
        "dropped": draw_dropped(jax.random.fold_in(key_list[15], 71), 0),
        "cotangent": scatter_about(key_list[5], (TOKENS, D), 1.0, 6.0, ((0, 32),)),
        "attn_norm": jnp.clip(1.0 + 0.1 * jax.random.normal(key_list[6], (D,), jnp.float32), 0.5, 1.5).astype(jnp.bfloat16),
        "ffn_norm": jnp.clip(1.0 + 0.1 * jax.random.normal(key_list[7], (D,), jnp.float32), 0.5, 1.5).astype(jnp.bfloat16),
        "w_qkv": scatter_about(key_list[8], (D, 3, HEADS * HD), D ** -0.5, 0.21875, ((0, 16), (2, 2))),
        "w_attn_out": scatter_about(key_list[9], (D, HEADS * HD), (HEADS * HD // 16) ** -0.5, 0.875, ((0, 16), (1, 2))),
        "w_router": scatter_about(key_list[10], (D, NE), (4 * D) ** -0.5, 0.109375, ((0, 32),)),
        "w_const_gate": scatter_about(key_list[11], (D, 4), D ** -0.5, 0.21875, ((0, 32),)),
        "w_const_value": scatter_about(key_list[12], (D, 2), 1.0, 5.0, ((0, 32),)),
        "w_expert_in": scatter_about(key_list[13], (EXP, D, 2, FF), D ** -0.5, 0.21875, ((1, 16), (3, 2))),
        "w_expert_out": scatter_about(key_list[14], (EXP, D, FF), (FF // 4) ** -0.5, 0.25, ((1, 16), (2, 2))),
    }


PRECISE = lax.Precision.HIGHEST
EPSILON = 1e-06
MASKED_SCORE = -1e+30

@jax.custom_vjp
def low(v):
    return lax.optimization_barrier(v.astype(jnp.bfloat16)).astype(jnp.float32)

@jax.custom_vjp
def low_back(v):
    return v

def low_keep(v):
    return (low(v), None)

def low_pass(kept, grad):
    return (grad,)

def back_keep(v):
    return (v, None)

def back_low(kept, grad):
    return (low(grad),)
low.defvjp(low_keep, low_pass)
low_back.defvjp(back_keep, back_low)

def rms_norm(values, gain):
    return values * lax.rsqrt(lax.optimization_barrier(jnp.mean(values * values, axis=-1, keepdims=True)) + EPSILON) * gain

def rotate(heads):
    length, half_dim = (heads.shape[0], heads.shape[2] // 2)
    positions = jnp.arange(length).astype(jnp.float32)
    inverse = jnp.power(10000.0, -jnp.arange(half_dim).astype(jnp.float32) / half_dim)
    angles = positions[:, None] * inverse[None, :]
    cosine = jnp.cos(angles)[:, None, :]
    sine_part = jnp.sin(angles)[:, None, :]
    lower_half, upper_half = (heads[..., :half_dim], heads[..., half_dim:])
    return jnp.concatenate([lower_half * cosine - upper_half * sine_part, upper_half * cosine + lower_half * sine_part], axis=-1)

def soft_last(scores):
    highest = lax.optimization_barrier(jnp.max(scores, axis=-1, keepdims=True))
    expanded = jnp.exp(scores - highest)
    return expanded / lax.optimization_barrier(jnp.sum(expanded, axis=-1, keepdims=True))

def swiglu(gate_part, up_part):
    return gate_part / (1.0 + jnp.exp(-gate_part)) * up_part

def sequence(weights, inputs):
    norm_one, norm_two, qkv_weight, attn_weight, router_weight, const_gate, const_value, expert_in, expert_out = weights
    hidden, prev_logits, routes, slot_rank, dropped = inputs
    length, width = hidden.shape
    head_count = qkv_weight.shape[2] // HD
    stream_one = low(rms_norm(hidden, norm_one))
    projected = jnp.dot(stream_one, qkv_weight.reshape(width, -1), precision=PRECISE).reshape(length, 3, head_count, HD)
    queries = low(rotate(low_back(projected[:, 0])))
    keys_rot = low(rotate(low_back(projected[:, 1])))
    values_all = low(low_back(projected[:, 2]))
    scores = low_back(jnp.einsum('qhd,khd->hqk', queries, keys_rot, precision=PRECISE) * HD ** (-0.5))
    block_ids = jnp.arange(length) // BLOCK
    allowed = block_ids[None, :] <= block_ids[:, None]
    scores = jnp.where(allowed[None], scores, MASKED_SCORE)
    attn_probs = low(soft_last(scores))
    mixed = low_back(low(jnp.einsum('hqk,khd->qhd', attn_probs, values_all, precision=PRECISE)))
    attended = low_back(jnp.dot(mixed.reshape(length, -1), attn_weight.T, precision=PRECISE))
    residual_mid = hidden + attended
    normed_two = rms_norm(residual_mid, norm_two)
    stream_two = low(normed_two)
    logits = jnp.dot(stream_two, router_weight, precision=PRECISE) + prev_logits
    gate_pair = soft_last(jnp.take_along_axis(logits, routes, axis=1))
    slot_index = routes * CAP + slot_rank
    kept_pair = (routes < EXP) & (dropped == 0)
    slot_range = jnp.arange(EXP * CAP)
    dispatch = jnp.zeros((EXP * CAP, length), jnp.float32)
    for member in range(2):
        slot_hit = (slot_index[:, member][None, :] == slot_range[:, None]) & kept_pair[:, member][None, :]
        dispatch = dispatch + slot_hit.astype(jnp.float32)
    packed = jnp.dot(dispatch, stream_two, precision=PRECISE).reshape(EXP, CAP, width)
    both_parts = jnp.einsum('ecd,edjf->ecjf', packed, expert_in, precision=PRECISE)
    gate_part = low_back(both_parts[:, :, 0])
    up_part = low_back(both_parts[:, :, 1])
    activated = low(swiglu(gate_part, up_part))
    results = low_back(jnp.einsum('ecf,edf->ecd', activated, expert_out, precision=PRECISE)).reshape(EXP * CAP, width)
    const_weights = soft_last(jnp.dot(normed_two, const_gate, precision=PRECISE).reshape(length, 2, 2))
    constants = const_weights[:, :, 0:1] * normed_two[:, None, :] + const_weights[:, :, 1:2] * const_value.T[None, :, :]
    mixture = jnp.zeros_like(hidden)
    for member in range(2):
        route_col = routes[:, member][:, None]
        taken_rows = jnp.take(results, jnp.clip(slot_index[:, member], 0, EXP * CAP - 1), axis=0)
        branch = jnp.where(kept_pair[:, member][:, None], taken_rows, 0.0)
        branch = branch + jnp.where(route_col == EXP + 1, normed_two, 0.0)
        branch = branch + jnp.where(route_col == EXP + 2, constants[:, 0], 0.0)
        branch = branch + jnp.where(route_col == EXP + 3, constants[:, 1], 0.0)
        mixture = mixture + gate_pair[:, member:member + 1] * branch
    return residual_mid + low_back(mixture)

def reference(hidden, prev_logits, routes, slot_rank, dropped, cotangent, attn_norm, ffn_norm, w_qkv, w_attn_out, w_router, w_const_gate, w_const_value, w_expert_in, w_expert_out):
    weights = tuple((weight.astype(jnp.float32) for weight in (attn_norm, ffn_norm, w_qkv, w_attn_out, w_router, w_const_gate, w_const_value, w_expert_in, w_expert_out)))
    groups = hidden.shape[0] // SEQ

    def split_rows(array):
        return array.reshape((groups, SEQ) + array.shape[1:])
    fixed_inputs = (split_rows(prev_logits), split_rows(routes), split_rows(slot_rank), split_rows(dropped))

    def forward(stream, params):

        def one_sequence(items):
            return sequence(params, items)
        return lax.map(jax.checkpoint(one_sequence), (stream,) + fixed_inputs)
    outputs, pullback = jax.vjp(forward, split_rows(hidden.astype(jnp.float32)), weights)
    grad_stream, grad_weights = pullback(split_rows(cotangent.astype(jnp.float32)))
    return (outputs.reshape(-1, D).astype(jnp.bfloat16), grad_stream.reshape(-1, D), grad_weights[0], grad_weights[1], grad_weights[2], grad_weights[3], grad_weights[4], grad_weights[5], grad_weights[6], grad_weights[7], grad_weights[8])
```

```python
import jax
import jax.numpy as jnp
from jax import lax
from jax.experimental import pallas as pl
from jax.experimental.pallas import tpu as pltpu
from jax.sharding import PartitionSpec as P

HD = 64
BLOCK = 256


PRECISE = lax.Precision.HIGHEST
EPSILON = 1e-06
MASKED_SCORE = -1e30


def rms_norm(values, gain):
    return values * lax.rsqrt(jnp.mean(values * values, axis=-1, keepdims=True) + EPSILON) * gain


def rotate(heads):
    length, half_dim = (heads.shape[0], heads.shape[2] // 2)
    positions = jnp.arange(length).astype(jnp.float32)
    inverse = jnp.power(10000.0, -jnp.arange(half_dim).astype(jnp.float32) / half_dim)
    angles = positions[:, None] * inverse[None, :]
    cosine = jnp.cos(angles)[:, None, :]
    sine_part = jnp.sin(angles)[:, None, :]
    lower_half, upper_half = (heads[..., :half_dim], heads[..., half_dim:])
    return jnp.concatenate(
        [
            lower_half * cosine - upper_half * sine_part,
            upper_half * cosine + lower_half * sine_part,
        ],
        axis=-1,
    )


def soft_last(scores):
    highest = jnp.max(scores, axis=-1, keepdims=True)
    expanded = jnp.exp(scores - highest)
    return expanded / jnp.sum(expanded, axis=-1, keepdims=True)


def swiglu(gate_part, up_part):
    return gate_part / (1.0 + jnp.exp(-gate_part)) * up_part


FB = 512


def swap(values):
    return lax.ppermute(values, "tp", [(0, 1), (1, 0)])


def gather_rows(values):
    other = swap(values)
    first = lax.axis_index("tp") == 0
    return jnp.concatenate(
        [jnp.where(first, values, other), jnp.where(first, other, values)], axis=0
    )


def own_half(values):
    half = values.shape[0] // 2
    return lax.dynamic_slice_in_dim(values, lax.axis_index("tp") * half, half, 0)


def other_half(values):
    half = values.shape[0] // 2
    return lax.dynamic_slice_in_dim(values, (1 - lax.axis_index("tp")) * half, half, 0)


def sum_rows(values):
    values = values.astype(jnp.bfloat16)
    received = swap(other_half(values))
    return own_half(values).astype(jnp.float32) + received.astype(jnp.float32)


def member_groups(size, experts):
    span = 2 * experts
    starts = range(0, size, span)
    same_core = [[start + 2 * e + c for e in range(experts)] for start in starts for c in range(2)]
    cores = [[start + 2 * e, start + 2 * e + 1] for start in starts for e in range(experts)]
    whole = [[start + r for r in range(span)] for start in starts]
    across = [[start + r for start in starts] for r in range(span)]
    return same_core, cores, whole, across


def blocked_weights(w_expert_in, w_expert_out):
    experts, rows, _, hidden = w_expert_in.shape
    tiles = hidden // FB
    both = jnp.concatenate(
        [
            w_expert_in.reshape(experts, rows, 2, tiles, FB),
            w_expert_out.reshape(experts, rows, 1, tiles, FB),
        ],
        axis=2,
    )
    return both.transpose(0, 1, 3, 2, 4).reshape(experts, rows, 3 * hidden)


def split_grads(blocked):
    experts, rows, total = blocked.shape
    hidden = total // 3
    tiles = hidden // FB
    parts = blocked.reshape(experts, rows, tiles, 3, FB).transpose(0, 1, 3, 2, 4)
    return (
        parts[:, :, :2].reshape(experts, rows, 2, hidden),
        parts[:, :, 2].reshape(experts, rows, hidden),
    )


def fetch_expert(blocked):
    experts = blocked.shape[0]
    size = lax.axis_size("fsdp")
    same_core, cores, _, across = member_groups(size, experts)
    got = lax.all_to_all(blocked, "fsdp", 0, 0, axis_index_groups=same_core, tiled=True)
    got = lax.all_gather(got, "fsdp", axis=1, axis_index_groups=cores, tiled=True)
    got = got.reshape(-1, got.shape[-1])
    if size > 2 * experts:
        got = lax.all_gather(got, "fsdp", axis=0, axis_index_groups=across, tiled=True)
    return lax.all_gather(got, "tp", axis=0)


def return_grads(grads, experts):
    size = lax.axis_size("fsdp")
    same_core, cores, _, across = member_groups(size, experts)
    columns = grads.shape[-1]
    if size > 2 * experts:
        grads = lax.psum_scatter(
            grads, "fsdp", scatter_dimension=1, axis_index_groups=across, tiled=True
        )
    grads = grads.reshape(2, experts, -1, columns)
    grads = lax.psum_scatter(
        grads, "fsdp", scatter_dimension=2, axis_index_groups=cores, tiled=True
    )
    grads = lax.psum_scatter(grads, "tp", scatter_dimension=0)
    return lax.all_to_all(grads, "fsdp", 0, 0, axis_index_groups=same_core, tiled=True)


def exchange(values, experts):
    whole = member_groups(lax.axis_size("fsdp"), experts)[2]
    return lax.all_to_all(values, "fsdp", 0, 0, axis_index_groups=whole, tiled=True)


def nt_dot(left, right):
    return lax.dot_general(left, right, (((1,), (1,)), ((), ())), preferred_element_type=jnp.float32)


def nn_dot(left, right):
    return jnp.dot(left, right, preferred_element_type=jnp.float32)


def expert_kernel(x_ref, g_ref, w_ref, back_ref, grads_ref, xt_ref, gt_ref, res_ref, dx_ref):
    step = pl.program_id(0)

    @pl.when(step == 0)
    def _():
        xt_ref[...] = x_ref[...].T
        gt_ref[...] = g_ref[...].T
        res_ref[...] = jnp.zeros_like(res_ref)
        dx_ref[...] = jnp.zeros_like(dx_ref)

    w_gate = w_ref[0, :, :FB]
    w_up = w_ref[0, :, FB : 2 * FB]
    w_out = w_ref[0, :, 2 * FB :]
    gate = nn_dot(x_ref[...], w_gate)
    up = nn_dot(x_ref[...], w_up)
    sig = 1.0 / (1.0 + jnp.exp(-gate))
    silu = gate * sig
    act = (silu * up).astype(jnp.bfloat16)
    res_ref[...] += nt_dot(act, w_out)
    grads_ref[0, :, 2 * FB :] = nn_dot(gt_ref[...], act).astype(jnp.bfloat16)
    d_act = nn_dot(g_ref[...], w_out)
    d_up = (d_act * silu).astype(jnp.bfloat16)
    d_gate = (d_act * up * sig * (1.0 + gate * (1.0 - sig))).astype(jnp.bfloat16)
    dx_ref[...] += nt_dot(d_gate, w_gate) + nt_dot(d_up, w_up)
    grads_ref[0, :, :FB] = nn_dot(xt_ref[...], d_gate).astype(jnp.bfloat16)
    grads_ref[0, :, FB : 2 * FB] = nn_dot(xt_ref[...], d_up).astype(jnp.bfloat16)

    @pl.when(step == pl.num_programs(0) - 1)
    def _():
        width = res_ref.shape[1]
        back_ref[:, :width] = res_ref[...].astype(jnp.bfloat16)
        back_ref[:, width:] = dx_ref[...].astype(jnp.bfloat16)


def run_expert(arrived, weights):
    rows = arrived.shape[0]
    width = arrived.shape[1] // 2
    halves, _, total = weights.shape
    tiles = total // (3 * FB)
    whole = pl.BlockSpec((rows, width), lambda j: (0, 0))
    return pl.pallas_call(
        expert_kernel,
        grid=(halves * tiles,),
        in_specs=[
            pl.BlockSpec((rows, width), lambda j: (0, 0)),
            pl.BlockSpec((rows, width), lambda j: (0, 1)),
            pl.BlockSpec((1, width, 3 * FB), lambda j: (j // tiles, 0, j % tiles)),
        ],
        out_specs=[
            pl.BlockSpec((rows, 2 * width), lambda j: (0, 0)),
            pl.BlockSpec((1, width, 3 * FB), lambda j: (j // tiles, 0, j % tiles)),
        ],
        out_shape=[
            jax.ShapeDtypeStruct((rows, 2 * width), jnp.bfloat16),
            jax.ShapeDtypeStruct(weights.shape, jnp.bfloat16),
        ],
        scratch_shapes=[
            pltpu.VMEM((width, rows), jnp.bfloat16),
            pltpu.VMEM((width, rows), jnp.bfloat16),
            pltpu.VMEM((rows, width), jnp.float32),
            pltpu.VMEM((rows, width), jnp.float32),
        ],
        compiler_params=pltpu.CompilerParams(vmem_limit_bytes=60 << 20),
        cost_estimate=pl.CostEstimate(
            flops=18 * rows * width * total * halves // 3,
            bytes_accessed=4 * weights.size + 8 * rows * width,
            transcendentals=rows * total * halves // 3,
        ),
    )(arrived, arrived, weights)


def query_blocks(length):
    base_rows = BLOCK * max(1, 512 // BLOCK)
    block_count = max(1, min(8, length // base_rows))
    return (block_count, length // block_count)


def allowed_mask(row_start, row_count, key_stop):
    query_block = (row_start + jnp.arange(row_count)) // BLOCK
    key_block = jnp.arange(key_stop) // BLOCK
    return key_block[None, :] <= query_block[:, None]


def special_mix(normed, gate_matrix, value_table, gate_pair, routes, experts):
    const_weights = soft_last(jnp.dot(normed, gate_matrix, precision=PRECISE).reshape(-1, 2, 2))
    constants = (
        const_weights[:, :, 0:1] * normed[:, None, :]
        + const_weights[:, :, 1:2] * value_table.T[None, :, :]
    )
    mixture = jnp.zeros_like(normed)
    for member in range(2):
        route_col = routes[:, member][:, None]
        branch = jnp.where(route_col == experts + 1, normed, 0.0)
        branch = branch + jnp.where(route_col == experts + 2, constants[:, 0], 0.0)
        branch = branch + jnp.where(route_col == experts + 3, constants[:, 1], 0.0)
        mixture = mixture + gate_pair[:, member : member + 1] * branch
    return mixture


def shards(
    hidden,
    prev_logits,
    routes,
    slot_rank,
    dropped,
    cotangent,
    attn_norm,
    ffn_norm,
    w_qkv,
    w_attn_out,
    w_router,
    w_const_gate,
    w_const_value,
    w_expert_in,
    w_expert_out,
):
    own_rows = hidden.shape[0]
    width = hidden.shape[1]
    length = own_rows * lax.axis_size("tp")
    experts = w_expert_in.shape[0]
    route_count = w_router.shape[1]
    capacity = 9 * length // (4 * route_count)
    scaling = HD ** (-0.5)
    blocked = fetch_expert(blocked_weights(w_expert_in, w_expert_out))
    heads_width = w_attn_out.shape[1]
    small = jnp.concatenate(
        [attn_norm[:, None], ffn_norm[:, None], w_router, w_const_gate, w_const_value], axis=1
    )
    small = jnp.pad(small, ((0, 0), (0, 128 - small.shape[1])))
    small = lax.all_gather(small, "tp", axis=0, tiled=True)
    packed_weights = lax.all_gather(
        jnp.concatenate([w_qkv.reshape(-1, 3 * heads_width), w_attn_out, small], axis=1),
        "fsdp",
        axis=0,
        tiled=True,
    )
    qkv_flat = packed_weights[:, : 3 * heads_width]
    attn_full = packed_weights[:, 3 * heads_width : 4 * heads_width]
    small = packed_weights[:, 4 * heads_width :]
    gain_one = small[:, 0].astype(jnp.float32)
    gain_two = small[:, 1].astype(jnp.float32)
    router = small[:, 2 : 2 + route_count]
    router_wide = router.astype(jnp.float32)
    gate_matrix = small[:, 2 + route_count : 6 + route_count].astype(jnp.float32)
    value_table = small[:, 6 + route_count : 8 + route_count].astype(jnp.float32)
    grad_wide = cotangent.astype(jnp.float32)
    cot_other = swap(cotangent)
    kept_own = (routes < experts) & (dropped == 0)
    target_own = jnp.where(kept_own, routes * capacity + slot_rank, -1).T
    target_other = swap(target_own)
    hidden_wide = hidden.astype(jnp.float32)
    normed_one, back_one = jax.vjp(rms_norm, hidden_wide, gain_one)
    stream_one = gather_rows(normed_one.astype(jnp.bfloat16))
    local_heads = heads_width // HD
    projected = jnp.dot(
        stream_one, qkv_flat, preferred_element_type=jnp.float32
    ).reshape(length, 3, local_heads, HD)
    query_pre = projected[:, 0]
    key_pre = projected[:, 1]
    values_all = projected[:, 2].astype(jnp.bfloat16)
    queries = rotate(query_pre).astype(jnp.bfloat16)
    keys_rot = rotate(key_pre).astype(jnp.bfloat16)
    block_count, block_rows = query_blocks(length)
    mixed_parts = []
    log_sums = []
    for block_no in range(block_count):
        row_start = block_no * block_rows
        key_stop = row_start + block_rows
        allowed = allowed_mask(row_start, block_rows, key_stop)
        scores = (
            jnp.einsum(
                "qhd,khd->hqk",
                queries[row_start:key_stop],
                keys_rot[:key_stop],
                preferred_element_type=jnp.float32,
            )
            * scaling
        )
        scores = jnp.where(allowed[None], scores, MASKED_SCORE)
        highest = jnp.max(scores, axis=-1, keepdims=True)
        expanded = jnp.exp(scores - highest)
        totals = jnp.sum(expanded, axis=-1, keepdims=True)
        attn_probs = (expanded / totals).astype(jnp.bfloat16)
        mixed_parts.append(
            jnp.einsum(
                "hqk,khd->qhd",
                attn_probs,
                values_all[:key_stop],
                preferred_element_type=jnp.float32,
            ).astype(jnp.bfloat16)
        )
        log_sums.append(highest + jnp.log(totals))
    mixed = jnp.concatenate(mixed_parts, axis=0).reshape(length, -1)
    attended = sum_rows(
        jnp.einsum("tf,df->td", mixed, attn_full, preferred_element_type=jnp.float32)
    )
    residual_mid = hidden_wide + attended
    normed_two, back_two = jax.vjp(rms_norm, residual_mid, gain_two)
    stream_own = normed_two.astype(jnp.bfloat16)
    logits = jnp.dot(stream_own, router, preferred_element_type=jnp.float32) + prev_logits
    columns = jnp.arange(route_count)
    named = [routes[:, member][:, None] == columns[None, :] for member in range(2)]
    gates_own = soft_last(
        jnp.stack([jnp.sum(jnp.where(hit, logits, 0.0), axis=1) for hit in named], axis=1)
    )
    gates_line = gates_own.T
    gates_other = swap(gates_line)
    stream_other = swap(stream_own)
    half = capacity // 2
    slot = jnp.arange(experts * half)
    slot = (slot // half) * capacity + lax.axis_index("tp") * half + slot % half
    hits_own = [target_own[member][None, :] == slot[:, None] for member in range(2)]
    hits_other = [target_other[member][None, :] == slot[:, None] for member in range(2)]
    send_own = (hits_own[0] | hits_own[1]).astype(jnp.bfloat16)
    send_other = (hits_other[0] | hits_other[1]).astype(jnp.bfloat16)
    slot_gate = sum(
        jnp.sum(jnp.where(hits[member], line[member][None, :], 0.0), axis=1)
        for hits, line in ((hits_own, gates_line), (hits_other, gates_other))
        for member in range(2)
    )
    packed = (nn_dot(send_own, stream_own) + nn_dot(send_other, stream_other)).astype(jnp.bfloat16)
    gated = (
        (nn_dot(send_own, cotangent) + nn_dot(send_other, cot_other)) * slot_gate[:, None]
    ).astype(jnp.bfloat16)
    arrived = exchange(jnp.concatenate([packed, gated], axis=1), experts)
    answer, grads_exp = run_expert(arrived, blocked)
    answer = exchange(answer, experts)
    grads_exp = return_grads(grads_exp, experts)
    slot_result = answer[:, :width].astype(jnp.float32)
    slot_share = jnp.sum(slot_result * gated.astype(jnp.float32), axis=1)
    placed = jnp.concatenate(
        [(slot_result * slot_gate[:, None]).astype(jnp.bfloat16), answer[:, width:]], axis=1
    )

    def token_rows(send):
        return lax.dot_general(
            send, placed, (((0,), (0,)), ((), ())), preferred_element_type=jnp.float32
        )

    def token_share(hits):
        return jnp.stack(
            [jnp.sum(jnp.where(hit, slot_share[:, None], 0.0), axis=0) for hit in hits], axis=0
        )

    mixed_rows = token_rows(send_own) + swap(token_rows(send_other).astype(jnp.bfloat16)).astype(
        jnp.float32
    )
    share = (token_share(hits_own) + swap(token_share(hits_other))).T

    def local_mix(normed, gate_weights, value_weights, gate_pair):
        return special_mix(normed, gate_weights, value_weights, gate_pair, routes, experts)

    special, back_special = jax.vjp(local_mix, normed_two, gate_matrix, value_table, gates_own)
    output = (residual_mid + mixed_rows[:, :width] + special).astype(jnp.bfloat16)
    grad_normed_spec, grad_gate_matrix, grad_value_table, grad_gate_spec = back_special(grad_wide)
    share = share + gates_own * grad_gate_spec
    local_grad = share - gates_own * jnp.sum(share, axis=-1, keepdims=True)
    grad_logit = sum(jnp.where(named[member], local_grad[:, member : member + 1], 0.0) for member in range(2))
    grad_router = lax.dot_general(
        stream_own.astype(jnp.float32),
        grad_logit,
        (((0,), (0,)), ((), ())),
        precision=PRECISE,
        preferred_element_type=jnp.float32,
    )
    grad_normed_two = (
        mixed_rows[:, width:]
        + grad_normed_spec
        + jnp.dot(grad_logit, router_wide.T, precision=PRECISE)
    )
    grad_mid, grad_gain_two = back_two(grad_normed_two)
    grad_mid = grad_mid + grad_wide
    grad_attended = gather_rows(grad_mid.astype(jnp.bfloat16))
    grad_attn_out = jnp.einsum(
        "td,tf->df", grad_attended, mixed, preferred_element_type=jnp.float32
    )
    grad_mixed = (
        jnp.dot(grad_attended, attn_full, preferred_element_type=jnp.float32)
        .astype(jnp.bfloat16)
        .reshape(length, local_heads, HD)
    )
    grad_values = jnp.zeros((length, local_heads, HD), jnp.float32)
    grad_keys = jnp.zeros((length, local_heads, HD), jnp.float32)
    grad_query_parts = []
    for block_no in range(block_count):
        row_start = block_no * block_rows
        key_stop = row_start + block_rows
        allowed = allowed_mask(row_start, block_rows, key_stop)
        scores = (
            jnp.einsum(
                "qhd,khd->hqk",
                queries[row_start:key_stop],
                keys_rot[:key_stop],
                preferred_element_type=jnp.float32,
            )
            * scaling
        )
        recomputed = jnp.where(allowed[None], jnp.exp(scores - log_sums[block_no]), 0.0)
        grad_block = grad_mixed[row_start:key_stop]
        grad_probs = jnp.einsum(
            "qhd,khd->hqk", grad_block, values_all[:key_stop], preferred_element_type=jnp.float32
        )
        grad_values = grad_values.at[:key_stop].add(
            jnp.einsum(
                "hqk,qhd->khd",
                recomputed.astype(jnp.bfloat16),
                grad_block,
                preferred_element_type=jnp.float32,
            )
        )
        grad_scores = (
            recomputed * (grad_probs - jnp.sum(recomputed * grad_probs, axis=-1, keepdims=True))
        ).astype(jnp.bfloat16)
        grad_query_parts.append(
            jnp.einsum(
                "hqk,khd->qhd", grad_scores, keys_rot[:key_stop], preferred_element_type=jnp.float32
            )
            * scaling
        )
        grad_keys = grad_keys.at[:key_stop].add(
            jnp.einsum(
                "hqk,qhd->khd",
                grad_scores,
                queries[row_start:key_stop],
                preferred_element_type=jnp.float32,
            )
            * scaling
        )
    grad_query_pre = jax.vjp(rotate, query_pre)[1](jnp.concatenate(grad_query_parts, axis=0))[0]
    grad_key_pre = jax.vjp(rotate, key_pre)[1](grad_keys)[0]
    grad_projected = (
        jnp.stack([grad_query_pre, grad_key_pre, grad_values], axis=1)
        .astype(jnp.bfloat16)
        .reshape(length, -1)
    )
    grad_qkv = jnp.einsum(
        "td,tf->df", stream_one, grad_projected, preferred_element_type=jnp.float32
    )
    grad_stream_one = jnp.einsum(
        "tf,df->td", grad_projected, qkv_flat, preferred_element_type=jnp.float32
    )
    grad_hidden_one = back_one(sum_rows(grad_stream_one))[0]
    grad_hidden = grad_mid + grad_hidden_one
    grad_small = jnp.concatenate(
        [grad_gain_two[:, None], grad_router, grad_gate_matrix, grad_value_table], axis=1
    )
    grad_small = jnp.pad(grad_small, ((0, 0), (0, 128 - grad_small.shape[1])))
    reduced = lax.psum_scatter(
        jnp.concatenate([grad_qkv, grad_attn_out, grad_small], axis=1).astype(jnp.bfloat16),
        "fsdp",
        scatter_dimension=0,
        tiled=True,
    ).astype(jnp.float32)
    grad_qkv = reduced[:, : 3 * heads_width].reshape(w_qkv.shape)
    grad_attn_out = reduced[:, 3 * heads_width : 4 * heads_width]
    gain_share = jnp.sum(grad_qkv * w_qkv.astype(jnp.float32), axis=(1, 2))
    tail = jnp.concatenate([gain_share[:, None], reduced[:, 4 * heads_width :]], axis=1)
    tail = own_half(tail) + swap(other_half(tail))
    grad_gain_one = tail[:, 0] / attn_norm.astype(jnp.float32)
    grad_gain_two = tail[:, 1]
    grad_router = tail[:, 2 : 2 + route_count]
    grad_gate_matrix = tail[:, 2 + route_count : 6 + route_count]
    grad_value_table = tail[:, 6 + route_count : 8 + route_count]
    grad_in_exp, grad_out_exp = split_grads(grads_exp.astype(jnp.float32))
    return (
        output,
        grad_hidden,
        grad_gain_one,
        grad_gain_two,
        grad_qkv,
        grad_attn_out,
        grad_router,
        grad_gate_matrix,
        grad_value_table,
        grad_in_exp,
        grad_out_exp,
    )


def solution(mesh):
    in_specs = (
        P(("fsdp", "tp"), None),
        P(("fsdp", "tp"), None),
        P(("fsdp", "tp"), None),
        P(("fsdp", "tp"), None),
        P(("fsdp", "tp"), None),
        P(("fsdp", "tp"), None),
        P(("fsdp", "tp")),
        P(("fsdp", "tp")),
        P("fsdp", None, "tp"),
        P("fsdp", "tp"),
        P(("fsdp", "tp"), None),
        P(("fsdp", "tp"), None),
        P(("fsdp", "tp"), None),
        P(None, "fsdp", None, "tp"),
        P(None, "fsdp", "tp"),
    )
    out_specs = (
        P(("fsdp", "tp"), None),
        P(("fsdp", "tp"), None),
        P(("fsdp", "tp")),
        P(("fsdp", "tp")),
        P("fsdp", None, "tp"),
        P("fsdp", "tp"),
        P(("fsdp", "tp"), None),
        P(("fsdp", "tp"), None),
        P(("fsdp", "tp"), None),
        P(None, "fsdp", None, "tp"),
        P(None, "fsdp", "tp"),
    )
    return jax.shard_map(shards, mesh=mesh, in_specs=in_specs, out_specs=out_specs, check_vma=False)
```

```python
import jax
import jax.numpy as jnp
import numpy as np
from jax import lax
from jax.experimental import pallas as pl
from jax.experimental.pallas import tpu as pltpu
from jax.sharding import PartitionSpec as P

HD = 64
BLOCK = 256


EPSILON = 1e-06
MESH = pl.DeviceIdType.MESH
PAIR = 2 * HD
SCALING = HD ** (-0.5)
ROUTER = 2
MIXING = 14
VALUE = 18
ROUTE = 20
TARGET = 22
GATE = 24
COPY = 9


FB = 512


def swap(values):
    return lax.ppermute(values, "tp", [(0, 1), (1, 0)])


def gather_rows(values):
    other = swap(values)
    first = lax.axis_index("tp") == 0
    return jnp.concatenate(
        [jnp.where(first, values, other), jnp.where(first, other, values)], axis=0
    )


def own_half(values):
    half = values.shape[0] // 2
    return lax.dynamic_slice_in_dim(values, lax.axis_index("tp") * half, half, 0)


def other_half(values):
    half = values.shape[0] // 2
    return lax.dynamic_slice_in_dim(values, (1 - lax.axis_index("tp")) * half, half, 0)


def gather_columns(values):
    other = swap(values)
    first = lax.axis_index("tp") == 0
    return jnp.concatenate(
        [jnp.where(first, values, other), jnp.where(first, other, values)], axis=1
    )


def member_groups(size, experts):
    span = 2 * experts
    starts = range(0, size, span)
    same_core = [[start + 2 * e + c for e in range(experts)] for start in starts for c in range(2)]
    cores = [[start + 2 * e, start + 2 * e + 1] for start in starts for e in range(experts)]
    whole = [[start + r for r in range(span)] for start in starts]
    across = [[start + r for start in starts] for r in range(span)]
    return same_core, cores, whole, across


def blocked_weights(w_expert_in, w_expert_out):
    experts, rows, _, hidden = w_expert_in.shape
    tiles = hidden // FB
    both = jnp.concatenate(
        [
            w_expert_in.reshape(experts, rows, 2, tiles, FB),
            w_expert_out.reshape(experts, rows, 1, tiles, FB),
        ],
        axis=2,
    )
    return both.transpose(0, 1, 3, 2, 4).reshape(experts, rows, 3 * hidden)


def split_grads(blocked):
    experts, rows, total = blocked.shape
    hidden = total // 3
    tiles = hidden // FB
    parts = blocked.reshape(experts, rows, tiles, 3, FB).transpose(0, 1, 3, 2, 4)
    return (
        parts[:, :, :2].reshape(experts, rows, 2, hidden),
        parts[:, :, 2].reshape(experts, rows, hidden),
    )


def fetch_expert(blocked):
    experts = blocked.shape[0]
    size = lax.axis_size("fsdp")
    same_core, cores, _, across = member_groups(size, experts)
    got = lax.all_to_all(blocked, "fsdp", 0, 0, axis_index_groups=same_core, tiled=True)
    got = lax.all_gather(got, "fsdp", axis=1, axis_index_groups=cores, tiled=True)
    got = got.reshape(-1, got.shape[-1])
    if size > 2 * experts:
        got = lax.all_gather(got, "fsdp", axis=0, axis_index_groups=across, tiled=True)
    return lax.all_gather(got, "tp", axis=0)


def return_grads(grads, experts):
    size = lax.axis_size("fsdp")
    same_core, cores, _, across = member_groups(size, experts)
    columns = grads.shape[-1]
    if size > 2 * experts:
        grads = lax.psum_scatter(
            grads, "fsdp", scatter_dimension=1, axis_index_groups=across, tiled=True
        )
    grads = grads.reshape(2, experts, -1, columns)
    grads = lax.psum_scatter(
        grads, "fsdp", scatter_dimension=2, axis_index_groups=cores, tiled=True
    )
    grads = lax.psum_scatter(grads, "tp", scatter_dimension=0)
    return lax.all_to_all(grads, "fsdp", 0, 0, axis_index_groups=same_core, tiled=True)


def exchange(values, experts):
    whole = member_groups(lax.axis_size("fsdp"), experts)[2]
    return lax.all_to_all(values, "fsdp", 0, 0, axis_index_groups=whole, tiled=True)


def nt_dot(left, right):
    return lax.dot_general(left, right, (((1,), (1,)), ((), ())), preferred_element_type=jnp.float32)


def nn_dot(left, right):
    return jnp.dot(left, right, preferred_element_type=jnp.float32)


def expert_kernel(x_ref, g_ref, w_ref, back_ref, grads_ref, xt_ref, gt_ref, res_ref, dx_ref):
    step = pl.program_id(0)

    @pl.when(step == 0)
    def _():
        xt_ref[...] = x_ref[...].T
        gt_ref[...] = g_ref[...].T
        res_ref[...] = jnp.zeros_like(res_ref)
        dx_ref[...] = jnp.zeros_like(dx_ref)

    w_gate = w_ref[0, :, :FB]
    w_up = w_ref[0, :, FB : 2 * FB]
    w_out = w_ref[0, :, 2 * FB :]
    gate = nn_dot(x_ref[...], w_gate)
    up = nn_dot(x_ref[...], w_up)
    sig = 1.0 / (1.0 + jnp.exp(-gate))
    silu = gate * sig
    act = (silu * up).astype(jnp.bfloat16)
    res_ref[...] += nt_dot(act, w_out)
    grads_ref[0, :, 2 * FB :] = nn_dot(gt_ref[...], act).astype(jnp.bfloat16)
    d_act = nn_dot(g_ref[...], w_out)
    d_up = (d_act * silu).astype(jnp.bfloat16)
    d_gate = (d_act * up * sig * (1.0 + gate * (1.0 - sig))).astype(jnp.bfloat16)
    dx_ref[...] += nt_dot(d_gate, w_gate) + nt_dot(d_up, w_up)
    grads_ref[0, :, :FB] = nn_dot(xt_ref[...], d_gate).astype(jnp.bfloat16)
    grads_ref[0, :, FB : 2 * FB] = nn_dot(xt_ref[...], d_up).astype(jnp.bfloat16)

    @pl.when(step == pl.num_programs(0) - 1)
    def _():
        width = res_ref.shape[1]
        back_ref[:, :width] = res_ref[...].astype(jnp.bfloat16)
        back_ref[:, width:] = dx_ref[...].astype(jnp.bfloat16)


def run_expert(arrived, weights):
    rows = arrived.shape[0]
    width = arrived.shape[1] // 2
    halves, _, total = weights.shape
    tiles = total // (3 * FB)
    return pl.pallas_call(
        expert_kernel,
        grid=(halves * tiles,),
        in_specs=[
            pl.BlockSpec((rows, width), lambda j: (0, 0)),
            pl.BlockSpec((rows, width), lambda j: (0, 1)),
            pl.BlockSpec((1, width, 3 * FB), lambda j: (j // tiles, 0, j % tiles)),
        ],
        out_specs=[
            pl.BlockSpec((rows, 2 * width), lambda j: (0, 0)),
            pl.BlockSpec((1, width, 3 * FB), lambda j: (j // tiles, 0, j % tiles)),
        ],
        out_shape=[
            jax.ShapeDtypeStruct((rows, 2 * width), jnp.bfloat16),
            jax.ShapeDtypeStruct(weights.shape, jnp.bfloat16),
        ],
        scratch_shapes=[
            pltpu.VMEM((width, rows), jnp.bfloat16),
            pltpu.VMEM((width, rows), jnp.bfloat16),
            pltpu.VMEM((rows, width), jnp.float32),
            pltpu.VMEM((rows, width), jnp.float32),
        ],
        compiler_params=pltpu.CompilerParams(vmem_limit_bytes=60 << 20),
        cost_estimate=pl.CostEstimate(
            flops=18 * rows * width * total * halves // 3,
            bytes_accessed=4 * weights.size + 8 * rows * width,
            transcendentals=rows * total * halves // 3,
        ),
    )(arrived, arrived, weights)


def tn_dot(left, right):
    return lax.dot_general(left, right, (((0,), (0,)), ((), ())), preferred_element_type=jnp.float32)


def low(values):
    return values.astype(jnp.bfloat16)


def wide(values):
    return values.astype(jnp.float32)


def rotary_tables(length):
    half = HD // 2
    positions = np.arange(length, dtype=np.float32)
    inverse = np.power(np.float32(10000.0), -np.arange(half, dtype=np.float32) / np.float32(half))
    angles = (positions[:, None] * inverse[None, :].astype(np.float32)).astype(np.float32)
    cosine = np.cos(angles.astype(np.float64)).astype(np.float32)
    sine = np.sin(angles.astype(np.float64)).astype(np.float32)
    return (
        np.concatenate([cosine] * 4, axis=1),
        np.concatenate([-sine, sine, -sine, sine], axis=1),
    )


def turn(values, cosine, sine):
    lane = lax.broadcasted_iota(jnp.int32, values.shape, 1)
    upper = lax.rem(lane, HD) >= HD // 2
    partner = jnp.where(
        upper, pltpu.roll(values, HD // 2, 1), pltpu.roll(values, PAIR - HD // 2, 1)
    )
    return values * cosine + partner * sine


def head_lanes(shape, half, axis):
    return (lax.broadcasted_iota(jnp.int32, shape, axis) >= HD) == bool(half)


def mean_last(values):
    return jnp.mean(values, axis=-1, keepdims=True)


def greet_partner():
    partner = 1 - lax.axis_index("tp")
    barrier = pltpu.get_barrier_semaphore()
    pl.semaphore_signal(barrier, inc=1, device_id={"tp": partner}, device_id_type=MESH)
    pl.semaphore_wait(barrier, 1)


def to_partner(source, target, send_sem, recv_sem):
    return pltpu.make_async_remote_copy(
        src_ref=source,
        dst_ref=target,
        send_sem=send_sem,
        recv_sem=recv_sem,
        device_id={"tp": 1 - lax.axis_index("tp")},
        device_id_type=MESH,
    )


def block_rows(block):
    return slice(block * BLOCK, (block + 1) * BLOCK)


def column(values, index):
    return values[:, index : index + 1]


def lane_matrix(shape, columns):
    lane = lax.broadcasted_iota(jnp.int32, shape, 1)
    total = jnp.zeros(shape, jnp.float32)
    for index, values in columns:
        total = jnp.where(lane == index, values, total)
    return total


def forward_kernel(
    hid_ref,
    tok_in_ref,
    wqkv_ref,
    wout_ref,
    small_ref,
    rows_ref,
    cos_ref,
    sin_ref,
    s1_ref,
    qkv_ref,
    lse_ref,
    mixed_ref,
    mid_ref,
    s2_ref,
    tok_ref,
    vt_ref,
    send_ref,
    recv_ref,
    send_sem,
    recv_sem,
):
    greet_partner()
    blocks = hid_ref.shape[0] // BLOCK
    heads_width = wout_ref.shape[1]
    pairs = heads_width // PAIR
    gain_one = rows_ref[0:1, :]
    gain_two = rows_ref[1:2, :]
    copies = []
    lse_ref[...] = jnp.zeros_like(lse_ref)
    for block in range(blocks):
        rows = block_rows(block)
        keys = (block + 1) * BLOCK
        source = wide(hid_ref[rows, :])
        s1 = low(source * lax.rsqrt(mean_last(source * source) + EPSILON) * gain_one)
        s1_ref[rows, :] = s1
        cosine, sine = cos_ref[rows, :], sin_ref[rows, :]
        for part in range(3):
            projected = nn_dot(s1, wqkv_ref[:, part * heads_width : (part + 1) * heads_width])
            for pair in range(pairs):
                chunk = projected[:, pair * PAIR : (pair + 1) * PAIR]
                if part < 2:
                    chunk = turn(chunk, cosine, sine)
                else:
                    vt_ref[pair * PAIR : (pair + 1) * PAIR, rows] = low(chunk.T)
                start = part * heads_width + pair * PAIR
                qkv_ref[rows, start : start + PAIR] = low(chunk)
        for pair in range(pairs):
            lanes = slice(pair * PAIR, (pair + 1) * PAIR)
            query = qkv_ref[rows, lanes] * jnp.bfloat16(SCALING)
            key = qkv_ref[:keys, heads_width + pair * PAIR : heads_width + (pair + 1) * PAIR]
            value_t = vt_ref[lanes, :keys]
            gathered = None
            for half in range(2):
                masked = jnp.where(head_lanes(query.shape, half, 1), query, jnp.bfloat16(0))
                scores = nt_dot(key, masked)
                highest = jnp.max(scores, axis=0, keepdims=True)
                expanded = jnp.exp(scores - highest)
                totals = jnp.sum(expanded, axis=0, keepdims=True)
                probs = low(expanded * (1.0 / totals))
                lse_ref[2 * pair + half : 2 * pair + half + 1, rows] = highest + jnp.log(totals)
                found = nn_dot(value_t, probs)
                gathered = (
                    found
                    if half == 0
                    else jnp.where(head_lanes(found.shape, 1, 0), found, gathered)
                )
            mixed_ref[rows, lanes] = low(gathered.T)
        send_ref[block] = low(nt_dot(mixed_ref[rows, :], wout_ref[...]))
        copy = to_partner(
            send_ref.at[block], recv_ref.at[block], send_sem.at[block], recv_sem.at[block]
        )
        copy.start()
        copies.append(copy)
    for block in range(blocks):
        rows = block_rows(block)
        copies[block].wait()
        mid = wide(hid_ref[rows, :]) + (wide(send_ref[block]) + wide(recv_ref[block]))
        mid_ref[rows, :] = mid
        s2 = low(mid * lax.rsqrt(mean_last(mid * mid) + EPSILON) * gain_two)
        s2_ref[rows, :] = s2
        tok = tok_in_ref[rows, :]
        lane = lax.broadcasted_iota(jnp.int32, tok.shape, 1)
        logits = nn_dot(s2, small_ref[...]) + tok
        picked = [
            jnp.sum(
                jnp.where(wide(lane - ROUTER) == column(tok, ROUTE + member), logits, 0.0),
                axis=1,
                keepdims=True,
            )
            for member in range(2)
        ]
        gate = [
            1.0 / (1.0 + jnp.exp(picked[1 - member] - picked[member])) for member in range(2)
        ]
        tok_ref[rows, :] = jnp.where(
            lane == GATE, gate[0], jnp.where(lane == GATE + 1, gate[1], tok)
        )


def backward_kernel(
    dx_ref,
    pres_ref,
    slot_ref,
    tok_ref,
    cot_ref,
    mid_ref,
    s1_ref,
    qkv_ref,
    lse_ref,
    mixed_ref,
    wqkv_ref,
    wout_ref,
    small_ref,
    rows_ref,
    cos_ref,
    sin_ref,
    own_ref,
    grad_ref,
    base_ref,
    other_ref,
    big_ref,
    gsend_ref,
    grecv_ref,
    hsend_ref,
    hrecv_ref,
    gmid_ref,
    gown_ref,
    kt_ref,
    gm_ref,
    dqt_ref,
    dk_ref,
    dv_ref,
    gp_ref,
    acc_qkv_ref,
    acc_out_ref,
    acc_small_ref,
    acc_gain_ref,
    gsend_sem,
    grecv_sem,
    hsend_sem,
    hrecv_sem,
):
    greet_partner()
    tp = lax.axis_index("tp")
    width = dx_ref.shape[1]
    blocks = cot_ref.shape[0] // BLOCK
    heads_width = wout_ref.shape[1]
    pairs = heads_width // PAIR
    gain_one = rows_ref[0:1, :]
    gain_two = rows_ref[1:2, :]
    slot_row = slot_ref[1:2, :]
    share_row = slot_ref[0:1, :]
    order = list(reversed(range(blocks)))
    first = order[0]
    gcopies = {}
    for block in order:
        rows = block_rows(block)
        tok = tok_ref[rows, :]
        hits = [column(tok, TARGET + member) == slot_row for member in range(2)]
        onehot = low(jnp.where(hits[0] | hits[1], 1.0, 0.0))
        shares = [
            jnp.sum(jnp.where(hit, share_row, 0.0), axis=1, keepdims=True) for hit in hits
        ]
        high = [wide(low(share)) for share in shares]
        gsend_ref[block, :, :width] = low(nn_dot(onehot, dx_ref[...]))
        gsend_ref[block, :, width:] = low(
            lane_matrix(
                tok.shape,
                [
                    (0, high[0]),
                    (1, shares[0] - high[0]),
                    (2, high[1]),
                    (3, shares[1] - high[1]),
                ],
            )
        )
        copy = to_partner(
            gsend_ref.at[block], grecv_ref.at[block], gsend_sem.at[block], grecv_sem.at[block]
        )
        copy.start()
        gcopies[block] = copy
        placed = nn_dot(onehot, pres_ref[...])
        slab = slice((block % 2) * BLOCK, (block % 2 + 1) * BLOCK)

        @pl.when(tp == block // 2)
        def _():
            base_ref[slab, :] = placed

        @pl.when(tp != block // 2)
        def _():
            other_ref[slab, :] = low(placed)

    kt_ref[...] = qkv_ref[:, heads_width : 2 * heads_width].T
    for block in order:
        rows = block_rows(block)
        keys = (block + 1) * BLOCK
        slab = slice((block % 2) * BLOCK, (block % 2 + 1) * BLOCK)
        mine = tp == block // 2
        mine_f = jnp.where(mine, 1.0, 0.0)
        mid = mid_ref[rows, :]
        cot = cot_ref[rows, :]
        cot_wide = wide(cot)
        tok = tok_ref[rows, :]
        scale = lax.rsqrt(mean_last(mid * mid) + EPSILON)
        unit = mid * scale
        normed = unit * gain_two
        s2 = low(normed)
        small = small_ref[...]
        mixing = nn_dot(s2, small)
        value_dot = nn_dot(cot, small)
        normed_dot = jnp.sum(normed * cot_wide, axis=1, keepdims=True)
        route = [column(tok, ROUTE + member) for member in range(2)]
        gate = [column(tok, GATE + member) for member in range(2)]

        def weight_of(expert):
            return sum(jnp.where(route[m] == expert, gate[m], 0.0) for m in range(2))

        copy_weight = weight_of(COPY)
        copy_share = [jnp.where(route[m] == COPY, normed_dot, 0.0) for m in range(2)]
        alpha = copy_weight
        columns = []
        value_columns = []
        for c in range(2):
            weight = weight_of(COPY + 1 + c)
            left = column(mixing, MIXING + 2 * c)
            right = column(mixing, MIXING + 2 * c + 1)
            a0 = 1.0 / (1.0 + jnp.exp(right - left))
            a1 = 1.0 / (1.0 + jnp.exp(left - right))
            vd = column(value_dot, VALUE + c)
            alpha = alpha + weight * a0
            for m in range(2):
                copy_share[m] = copy_share[m] + jnp.where(
                    route[m] == COPY + 1 + c, a0 * normed_dot + a1 * vd, 0.0
                )
            slope = a0 * a1 * weight * (normed_dot - vd)
            columns.append((MIXING + 2 * c, slope))
            columns.append((MIXING + 2 * c + 1, -slope))
            value_columns.append((VALUE + c, weight * a1))
        value_matrix = lane_matrix(tok.shape, value_columns)
        base = mid + alpha * normed + nt_dot(low(value_matrix), small)

        @pl.when(mine)
        def _():
            base_ref[slab, :] += base

        gcopies[block].wait()
        extra = wide(gsend_ref[block, :, width:]) + wide(grecv_ref[block, :, width:])
        share = [
            column(extra, 2 * m) + column(extra, 2 * m + 1) + gate[m] * copy_share[m]
            for m in range(2)
        ]
        lane = lax.broadcasted_iota(jnp.int32, tok.shape, 1)
        slopes = lane_matrix(tok.shape, columns)
        for m in range(2):
            local = share[m] - gate[m] * (share[0] + share[1])
            slopes = slopes + jnp.where(wide(lane - ROUTER) == route[m], local, 0.0)
        slopes_low = low(slopes)
        grad_normed = (
            wide(gsend_ref[block, :, :width])
            + wide(grecv_ref[block, :, :width])
            + alpha * cot_wide
            + nt_dot(slopes_low, small)
        )
        small_grad = tn_dot(s2, low(slopes * mine_f)) + tn_dot(cot, low(value_matrix * mine_f))
        gain_grad = jnp.sum(unit * grad_normed, axis=0, keepdims=True) * mine_f
        scaled = grad_normed * gain_two
        grad_mid = cot_wide + scale * (scaled - unit * mean_last(scaled * unit))
        gmid_ref[rows, :] = grad_mid
        attended = low(grad_mid)
        out_grad = tn_dot(attended, mixed_ref[rows, :])
        gm_ref[...] = low(nn_dot(attended, wout_ref[...]))
        if block == first:
            acc_small_ref[...] = small_grad
            acc_gain_ref[...] = jnp.broadcast_to(gain_grad, acc_gain_ref.shape)
            acc_out_ref[...] = out_grad
        else:
            acc_small_ref[...] += small_grad
            acc_gain_ref[...] += jnp.broadcast_to(gain_grad, acc_gain_ref.shape)
            acc_out_ref[...] += out_grad
        cosine, sine = cos_ref[rows, :], sin_ref[rows, :]

        def one_pair(pair, carry):
            start = pl.multiple_of(pair * PAIR, PAIR)
            lanes = pl.ds(start, PAIR)
            key_lanes = pl.ds(pl.multiple_of(heads_width + start, PAIR), PAIR)
            value_lanes = pl.ds(pl.multiple_of(2 * heads_width + start, PAIR), PAIR)
            query = qkv_ref[rows, lanes] * jnp.bfloat16(SCALING)
            key = qkv_ref[:keys, key_lanes]
            value = qkv_ref[:keys, value_lanes]
            grad_out = gm_ref[:, lanes]
            key_t = kt_ref[lanes, :keys]
            grad_value = None
            for half in range(2):
                keep = head_lanes(query.shape, half, 1)
                q_half = jnp.where(keep, query, jnp.bfloat16(0))
                g_half = jnp.where(keep, grad_out, jnp.bfloat16(0))
                probs = jnp.exp(nt_dot(key, q_half) - lse_ref[pl.ds(2 * pair + half, 1), rows])
                grad_probs = nt_dot(value, g_half)
                inner = jnp.sum(probs * grad_probs, axis=0, keepdims=True)
                grad_scores = low(probs * (grad_probs - inner))
                value_part = nn_dot(low(probs), g_half)
                key_part = nn_dot(grad_scores, q_half)
                query_part = nn_dot(key_t, grad_scores)
                if half == 0:
                    grad_value, grad_key, grad_query = value_part, key_part, query_part
                else:
                    grad_value = grad_value + value_part
                    grad_key = grad_key + key_part
                    grad_query = jnp.where(
                        head_lanes(query_part.shape, 1, 0), query_part, grad_query
                    )
            if block == first:
                dv_ref[:keys, lanes] = grad_value
                dk_ref[:keys, lanes] = grad_key
            else:
                dv_ref[:keys, lanes] += grad_value
                dk_ref[:keys, lanes] += grad_key
            gp_ref[:, lanes] = low(turn(grad_query.T * SCALING, cosine, -sine))
            gp_ref[:, key_lanes] = low(turn(dk_ref[rows, lanes], cosine, -sine))
            gp_ref[:, value_lanes] = low(dv_ref[rows, lanes])
            return carry

        lax.fori_loop(0, pairs, one_pair, 0)
        gp = gp_ref[...]
        qkv_grad = tn_dot(s1_ref[rows, :], gp)
        if block == first:
            acc_qkv_ref[...] = qkv_grad
        else:
            acc_qkv_ref[...] += qkv_grad
        stream_grad = nt_dot(gp, wqkv_ref[...])

        @pl.when(mine)
        def _():
            gown_ref[block % 2] = stream_grad

        @pl.when(jnp.logical_not(mine))
        def _():
            hsend_ref[block % 2] = low(stream_grad)
            to_partner(
                hsend_ref.at[block % 2],
                hrecv_ref.at[block % 2],
                hsend_sem.at[block % 2],
                hrecv_sem.at[block % 2],
            ).start()

    big_ref[:, : 3 * heads_width] = low(acc_qkv_ref[...])
    big_ref[:, 3 * heads_width : 4 * heads_width] = low(acc_out_ref[...])
    gain_rows = acc_gain_ref[0:1, :]
    tall = jnp.where(
        lax.broadcasted_iota(jnp.int32, (PAIR, width), 0) == 1,
        jnp.broadcast_to(gain_rows, (PAIR, width)),
        0.0,
    )
    big_ref[:, 4 * heads_width :] = low(acc_small_ref[...] + tall.T)
    for slot in reversed(range(2)):
        slab = slice(slot * BLOCK, (slot + 1) * BLOCK)
        to_partner(
            hsend_ref.at[slot], hrecv_ref.at[slot], hsend_sem.at[slot], hrecv_sem.at[slot]
        ).wait()
        source = wide(own_ref[slab, :])
        scale = lax.rsqrt(mean_last(source * source) + EPSILON)
        unit = source * scale
        scaled = (gown_ref[slot] + wide(hrecv_ref[slot])) * gain_one
        mid_rows = pl.ds(pl.multiple_of(tp * 2 * BLOCK + slot * BLOCK, BLOCK), BLOCK)
        grad_ref[slab, :] = gmid_ref[mid_rows, :] + scale * (
            scaled - unit * mean_last(scaled * unit)
        )


def run_forward(hid, tok, wqkv, wout, small, rows, cosine, sine):
    length, width = hid.shape
    heads_width = wout.shape[1]
    blocks = length // BLOCK
    vmem = pl.BlockSpec(memory_space=pltpu.VMEM)
    low_t, wide_t = jnp.bfloat16, jnp.float32
    return pl.pallas_call(
        forward_kernel,
        in_specs=[vmem] * 8,
        out_specs=[vmem] * 7,
        out_shape=[
            jax.ShapeDtypeStruct((length, width), low_t),
            jax.ShapeDtypeStruct((length, 3 * heads_width), low_t),
            jax.ShapeDtypeStruct((8, length), wide_t),
            jax.ShapeDtypeStruct((length, heads_width), low_t),
            jax.ShapeDtypeStruct((length, width), wide_t),
            jax.ShapeDtypeStruct((length, width), low_t),
            jax.ShapeDtypeStruct((length, PAIR), wide_t),
        ],
        scratch_shapes=[
            pltpu.VMEM((heads_width, length), low_t),
            pltpu.VMEM((blocks, BLOCK, width), low_t),
            pltpu.VMEM((blocks, BLOCK, width), low_t),
            pltpu.SemaphoreType.DMA((blocks,)),
            pltpu.SemaphoreType.DMA((blocks,)),
        ],
        compiler_params=pltpu.CompilerParams(
            collective_id=0, has_side_effects=True, vmem_limit_bytes=60 << 20
        ),
    )(hid, tok, wqkv, wout, small, rows, cosine, sine)


def run_backward(*operands):
    dx, tok, cot, own, wout = operands[0], operands[3], operands[4], operands[16], operands[11]
    length, width = cot.shape
    heads_width = wout.shape[1]
    blocks = length // BLOCK
    own_rows = own.shape[0]
    vmem = pl.BlockSpec(memory_space=pltpu.VMEM)
    low_t, wide_t = jnp.bfloat16, jnp.float32
    dma = pltpu.SemaphoreType.DMA
    return pl.pallas_call(
        backward_kernel,
        in_specs=[vmem] * 17,
        out_specs=[vmem] * 4,
        out_shape=[
            jax.ShapeDtypeStruct((own_rows, width), wide_t),
            jax.ShapeDtypeStruct((own_rows, width), wide_t),
            jax.ShapeDtypeStruct((own_rows, width), low_t),
            jax.ShapeDtypeStruct((width, 4 * heads_width + PAIR), low_t),
        ],
        scratch_shapes=[
            pltpu.VMEM((blocks, BLOCK, width + PAIR), low_t),
            pltpu.VMEM((blocks, BLOCK, width + PAIR), low_t),
            pltpu.VMEM((2, BLOCK, width), low_t),
            pltpu.VMEM((2, BLOCK, width), low_t),
            pltpu.VMEM((length, width), wide_t),
            pltpu.VMEM((2, BLOCK, width), wide_t),
            pltpu.VMEM((heads_width, length), low_t),
            pltpu.VMEM((BLOCK, heads_width), low_t),
            pltpu.VMEM((PAIR, BLOCK), wide_t),
            pltpu.VMEM((length, heads_width), wide_t),
            pltpu.VMEM((length, heads_width), wide_t),
            pltpu.VMEM((BLOCK, 3 * heads_width), low_t),
            pltpu.VMEM((width, 3 * heads_width), wide_t),
            pltpu.VMEM((width, heads_width), wide_t),
            pltpu.VMEM((width, PAIR), wide_t),
            pltpu.VMEM((8, width), wide_t),
            dma((blocks,)),
            dma((blocks,)),
            dma((2,)),
            dma((2,)),
        ],
        compiler_params=pltpu.CompilerParams(
            collective_id=1, has_side_effects=True, vmem_limit_bytes=60 << 20
        ),
    )(*operands)


def shards(
    hidden,
    prev_logits,
    routes,
    slot_rank,
    dropped,
    cotangent,
    attn_norm,
    ffn_norm,
    w_qkv,
    w_attn_out,
    w_router,
    w_const_gate,
    w_const_value,
    w_expert_in,
    w_expert_out,
):
    own_rows, width = hidden.shape
    length = own_rows * lax.axis_size("tp")
    experts = w_expert_in.shape[0]
    route_count = w_router.shape[1]
    capacity = 9 * length // (4 * route_count)
    blocked = fetch_expert(blocked_weights(w_expert_in, w_expert_out))
    heads_width = w_attn_out.shape[1]
    small = jnp.concatenate(
        [attn_norm[:, None], ffn_norm[:, None], w_router, w_const_gate, w_const_value], axis=1
    )
    small = jnp.pad(small, ((0, 0), (0, PAIR - small.shape[1])))
    small = lax.all_gather(small, "tp", axis=0, tiled=True)
    packed_weights = lax.all_gather(
        jnp.concatenate([w_qkv.reshape(-1, 3 * heads_width), w_attn_out, small], axis=1),
        "fsdp",
        axis=0,
        tiled=True,
    )
    wqkv = packed_weights[:, : 3 * heads_width]
    wout = packed_weights[:, 3 * heads_width : 4 * heads_width]
    small = packed_weights[:, 4 * heads_width :]
    rows = small[:, :8].T.astype(jnp.float32)
    cosine, sine = (jnp.asarray(table) for table in rotary_tables(length))
    kept = (routes < experts) & (dropped == 0)
    target = jnp.where(kept, routes * capacity + slot_rank, -1)
    tok = jnp.concatenate(
        [prev_logits.T, wide(routes).T, wide(target).T], axis=0
    )
    tok = gather_columns(tok)
    tok = jnp.concatenate(
        [
            jnp.zeros((ROUTER, length), jnp.float32),
            tok[:route_count],
            jnp.zeros((ROUTE - ROUTER - route_count, length), jnp.float32),
            tok[route_count:],
            jnp.zeros((PAIR - ROUTE - 4, length), jnp.float32),
        ],
        axis=0,
    ).T
    hid = gather_rows(hidden)
    cot = gather_rows(cotangent)
    s1, qkv, lse, mixed, mid, s2, tok = run_forward(
        hid, tok, wqkv, wout, small, rows, cosine, sine
    )
    half = capacity // 2
    slot = jnp.arange(experts * half)
    slot = (slot // half) * capacity + lax.axis_index("tp") * half + slot % half
    lines = tok[:, TARGET : TARGET + 4].T
    hits = [lines[member][None, :] == wide(slot)[:, None] for member in range(2)]
    dispatch = low(hits[0] | hits[1])
    slot_gate = sum(
        jnp.sum(jnp.where(hits[member], lines[2 + member][None, :], 0.0), axis=1)
        for member in range(2)
    )
    packed = low(nn_dot(dispatch, s2))
    gated = low(nn_dot(dispatch, cot) * slot_gate[:, None])
    arrived = exchange(jnp.concatenate([packed, gated], axis=1), experts)
    answer, grads_exp = run_expert(arrived, blocked)
    answer = exchange(answer, experts)
    grads_exp = return_grads(grads_exp, experts)
    slot_result = wide(answer[:, :width])
    slot_share = jnp.sum(slot_result * wide(gated), axis=1)
    slot_rows = jnp.concatenate(
        [slot_share[None, :], wide(slot)[None, :], jnp.zeros((6, slot.shape[0]), jnp.float32)],
        axis=0,
    )
    grad_hidden, base, for_other, big = run_backward(
        answer[:, width:],
        low(slot_result * slot_gate[:, None]),
        slot_rows,
        tok,
        cot,
        mid,
        s1,
        qkv,
        lse,
        mixed,
        wqkv,
        wout,
        small,
        rows,
        cosine,
        sine,
        hidden,
    )
    output = low(base + wide(swap(for_other)))
    reduced = wide(lax.psum_scatter(big, "fsdp", scatter_dimension=0, tiled=True))
    grad_qkv = reduced[:, : 3 * heads_width].reshape(w_qkv.shape)
    grad_attn_out = reduced[:, 3 * heads_width : 4 * heads_width]
    gain_share = jnp.sum(grad_qkv * wide(w_qkv), axis=(1, 2))
    last = jnp.concatenate([gain_share[:, None], reduced[:, 4 * heads_width + 1 :]], axis=1)
    last = own_half(last) + swap(other_half(last))
    grad_in_exp, grad_out_exp = split_grads(wide(grads_exp))
    return (
        output,
        grad_hidden,
        last[:, 0] / wide(attn_norm),
        last[:, 1],
        grad_qkv,
        grad_attn_out,
        last[:, ROUTER:MIXING],
        last[:, MIXING:VALUE],
        last[:, VALUE : VALUE + 2],
        grad_in_exp,
        grad_out_exp,
    )


def solution(mesh):
    in_specs = (
        P(("fsdp", "tp"), None),
        P(("fsdp", "tp"), None),
        P(("fsdp", "tp"), None),
        P(("fsdp", "tp"), None),
        P(("fsdp", "tp"), None),
        P(("fsdp", "tp"), None),
        P(("fsdp", "tp")),
        P(("fsdp", "tp")),
        P("fsdp", None, "tp"),
        P("fsdp", "tp"),
        P(("fsdp", "tp"), None),
        P(("fsdp", "tp"), None),
        P(("fsdp", "tp"), None),
        P(None, "fsdp", None, "tp"),
        P(None, "fsdp", "tp"),
    )
    out_specs = (
        P(("fsdp", "tp"), None),
        P(("fsdp", "tp"), None),
        P(("fsdp", "tp")),
        P(("fsdp", "tp")),
        P("fsdp", None, "tp"),
        P("fsdp", "tp"),
        P(("fsdp", "tp"), None),
        P(("fsdp", "tp"), None),
        P(("fsdp", "tp"), None),
        P(None, "fsdp", None, "tp"),
        P(None, "fsdp", "tp"),
    )
    return jax.shard_map(shards, mesh=mesh, in_specs=in_specs, out_specs=out_specs, check_vma=False)
```

```python
import jax
import jax.numpy as jnp
import numpy as np
from jax import lax
from jax.experimental import pallas as pl
from jax.experimental.pallas import tpu as pltpu
from jax.sharding import PartitionSpec as P

HD = 64
BLOCK = 256


EPSILON = 1e-06
MESH = pl.DeviceIdType.MESH
PAIR = 2 * HD
SCALING = HD ** (-0.5)
ROUTER = 2
MIXING = 14
VALUE = 18
ROUTE = 20
TARGET = 24
GATE = 26
COPY = 9


TILE = 256


def swap(values):
    return lax.ppermute(values, "tp", [(0, 1), (1, 0)])


def gather_rows(values):
    other = swap(values)
    first = lax.axis_index("tp") == 0
    return jnp.concatenate(
        [jnp.where(first, values, other), jnp.where(first, other, values)], axis=0
    )


def own_half(values):
    half = values.shape[0] // 2
    return lax.dynamic_slice_in_dim(values, lax.axis_index("tp") * half, half, 0)


def other_half(values):
    half = values.shape[0] // 2
    return lax.dynamic_slice_in_dim(values, (1 - lax.axis_index("tp")) * half, half, 0)


def member_groups(size, experts):
    span = 2 * experts
    starts = range(0, size, span)
    cores = [[start + 2 * e, start + 2 * e + 1] for start in starts for e in range(experts)]
    across = [[start + r for start in starts] for r in range(span)]
    return cores, across


def own_core(values, rows):
    parts = values.reshape(-1, 2, rows, values.shape[-1])
    return lax.dynamic_index_in_dim(parts, lax.axis_index("fsdp") % 2, 1, keepdims=False)


def join_weights(got, experts):
    size = lax.axis_size("fsdp")
    if size == 2 * experts:
        return got
    cores, across = member_groups(size, experts)
    got = lax.all_gather(got, "fsdp", axis=1, axis_index_groups=cores, tiled=True)
    got = got.reshape(-1, got.shape[-1])
    got = lax.all_gather(got, "fsdp", axis=0, axis_index_groups=across, tiled=True)
    return own_core(got, got.shape[0] // (2 * experts))


def split_grads(grads):
    experts, _, columns = grads.shape
    size = lax.axis_size("fsdp")
    if size == 2 * experts:
        return grads
    cores, across = member_groups(size, experts)
    grads = lax.all_gather(grads[:, None], "fsdp", axis=1, axis_index_groups=cores, tiled=True)
    grads = grads.reshape(-1, columns)
    grads = lax.psum_scatter(
        grads, "fsdp", scatter_dimension=0, axis_index_groups=across, tiled=True
    )
    return own_core(grads, grads.shape[0] // (2 * experts))


def gather_plain(block, small, tok, hid, cot):
    size = lax.axis_size("fsdp")
    small = lax.all_gather(small, ("fsdp", "tp"), axis=0, tiled=True)
    tok = lax.all_gather(tok, "tp", axis=1, tiled=True).T
    return (
        lax.all_gather(block, "fsdp", axis=0),
        low(small),
        small.T[:8],
        tok,
        gather_rows(hid),
        gather_rows(cot),
    )


def finish_plain(big, wqkv, other, base, arrived):
    heads_width = (big.shape[1] - PAIR) // 4
    reduced = wide(lax.psum_scatter(big, "fsdp", scatter_dimension=0, tiled=True))
    flat = reduced[:, : 3 * heads_width]
    share = jnp.sum(flat * wide(wqkv), axis=1, keepdims=True)
    last = jnp.concatenate([share, reduced[:, 4 * heads_width + 1 :]], axis=1)
    experts, rows, columns = arrived.shape
    hidden = columns // 3
    wide_grads = wide(arrived)
    return (
        low(base + wide(swap(other))),
        flat.reshape(-1, 3, heads_width),
        reduced[:, 3 * heads_width : 4 * heads_width],
        own_half(last) + swap(other_half(last)),
        wide_grads[:, :, : 2 * hidden].reshape(experts, rows, 2, hidden),
        wide_grads[:, :, 2 * hidden :],
    )


def nt_dot(left, right):
    return lax.dot_general(left, right, (((1,), (1,)), ((), ())), preferred_element_type=jnp.float32)


def nn_dot(left, right):
    return jnp.dot(left, right, preferred_element_type=jnp.float32)


def tn_dot(left, right):
    return lax.dot_general(left, right, (((0,), (0,)), ((), ())), preferred_element_type=jnp.float32)


def low(values):
    return values.astype(jnp.bfloat16)


def wide(values):
    return values.astype(jnp.float32)


def rotary_tables(length):
    half = HD // 2
    positions = np.arange(length, dtype=np.float32)
    inverse = np.power(np.float32(10000.0), -np.arange(half, dtype=np.float32) / np.float32(half))
    angles = (positions[:, None] * inverse[None, :].astype(np.float32)).astype(np.float32)
    cosine = np.cos(angles.astype(np.float64)).astype(np.float32)
    sine = np.sin(angles.astype(np.float64)).astype(np.float32)
    return (
        np.concatenate([cosine] * 4, axis=1),
        np.concatenate([-sine, sine, -sine, sine], axis=1),
    )


def turn(values, cosine, sine):
    lane = lax.broadcasted_iota(jnp.int32, values.shape, 1)
    upper = lax.rem(lane, HD) >= HD // 2
    partner = jnp.where(
        upper, pltpu.roll(values, HD // 2, 1), pltpu.roll(values, PAIR - HD // 2, 1)
    )
    return values * cosine + partner * sine


def head_lanes(shape, half, axis):
    return (lax.broadcasted_iota(jnp.int32, shape, axis) >= HD) == bool(half)


def mean_last(values):
    return jnp.mean(values, axis=-1, keepdims=True)


def to_partner(source, target, send_sem, recv_sem):
    return pltpu.make_async_remote_copy(
        src_ref=source,
        dst_ref=target,
        send_sem=send_sem,
        recv_sem=recv_sem,
        device_id={"tp": 1 - lax.axis_index("tp")},
        device_id_type=MESH,
    )


def block_rows(block):
    return slice(block * BLOCK, (block + 1) * BLOCK)


def column(values, index):
    return values[:, index : index + 1]


def lane_matrix(shape, columns):
    lane = lax.broadcasted_iota(jnp.int32, shape, 1)
    total = jnp.zeros(shape, jnp.float32)
    for index, values in columns:
        total = jnp.where(lane == index, values, total)
    return total


def send_to(source, target, send_sem, recv_sem, device):
    return pltpu.make_async_remote_copy(
        src_ref=source,
        dst_ref=target,
        send_sem=send_sem,
        recv_sem=recv_sem,
        device_id=device,
        device_id_type=MESH,
    )


def greet_group(peers):
    me = lax.axis_index("fsdp")
    rank = lax.rem(me, peers)
    barrier = pltpu.get_barrier_semaphore()
    for k in range(1, peers):
        pl.semaphore_signal(
            barrier,
            inc=1,
            device_id={"fsdp": me - rank + lax.rem(rank + k, peers)},
            device_id_type=MESH,
        )
    pl.semaphore_signal(
        barrier, inc=1, device_id={"tp": 1 - lax.axis_index("tp")}, device_id_type=MESH
    )
    pl.semaphore_wait(barrier, peers)


def each(first, last, body):
    def step(k, carry):
        body(k)
        return carry

    lax.fori_loop(first, last, step, 0)


class CoreExchange:
    def __init__(self, source, target, send_sem, recv_sem):
        experts = source.shape[0]
        me = lax.axis_index("fsdp")
        rank = lax.rem(me, 2 * experts)
        core = lax.rem(rank, 2)
        mine = rank // 2

        def copy(k):
            ahead = lax.rem(mine + k, experts)
            return send_to(
                source.at[ahead],
                target.at[mine],
                send_sem.at[k],
                recv_sem.at[k],
                {"fsdp": me - rank + 2 * ahead + core},
            )

        def arrival(k):
            behind = lax.rem(mine + experts - k, experts)
            return send_to(
                source.at[behind],
                target.at[behind],
                send_sem.at[k],
                recv_sem.at[k],
                {"fsdp": me - rank + 2 * behind + core},
            )

        self.experts, self.copy, self.arrival = experts, copy, arrival
        self.source, self.target, self.mine = source, target, mine

    def start(self):
        each(1, self.experts, lambda k: self.copy(k).start())
        self.target[self.mine] = self.source[self.mine]

    def wait(self):
        each(1, self.experts, lambda k: self.copy(k).wait_send())
        each(1, self.experts, lambda k: self.arrival(k).wait_recv())


def gather_kernel(
    block_ref,
    small_ref,
    tok_ref,
    hid_ref,
    cot_ref,
    all_ref,
    small_out_ref,
    rows_out_ref,
    tok_out_ref,
    hid_out_ref,
    cot_out_ref,
    small_all_ref,
    tok_all_ref,
    y_send,
    y_recv,
    up_send,
    up_recv,
    down_send,
    down_recv,
    x_send,
    x_recv,
    core_send,
    core_recv,
):
    size = all_ref.shape[0]
    planes = size // 4
    me = lax.axis_index("fsdp")
    tp = lax.axis_index("tp")
    z, x, core = me // 4, lax.rem(me // 2, 2), lax.rem(me, 2)
    shard = small_ref.shape[0]
    own_rows = hid_ref.shape[0]
    greet_group(size)
    partner = {"tp": 1 - tp}
    small_all_ref[me, tp] = small_ref[...]
    small_y = send_to(small_ref, small_all_ref.at[me, tp], y_send.at[0], y_recv.at[0], partner)
    small_y.start()
    all_ref[me] = block_ref[...]
    mine = pl.ds(pl.multiple_of(tp * own_rows, own_rows), own_rows)
    hid_y = send_to(hid_ref, hid_out_ref.at[mine], y_send.at[1], y_recv.at[1], partner)
    tok_y = send_to(tok_ref, tok_all_ref.at[tp], y_send.at[2], y_recv.at[2], partner)
    cot_y = send_to(cot_ref, cot_out_ref.at[mine], y_send.at[3], y_recv.at[3], partner)
    hid_y.start()
    tok_y.start()

    def number(plane, line):
        return plane * 4 + line * 2 + core

    def pieces(number_of, send, recv, slot, device, source=None):
        first = all_ref.at[number_of] if source is None else source
        return (
            send_to(first, all_ref.at[number_of], send.at[0, slot], recv.at[0, slot], device),
            send_to(
                small_all_ref.at[number_of],
                small_all_ref.at[number_of],
                send.at[1, slot],
                recv.at[1, slot],
                device,
            ),
        )

    def up(step, plane):
        return pieces(
            number(plane, x),
            up_send,
            up_recv,
            step,
            {"fsdp": number(lax.min(z + 1, planes - 1), x)},
        )

    def down(step, plane):
        return pieces(
            number(plane, x), down_send, down_recv, step, {"fsdp": number(lax.max(z - 1, 0), x)}
        )

    def side(plane, line):
        return pieces(number(plane, line), x_send, x_recv, plane, {"fsdp": number(z, 1 - x)})

    def sibling(plane, line, parity):
        return pieces(
            plane * 4 + line * 2 + parity,
            core_send,
            core_recv,
            plane * 2 + line,
            {"fsdp": me + 1 - 2 * core},
        )

    def run(group, verb):
        for item in group:
            getattr(item, verb)()

    def spread(step, plane):
        run(side(plane, x), "start")
        run(sibling(plane, x, core), "start")

    small_y.wait()
    hid_out_ref[mine, :] = hid_ref[...]

    @pl.when(z < planes - 1)
    def _():
        run(up(0, z), "start")

    @pl.when(z > 0)
    def _():
        run(down(0, z), "start")

    spread(0, z)
    cot_y.start()
    tok_all_ref[tp] = tok_ref[...]
    cot_out_ref[mine, :] = cot_ref[...]
    for step in range(1, planes):

        @pl.when(z >= step)
        def _():
            run(up(step - 1, z - step), "wait_recv")

            @pl.when(z < planes - 1)
            def _():
                run(up(step, z - step), "start")

            spread(step, z - step)

        @pl.when(z + step < planes)
        def _():
            run(down(step - 1, z + step), "wait_recv")

            @pl.when(z > 0)
            def _():
                run(down(step, z + step), "start")

            spread(step, z + step)

    for distance in range(planes):
        plane = lax.rem(z + distance, planes)
        run(side(plane, 1 - x), "wait_recv")
        run(sibling(plane, 1 - x, core), "start")
    for plane in range(planes):
        for line in range(2):
            run(sibling(plane, line, 1 - core), "wait_recv")
    small_all = small_all_ref[...].reshape(size * 2 * shard, small_ref.shape[1])
    small_out_ref[...] = low(small_all)
    rows_out_ref[...] = small_all.T[:8, :]
    tok_y.wait()
    for part in range(2):
        lanes = slice(part * own_rows, (part + 1) * own_rows)
        tok_out_ref[lanes, :] = tok_all_ref[part].T
    for step in range(planes):

        @pl.when(jnp.logical_and(z >= step, z < planes - 1))
        def _():
            run(up(step, z - step), "wait_send")

        @pl.when(jnp.logical_and(z + step < planes, z > 0))
        def _():
            run(down(step, z + step), "wait_send")

    for plane in range(planes):
        run(side(plane, x), "wait_send")
        for line in range(2):
            run(sibling(plane, line, core), "wait_send")
    hid_y.wait()
    cot_y.wait()


def run_gather(block, small, tok, hid, cot):
    size = lax.axis_size("fsdp")
    own_rows, width = hid.shape
    vmem = pl.BlockSpec(memory_space=pltpu.VMEM)
    low_t, wide_t = jnp.bfloat16, jnp.float32
    dma = pltpu.SemaphoreType.DMA
    return pl.pallas_call(
        gather_kernel,
        in_specs=[vmem] * 5,
        out_specs=[vmem] * 6,
        out_shape=[
            jax.ShapeDtypeStruct((size,) + block.shape, low_t),
            jax.ShapeDtypeStruct((width, PAIR), low_t),
            jax.ShapeDtypeStruct((8, width), wide_t),
            jax.ShapeDtypeStruct((2 * own_rows, PAIR), wide_t),
            jax.ShapeDtypeStruct((2 * own_rows, width), low_t),
            jax.ShapeDtypeStruct((2 * own_rows, width), low_t),
        ],
        scratch_shapes=[
            pltpu.VMEM((size, 2) + small.shape, wide_t),
            pltpu.VMEM((2,) + tok.shape, wide_t),
            dma((4,)),
            dma((4,)),
        ]
        + [dma((2, size // 4))] * 6
        + [dma((2, size // 2))] * 2,
        compiler_params=pltpu.CompilerParams(
            collective_id=3, has_side_effects=True, vmem_limit_bytes=60 << 20
        ),
    )(block, small, tok, hid, cot)


def finish_kernel(
    big_ref,
    wqkv_ref,
    other_ref,
    base_ref,
    expert_ref,
    out_ref,
    qkv_ref,
    attn_ref,
    tail_ref,
    in_ref,
    down_ref,
    sum_ref,
    core_ref,
    side_ref,
    acc_ref,
    usend_ref,
    urecv_ref,
    dsend_ref,
    drecv_ref,
    y_ref,
    tsend_ref,
    trecv_ref,
    core_send,
    core_recv,
    x_send,
    x_recv,
    up_send,
    up_recv,
    dn_send,
    dn_recv,
    y_send,
    y_recv,
):
    size = big_ref.shape[0]
    planes = size // 4
    me = lax.axis_index("fsdp")
    tp = lax.axis_index("tp")
    z, x, core = me // 4, lax.rem(me // 2, 2), lax.rem(me, 2)
    heads_width = attn_ref.shape[1]
    greet_group(size)
    partner = {"tp": 1 - tp}

    def to_core(plane, line):
        slot = plane * 2 + line
        return send_to(
            big_ref.at[plane * 4 + line * 2 + 1 - core],
            core_ref.at[slot],
            core_send.at[slot],
            core_recv.at[slot],
            {"fsdp": me + 1 - 2 * core},
        )

    def to_side(plane):
        return send_to(
            sum_ref.at[plane],
            side_ref.at[plane],
            x_send.at[plane],
            x_recv.at[plane],
            {"fsdp": z * 4 + (1 - x) * 2 + core},
        )

    def to_up(plane):
        return send_to(
            usend_ref.at[plane],
            urecv_ref.at[plane],
            up_send.at[plane],
            up_recv.at[plane],
            {"fsdp": lax.min(z + 1, planes - 1) * 4 + x * 2 + core},
        )

    def to_down(plane):
        return send_to(
            dsend_ref.at[plane],
            drecv_ref.at[plane],
            dn_send.at[plane],
            dn_recv.at[plane],
            {"fsdp": lax.max(z - 1, 0) * 4 + x * 2 + core},
        )

    for plane in range(planes):
        to_core(plane, 1 - x).start()
    for plane in range(planes):
        to_core(plane, x).start()
    out_y = send_to(other_ref, y_ref, y_send.at[0], y_recv.at[0], partner)
    out_y.start()

    def joined(plane, line):
        to_core(plane, line).wait_recv()
        return wide(big_ref[plane * 4 + line * 2 + core]) + wide(core_ref[plane * 2 + line])

    for plane in range(planes):
        sum_ref[plane] = low(joined(plane, 1 - x))
        to_side(plane).start()
    for plane in range(planes):
        acc_ref[plane] = joined(plane, x)
    experts, shard, total = expert_ref.shape
    hidden = total // 3

    def lay_out(e):
        values = wide(expert_ref[e])
        in_ref[e, :, 0, :] = values[:, :hidden]
        in_ref[e, :, 1, :] = values[:, hidden : 2 * hidden]
        down_ref[e] = values[:, 2 * hidden :]

    each(0, experts, lay_out)
    for plane in range(planes):
        to_side(plane).wait_recv()
        acc_ref[plane] += wide(side_ref[plane])

    def rise(plane):
        @pl.when(jnp.logical_and(z > 0, z <= plane))
        def _():
            to_up(plane).wait_recv()
            acc_ref[plane] += wide(urecv_ref[plane])

        @pl.when(z < plane)
        def _():
            usend_ref[plane] = low(acc_ref[plane])
            to_up(plane).start()

    def fall(plane):
        @pl.when(jnp.logical_and(z < planes - 1, z >= plane))
        def _():
            to_down(plane).wait_recv()
            acc_ref[plane] += wide(drecv_ref[plane])

        @pl.when(z > plane)
        def _():
            dsend_ref[plane] = low(acc_ref[plane])
            to_down(plane).start()

    for step in range(planes):
        rise(planes - 1 - step)
        fall(step)
    values = acc_ref[z]
    flat = values[:, : 3 * heads_width]
    for part in range(3):
        qkv_ref[:, part, :] = flat[:, part * heads_width : (part + 1) * heads_width]
    attn_ref[...] = values[:, 3 * heads_width : 4 * heads_width]
    share = jnp.sum(flat * wide(wqkv_ref[...]), axis=1, keepdims=True)
    last = values[:, 4 * heads_width :]
    last = jnp.where(lax.broadcasted_iota(jnp.int32, last.shape, 1) == 0, share, last)
    part_rows = tail_ref.shape[0]
    tsend_ref[0] = last[:part_rows, :]
    tsend_ref[1] = last[part_rows:, :]
    tail_y = send_to(tsend_ref.at[1 - tp], trecv_ref, y_send.at[1], y_recv.at[1], partner)
    tail_y.start()
    out_y.wait()
    out_ref[...] = low(base_ref[...] + wide(y_ref[...]))
    tail_y.wait()
    tail_ref[...] = tsend_ref[tp] + trecv_ref[...]
    for plane in range(planes):
        to_core(plane, 1 - x).wait_send()
        to_core(plane, x).wait_send()
        to_side(plane).wait_send()

        @pl.when(z < plane)
        def _():
            to_up(plane).wait_send()

        @pl.when(z > plane)
        def _():
            to_down(plane).wait_send()


def run_finish(big, wqkv, other, base, arrived):
    size = lax.axis_size("fsdp")
    planes = size // 4
    own_rows, width = base.shape
    columns = big.shape[1]
    heads_width = (columns - PAIR) // 4
    shard = width // size
    experts, _, total = arrived.shape
    hidden = total // 3
    vmem = pl.BlockSpec(memory_space=pltpu.VMEM)
    low_t, wide_t = jnp.bfloat16, jnp.float32
    dma = pltpu.SemaphoreType.DMA
    line = (planes, shard, columns)
    return pl.pallas_call(
        finish_kernel,
        in_specs=[vmem] * 5,
        out_specs=[vmem] * 6,
        out_shape=[
            jax.ShapeDtypeStruct((own_rows, width), low_t),
            jax.ShapeDtypeStruct((shard, 3, heads_width), wide_t),
            jax.ShapeDtypeStruct((shard, heads_width), wide_t),
            jax.ShapeDtypeStruct((shard // 2, PAIR), wide_t),
            jax.ShapeDtypeStruct((experts, shard, 2, hidden), wide_t),
            jax.ShapeDtypeStruct((experts, shard, hidden), wide_t),
        ],
        scratch_shapes=[
            pltpu.VMEM(line, low_t),
            pltpu.VMEM((2 * planes, shard, columns), low_t),
            pltpu.VMEM(line, low_t),
            pltpu.VMEM(line, wide_t),
            pltpu.VMEM(line, low_t),
            pltpu.VMEM(line, low_t),
            pltpu.VMEM(line, low_t),
            pltpu.VMEM(line, low_t),
            pltpu.VMEM((own_rows, width), low_t),
            pltpu.VMEM((2, shard // 2, PAIR), wide_t),
            pltpu.VMEM((shard // 2, PAIR), wide_t),
            dma((2 * planes,)),
            dma((2 * planes,)),
        ]
        + [dma((planes,))] * 6
        + [dma((2,))] * 2,
        compiler_params=pltpu.CompilerParams(
            collective_id=4, has_side_effects=True, vmem_limit_bytes=60 << 20
        ),
    )(big.reshape(size, shard, columns), wqkv, other, base, arrived)


def expert_kernel(
    s2_ref,
    cot_ref,
    line_ref,
    slot_ref,
    weight_ref,
    res_out_ref,
    dx_out_ref,
    grads_out_ref,
    xs_ref,
    gs_ref,
    x_ref,
    g_ref,
    w_ref,
    gate_ref,
    up_ref,
    xt_ref,
    gt_ref,
    acc_ref,
    grads_ref,
    sibling_ref,
    ysend_ref,
    yrecv_ref,
    w_sem,
    grad_sem,
    xs_sem,
    xr_sem,
    gs_sem,
    gr_sem,
    xfs_sem,
    xfr_sem,
    gfs_sem,
    gfr_sem,
    ys_sem,
    yr_sem,
    rs_sem,
    rr_sem,
    ds_sem,
    dr_sem,
):
    peers, rows, width = xs_ref.shape
    total = peers * rows
    hidden = gate_ref.shape[1]
    tiles = hidden // TILE
    chunks = ysend_ref.shape[1]
    chunk = total // chunks
    group = peers // chunks
    me = lax.axis_index("fsdp")
    tp = lax.axis_index("tp")
    rank = lax.rem(me, peers)
    core = lax.rem(rank, 2)
    start = me - rank

    def ahead(k):
        return start + lax.rem(rank + k, peers)

    def behind(k):
        return start + lax.rem(rank + peers - k, peers)

    partner = {"tp": 1 - tp}
    sibling = {"fsdp": start + rank + 1 - 2 * core}

    def out_x(k):
        return send_to(xs_ref.at[k], x_ref.at[0, k], xs_sem.at[k], xr_sem.at[k], {"fsdp": ahead(k)})

    def out_g(k):
        return send_to(gs_ref.at[k], g_ref.at[0, k], gs_sem.at[k], gr_sem.at[k], {"fsdp": ahead(k)})

    def pass_x(k):
        return send_to(x_ref.at[0, k], x_ref.at[1, k], xfs_sem.at[k], xfr_sem.at[k], partner)

    def pass_g(k):
        return send_to(g_ref.at[0, k], g_ref.at[1, k], gfs_sem.at[k], gfr_sem.at[k], partner)

    def across(index, q):
        return send_to(
            ysend_ref.at[index, q],
            yrecv_ref.at[index, q],
            ys_sem.at[index, q],
            yr_sem.at[index, q],
            partner,
        )

    def back_res(k):
        return send_to(
            xs_ref.at[k], res_out_ref.at[k], rs_sem.at[k], rr_sem.at[k], {"fsdp": behind(k)}
        )

    def back_dx(k):
        return send_to(
            gs_ref.at[k], dx_out_ref.at[k], ds_sem.at[k], dr_sem.at[k], {"fsdp": behind(k)}
        )

    greet_group(peers)
    here = pltpu.make_async_copy(weight_ref, w_ref.at[:, core], w_sem.at[0])
    here.start()
    there = send_to(weight_ref, w_ref.at[:, core], w_sem.at[1], w_sem.at[2], sibling)
    there.start()

    half = total // 2
    halves = []
    for part in range(2):
        blocks = slice(part * peers // 2, (part + 1) * peers // 2)
        ids = slot_ref[part * half : (part + 1) * half, 0:1]
        hits = [line_ref[m : m + 1, :] == ids for m in range(2)]
        gate = sum(
            jnp.sum(jnp.where(hits[m], line_ref[2 + m : 3 + m, :], 0.0), axis=1, keepdims=True)
            for m in range(2)
        )
        onehot = low(jnp.where(hits[0] | hits[1], 1.0, 0.0))
        xs_ref[blocks] = low(nn_dot(onehot, s2_ref[...])).reshape(peers // 2, rows, width)
        if part == 0:
            x_ref[0, 0] = xs_ref[0]
            pass_x(0).start()
        each(max(1, part * peers // 2), (part + 1) * peers // 2, lambda k: out_x(k).start())
        halves.append((blocks, onehot, gate))
    for part in range(2):
        blocks, onehot, gate = halves[part]
        gs_ref[blocks] = low(nn_dot(onehot, cot_ref[...]) * gate).reshape(peers // 2, rows, width)
        if part == 0:
            g_ref[0, 0] = gs_ref[0]
            pass_g(0).start()
        each(max(1, part * peers // 2), (part + 1) * peers // 2, lambda k: out_g(k).start())

    def forward_x(k):
        out_x(k).wait_recv()
        pass_x(k).start()

    each(1, peers, forward_x)
    here.wait()
    send_to(weight_ref, w_ref.at[:, 1 - core], w_sem.at[1], w_sem.at[2], sibling).wait_recv()
    there.wait_send()
    each(0, peers, lambda k: pass_x(k).wait_recv())

    def weights(which, lanes):
        return w_ref[:, :, :, pl.ds(pl.multiple_of(which * hidden + lanes, TILE), TILE)].reshape(
            width, TILE
        )

    acc_ref[...] = jnp.zeros_like(acc_ref)

    def forward_tile(tile, carry):
        lanes = pl.multiple_of(tile * TILE, TILE)
        x = x_ref[...].reshape(2 * total, width)
        gate = nn_dot(x, weights(0, lanes))
        up = nn_dot(x, weights(1, lanes))
        gate_ref[:, pl.ds(lanes, TILE)] = low(gate)
        up_ref[:, pl.ds(lanes, TILE)] = low(up)
        act = low(gate / (1.0 + jnp.exp(-gate)) * up)
        acc_ref[...] += nt_dot(act, weights(2, lanes))

        def forward_g(k):
            @pl.when(k > 0)
            def _():
                out_g(k).wait_recv()
                pass_g(k).start()

        each(tile * (peers // tiles), (tile + 1) * (peers // tiles), forward_g)
        return carry

    lax.fori_loop(0, tiles, forward_tile, 0)
    each(1, peers, lambda k: out_x(k).wait_send())
    xs_ref[...] = low(acc_ref[:total, :]).reshape(peers, rows, width)
    ysend_ref[0] = low(acc_ref[total:, :]).reshape(chunks, chunk, width)
    for q in range(chunks):
        across(0, q).start()
    xt_ref[...] = x_ref[...].reshape(2 * total, width).T
    acc_ref[...] = jnp.zeros_like(acc_ref)
    each(0, peers, lambda k: pass_g(k).wait_recv())
    gt_ref[...] = g_ref[...].reshape(2 * total, width).T

    def backward_tile(tile, carry):
        lanes = pl.multiple_of(tile * TILE, TILE)
        gate = wide(gate_ref[:, pl.ds(lanes, TILE)])
        up = wide(up_ref[:, pl.ds(lanes, TILE)])
        sig = 1.0 / (1.0 + jnp.exp(-gate))
        silu = gate * sig
        act = low(silu * up)
        d_act = nn_dot(g_ref[...].reshape(2 * total, width), weights(2, lanes))
        d_up = low(d_act * silu)
        d_gate = low(d_act * up * sig * (1.0 + gate * (1.0 - sig)))
        acc_ref[...] += nt_dot(d_gate, weights(0, lanes)) + nt_dot(d_up, weights(1, lanes))

        def keep(which, values):
            grads_ref[
                :, :, :, pl.ds(pl.multiple_of(which * hidden + lanes, TILE), TILE)
            ] = low(values).reshape(peers // 2, 2, rows, TILE)

        keep(0, nn_dot(xt_ref[...], d_gate))
        keep(1, nn_dot(xt_ref[...], d_up))
        keep(2, nn_dot(gt_ref[...], act))

        @pl.when(tile == 1)
        def _():
            for q in range(chunks):
                across(0, q).wait_recv()
                part = slice(q * group, (q + 1) * group)
                xs_ref[part] = low(
                    wide(xs_ref[part]) + wide(yrecv_ref[0, q]).reshape(group, rows, width)
                )
            res_out_ref[0] = xs_ref[0]
            each(1, peers, lambda k: back_res(k).start())

        return carry

    lax.fori_loop(0, tiles, backward_tile, 0)
    for q in range(chunks):
        ysend_ref[1, q] = low(acc_ref[total + q * chunk : total + (q + 1) * chunk, :])
        across(1, q).start()
    swap_grads = send_to(
        grads_ref.at[:, 1 - core], sibling_ref, grad_sem.at[0], grad_sem.at[1], sibling
    )
    swap_grads.start()
    each(1, peers, lambda k: out_g(k).wait_send())
    for q in range(chunks):
        across(1, q).wait_recv()
        part = slice(q * group, (q + 1) * group)
        gs_ref[part] = low(
            acc_ref[q * chunk : (q + 1) * chunk, :] + wide(yrecv_ref[1, q])
        ).reshape(group, rows, width)
        if q == 0:
            dx_out_ref[0] = gs_ref[0]
        each(max(1, q * group), (q + 1) * group, lambda k: back_dx(k).start())
    swap_grads.wait()
    grads_out_ref[...] = low(wide(grads_ref[:, core]) + wide(sibling_ref[...]))
    for q in range(chunks):
        across(0, q).wait_send()
        across(1, q).wait_send()
    each(0, peers, lambda k: pass_x(k).wait_send())
    each(0, peers, lambda k: pass_g(k).wait_send())
    each(1, peers, lambda k: back_res(k).wait())
    each(1, peers, lambda k: back_dx(k).wait())


def run_expert(s2, cot, lines, slots, weights):
    length, width = s2.shape
    experts, shard, total = weights.shape
    peers = 2 * experts
    rows = slots.shape[0] // peers
    hidden = total // 3
    both = 2 * peers * rows
    chunks = 4
    vmem = pl.BlockSpec(memory_space=pltpu.VMEM)
    low_t, wide_t = jnp.bfloat16, jnp.float32
    dma = pltpu.SemaphoreType.DMA
    block = (peers, rows, width)
    return pl.pallas_call(
        expert_kernel,
        in_specs=[vmem] * 4 + [pl.BlockSpec(memory_space=pl.ANY)],
        out_specs=[vmem] * 3,
        out_shape=[
            jax.ShapeDtypeStruct(block, low_t),
            jax.ShapeDtypeStruct(block, low_t),
            jax.ShapeDtypeStruct(weights.shape, low_t),
        ],
        scratch_shapes=[
            pltpu.VMEM(block, low_t),
            pltpu.VMEM(block, low_t),
            pltpu.VMEM((2,) + block, low_t),
            pltpu.VMEM((2,) + block, low_t),
            pltpu.VMEM((experts, 2, shard, total), low_t),
            pltpu.VMEM((both, hidden), low_t),
            pltpu.VMEM((both, hidden), low_t),
            pltpu.VMEM((width, both), low_t),
            pltpu.VMEM((width, both), low_t),
            pltpu.VMEM((both, width), wide_t),
            pltpu.VMEM((experts, 2, shard, total), low_t),
            pltpu.VMEM((experts, shard, total), low_t),
            pltpu.VMEM((2, chunks, both // (2 * chunks), width), low_t),
            pltpu.VMEM((2, chunks, both // (2 * chunks), width), low_t),
            dma((3,)),
            dma((2,)),
        ]
        + [dma((peers,))] * 8
        + [dma((2, chunks))] * 2
        + [dma((peers,))] * 4,
            cost_estimate=pl.CostEstimate(
            flops=36 * peers * rows * width * hidden, bytes_accessed=1 << 28, transcendentals=0
        ),
        compiler_params=pltpu.CompilerParams(
            collective_id=2, has_side_effects=True, vmem_limit_bytes=67043328
        ),
    )(s2, cot, lines, slots, weights)


def forward_kernel(
    hid_ref,
    tok_in_ref,
    wqkv_ref,
    wout_ref,
    small_ref,
    rows_ref,
    cos_ref,
    sin_ref,
    shard_ref,
    s1_ref,
    qkv_ref,
    lse_ref,
    mixed_ref,
    mid_ref,
    s2_ref,
    tok_ref,
    line_ref,
    expert_ref,
    vt_ref,
    send_ref,
    recv_ref,
    send_sem,
    recv_sem,
    wsend_sem,
    wrecv_sem,
):
    greet_group(2 * shard_ref.shape[0])
    experts = CoreExchange(shard_ref, expert_ref, wsend_sem, wrecv_sem)
    experts.start()
    blocks = hid_ref.shape[0] // BLOCK
    heads_width = wout_ref.shape[1]
    pairs = heads_width // PAIR
    gain_one = rows_ref[0:1, :]
    gain_two = rows_ref[1:2, :]
    copies = []
    lse_ref[...] = jnp.zeros_like(lse_ref)
    for block in range(blocks):
        rows = block_rows(block)
        keys = (block + 1) * BLOCK
        source = wide(hid_ref[rows, :])
        s1 = low(source * lax.rsqrt(mean_last(source * source) + EPSILON) * gain_one)
        s1_ref[rows, :] = s1
        cosine, sine = cos_ref[rows, :], sin_ref[rows, :]
        for part in range(3):
            projected = nn_dot(s1, wqkv_ref[:, part * heads_width : (part + 1) * heads_width])
            for pair in range(pairs):
                chunk = projected[:, pair * PAIR : (pair + 1) * PAIR]
                if part < 2:
                    chunk = turn(chunk, cosine, sine)
                else:
                    vt_ref[pair * PAIR : (pair + 1) * PAIR, rows] = low(chunk.T)
                start = part * heads_width + pair * PAIR
                qkv_ref[rows, start : start + PAIR] = low(chunk)
        for pair in range(pairs):
            lanes = slice(pair * PAIR, (pair + 1) * PAIR)
            query = qkv_ref[rows, lanes] * jnp.bfloat16(SCALING)
            key = qkv_ref[:keys, heads_width + pair * PAIR : heads_width + (pair + 1) * PAIR]
            value_t = vt_ref[lanes, :keys]
            gathered = None
            for half in range(2):
                masked = jnp.where(head_lanes(query.shape, half, 1), query, jnp.bfloat16(0))
                scores = nt_dot(key, masked)
                highest = jnp.max(scores, axis=0, keepdims=True)
                expanded = jnp.exp(scores - highest)
                totals = jnp.sum(expanded, axis=0, keepdims=True)
                probs = low(expanded * (1.0 / totals))
                lse_ref[2 * pair + half : 2 * pair + half + 1, rows] = highest + jnp.log(totals)
                found = nn_dot(value_t, probs)
                gathered = (
                    found
                    if half == 0
                    else jnp.where(head_lanes(found.shape, 1, 0), found, gathered)
                )
            mixed_ref[rows, lanes] = low(gathered.T)
        send_ref[block] = low(nt_dot(mixed_ref[rows, :], wout_ref[...]))
        copy = to_partner(
            send_ref.at[block], recv_ref.at[block], send_sem.at[block], recv_sem.at[block]
        )
        copy.start()
        copies.append(copy)
    for block in range(blocks):
        rows = block_rows(block)
        copies[block].wait()
        mid = wide(hid_ref[rows, :]) + (wide(send_ref[block]) + wide(recv_ref[block]))
        mid_ref[rows, :] = mid
        s2 = low(mid * lax.rsqrt(mean_last(mid * mid) + EPSILON) * gain_two)
        s2_ref[rows, :] = s2
        tok = tok_in_ref[rows, :]
        lane = lax.broadcasted_iota(jnp.int32, tok.shape, 1)
        logits = nn_dot(s2, small_ref[...]) + tok
        picked = [
            jnp.sum(
                jnp.where(wide(lane - ROUTER) == column(tok, ROUTE + member), logits, 0.0),
                axis=1,
                keepdims=True,
            )
            for member in range(2)
        ]
        gate = [
            1.0 / (1.0 + jnp.exp(picked[1 - member] - picked[member])) for member in range(2)
        ]
        tok = jnp.where(lane == GATE, gate[0], jnp.where(lane == GATE + 1, gate[1], tok))
        tok_ref[rows, :] = tok
        line_ref[:, rows] = tok.T[TARGET : TARGET + 8, :]
    experts.wait()


def backward_kernel(
    res_ref,
    dx_ref,
    slot_ref,
    tok_ref,
    cot_ref,
    mid_ref,
    s1_ref,
    qkv_ref,
    lse_ref,
    mixed_ref,
    wqkv_ref,
    wout_ref,
    small_ref,
    rows_ref,
    cos_ref,
    sin_ref,
    own_ref,
    egrad_ref,
    grad_ref,
    base_ref,
    other_ref,
    big_ref,
    arrived_ref,
    gsend_ref,
    grecv_ref,
    hsend_ref,
    hrecv_ref,
    gmid_ref,
    gown_ref,
    kt_ref,
    gm_ref,
    dqt_ref,
    dk_ref,
    dv_ref,
    gp_ref,
    acc_qkv_ref,
    acc_out_ref,
    acc_small_ref,
    acc_gain_ref,
    gsend_sem,
    grecv_sem,
    hsend_sem,
    hrecv_sem,
    esend_sem,
    erecv_sem,
):
    greet_group(2 * egrad_ref.shape[0])
    experts = CoreExchange(egrad_ref, arrived_ref, esend_sem, erecv_sem)
    experts.start()
    tp = lax.axis_index("tp")
    width = dx_ref.shape[1]
    blocks = cot_ref.shape[0] // BLOCK
    heads_width = wout_ref.shape[1]
    pairs = heads_width // PAIR
    gain_one = rows_ref[0:1, :]
    gain_two = rows_ref[1:2, :]
    slot_row = slot_ref[0:1, :]
    order = list(reversed(range(blocks)))
    first = order[0]
    gcopies = {}
    for block in order:
        rows = block_rows(block)
        tok = tok_ref[rows, :]
        onehots = [
            low(jnp.where(column(tok, TARGET + m) == slot_row, 1.0, 0.0)) for m in range(2)
        ]
        placed = [nn_dot(onehot, res_ref[...]) for onehot in onehots]
        cot_wide = wide(cot_ref[rows, :])
        shares = [
            column(tok, GATE + m) * jnp.sum(placed[m] * cot_wide, axis=1, keepdims=True)
            for m in range(2)
        ]
        high = [wide(low(share)) for share in shares]
        gsend_ref[block, :, :width] = low(nn_dot(onehots[0] + onehots[1], dx_ref[...]))
        gsend_ref[block, :, width:] = low(
            lane_matrix(
                tok.shape,
                [
                    (0, high[0]),
                    (1, shares[0] - high[0]),
                    (2, high[1]),
                    (3, shares[1] - high[1]),
                ],
            )
        )
        copy = to_partner(
            gsend_ref.at[block], grecv_ref.at[block], gsend_sem.at[block], grecv_sem.at[block]
        )
        copy.start()
        gcopies[block] = copy
        placed = column(tok, GATE) * placed[0] + column(tok, GATE + 1) * placed[1]
        slab = slice((block % 2) * BLOCK, (block % 2 + 1) * BLOCK)

        @pl.when(tp == block // 2)
        def _():
            base_ref[slab, :] = placed

        @pl.when(tp != block // 2)
        def _():
            other_ref[slab, :] = low(placed)

    kt_ref[...] = qkv_ref[:, heads_width : 2 * heads_width].T
    for block in order:
        rows = block_rows(block)
        keys = (block + 1) * BLOCK
        slab = slice((block % 2) * BLOCK, (block % 2 + 1) * BLOCK)
        mine = tp == block // 2
        mine_f = jnp.where(mine, 1.0, 0.0)
        mid = mid_ref[rows, :]
        cot = cot_ref[rows, :]
        cot_wide = wide(cot)
        tok = tok_ref[rows, :]
        scale = lax.rsqrt(mean_last(mid * mid) + EPSILON)
        unit = mid * scale
        normed = unit * gain_two
        s2 = low(normed)
        small = small_ref[...]
        mixing = nn_dot(s2, small)
        value_dot = nn_dot(cot, small)
        normed_dot = jnp.sum(normed * cot_wide, axis=1, keepdims=True)
        route = [column(tok, ROUTE + member) for member in range(2)]
        gate = [column(tok, GATE + member) for member in range(2)]

        def weight_of(expert):
            return sum(jnp.where(route[m] == expert, gate[m], 0.0) for m in range(2))

        copy_weight = weight_of(COPY)
        copy_share = [jnp.where(route[m] == COPY, normed_dot, 0.0) for m in range(2)]
        alpha = copy_weight
        columns = []
        value_columns = []
        for c in range(2):
            weight = weight_of(COPY + 1 + c)
            left = column(mixing, MIXING + 2 * c)
            right = column(mixing, MIXING + 2 * c + 1)
            a0 = 1.0 / (1.0 + jnp.exp(right - left))
            a1 = 1.0 / (1.0 + jnp.exp(left - right))
            vd = column(value_dot, VALUE + c)
            alpha = alpha + weight * a0
            for m in range(2):
                copy_share[m] = copy_share[m] + jnp.where(
                    route[m] == COPY + 1 + c, a0 * normed_dot + a1 * vd, 0.0
                )
            slope = a0 * a1 * weight * (normed_dot - vd)
            columns.append((MIXING + 2 * c, slope))
            columns.append((MIXING + 2 * c + 1, -slope))
            value_columns.append((VALUE + c, weight * a1))
        value_matrix = lane_matrix(tok.shape, value_columns)
        base = mid + alpha * normed + nt_dot(low(value_matrix), small)

        @pl.when(mine)
        def _():
            base_ref[slab, :] += base

        gcopies[block].wait()
        extra = wide(gsend_ref[block, :, width:]) + wide(grecv_ref[block, :, width:])
        share = [
            column(extra, 2 * m) + column(extra, 2 * m + 1) + gate[m] * copy_share[m]
            for m in range(2)
        ]
        lane = lax.broadcasted_iota(jnp.int32, tok.shape, 1)
        slopes = lane_matrix(tok.shape, columns)
        for m in range(2):
            local = share[m] - gate[m] * (share[0] + share[1])
            slopes = slopes + jnp.where(wide(lane - ROUTER) == route[m], local, 0.0)
        slopes_low = low(slopes)
        grad_normed = (
            wide(gsend_ref[block, :, :width])
            + wide(grecv_ref[block, :, :width])
            + alpha * cot_wide
            + nt_dot(slopes_low, small)
        )
        small_grad = tn_dot(s2, low(slopes * mine_f)) + tn_dot(cot, low(value_matrix * mine_f))
        gain_grad = jnp.sum(unit * grad_normed, axis=0, keepdims=True) * mine_f
        scaled = grad_normed * gain_two
        grad_mid = cot_wide + scale * (scaled - unit * mean_last(scaled * unit))
        gmid_ref[rows, :] = grad_mid
        attended = low(grad_mid)
        out_grad = tn_dot(attended, mixed_ref[rows, :])
        gm_ref[...] = low(nn_dot(attended, wout_ref[...]))
        if block == first:
            acc_small_ref[...] = small_grad
            acc_gain_ref[...] = jnp.broadcast_to(gain_grad, acc_gain_ref.shape)
            acc_out_ref[...] = out_grad
        else:
            acc_small_ref[...] += small_grad
            acc_gain_ref[...] += jnp.broadcast_to(gain_grad, acc_gain_ref.shape)
            acc_out_ref[...] += out_grad
        cosine, sine = cos_ref[rows, :], sin_ref[rows, :]

        def one_pair(pair, carry):
            start = pl.multiple_of(pair * PAIR, PAIR)
            lanes = pl.ds(start, PAIR)
            key_lanes = pl.ds(pl.multiple_of(heads_width + start, PAIR), PAIR)
            value_lanes = pl.ds(pl.multiple_of(2 * heads_width + start, PAIR), PAIR)
            query = qkv_ref[rows, lanes] * jnp.bfloat16(SCALING)
            key = qkv_ref[:keys, key_lanes]
            value = qkv_ref[:keys, value_lanes]
            grad_out = gm_ref[:, lanes]
            key_t = kt_ref[lanes, :keys]
            grad_value = None
            for half in range(2):
                keep = head_lanes(query.shape, half, 1)
                q_half = jnp.where(keep, query, jnp.bfloat16(0))
                g_half = jnp.where(keep, grad_out, jnp.bfloat16(0))
                probs = jnp.exp(nt_dot(key, q_half) - lse_ref[pl.ds(2 * pair + half, 1), rows])
                grad_probs = nt_dot(value, g_half)
                inner = jnp.sum(probs * grad_probs, axis=0, keepdims=True)
                grad_scores = low(probs * (grad_probs - inner))
                value_part = nn_dot(low(probs), g_half)
                key_part = nn_dot(grad_scores, q_half)
                query_part = nn_dot(key_t, grad_scores)
                if half == 0:
                    grad_value, grad_key, grad_query = value_part, key_part, query_part
                else:
                    grad_value = grad_value + value_part
                    grad_key = grad_key + key_part
                    grad_query = jnp.where(
                        head_lanes(query_part.shape, 1, 0), query_part, grad_query
                    )
            if block == first:
                dv_ref[:keys, lanes] = grad_value
                dk_ref[:keys, lanes] = grad_key
            else:
                dv_ref[:keys, lanes] += grad_value
                dk_ref[:keys, lanes] += grad_key
            gp_ref[:, lanes] = low(turn(grad_query.T * SCALING, cosine, -sine))
            gp_ref[:, key_lanes] = low(turn(dk_ref[rows, lanes], cosine, -sine))
            gp_ref[:, value_lanes] = low(dv_ref[rows, lanes])
            return carry

        lax.fori_loop(0, pairs, one_pair, 0)
        gp = gp_ref[...]
        qkv_grad = tn_dot(s1_ref[rows, :], gp)
        if block == first:
            acc_qkv_ref[...] = qkv_grad
        else:
            acc_qkv_ref[...] += qkv_grad
        stream_grad = nt_dot(gp, wqkv_ref[...])

        @pl.when(mine)
        def _():
            gown_ref[block % 2] = stream_grad

        @pl.when(jnp.logical_not(mine))
        def _():
            hsend_ref[block % 2] = low(stream_grad)
            to_partner(
                hsend_ref.at[block % 2],
                hrecv_ref.at[block % 2],
                hsend_sem.at[block % 2],
                hrecv_sem.at[block % 2],
            ).start()

    big_ref[:, : 3 * heads_width] = low(acc_qkv_ref[...])
    big_ref[:, 3 * heads_width : 4 * heads_width] = low(acc_out_ref[...])
    gain_rows = acc_gain_ref[0:1, :]
    tall = jnp.where(
        lax.broadcasted_iota(jnp.int32, (PAIR, width), 0) == 1,
        jnp.broadcast_to(gain_rows, (PAIR, width)),
        0.0,
    )
    big_ref[:, 4 * heads_width :] = low(acc_small_ref[...] + tall.T)
    for slot in reversed(range(2)):
        slab = slice(slot * BLOCK, (slot + 1) * BLOCK)
        to_partner(
            hsend_ref.at[slot], hrecv_ref.at[slot], hsend_sem.at[slot], hrecv_sem.at[slot]
        ).wait()
        source = wide(own_ref[slab, :])
        scale = lax.rsqrt(mean_last(source * source) + EPSILON)
        unit = source * scale
        scaled = (gown_ref[slot] + wide(hrecv_ref[slot])) * gain_one
        mid_rows = pl.ds(pl.multiple_of(tp * 2 * BLOCK + slot * BLOCK, BLOCK), BLOCK)
        grad_ref[slab, :] = gmid_ref[mid_rows, :] + scale * (
            scaled - unit * mean_last(scaled * unit)
        )
    experts.wait()


def run_forward(hid, tok, wqkv, wout, small, rows, cosine, sine, shard):
    length, width = hid.shape
    heads_width = wout.shape[1]
    blocks = length // BLOCK
    vmem = pl.BlockSpec(memory_space=pltpu.VMEM)
    low_t, wide_t = jnp.bfloat16, jnp.float32
    return pl.pallas_call(
        forward_kernel,
        in_specs=[vmem] * 9,
        out_specs=[vmem] * 9,
        out_shape=[
            jax.ShapeDtypeStruct((length, width), low_t),
            jax.ShapeDtypeStruct((length, 3 * heads_width), low_t),
            jax.ShapeDtypeStruct((8, length), wide_t),
            jax.ShapeDtypeStruct((length, heads_width), low_t),
            jax.ShapeDtypeStruct((length, width), wide_t),
            jax.ShapeDtypeStruct((length, width), low_t),
            jax.ShapeDtypeStruct((length, PAIR), wide_t),
            jax.ShapeDtypeStruct((8, length), wide_t),
            jax.ShapeDtypeStruct(shard.shape, low_t),
        ],
        scratch_shapes=[
            pltpu.VMEM((heads_width, length), low_t),
            pltpu.VMEM((blocks, BLOCK, width), low_t),
            pltpu.VMEM((blocks, BLOCK, width), low_t),
            pltpu.SemaphoreType.DMA((blocks,)),
            pltpu.SemaphoreType.DMA((blocks,)),
            pltpu.SemaphoreType.DMA((shard.shape[0],)),
            pltpu.SemaphoreType.DMA((shard.shape[0],)),
        ],
        cost_estimate=pl.CostEstimate(
            flops=16 * length * width * heads_width, bytes_accessed=1 << 27, transcendentals=0
        ),
        compiler_params=pltpu.CompilerParams(
            collective_id=0, has_side_effects=True, vmem_limit_bytes=60 << 20
        ),
    )(hid, tok, wqkv, wout, small, rows, cosine, sine, shard)


def run_backward(*operands):
    cot, own, wout, egrads = operands[4], operands[16], operands[11], operands[17]
    length, width = cot.shape
    heads_width = wout.shape[1]
    blocks = length // BLOCK
    own_rows = own.shape[0]
    vmem = pl.BlockSpec(memory_space=pltpu.VMEM)
    low_t, wide_t = jnp.bfloat16, jnp.float32
    dma = pltpu.SemaphoreType.DMA
    return pl.pallas_call(
        backward_kernel,
        in_specs=[vmem] * 18,
        out_specs=[vmem] * 5,
        out_shape=[
            jax.ShapeDtypeStruct((own_rows, width), wide_t),
            jax.ShapeDtypeStruct((own_rows, width), wide_t),
            jax.ShapeDtypeStruct((own_rows, width), low_t),
            jax.ShapeDtypeStruct((width, 4 * heads_width + PAIR), low_t),
            jax.ShapeDtypeStruct(egrads.shape, low_t),
        ],
        scratch_shapes=[
            pltpu.VMEM((blocks, BLOCK, width + PAIR), low_t),
            pltpu.VMEM((blocks, BLOCK, width + PAIR), low_t),
            pltpu.VMEM((2, BLOCK, width), low_t),
            pltpu.VMEM((2, BLOCK, width), low_t),
            pltpu.VMEM((length, width), wide_t),
            pltpu.VMEM((2, BLOCK, width), wide_t),
            pltpu.VMEM((heads_width, length), low_t),
            pltpu.VMEM((BLOCK, heads_width), low_t),
            pltpu.VMEM((PAIR, BLOCK), wide_t),
            pltpu.VMEM((length, heads_width), wide_t),
            pltpu.VMEM((length, heads_width), wide_t),
            pltpu.VMEM((BLOCK, 3 * heads_width), low_t),
            pltpu.VMEM((width, 3 * heads_width), wide_t),
            pltpu.VMEM((width, heads_width), wide_t),
            pltpu.VMEM((width, PAIR), wide_t),
            pltpu.VMEM((8, width), wide_t),
            dma((blocks,)),
            dma((blocks,)),
            dma((2,)),
            dma((2,)),
            dma((egrads.shape[0],)),
            dma((egrads.shape[0],)),
        ],
        cost_estimate=pl.CostEstimate(
            flops=32 * length * width * heads_width, bytes_accessed=1 << 27, transcendentals=0
        ),
        compiler_params=pltpu.CompilerParams(
            collective_id=1, has_side_effects=True, vmem_limit_bytes=60 << 20
        ),
    )(*operands)


def shards(
    hidden,
    prev_logits,
    routes,
    slot_rank,
    dropped,
    cotangent,
    attn_norm,
    ffn_norm,
    w_qkv,
    w_attn_out,
    w_router,
    w_const_gate,
    w_const_value,
    w_expert_in,
    w_expert_out,
):
    own_rows, width = hidden.shape
    length = own_rows * lax.axis_size("tp")
    experts = w_expert_in.shape[0]
    route_count = w_router.shape[1]
    capacity = 9 * length // (4 * route_count)
    heads_width = w_attn_out.shape[1]
    planned = lax.axis_size("fsdp") == 16
    small = jnp.concatenate(
        [
            wide(values)
            for values in (
                attn_norm[:, None],
                ffn_norm[:, None],
                w_router,
                w_const_gate,
                w_const_value,
            )
        ],
        axis=1,
    )
    small = jnp.pad(small, ((0, 0), (0, PAIR - small.shape[1])))
    wqkv_own = w_qkv.reshape(-1, 3 * heads_width)
    kept = (routes < experts) & (dropped == 0)
    target = jnp.where(kept, routes * capacity + slot_rank, -1)
    blank = jnp.zeros((own_rows, 2), jnp.float32)
    tok = jnp.concatenate(
        [blank, prev_logits, blank, blank, blank, wide(routes), blank, wide(target)], axis=1
    )
    tok = jnp.pad(tok, ((0, 0), (0, PAIR - tok.shape[1]))).T
    blocks, small, rows, tok, hid, cot = (run_gather if planned else gather_plain)(
        jnp.concatenate([wqkv_own, w_attn_out], axis=1), small, tok, hidden, cotangent
    )
    blocks = blocks.reshape(width, -1)
    wqkv = blocks[:, : 3 * heads_width]
    wout = blocks[:, 3 * heads_width :]
    cosine, sine = (jnp.asarray(table) for table in rotary_tables(length))
    shard_rows, hidden_units = w_expert_out.shape[1:]
    shard = jnp.concatenate(
        [w_expert_in.reshape(experts, shard_rows, 2 * hidden_units), w_expert_out], axis=2
    )
    s1, qkv, lse, mixed, mid, s2, tok, lines, gathered = run_forward(
        hid, tok, wqkv, wout, small, rows, cosine, sine, shard
    )
    expert_weights = join_weights(gathered, experts)
    peers = 2 * experts
    half = capacity // 2
    block = half // 2
    place = jnp.arange(peers * block)
    owner = (lax.axis_index("fsdp") + place // block) % peers
    slot = wide(
        (owner // 2) * capacity
        + lax.axis_index("tp") * half
        + (owner % 2) * block
        + place % block
    )
    results, grad_rows, grads_exp = run_expert(
        s2, cot, lines, jnp.broadcast_to(slot[:, None], (slot.shape[0], PAIR)), expert_weights
    )
    grad_hidden, base, for_other, big, arrived = run_backward(
        results.reshape(-1, width),
        grad_rows.reshape(-1, width),
        jnp.broadcast_to(slot[None, :], (8, slot.shape[0])),
        tok,
        cot,
        mid,
        s1,
        qkv,
        lse,
        mixed,
        wqkv,
        wout,
        small,
        rows,
        cosine,
        sine,
        hidden,
        split_grads(grads_exp),
    )
    finish = run_finish if planned else finish_plain
    output, grad_qkv, grad_attn_out, last, grad_in_exp, grad_out_exp = finish(
        big, wqkv_own, for_other, base, arrived
    )
    return (
        output,
        grad_hidden,
        last[:, 0] / wide(attn_norm),
        last[:, 1],
        grad_qkv,
        grad_attn_out,
        last[:, ROUTER:MIXING],
        last[:, MIXING:VALUE],
        last[:, VALUE : VALUE + 2],
        grad_in_exp,
        grad_out_exp,
    )


def solution(mesh):
    in_specs = (
        P(("fsdp", "tp"), None),
        P(("fsdp", "tp"), None),
        P(("fsdp", "tp"), None),
        P(("fsdp", "tp"), None),
        P(("fsdp", "tp"), None),
        P(("fsdp", "tp"), None),
        P(("fsdp", "tp")),
        P(("fsdp", "tp")),
        P("fsdp", None, "tp"),
        P("fsdp", "tp"),
        P(("fsdp", "tp"), None),
        P(("fsdp", "tp"), None),
        P(("fsdp", "tp"), None),
        P(None, "fsdp", None, "tp"),
        P(None, "fsdp", "tp"),
    )
    out_specs = (
        P(("fsdp", "tp"), None),
        P(("fsdp", "tp"), None),
        P(("fsdp", "tp")),
        P(("fsdp", "tp")),
        P("fsdp", None, "tp"),
        P("fsdp", "tp"),
        P(("fsdp", "tp"), None),
        P(("fsdp", "tp"), None),
        P(("fsdp", "tp"), None),
        P(None, "fsdp", None, "tp"),
        P(None, "fsdp", "tp"),
    )
    return jax.shard_map(shards, mesh=mesh, in_specs=in_specs, out_specs=out_specs, check_vma=False)
```

```python
import jax
import jax.numpy as jnp
import numpy as np
from jax import lax
from jax.experimental import pallas as pl
from jax.experimental.pallas import tpu as pltpu
from jax.sharding import PartitionSpec as P

HD = 64
BLOCK = 256


EPSILON = 1e-06
MESH = pl.DeviceIdType.MESH
PAIR = 2 * HD
SCALING = HD ** (-0.5)
ROUTER = 2
MIXING = 14
VALUE = 18
ROUTE = 20
TARGET = 24
GATE = 26
COPY = 9


TILE = 256


def swap(values):
    return lax.ppermute(values, "tp", [(0, 1), (1, 0)])


def gather_rows(values):
    other = swap(values)
    first = lax.axis_index("tp") == 0
    return jnp.concatenate(
        [jnp.where(first, values, other), jnp.where(first, other, values)], axis=0
    )


def own_half(values):
    half = values.shape[0] // 2
    return lax.dynamic_slice_in_dim(values, lax.axis_index("tp") * half, half, 0)


def other_half(values):
    half = values.shape[0] // 2
    return lax.dynamic_slice_in_dim(values, (1 - lax.axis_index("tp")) * half, half, 0)


def member_groups(size, experts):
    span = 2 * experts
    starts = range(0, size, span)
    cores = [[start + 2 * e, start + 2 * e + 1] for start in starts for e in range(experts)]
    across = [[start + r for start in starts] for r in range(span)]
    return cores, across


def own_core(values, rows):
    parts = values.reshape(-1, 2, rows, values.shape[-1])
    return lax.dynamic_index_in_dim(parts, lax.axis_index("fsdp") % 2, 1, keepdims=False)


def join_weights(got, experts):
    size = lax.axis_size("fsdp")
    if size == 2 * experts:
        return got
    cores, across = member_groups(size, experts)
    got = lax.all_gather(got, "fsdp", axis=1, axis_index_groups=cores, tiled=True)
    got = got.reshape(-1, got.shape[-1])
    got = lax.all_gather(got, "fsdp", axis=0, axis_index_groups=across, tiled=True)
    return own_core(got, got.shape[0] // (2 * experts))


def split_grads(grads):
    experts, _, columns = grads.shape
    size = lax.axis_size("fsdp")
    if size == 2 * experts:
        return grads
    cores, across = member_groups(size, experts)
    grads = lax.all_gather(grads[:, None], "fsdp", axis=1, axis_index_groups=cores, tiled=True)
    grads = grads.reshape(-1, columns)
    grads = lax.psum_scatter(
        grads, "fsdp", scatter_dimension=0, axis_index_groups=across, tiled=True
    )
    return own_core(grads, grads.shape[0] // (2 * experts))


def gather_plain(block, small, tok, hid):
    size = lax.axis_size("fsdp")
    small = lax.all_gather(small, ("fsdp", "tp"), axis=0, tiled=True)
    tok = lax.all_gather(tok, "tp", axis=1, tiled=True).T
    tok = jnp.pad(tok, ((0, 0), (0, PAIR - tok.shape[1])))
    return (
        lax.all_gather(block, "fsdp", axis=0),
        low(small),
        small.T[:8],
        tok,
        gather_rows(hid),
    )


def finish_plain(big, wqkv, other, base, arrived):
    heads_width = (big.shape[1] - PAIR) // 4
    reduced = wide(lax.psum_scatter(big, "fsdp", scatter_dimension=0, tiled=True))
    flat = reduced[:, : 3 * heads_width]
    share = jnp.sum(flat * wide(wqkv), axis=1, keepdims=True)
    last = jnp.concatenate([share, reduced[:, 4 * heads_width + 1 :]], axis=1)
    experts, rows, columns = arrived.shape
    hidden = columns // 3
    wide_grads = wide(arrived)
    return (
        low(base + wide(swap(other))),
        flat.reshape(-1, 3, heads_width),
        reduced[:, 3 * heads_width : 4 * heads_width],
        own_half(last) + swap(other_half(last)),
        wide_grads[:, :, : 2 * hidden].reshape(experts, rows, 2, hidden),
        wide_grads[:, :, 2 * hidden :],
    )


def nt_dot(left, right):
    return lax.dot_general(left, right, (((1,), (1,)), ((), ())), preferred_element_type=jnp.float32)


def nn_dot(left, right):
    return jnp.dot(left, right, preferred_element_type=jnp.float32)


def tn_dot(left, right):
    return lax.dot_general(left, right, (((0,), (0,)), ((), ())), preferred_element_type=jnp.float32)


def low(values):
    return values.astype(jnp.bfloat16)


def wide(values):
    return values.astype(jnp.float32)


def rotary_tables(length):
    half = HD // 2
    positions = np.arange(length, dtype=np.float32)
    inverse = np.power(np.float32(10000.0), -np.arange(half, dtype=np.float32) / np.float32(half))
    angles = (positions[:, None] * inverse[None, :].astype(np.float32)).astype(np.float32)
    cosine = np.cos(angles.astype(np.float64)).astype(np.float32)
    sine = np.sin(angles.astype(np.float64)).astype(np.float32)
    return (
        np.concatenate([cosine] * 4, axis=1),
        np.concatenate([-sine, sine, -sine, sine], axis=1),
    )


def turn(values, cosine, sine):
    lane = lax.broadcasted_iota(jnp.int32, values.shape, 1)
    upper = lax.rem(lane, HD) >= HD // 2
    partner = jnp.where(
        upper, pltpu.roll(values, HD // 2, 1), pltpu.roll(values, PAIR - HD // 2, 1)
    )
    return values * cosine + partner * sine


def head_lanes(shape, half, axis):
    return (lax.broadcasted_iota(jnp.int32, shape, axis) >= HD) == bool(half)


def mean_last(values):
    return jnp.mean(values, axis=-1, keepdims=True)


def to_partner(source, target, send_sem, recv_sem):
    return pltpu.make_async_remote_copy(
        src_ref=source,
        dst_ref=target,
        send_sem=send_sem,
        recv_sem=recv_sem,
        device_id={"tp": 1 - lax.axis_index("tp")},
        device_id_type=MESH,
    )


def block_rows(block):
    return slice(block * BLOCK, (block + 1) * BLOCK)


def column(values, index):
    return values[:, index : index + 1]


def lane_matrix(shape, columns):
    lane = lax.broadcasted_iota(jnp.int32, shape, 1)
    total = jnp.zeros(shape, jnp.float32)
    for index, values in columns:
        total = jnp.where(lane == index, values, total)
    return total


def send_to(source, target, send_sem, recv_sem, device):
    return pltpu.make_async_remote_copy(
        src_ref=source,
        dst_ref=target,
        send_sem=send_sem,
        recv_sem=recv_sem,
        device_id=device,
        device_id_type=MESH,
    )


def greet_group(peers):
    me = lax.axis_index("fsdp")
    rank = lax.rem(me, peers)
    barrier = pltpu.get_barrier_semaphore()
    for k in range(1, peers):
        pl.semaphore_signal(
            barrier,
            inc=1,
            device_id={"fsdp": me - rank + lax.rem(rank + k, peers)},
            device_id_type=MESH,
        )
    pl.semaphore_signal(
        barrier, inc=1, device_id={"tp": 1 - lax.axis_index("tp")}, device_id_type=MESH
    )
    pl.semaphore_wait(barrier, peers)


def each(first, last, body):
    def step(k, carry):
        body(k)
        return carry

    lax.fori_loop(first, last, step, 0)


class CoreExchange:
    def __init__(self, source, target, send_sem, recv_sem):
        experts = source.shape[0]
        me = lax.axis_index("fsdp")
        rank = lax.rem(me, 2 * experts)
        core = lax.rem(rank, 2)
        mine = rank // 2

        def copy(k):
            ahead = lax.rem(mine + k, experts)
            return send_to(
                source.at[ahead],
                target.at[mine],
                send_sem.at[k],
                recv_sem.at[k],
                {"fsdp": me - rank + 2 * ahead + core},
            )

        def arrival(k):
            behind = lax.rem(mine + experts - k, experts)
            return send_to(
                source.at[behind],
                target.at[behind],
                send_sem.at[k],
                recv_sem.at[k],
                {"fsdp": me - rank + 2 * behind + core},
            )

        self.experts, self.copy, self.arrival = experts, copy, arrival
        self.source, self.target, self.mine = source, target, mine

    def start(self):
        each(1, self.experts, lambda k: self.copy(k).start())
        self.target[self.mine] = self.source[self.mine]

    def wait(self):
        each(1, self.experts, lambda k: self.copy(k).wait_send())
        each(1, self.experts, lambda k: self.arrival(k).wait_recv())


def gather_kernel(
    block_ref,
    small_ref,
    tok_ref,
    hid_ref,
    all_ref,
    small_out_ref,
    rows_out_ref,
    tok_out_ref,
    hid_out_ref,
    small_all_ref,
    tok_all_ref,
    y_send,
    y_recv,
    up_send,
    up_recv,
    down_send,
    down_recv,
    x_send,
    x_recv,
    core_send,
    core_recv,
):
    size = all_ref.shape[0]
    planes = size // 4
    me = lax.axis_index("fsdp")
    tp = lax.axis_index("tp")
    z, x, core = me // 4, lax.rem(me // 2, 2), lax.rem(me, 2)
    shard = small_ref.shape[0]
    own_rows = hid_ref.shape[0]
    greet_group(size)
    partner = {"tp": 1 - tp}
    small_y = send_to(small_ref, small_all_ref.at[me, tp], y_send.at[0], y_recv.at[0], partner)
    small_y.start()
    all_ref[me] = block_ref[...]
    small_all_ref[me, tp] = small_ref[...]
    mine = pl.ds(pl.multiple_of(tp * own_rows, own_rows), own_rows)
    hid_y = send_to(hid_ref, hid_out_ref.at[mine], y_send.at[1], y_recv.at[1], partner)
    tok_y = send_to(tok_ref, tok_all_ref.at[tp], y_send.at[2], y_recv.at[2], partner)
    hid_y.start()
    tok_y.start()

    def number(plane, line):
        return plane * 4 + line * 2 + core

    def piece(kind, number_of, send, recv, slot, device):
        array = small_all_ref if kind else all_ref
        return send_to(
            array.at[number_of],
            array.at[number_of],
            send.at[kind, slot],
            recv.at[kind, slot],
            device,
        )

    def up(kind, step, plane):
        device = {"fsdp": number(lax.min(z + 1, planes - 1), x)}
        return piece(kind, number(plane, x), up_send, up_recv, step, device)

    def down(kind, step, plane):
        device = {"fsdp": number(lax.max(z - 1, 0), x)}
        return piece(kind, number(plane, x), down_send, down_recv, step, device)

    def side(kind, plane, line):
        device = {"fsdp": number(z, 1 - x)}
        return piece(kind, number(plane, line), x_send, x_recv, plane, device)

    def sibling(kind, plane, line, parity):
        return piece(
            kind,
            plane * 4 + line * 2 + parity,
            core_send,
            core_recv,
            plane * 2 + line,
            {"fsdp": me + 1 - 2 * core},
        )

    def launch(kind):
        @pl.when(z < planes - 1)
        def _():
            up(kind, 0, z).start()

        @pl.when(z > 0)
        def _():
            down(kind, 0, z).start()

        side(kind, z, x).start()
        sibling(kind, z, x, core).start()

    launch(0)
    hid_out_ref[mine, :] = hid_ref[...]
    tok_all_ref[tp] = tok_ref[...]
    small_y.wait()
    launch(1)
    for step in range(1, planes):
        for kind in range(2):

            @pl.when(z >= step)
            def _():
                up(kind, step - 1, z - step).wait_recv()

                @pl.when(z < planes - 1)
                def _():
                    up(kind, step, z - step).start()

                side(kind, z - step, x).start()
                sibling(kind, z - step, x, core).start()

            @pl.when(z + step < planes)
            def _():
                down(kind, step - 1, z + step).wait_recv()

                @pl.when(z > 0)
                def _():
                    down(kind, step, z + step).start()

                side(kind, z + step, x).start()
                sibling(kind, z + step, x, core).start()

    for step in range(planes):
        for kind in range(2):

            @pl.when(z >= step)
            def _():
                side(kind, z - step, 1 - x).wait_recv()
                sibling(kind, z - step, 1 - x, core).start()

            if step > 0:

                @pl.when(z + step < planes)
                def _():
                    side(kind, z + step, 1 - x).wait_recv()
                    sibling(kind, z + step, 1 - x, core).start()

    for plane in range(planes):
        for line in range(2):
            for kind in range(2):
                sibling(kind, plane, line, 1 - core).wait_recv()
    small_all = small_all_ref[...].reshape(size * 2 * shard, small_ref.shape[1])
    small_out_ref[...] = low(small_all)
    rows_out_ref[...] = small_all.T[:8, :]
    tok_y.wait()
    for part in range(2):
        lanes = slice(part * own_rows, (part + 1) * own_rows)
        tok_pad = jnp.zeros((PAIR - tok_ref.shape[0], own_rows), jnp.float32)
        tok_out_ref[lanes, :] = jnp.concatenate([tok_all_ref[part], tok_pad], axis=0).T
    for kind in range(2):
        for step in range(planes):

            @pl.when(jnp.logical_and(z >= step, z < planes - 1))
            def _():
                up(kind, step, z - step).wait_send()

            @pl.when(jnp.logical_and(z + step < planes, z > 0))
            def _():
                down(kind, step, z + step).wait_send()

        for plane in range(planes):
            side(kind, plane, x).wait_send()
            for line in range(2):
                sibling(kind, plane, line, core).wait_send()
    hid_y.wait()


def run_gather(block, small, tok, hid):
    size = lax.axis_size("fsdp")
    own_rows, width = hid.shape
    vmem = pl.BlockSpec(memory_space=pltpu.VMEM)
    low_t, wide_t = jnp.bfloat16, jnp.float32
    dma = pltpu.SemaphoreType.DMA
    return pl.pallas_call(
        gather_kernel,
        in_specs=[vmem] * 4,
        out_specs=[vmem] * 5,
        out_shape=[
            jax.ShapeDtypeStruct((size,) + block.shape, low_t),
            jax.ShapeDtypeStruct((width, PAIR), low_t),
            jax.ShapeDtypeStruct((8, width), wide_t),
            jax.ShapeDtypeStruct((2 * own_rows, PAIR), wide_t),
            jax.ShapeDtypeStruct((2 * own_rows, width), low_t),
        ],
        scratch_shapes=[
            pltpu.VMEM((size, 2) + small.shape, wide_t),
            pltpu.VMEM((2,) + tok.shape, wide_t),
            dma((3,)),
            dma((3,)),
        ]
        + [dma((2, size // 4))] * 6
        + [dma((2, size // 2))] * 2,
        compiler_params=pltpu.CompilerParams(
            collective_id=3, has_side_effects=True, vmem_limit_bytes=60 << 20
        ),
    )(block, small, tok, hid)


def finish_kernel(
    big_ref,
    wqkv_ref,
    other_ref,
    base_ref,
    expert_ref,
    out_ref,
    qkv_ref,
    attn_ref,
    tail_ref,
    in_ref,
    down_ref,
    sum_ref,
    core_ref,
    side_ref,
    acc_ref,
    usend_ref,
    urecv_ref,
    dsend_ref,
    drecv_ref,
    y_ref,
    tsend_ref,
    trecv_ref,
    core_send,
    core_recv,
    x_send,
    x_recv,
    up_send,
    up_recv,
    dn_send,
    dn_recv,
    y_send,
    y_recv,
):
    size = big_ref.shape[0]
    planes = size // 4
    me = lax.axis_index("fsdp")
    tp = lax.axis_index("tp")
    z, x, core = me // 4, lax.rem(me // 2, 2), lax.rem(me, 2)
    heads_width = attn_ref.shape[1]
    greet_group(size)
    partner = {"tp": 1 - tp}

    def to_core(plane, line):
        slot = plane * 2 + line
        return send_to(
            big_ref.at[plane * 4 + line * 2 + 1 - core],
            core_ref.at[slot],
            core_send.at[slot],
            core_recv.at[slot],
            {"fsdp": me + 1 - 2 * core},
        )

    def to_side(plane):
        return send_to(
            sum_ref.at[plane],
            side_ref.at[plane],
            x_send.at[plane],
            x_recv.at[plane],
            {"fsdp": z * 4 + (1 - x) * 2 + core},
        )

    def to_up(plane):
        return send_to(
            usend_ref.at[plane],
            urecv_ref.at[plane],
            up_send.at[plane],
            up_recv.at[plane],
            {"fsdp": lax.min(z + 1, planes - 1) * 4 + x * 2 + core},
        )

    def to_down(plane):
        return send_to(
            dsend_ref.at[plane],
            drecv_ref.at[plane],
            dn_send.at[plane],
            dn_recv.at[plane],
            {"fsdp": lax.max(z - 1, 0) * 4 + x * 2 + core},
        )

    order = [planes - 1, 0, 2, 1]
    for plane in order:
        to_core(plane, 1 - x).start()
    for plane in order:
        to_core(plane, x).start()
    out_y = send_to(other_ref, y_ref, y_send.at[0], y_recv.at[0], partner)
    out_y.start()

    def joined(plane, line):
        to_core(plane, line).wait_recv()
        return wide(big_ref[plane * 4 + line * 2 + core]) + wide(core_ref[plane * 2 + line])

    for plane in order:
        sum_ref[plane] = low(joined(plane, 1 - x))
        to_side(plane).start()
    for plane in order:
        acc_ref[plane] = joined(plane, x)
    experts, shard, total = expert_ref.shape
    hidden = total // 3

    def lay_out(e):
        values = wide(expert_ref[e])
        in_ref[e, :, 0, :] = values[:, :hidden]
        in_ref[e, :, 1, :] = values[:, hidden : 2 * hidden]
        down_ref[e] = values[:, 2 * hidden :]

    each(0, experts, lay_out)

    def ready(plane):
        to_side(plane).wait_recv()
        acc_ref[plane] += wide(side_ref[plane])

    def rise(plane):
        @pl.when(jnp.logical_and(z > 0, z <= plane))
        def _():
            to_up(plane).wait_recv()
            acc_ref[plane] += wide(urecv_ref[plane])

        @pl.when(z < plane)
        def _():
            usend_ref[plane] = low(acc_ref[plane])
            to_up(plane).start()

    def fall(plane):
        @pl.when(jnp.logical_and(z < planes - 1, z >= plane))
        def _():
            to_down(plane).wait_recv()
            acc_ref[plane] += wide(drecv_ref[plane])

        @pl.when(z > plane)
        def _():
            dsend_ref[plane] = low(acc_ref[plane])
            to_down(plane).start()

    ready(3)
    rise(3)
    ready(0)
    fall(0)
    ready(2)
    rise(2)
    ready(1)
    fall(1)
    rise(1)
    fall(2)
    rise(0)
    fall(3)
    values = acc_ref[z]
    flat = values[:, : 3 * heads_width]
    for part in range(3):
        qkv_ref[:, part, :] = flat[:, part * heads_width : (part + 1) * heads_width]
    attn_ref[...] = values[:, 3 * heads_width : 4 * heads_width]
    share = jnp.sum(flat * wide(wqkv_ref[...]), axis=1, keepdims=True)
    last = values[:, 4 * heads_width :]
    last = jnp.where(lax.broadcasted_iota(jnp.int32, last.shape, 1) == 0, share, last)
    part_rows = tail_ref.shape[0]
    tsend_ref[0] = last[:part_rows, :]
    tsend_ref[1] = last[part_rows:, :]
    tail_y = send_to(tsend_ref.at[1 - tp], trecv_ref, y_send.at[1], y_recv.at[1], partner)
    tail_y.start()
    out_y.wait()
    out_ref[...] = low(base_ref[...] + wide(y_ref[...]))
    tail_y.wait()
    tail_ref[...] = tsend_ref[tp] + trecv_ref[...]
    for plane in range(planes):
        to_core(plane, 1 - x).wait_send()
        to_core(plane, x).wait_send()
        to_side(plane).wait_send()

        @pl.when(z < plane)
        def _():
            to_up(plane).wait_send()

        @pl.when(z > plane)
        def _():
            to_down(plane).wait_send()


def run_finish(big, wqkv, other, base, arrived):
    size = lax.axis_size("fsdp")
    planes = size // 4
    own_rows, width = base.shape
    columns = big.shape[1]
    heads_width = (columns - PAIR) // 4
    shard = width // size
    experts, _, total = arrived.shape
    hidden = total // 3
    vmem = pl.BlockSpec(memory_space=pltpu.VMEM)
    low_t, wide_t = jnp.bfloat16, jnp.float32
    dma = pltpu.SemaphoreType.DMA
    line = (planes, shard, columns)
    return pl.pallas_call(
        finish_kernel,
        in_specs=[vmem] * 5,
        out_specs=[vmem] * 6,
        out_shape=[
            jax.ShapeDtypeStruct((own_rows, width), low_t),
            jax.ShapeDtypeStruct((shard, 3, heads_width), wide_t),
            jax.ShapeDtypeStruct((shard, heads_width), wide_t),
            jax.ShapeDtypeStruct((shard // 2, PAIR), wide_t),
            jax.ShapeDtypeStruct((experts, shard, 2, hidden), wide_t),
            jax.ShapeDtypeStruct((experts, shard, hidden), wide_t),
        ],
        scratch_shapes=[
            pltpu.VMEM(line, low_t),
            pltpu.VMEM((2 * planes, shard, columns), low_t),
            pltpu.VMEM(line, low_t),
            pltpu.VMEM(line, wide_t),
            pltpu.VMEM(line, low_t),
            pltpu.VMEM(line, low_t),
            pltpu.VMEM(line, low_t),
            pltpu.VMEM(line, low_t),
            pltpu.VMEM((own_rows, width), low_t),
            pltpu.VMEM((2, shard // 2, PAIR), wide_t),
            pltpu.VMEM((shard // 2, PAIR), wide_t),
            dma((2 * planes,)),
            dma((2 * planes,)),
        ]
        + [dma((planes,))] * 6
        + [dma((2,))] * 2,
        compiler_params=pltpu.CompilerParams(
            collective_id=4, has_side_effects=True, vmem_limit_bytes=60 << 20
        ),
    )(big.reshape(size, shard, columns), wqkv, other, base, arrived)


def expert_kernel(
    s2_ref,
    cot_ref,
    line_ref,
    slot_ref,
    weight_ref,
    res_out_ref,
    dx_out_ref,
    grads_out_ref,
    xs_ref,
    gs_ref,
    x_ref,
    g_ref,
    w_ref,
    gate_ref,
    up_ref,
    act_ref,
    xt_ref,
    gt_ref,
    acc_ref,
    grads_ref,
    sibling_ref,
    ysend_ref,
    yrecv_ref,
    w_sem,
    grad_sem,
    xs_sem,
    xr_sem,
    gs_sem,
    gr_sem,
    xfs_sem,
    xfr_sem,
    gfs_sem,
    gfr_sem,
    ys_sem,
    yr_sem,
    rs_sem,
    rr_sem,
    ds_sem,
    dr_sem,
):
    peers, rows, width = xs_ref.shape
    total = peers * rows
    hidden = gate_ref.shape[1]
    tiles = hidden // TILE
    me = lax.axis_index("fsdp")
    tp = lax.axis_index("tp")
    rank = lax.rem(me, peers)
    core = lax.rem(rank, 2)
    start = me - rank

    def peer(k):
        other = start
        bit = 1
        while bit < peers:
            ours, theirs = lax.rem(rank // bit, 2), lax.rem(k // bit, 2)
            other = other + bit * (ours + theirs - 2 * ours * theirs)
            bit *= 2
        return {"fsdp": other}

    partner = {"tp": 1 - tp}
    sibling = {"fsdp": start + rank + 1 - 2 * core}

    def out_x(k):
        return send_to(xs_ref.at[k], x_ref.at[0, k], xs_sem.at[k], xr_sem.at[k], peer(k))

    def out_g(k):
        return send_to(gs_ref.at[k], g_ref.at[0, k], gs_sem.at[k], gr_sem.at[k], peer(k))

    def pass_x(k):
        return send_to(x_ref.at[0, k], x_ref.at[1, k], xfs_sem.at[k], xfr_sem.at[k], partner)

    def pass_g(k):
        return send_to(g_ref.at[0, k], g_ref.at[1, k], gfs_sem.at[k], gfr_sem.at[k], partner)

    def across(index, k):
        return send_to(
            ysend_ref.at[index, k],
            yrecv_ref.at[index, k],
            ys_sem.at[index, k],
            yr_sem.at[index, k],
            partner,
        )

    def back(index, k):
        if index == 0:
            return send_to(xs_ref.at[k], res_out_ref.at[k], rs_sem.at[k], rr_sem.at[k], peer(k))
        return send_to(gs_ref.at[k], dx_out_ref.at[k], ds_sem.at[k], dr_sem.at[k], peer(k))

    def return_order(body):
        def step(j, carry):
            body(8 + 2 * j)
            body(4 + j)
            body(9 + 2 * j)
            return carry

        lax.fori_loop(0, 4, step, 0)
        for k in (2, 3, 1, 0):
            body(k)

    def join(index, k):
        across(index, k).wait_recv()
        own = xs_ref if index == 0 else gs_ref
        own[k] = low(wide(own[k]) + wide(yrecv_ref[index, k]))
        back(index, k).start()

    def join_some(index, tile):
        join(index, 8 + 2 * tile)
        join(index, 4 + tile)
        join(index, 9 + 2 * tile)

    def join_last(index):
        for k in (2, 3, 1):
            join(index, k)
        across(index, 0).wait_recv()
        own, target = (xs_ref, res_out_ref) if index == 0 else (gs_ref, dx_out_ref)
        target[0] = low(wide(own[0]) + wide(yrecv_ref[index, 0]))

    greet_group(peers)
    here = pltpu.make_async_copy(weight_ref, w_ref.at[:, core], w_sem.at[0])
    here.start()
    there = send_to(weight_ref, w_ref.at[:, core], w_sem.at[1], w_sem.at[2], sibling)
    half = total // 2
    halves = []
    for part in range(2):
        blocks = slice(part * peers // 2, (part + 1) * peers // 2)
        ids = slot_ref[part * half : (part + 1) * half, 0:1]
        hits = [line_ref[m : m + 1, :] == ids for m in range(2)]
        onehot = low(jnp.where(hits[0] | hits[1], 1.0, 0.0))
        xs_ref[blocks] = low(nn_dot(onehot, s2_ref[...])).reshape(peers // 2, rows, width)
        if part == 0:
            x_ref[0, 0] = xs_ref[0]
            pass_x(0).start()
        each(max(1, part * peers // 2), (part + 1) * peers // 2, lambda k: out_x(k).start())
        halves.append((blocks, onehot, hits))
    there.start()
    for part in range(2):
        blocks, onehot, hits = halves[part]
        gate = sum(
            jnp.sum(jnp.where(hits[m], line_ref[2 + m : 3 + m, :], 0.0), axis=1, keepdims=True)
            for m in range(2)
        )
        gs_ref[blocks] = low(nn_dot(onehot, cot_ref[...]) * gate).reshape(peers // 2, rows, width)
        if part == 0:
            g_ref[0, 0] = gs_ref[0]
        each(max(1, part * peers // 2), (part + 1) * peers // 2, lambda k: out_g(k).start())

    def forward_x(k):
        out_x(k).wait_recv()
        pass_x(k).start()

    each(1, peers, forward_x)
    pass_g(0).start()
    here.wait()
    send_to(weight_ref, w_ref.at[:, 1 - core], w_sem.at[1], w_sem.at[2], sibling).wait_recv()
    there.wait_send()
    each(0, peers, lambda k: pass_x(k).wait_recv())

    def weights(which, lanes):
        return w_ref[:, :, :, pl.ds(pl.multiple_of(which * hidden + lanes, TILE), TILE)].reshape(
            width, TILE
        )

    acc_ref[...] = jnp.zeros_like(acc_ref)

    def forward_tile(tile, carry):
        lanes = pl.multiple_of(tile * TILE, TILE)
        here_lanes = pl.ds(lanes, TILE)
        x = x_ref[...].reshape(2 * total, width)
        gate = nn_dot(x, weights(0, lanes))
        up = nn_dot(x, weights(1, lanes))
        gate_ref[:, here_lanes] = low(gate)
        up_ref[:, here_lanes] = low(up)
        act = low(gate / (1.0 + jnp.exp(-gate)) * up)
        act_ref[:, here_lanes] = act
        acc_ref[...] += nt_dot(act, weights(2, lanes))

        def forward_g(k):
            @pl.when(k > 0)
            def _():
                out_g(k).wait_recv()
                pass_g(k).start()

        each(tile * (peers // tiles), (tile + 1) * (peers // tiles), forward_g)
        return carry

    lax.fori_loop(0, tiles, forward_tile, 0)
    each(1, peers, lambda k: out_x(k).wait_send())
    xs_ref[...] = low(acc_ref[:total, :]).reshape(peers, rows, width)
    ysend_ref[0] = low(acc_ref[total:, :]).reshape(peers, rows, width)
    return_order(lambda k: across(0, k).start())
    xt_ref[...] = x_ref[...].reshape(2 * total, width).T
    acc_ref[...] = jnp.zeros_like(acc_ref)
    each(0, peers, lambda k: pass_g(k).wait_recv())

    def slope_tile(tile, carry):
        lanes = pl.multiple_of(tile * TILE, TILE)
        here_lanes = pl.ds(lanes, TILE)
        gate = wide(gate_ref[:, here_lanes])
        up = wide(up_ref[:, here_lanes])
        sig = 1.0 / (1.0 + jnp.exp(-gate))
        d_act = nn_dot(g_ref[...].reshape(2 * total, width), weights(2, lanes))
        d_up = low(d_act * gate * sig)
        d_gate = low(d_act * up * sig * (1.0 + gate * (1.0 - sig)))
        gate_ref[:, here_lanes] = d_gate
        up_ref[:, here_lanes] = d_up
        acc_ref[...] += nt_dot(d_gate, weights(0, lanes)) + nt_dot(d_up, weights(1, lanes))
        join_some(0, tile)
        return carry

    lax.fori_loop(0, tiles, slope_tile, 0)
    join_last(0)
    each(1, peers, lambda k: out_g(k).wait_send())
    gs_ref[...] = low(acc_ref[:total, :]).reshape(peers, rows, width)
    ysend_ref[1] = low(acc_ref[total:, :]).reshape(peers, rows, width)
    return_order(lambda k: across(1, k).start())
    gt_ref[...] = g_ref[...].reshape(2 * total, width).T

    def weight_tile(tile, carry):
        lanes = pl.multiple_of(tile * TILE, TILE)
        here_lanes = pl.ds(lanes, TILE)

        def keep(which, values):
            grads_ref[
                :, :, :, pl.ds(pl.multiple_of(which * hidden + lanes, TILE), TILE)
            ] = low(values).reshape(peers // 2, 2, rows, TILE)

        keep(0, nn_dot(xt_ref[...], gate_ref[:, here_lanes]))
        keep(1, nn_dot(xt_ref[...], up_ref[:, here_lanes]))
        keep(2, nn_dot(gt_ref[...], act_ref[:, here_lanes]))
        join_some(1, tile)
        return carry

    lax.fori_loop(0, tiles, weight_tile, 0)
    join_last(1)
    swap_grads = send_to(
        grads_ref.at[:, 1 - core], sibling_ref, grad_sem.at[0], grad_sem.at[1], sibling
    )
    swap_grads.start()
    each(0, peers, lambda k: pass_x(k).wait_send())
    each(0, peers, lambda k: pass_g(k).wait_send())
    for index in range(2):
        each(0, peers, lambda k: across(index, k).wait_send())
        each(1, peers, lambda k: back(index, k).wait_send())
    swap_grads.wait()
    grads_out_ref[...] = low(wide(grads_ref[:, core]) + wide(sibling_ref[...]))
    for index in range(2):
        each(1, peers, lambda k: back(index, k).wait_recv())


def run_expert(s2, cot, lines, slots, weights):
    length, width = s2.shape
    experts, shard, total = weights.shape
    peers = 2 * experts
    rows = slots.shape[0] // peers
    hidden = total // 3
    both = 2 * peers * rows
    vmem = pl.BlockSpec(memory_space=pltpu.VMEM)
    low_t, wide_t = jnp.bfloat16, jnp.float32
    dma = pltpu.SemaphoreType.DMA
    block = (peers, rows, width)
    return pl.pallas_call(
        expert_kernel,
        in_specs=[vmem] * 4 + [pl.BlockSpec(memory_space=pl.ANY)],
        out_specs=[vmem] * 3,
        out_shape=[
            jax.ShapeDtypeStruct(block, low_t),
            jax.ShapeDtypeStruct(block, low_t),
            jax.ShapeDtypeStruct(weights.shape, low_t),
        ],
        scratch_shapes=[
            pltpu.VMEM(block, low_t),
            pltpu.VMEM(block, low_t),
            pltpu.VMEM((2,) + block, low_t),
            pltpu.VMEM((2,) + block, low_t),
            pltpu.VMEM((experts, 2, shard, total), low_t),
            pltpu.VMEM((both, hidden), low_t),
            pltpu.VMEM((both, hidden), low_t),
            pltpu.VMEM((both, hidden), low_t),
            pltpu.VMEM((width, both), low_t),
            pltpu.VMEM((width, both), low_t),
            pltpu.VMEM((both, width), wide_t),
            pltpu.VMEM((experts, 2, shard, total), low_t),
            pltpu.VMEM((experts, shard, total), low_t),
            pltpu.VMEM((2,) + block, low_t),
            pltpu.VMEM((2,) + block, low_t),
            dma((3,)),
            dma((2,)),
        ]
        + [dma((peers,))] * 8
        + [dma((2, peers))] * 2
        + [dma((peers,))] * 4,
        compiler_params=pltpu.CompilerParams(
            collective_id=2, has_side_effects=True, vmem_limit_bytes=67043328
        ),
    )(s2, cot, lines, slots, weights)


def forward_kernel(
    hid_ref,
    tok_in_ref,
    wqkv_ref,
    wout_ref,
    small_ref,
    rows_ref,
    cos_ref,
    sin_ref,
    shard_ref,
    cot_ref,
    s1_ref,
    qkv_ref,
    lse_ref,
    mixed_ref,
    mid_ref,
    s2_ref,
    tok_ref,
    line_ref,
    expert_ref,
    cot_all_ref,
    vt_ref,
    send_ref,
    recv_ref,
    send_sem,
    recv_sem,
    wsend_sem,
    wrecv_sem,
    cot_sem,
):
    greet_group(2 * shard_ref.shape[0])
    own_rows = cot_ref.shape[0]
    mine = pl.ds(pl.multiple_of(lax.axis_index("tp") * own_rows, own_rows), own_rows)
    cot_copy = to_partner(cot_ref, cot_all_ref.at[mine], cot_sem.at[0], cot_sem.at[1])
    cot_copy.start()
    experts = CoreExchange(shard_ref, expert_ref, wsend_sem, wrecv_sem)
    experts.start()
    cot_all_ref[mine, :] = cot_ref[...]
    blocks = hid_ref.shape[0] // BLOCK
    heads_width = wout_ref.shape[1]
    pairs = heads_width // PAIR
    gain_one = rows_ref[0:1, :]
    gain_two = rows_ref[1:2, :]
    copies = []
    lse_ref[...] = jnp.zeros_like(lse_ref)
    for block in range(blocks):
        rows = block_rows(block)
        keys = (block + 1) * BLOCK
        source = wide(hid_ref[rows, :])
        s1 = low(source * lax.rsqrt(mean_last(source * source) + EPSILON) * gain_one)
        s1_ref[rows, :] = s1
        cosine, sine = cos_ref[rows, :], sin_ref[rows, :]
        for part in range(3):
            projected = nn_dot(s1, wqkv_ref[:, part * heads_width : (part + 1) * heads_width])
            for pair in range(pairs):
                chunk = projected[:, pair * PAIR : (pair + 1) * PAIR]
                if part < 2:
                    chunk = turn(chunk, cosine, sine)
                else:
                    vt_ref[pair * PAIR : (pair + 1) * PAIR, rows] = low(chunk.T)
                start = part * heads_width + pair * PAIR
                qkv_ref[rows, start : start + PAIR] = low(chunk)
        for pair in range(pairs):
            lanes = slice(pair * PAIR, (pair + 1) * PAIR)
            query = qkv_ref[rows, lanes] * jnp.bfloat16(SCALING)
            key = qkv_ref[:keys, heads_width + pair * PAIR : heads_width + (pair + 1) * PAIR]
            value_t = vt_ref[lanes, :keys]
            gathered = None
            for half in range(2):
                masked = jnp.where(head_lanes(query.shape, half, 1), query, jnp.bfloat16(0))
                scores = nt_dot(key, masked)
                highest = jnp.max(scores, axis=0, keepdims=True)
                expanded = jnp.exp(scores - highest)
                totals = jnp.sum(expanded, axis=0, keepdims=True)
                probs = low(expanded * (1.0 / totals))
                lse_ref[2 * pair + half : 2 * pair + half + 1, rows] = highest + jnp.log(totals)
                found = nn_dot(value_t, probs)
                gathered = (
                    found
                    if half == 0
                    else jnp.where(head_lanes(found.shape, 1, 0), found, gathered)
                )
            mixed_ref[rows, lanes] = low(gathered.T)
        send_ref[block] = low(nt_dot(mixed_ref[rows, :], wout_ref[...]))
        copy = to_partner(
            send_ref.at[block], recv_ref.at[block], send_sem.at[block], recv_sem.at[block]
        )
        copy.start()
        copies.append(copy)
    for block in range(blocks):
        rows = block_rows(block)
        copies[block].wait()
        mid = wide(hid_ref[rows, :]) + (wide(send_ref[block]) + wide(recv_ref[block]))
        mid_ref[rows, :] = mid
        s2 = low(mid * lax.rsqrt(mean_last(mid * mid) + EPSILON) * gain_two)
        s2_ref[rows, :] = s2
        tok = tok_in_ref[rows, :]
        lane = lax.broadcasted_iota(jnp.int32, tok.shape, 1)
        logits = nn_dot(s2, small_ref[...]) + tok
        picked = [
            jnp.sum(
                jnp.where(wide(lane - ROUTER) == column(tok, ROUTE + member), logits, 0.0),
                axis=1,
                keepdims=True,
            )
            for member in range(2)
        ]
        gate = [
            1.0 / (1.0 + jnp.exp(picked[1 - member] - picked[member])) for member in range(2)
        ]
        tok = jnp.where(lane == GATE, gate[0], jnp.where(lane == GATE + 1, gate[1], tok))
        tok_ref[rows, :] = tok
        line_ref[:, rows] = tok.T[TARGET : TARGET + 8, :]
    cot_copy.wait()
    experts.wait()


def backward_kernel(
    res_ref,
    dx_ref,
    slot_ref,
    tok_ref,
    cot_ref,
    mid_ref,
    s1_ref,
    qkv_ref,
    lse_ref,
    mixed_ref,
    wqkv_ref,
    wout_ref,
    small_ref,
    rows_ref,
    cos_ref,
    sin_ref,
    own_ref,
    egrad_ref,
    grad_ref,
    base_ref,
    other_ref,
    big_ref,
    arrived_ref,
    gsend_ref,
    grecv_ref,
    hsend_ref,
    hrecv_ref,
    gmid_ref,
    gown_ref,
    kt_ref,
    gm_ref,
    dqt_ref,
    dk_ref,
    dv_ref,
    gp_ref,
    acc_qkv_ref,
    acc_out_ref,
    acc_small_ref,
    acc_gain_ref,
    gsend_sem,
    grecv_sem,
    hsend_sem,
    hrecv_sem,
    esend_sem,
    erecv_sem,
):
    greet_group(2 * egrad_ref.shape[0])
    experts = CoreExchange(egrad_ref, arrived_ref, esend_sem, erecv_sem)
    experts.start()
    tp = lax.axis_index("tp")
    width = dx_ref.shape[1]
    blocks = cot_ref.shape[0] // BLOCK
    heads_width = wout_ref.shape[1]
    pairs = heads_width // PAIR
    gain_one = rows_ref[0:1, :]
    gain_two = rows_ref[1:2, :]
    slot_row = slot_ref[0:1, :]
    order = list(reversed(range(blocks)))
    first = order[0]
    gcopies = {}
    for block in order:
        rows = block_rows(block)
        tok = tok_ref[rows, :]
        onehots = [
            low(jnp.where(column(tok, TARGET + m) == slot_row, 1.0, 0.0)) for m in range(2)
        ]
        placed = [nn_dot(onehot, res_ref[...]) for onehot in onehots]
        cot_wide = wide(cot_ref[rows, :])
        shares = [
            column(tok, GATE + m) * jnp.sum(placed[m] * cot_wide, axis=1, keepdims=True)
            for m in range(2)
        ]
        high = [wide(low(share)) for share in shares]
        gsend_ref[block, :, :width] = low(nn_dot(onehots[0] + onehots[1], dx_ref[...]))
        gsend_ref[block, :, width:] = low(
            lane_matrix(
                tok.shape,
                [
                    (0, high[0]),
                    (1, shares[0] - high[0]),
                    (2, high[1]),
                    (3, shares[1] - high[1]),
                ],
            )
        )
        copy = to_partner(
            gsend_ref.at[block], grecv_ref.at[block], gsend_sem.at[block], grecv_sem.at[block]
        )
        copy.start()
        gcopies[block] = copy
        placed = column(tok, GATE) * placed[0] + column(tok, GATE + 1) * placed[1]
        slab = slice((block % 2) * BLOCK, (block % 2 + 1) * BLOCK)

        @pl.when(tp == block // 2)
        def _():
            base_ref[slab, :] = placed

        @pl.when(tp != block // 2)
        def _():
            other_ref[slab, :] = low(placed)

    kt_ref[...] = qkv_ref[:, heads_width : 2 * heads_width].T
    for block in order:
        rows = block_rows(block)
        keys = (block + 1) * BLOCK
        slab = slice((block % 2) * BLOCK, (block % 2 + 1) * BLOCK)
        mine = tp == block // 2
        mine_f = jnp.where(mine, 1.0, 0.0)
        mid = mid_ref[rows, :]
        cot = cot_ref[rows, :]
        cot_wide = wide(cot)
        tok = tok_ref[rows, :]
        scale = lax.rsqrt(mean_last(mid * mid) + EPSILON)
        unit = mid * scale
        normed = unit * gain_two
        s2 = low(normed)
        small = small_ref[...]
        mixing = nn_dot(s2, small)
        value_dot = nn_dot(cot, small)
        normed_dot = jnp.sum(normed * cot_wide, axis=1, keepdims=True)
        route = [column(tok, ROUTE + member) for member in range(2)]
        gate = [column(tok, GATE + member) for member in range(2)]

        def weight_of(expert):
            return sum(jnp.where(route[m] == expert, gate[m], 0.0) for m in range(2))

        copy_weight = weight_of(COPY)
        copy_share = [jnp.where(route[m] == COPY, normed_dot, 0.0) for m in range(2)]
        alpha = copy_weight
        columns = []
        value_columns = []
        for c in range(2):
            weight = weight_of(COPY + 1 + c)
            left = column(mixing, MIXING + 2 * c)
            right = column(mixing, MIXING + 2 * c + 1)
            a0 = 1.0 / (1.0 + jnp.exp(right - left))
            a1 = 1.0 / (1.0 + jnp.exp(left - right))
            vd = column(value_dot, VALUE + c)
            alpha = alpha + weight * a0
            for m in range(2):
                copy_share[m] = copy_share[m] + jnp.where(
                    route[m] == COPY + 1 + c, a0 * normed_dot + a1 * vd, 0.0
                )
            slope = a0 * a1 * weight * (normed_dot - vd)
            columns.append((MIXING + 2 * c, slope))
            columns.append((MIXING + 2 * c + 1, -slope))
            value_columns.append((VALUE + c, weight * a1))
        value_matrix = lane_matrix(tok.shape, value_columns)
        base = mid + alpha * normed + nt_dot(low(value_matrix), small)

        @pl.when(mine)
        def _():
            base_ref[slab, :] += base

        gcopies[block].wait()
        extra = wide(gsend_ref[block, :, width:]) + wide(grecv_ref[block, :, width:])
        share = [
            column(extra, 2 * m) + column(extra, 2 * m + 1) + gate[m] * copy_share[m]
            for m in range(2)
        ]
        lane = lax.broadcasted_iota(jnp.int32, tok.shape, 1)
        slopes = lane_matrix(tok.shape, columns)
        for m in range(2):
            local = share[m] - gate[m] * (share[0] + share[1])
            slopes = slopes + jnp.where(wide(lane - ROUTER) == route[m], local, 0.0)
        slopes_low = low(slopes)
        grad_normed = (
            wide(gsend_ref[block, :, :width])
            + wide(grecv_ref[block, :, :width])
            + alpha * cot_wide
            + nt_dot(slopes_low, small)
        )
        small_grad = tn_dot(s2, low(slopes * mine_f)) + tn_dot(cot, low(value_matrix * mine_f))
        gain_grad = jnp.sum(unit * grad_normed, axis=0, keepdims=True) * mine_f
        scaled = grad_normed * gain_two
        grad_mid = cot_wide + scale * (scaled - unit * mean_last(scaled * unit))
        gmid_ref[rows, :] = grad_mid
        attended = low(grad_mid)
        out_grad = tn_dot(attended, mixed_ref[rows, :])
        gm_ref[...] = low(nn_dot(attended, wout_ref[...]))
        if block == first:
            acc_small_ref[...] = small_grad
            acc_gain_ref[...] = jnp.broadcast_to(gain_grad, acc_gain_ref.shape)
            acc_out_ref[...] = out_grad
        else:
            acc_small_ref[...] += small_grad
            acc_gain_ref[...] += jnp.broadcast_to(gain_grad, acc_gain_ref.shape)
            acc_out_ref[...] += out_grad
        cosine, sine = cos_ref[rows, :], sin_ref[rows, :]

        def one_pair(pair, carry):
            start = pl.multiple_of(pair * PAIR, PAIR)
            lanes = pl.ds(start, PAIR)
            key_lanes = pl.ds(pl.multiple_of(heads_width + start, PAIR), PAIR)
            value_lanes = pl.ds(pl.multiple_of(2 * heads_width + start, PAIR), PAIR)
            query = qkv_ref[rows, lanes] * jnp.bfloat16(SCALING)
            key = qkv_ref[:keys, key_lanes]
            value = qkv_ref[:keys, value_lanes]
            grad_out = gm_ref[:, lanes]
            key_t = kt_ref[lanes, :keys]
            grad_value = None
            for half in range(2):
                keep = head_lanes(query.shape, half, 1)
                q_half = jnp.where(keep, query, jnp.bfloat16(0))
                g_half = jnp.where(keep, grad_out, jnp.bfloat16(0))
                probs = jnp.exp(nt_dot(key, q_half) - lse_ref[pl.ds(2 * pair + half, 1), rows])
                grad_probs = nt_dot(value, g_half)
                inner = jnp.sum(probs * grad_probs, axis=0, keepdims=True)
                grad_scores = low(probs * (grad_probs - inner))
                value_part = nn_dot(low(probs), g_half)
                key_part = nn_dot(grad_scores, q_half)
                query_part = nn_dot(key_t, grad_scores)
                if half == 0:
                    grad_value, grad_key, grad_query = value_part, key_part, query_part
                else:
                    grad_value = grad_value + value_part
                    grad_key = grad_key + key_part
                    grad_query = jnp.where(
                        head_lanes(query_part.shape, 1, 0), query_part, grad_query
                    )
            if block == first:
                dv_ref[:keys, lanes] = grad_value
                dk_ref[:keys, lanes] = grad_key
            else:
                dv_ref[:keys, lanes] += grad_value
                dk_ref[:keys, lanes] += grad_key
            gp_ref[:, lanes] = low(turn(grad_query.T * SCALING, cosine, -sine))
            gp_ref[:, key_lanes] = low(turn(dk_ref[rows, lanes], cosine, -sine))
            gp_ref[:, value_lanes] = low(dv_ref[rows, lanes])
            return carry

        lax.fori_loop(0, pairs, one_pair, 0)
        gp = gp_ref[...]
        qkv_grad = tn_dot(s1_ref[rows, :], gp)
        if block == first:
            acc_qkv_ref[...] = qkv_grad
        else:
            acc_qkv_ref[...] += qkv_grad
        stream_grad = nt_dot(gp, wqkv_ref[...])

        @pl.when(mine)
        def _():
            gown_ref[block % 2] = stream_grad

        @pl.when(jnp.logical_not(mine))
        def _():
            hsend_ref[block % 2] = low(stream_grad)
            to_partner(
                hsend_ref.at[block % 2],
                hrecv_ref.at[block % 2],
                hsend_sem.at[block % 2],
                hrecv_sem.at[block % 2],
            ).start()

    big_ref[:, : 3 * heads_width] = low(acc_qkv_ref[...])
    big_ref[:, 3 * heads_width : 4 * heads_width] = low(acc_out_ref[...])
    gain_rows = acc_gain_ref[0:1, :]
    tall = jnp.where(
        lax.broadcasted_iota(jnp.int32, (PAIR, width), 0) == 1,
        jnp.broadcast_to(gain_rows, (PAIR, width)),
        0.0,
    )
    big_ref[:, 4 * heads_width :] = low(acc_small_ref[...] + tall.T)
    for slot in reversed(range(2)):
        slab = slice(slot * BLOCK, (slot + 1) * BLOCK)
        to_partner(
            hsend_ref.at[slot], hrecv_ref.at[slot], hsend_sem.at[slot], hrecv_sem.at[slot]
        ).wait()
        source = wide(own_ref[slab, :])
        scale = lax.rsqrt(mean_last(source * source) + EPSILON)
        unit = source * scale
        scaled = (gown_ref[slot] + wide(hrecv_ref[slot])) * gain_one
        mid_rows = pl.ds(pl.multiple_of(tp * 2 * BLOCK + slot * BLOCK, BLOCK), BLOCK)
        grad_ref[slab, :] = gmid_ref[mid_rows, :] + scale * (
            scaled - unit * mean_last(scaled * unit)
        )
    experts.wait()


def run_forward(hid, tok, wqkv, wout, small, rows, cosine, sine, shard, cot):
    length, width = hid.shape
    heads_width = wout.shape[1]
    blocks = length // BLOCK
    vmem = pl.BlockSpec(memory_space=pltpu.VMEM)
    low_t, wide_t = jnp.bfloat16, jnp.float32
    return pl.pallas_call(
        forward_kernel,
        in_specs=[vmem] * 10,
        out_specs=[vmem] * 10,
        out_shape=[
            jax.ShapeDtypeStruct((length, width), low_t),
            jax.ShapeDtypeStruct((length, 3 * heads_width), low_t),
            jax.ShapeDtypeStruct((8, length), wide_t),
            jax.ShapeDtypeStruct((length, heads_width), low_t),
            jax.ShapeDtypeStruct((length, width), wide_t),
            jax.ShapeDtypeStruct((length, width), low_t),
            jax.ShapeDtypeStruct((length, PAIR), wide_t),
            jax.ShapeDtypeStruct((8, length), wide_t),
            jax.ShapeDtypeStruct(shard.shape, low_t),
            jax.ShapeDtypeStruct((length, width), low_t),
        ],
        scratch_shapes=[
            pltpu.VMEM((heads_width, length), low_t),
            pltpu.VMEM((blocks, BLOCK, width), low_t),
            pltpu.VMEM((blocks, BLOCK, width), low_t),
            pltpu.SemaphoreType.DMA((blocks,)),
            pltpu.SemaphoreType.DMA((blocks,)),
            pltpu.SemaphoreType.DMA((shard.shape[0],)),
            pltpu.SemaphoreType.DMA((shard.shape[0],)),
            pltpu.SemaphoreType.DMA((2,)),
        ],
        cost_estimate=pl.CostEstimate(
            flops=16 * length * width * heads_width, bytes_accessed=1 << 27, transcendentals=0
        ),
        compiler_params=pltpu.CompilerParams(
            collective_id=0, has_side_effects=True, vmem_limit_bytes=60 << 20
        ),
    )(hid, tok, wqkv, wout, small, rows, cosine, sine, shard, cot)


def run_backward(*operands):
    cot, own, wout, egrads = operands[4], operands[16], operands[11], operands[17]
    length, width = cot.shape
    heads_width = wout.shape[1]
    blocks = length // BLOCK
    own_rows = own.shape[0]
    vmem = pl.BlockSpec(memory_space=pltpu.VMEM)
    low_t, wide_t = jnp.bfloat16, jnp.float32
    dma = pltpu.SemaphoreType.DMA
    return pl.pallas_call(
        backward_kernel,
        in_specs=[vmem] * 18,
        out_specs=[vmem] * 5,
        out_shape=[
            jax.ShapeDtypeStruct((own_rows, width), wide_t),
            jax.ShapeDtypeStruct((own_rows, width), wide_t),
            jax.ShapeDtypeStruct((own_rows, width), low_t),
            jax.ShapeDtypeStruct((width, 4 * heads_width + PAIR), low_t),
            jax.ShapeDtypeStruct(egrads.shape, low_t),
        ],
        scratch_shapes=[
            pltpu.VMEM((blocks, BLOCK, width + PAIR), low_t),
            pltpu.VMEM((blocks, BLOCK, width + PAIR), low_t),
            pltpu.VMEM((2, BLOCK, width), low_t),
            pltpu.VMEM((2, BLOCK, width), low_t),
            pltpu.VMEM((length, width), wide_t),
            pltpu.VMEM((2, BLOCK, width), wide_t),
            pltpu.VMEM((heads_width, length), low_t),
            pltpu.VMEM((BLOCK, heads_width), low_t),
            pltpu.VMEM((PAIR, BLOCK), wide_t),
            pltpu.VMEM((length, heads_width), wide_t),
            pltpu.VMEM((length, heads_width), wide_t),
            pltpu.VMEM((BLOCK, 3 * heads_width), low_t),
            pltpu.VMEM((width, 3 * heads_width), wide_t),
            pltpu.VMEM((width, heads_width), wide_t),
            pltpu.VMEM((width, PAIR), wide_t),
            pltpu.VMEM((8, width), wide_t),
            dma((blocks,)),
            dma((blocks,)),
            dma((2,)),
            dma((2,)),
            dma((egrads.shape[0],)),
            dma((egrads.shape[0],)),
        ],
        cost_estimate=pl.CostEstimate(
            flops=32 * length * width * heads_width, bytes_accessed=1 << 27, transcendentals=0
        ),
        compiler_params=pltpu.CompilerParams(
            collective_id=1, has_side_effects=True, vmem_limit_bytes=60 << 20
        ),
    )(*operands)


def shards(
    hidden,
    prev_logits,
    routes,
    slot_rank,
    dropped,
    cotangent,
    attn_norm,
    ffn_norm,
    w_qkv,
    w_attn_out,
    w_router,
    w_const_gate,
    w_const_value,
    w_expert_in,
    w_expert_out,
):
    own_rows, width = hidden.shape
    length = own_rows * lax.axis_size("tp")
    experts = w_expert_in.shape[0]
    route_count = w_router.shape[1]
    capacity = 9 * length // (4 * route_count)
    heads_width = w_attn_out.shape[1]
    planned = lax.axis_size("fsdp") == 16
    small = jnp.concatenate(
        [
            wide(values)
            for values in (
                attn_norm[:, None],
                ffn_norm[:, None],
                w_router,
                w_const_gate,
                w_const_value,
            )
        ],
        axis=1,
    )
    small = jnp.pad(small, ((0, 0), (0, PAIR - small.shape[1])))
    wqkv_own = w_qkv.reshape(-1, 3 * heads_width)
    kept = (routes < experts) & (dropped == 0)
    target = jnp.where(kept, routes * capacity + slot_rank, -1)
    blank = jnp.zeros((own_rows, 2), jnp.float32)
    tok = jnp.concatenate(
        [blank, prev_logits, blank, blank, blank, wide(routes), blank, wide(target)], axis=1
    )
    tok = jnp.pad(tok, ((0, 0), (0, 32 - tok.shape[1]))).T
    blocks, small, rows, tok, hid = (run_gather if planned else gather_plain)(
        jnp.concatenate([wqkv_own, w_attn_out], axis=1), small, tok, hidden
    )
    blocks = blocks.reshape(width, -1)
    wqkv = blocks[:, : 3 * heads_width]
    wout = blocks[:, 3 * heads_width :]
    cosine, sine = (jnp.asarray(table) for table in rotary_tables(length))
    shard_rows, hidden_units = w_expert_out.shape[1:]
    shard = jnp.concatenate(
        [w_expert_in.reshape(experts, shard_rows, 2 * hidden_units), w_expert_out], axis=2
    )
    s1, qkv, lse, mixed, mid, s2, tok, lines, gathered, cot = run_forward(
        hid, tok, wqkv, wout, small, rows, cosine, sine, shard, cotangent
    )
    expert_weights = join_weights(gathered, experts)
    peers = 2 * experts
    half = capacity // 2
    block = half // 2
    place = jnp.arange(peers * block)
    owner = (lax.axis_index("fsdp") % peers) ^ (place // block)
    slot = wide(
        (owner // 2) * capacity
        + lax.axis_index("tp") * half
        + (owner % 2) * block
        + place % block
    )
    results, grad_rows, grads_exp = run_expert(
        s2, cot, lines, jnp.broadcast_to(slot[:, None], (slot.shape[0], PAIR)), expert_weights
    )
    grad_hidden, base, for_other, big, arrived = run_backward(
        results.reshape(-1, width),
        grad_rows.reshape(-1, width),
        jnp.broadcast_to(slot[None, :], (8, slot.shape[0])),
        tok,
        cot,
        mid,
        s1,
        qkv,
        lse,
        mixed,
        wqkv,
        wout,
        small,
        rows,
        cosine,
        sine,
        hidden,
        split_grads(grads_exp),
    )
    finish = run_finish if planned else finish_plain
    output, grad_qkv, grad_attn_out, last, grad_in_exp, grad_out_exp = finish(
        big, wqkv_own, for_other, base, arrived
    )
    return (
        output,
        grad_hidden,
        last[:, 0] / wide(attn_norm),
        last[:, 1],
        grad_qkv,
        grad_attn_out,
        last[:, ROUTER:MIXING],
        last[:, MIXING:VALUE],
        last[:, VALUE : VALUE + 2],
        grad_in_exp,
        grad_out_exp,
    )


def solution(mesh):
    in_specs = (
        P(("fsdp", "tp"), None),
        P(("fsdp", "tp"), None),
        P(("fsdp", "tp"), None),
        P(("fsdp", "tp"), None),
        P(("fsdp", "tp"), None),
        P(("fsdp", "tp"), None),
        P(("fsdp", "tp")),
        P(("fsdp", "tp")),
        P("fsdp", None, "tp"),
        P("fsdp", "tp"),
        P(("fsdp", "tp"), None),
        P(("fsdp", "tp"), None),
        P(("fsdp", "tp"), None),
        P(None, "fsdp", None, "tp"),
        P(None, "fsdp", "tp"),
    )
    out_specs = (
        P(("fsdp", "tp"), None),
        P(("fsdp", "tp"), None),
        P(("fsdp", "tp")),
        P(("fsdp", "tp")),
        P("fsdp", None, "tp"),
        P("fsdp", "tp"),
        P(("fsdp", "tp"), None),
        P(("fsdp", "tp"), None),
        P(("fsdp", "tp"), None),
        P(None, "fsdp", None, "tp"),
        P(None, "fsdp", "tp"),
    )
    return jax.shard_map(shards, mesh=mesh, in_specs=in_specs, out_specs=out_specs, check_vma=False)
```

```python
import jax
import jax.numpy as jnp
import numpy as np
from jax import lax
from jax.experimental import pallas as pl
from jax.experimental.pallas import tpu as pltpu
from jax.sharding import PartitionSpec as P

HD = 64
BLOCK = 256


EPSILON = 1e-06
MESH = pl.DeviceIdType.MESH
PAIR = 2 * HD
SCALING = HD ** (-0.5)
ROUTER = 2
MIXING = 14
VALUE = 18
ROUTE = 20
TARGET = 24
GATE = 26
COPY = 9


TILE = 256


def swap(values):
    return lax.ppermute(values, "tp", [(0, 1), (1, 0)])


def gather_rows(values):
    other = swap(values)
    first = lax.axis_index("tp") == 0
    return jnp.concatenate(
        [jnp.where(first, values, other), jnp.where(first, other, values)], axis=0
    )


def own_half(values):
    half = values.shape[0] // 2
    return lax.dynamic_slice_in_dim(values, lax.axis_index("tp") * half, half, 0)


def other_half(values):
    half = values.shape[0] // 2
    return lax.dynamic_slice_in_dim(values, (1 - lax.axis_index("tp")) * half, half, 0)


def member_groups(size, experts):
    span = 2 * experts
    starts = range(0, size, span)
    cores = [[start + 2 * e, start + 2 * e + 1] for start in starts for e in range(experts)]
    across = [[start + r for start in starts] for r in range(span)]
    return cores, across


def own_core(values, rows):
    parts = values.reshape(-1, 2, rows, values.shape[-1])
    return lax.dynamic_index_in_dim(parts, lax.axis_index("fsdp") % 2, 1, keepdims=False)


def join_weights(got, experts):
    size = lax.axis_size("fsdp")
    if size == 2 * experts:
        return got
    cores, across = member_groups(size, experts)
    got = lax.all_gather(got, "fsdp", axis=1, axis_index_groups=cores, tiled=True)
    got = got.reshape(-1, got.shape[-1])
    got = lax.all_gather(got, "fsdp", axis=0, axis_index_groups=across, tiled=True)
    return own_core(got, got.shape[0] // (2 * experts))


def split_grads(grads):
    experts, _, columns = grads.shape
    size = lax.axis_size("fsdp")
    if size == 2 * experts:
        return grads
    cores, across = member_groups(size, experts)
    grads = lax.all_gather(grads[:, None], "fsdp", axis=1, axis_index_groups=cores, tiled=True)
    grads = grads.reshape(-1, columns)
    grads = lax.psum_scatter(
        grads, "fsdp", scatter_dimension=0, axis_index_groups=across, tiled=True
    )
    return own_core(grads, grads.shape[0] // (2 * experts))


def finish_plain(big, wqkv, other):
    heads_width = (big.shape[1] - PAIR) // 4
    reduced = wide(lax.psum_scatter(big, "fsdp", scatter_dimension=0, tiled=True))
    parts = reduced[:, : 3 * heads_width].reshape(-1, 3, heads_width).transpose(1, 0, 2)
    share = jnp.sum(parts * wide(wqkv), axis=(0, 2))
    last = jnp.concatenate([share[:, None], reduced[:, 4 * heads_width + 1 :]], axis=1)
    return (
        swap(other),
        reduced[:, : 4 * heads_width],
        own_half(last) + swap(other_half(last)),
    )


def forward_plain(operands, cosine, sine):
    (
        hidden,
        cotangent,
        logits,
        routes,
        rank,
        dropped,
        gains,
        router,
        mixing,
        value,
        wqkv,
        wout,
        w_in,
        w_down,
    ) = operands
    own_rows, width = hidden.shape
    experts, shard, units = w_down.shape
    small = jnp.concatenate([wide(v) for v in (gains, router, mixing, value)], axis=0)
    small = jnp.pad(small, ((0, PAIR - small.shape[0]), (0, 0))).T
    small = lax.all_gather(small, ("fsdp", "tp"), axis=0, tiled=True)
    capacity = own_rows * 2 * 9 // 48
    kept = (routes < experts) & (dropped == 0)
    target = jnp.where(kept, routes * capacity + rank, -1)
    blank = jnp.zeros((2, own_rows), jnp.float32)
    tok = jnp.concatenate(
        [blank, logits, blank, blank, blank, wide(routes), blank, wide(target)], axis=0
    )
    tok = lax.all_gather(tok, "tp", axis=1, tiled=True).T
    tok = jnp.pad(tok, ((0, 0), (0, PAIR - tok.shape[1])))
    blocks = jnp.concatenate([wqkv[0], wqkv[1], wqkv[2], wout], axis=1)
    blocks = lax.all_gather(blocks, "fsdp", axis=0, tiled=True).reshape(2 * experts, -1, blocks.shape[1])
    rows = small.T[:8]
    small = low(small)
    shards_flat = jnp.concatenate([w_in.reshape(experts, shard, 2 * units), w_down], axis=2)
    return (blocks, small, rows) + tuple(
        run_forward_plain(
            gather_rows(hidden), tok, blocks, small, rows, cosine, sine, shards_flat, cotangent
        )
    )


def nt_dot(left, right):
    return lax.dot_general(left, right, (((1,), (1,)), ((), ())), preferred_element_type=jnp.float32)


def nn_dot(left, right):
    return jnp.dot(left, right, preferred_element_type=jnp.float32)


def tn_dot(left, right):
    return lax.dot_general(left, right, (((0,), (0,)), ((), ())), preferred_element_type=jnp.float32)


def low(values):
    return values.astype(jnp.bfloat16)


def wide(values):
    return values.astype(jnp.float32)


def rotary_tables(length):
    half = HD // 2
    positions = np.arange(length, dtype=np.float32)
    inverse = np.power(np.float32(10000.0), -np.arange(half, dtype=np.float32) / np.float32(half))
    angles = (positions[:, None] * inverse[None, :].astype(np.float32)).astype(np.float32)
    cosine = np.cos(angles.astype(np.float64)).astype(np.float32)
    sine = np.sin(angles.astype(np.float64)).astype(np.float32)
    return (
        np.concatenate([cosine] * 4, axis=1),
        np.concatenate([-sine, sine, -sine, sine], axis=1),
    )


def turn(values, cosine, sine):
    lane = lax.broadcasted_iota(jnp.int32, values.shape, 1)
    upper = lax.rem(lane, HD) >= HD // 2
    partner = jnp.where(
        upper, pltpu.roll(values, HD // 2, 1), pltpu.roll(values, PAIR - HD // 2, 1)
    )
    return values * cosine + partner * sine


def head_lanes(shape, half, axis):
    return (lax.broadcasted_iota(jnp.int32, shape, axis) >= HD) == bool(half)


def mean_last(values):
    return jnp.mean(values, axis=-1, keepdims=True)


def to_partner(source, target, send_sem, recv_sem):
    return pltpu.make_async_remote_copy(
        src_ref=source,
        dst_ref=target,
        send_sem=send_sem,
        recv_sem=recv_sem,
        device_id={"tp": 1 - lax.axis_index("tp")},
        device_id_type=MESH,
    )


def block_rows(block):
    return slice(block * BLOCK, (block + 1) * BLOCK)


def column(values, index):
    return values[:, index : index + 1]


def lane_matrix(shape, columns):
    lane = lax.broadcasted_iota(jnp.int32, shape, 1)
    total = jnp.zeros(shape, jnp.float32)
    for index, values in columns:
        total = jnp.where(lane == index, values, total)
    return total


def send_to(source, target, send_sem, recv_sem, device):
    return pltpu.make_async_remote_copy(
        src_ref=source,
        dst_ref=target,
        send_sem=send_sem,
        recv_sem=recv_sem,
        device_id=device,
        device_id_type=MESH,
    )


def greet_group(peers):
    me = lax.axis_index("fsdp")
    rank = lax.rem(me, peers)
    barrier = pltpu.get_barrier_semaphore()
    for k in range(1, peers):
        pl.semaphore_signal(
            barrier,
            inc=1,
            device_id={"fsdp": me - rank + lax.rem(rank + k, peers)},
            device_id_type=MESH,
        )
    pl.semaphore_signal(
        barrier, inc=1, device_id={"tp": 1 - lax.axis_index("tp")}, device_id_type=MESH
    )
    pl.semaphore_wait(barrier, peers)


def each(first, last, body):
    def step(k, carry):
        body(k)
        return carry

    lax.fori_loop(first, last, step, 0)


def flipped(value, k, bits):
    other = 0
    bit = 1
    while bit < bits:
        ours, theirs = lax.rem(value // bit, 2), lax.rem(k // bit, 2)
        other = other + bit * (ours + theirs - 2 * ours * theirs)
        bit *= 2
    return other


class CoreExchange:
    def __init__(self, source, target, send_sem, recv_sem):
        experts = source.shape[0]
        me = lax.axis_index("fsdp")
        rank = lax.rem(me, 2 * experts)
        core = lax.rem(rank, 2)
        mine = rank // 2

        def device(k):
            return {"fsdp": me - rank + 2 * flipped(mine, k, experts) + core}

        def copy(k):
            there = flipped(mine, k, experts)
            return send_to(
                source.at[there], target.at[mine], send_sem.at[k], recv_sem.at[k], device(k)
            )

        def arrival(k):
            there = flipped(mine, k, experts)
            return send_to(
                source.at[there], target.at[there], send_sem.at[k], recv_sem.at[k], device(k)
            )

        self.experts, self.copy, self.arrival = experts, copy, arrival
        self.local = pltpu.make_async_copy(source.at[mine], target.at[mine], send_sem.at[0])

    def start(self):
        self.local.start()
        each(1, self.experts, lambda k: self.copy(k).start())

    def wait(self):
        each(1, self.experts, lambda k: self.copy(k).wait_send())
        each(1, self.experts, lambda k: self.arrival(k).wait_recv())
        self.local.wait()


def finish_kernel(
    big_ref,
    wqkv_ref,
    other_ref,
    y_ref,
    red_ref,
    tail_ref,
    sum_ref,
    core_ref,
    side_ref,
    acc_ref,
    usend_ref,
    urecv_ref,
    dsend_ref,
    drecv_ref,
    tsend_ref,
    trecv_ref,
    core_send,
    core_recv,
    x_send,
    x_recv,
    up_send,
    up_recv,
    dn_send,
    dn_recv,
    y_send,
    y_recv,
):
    size = big_ref.shape[0]
    planes = size // 4
    me = lax.axis_index("fsdp")
    tp = lax.axis_index("tp")
    z, x, core = me // 4, lax.rem(me // 2, 2), lax.rem(me, 2)
    heads_width = wqkv_ref.shape[2]
    greet_group(size)
    partner = {"tp": 1 - tp}

    def to_core(plane, line):
        slot = plane * 2 + line
        return send_to(
            big_ref.at[plane * 4 + line * 2 + 1 - core],
            core_ref.at[slot],
            core_send.at[slot],
            core_recv.at[slot],
            {"fsdp": me + 1 - 2 * core},
        )

    def to_side(plane):
        return send_to(
            sum_ref.at[plane],
            side_ref.at[plane],
            x_send.at[plane],
            x_recv.at[plane],
            {"fsdp": z * 4 + (1 - x) * 2 + core},
        )

    def to_up(plane):
        return send_to(
            usend_ref.at[plane],
            urecv_ref.at[plane],
            up_send.at[plane],
            up_recv.at[plane],
            {"fsdp": lax.min(z + 1, planes - 1) * 4 + x * 2 + core},
        )

    def to_down(plane):
        return send_to(
            dsend_ref.at[plane],
            drecv_ref.at[plane],
            dn_send.at[plane],
            dn_recv.at[plane],
            {"fsdp": lax.max(z - 1, 0) * 4 + x * 2 + core},
        )

    order = [planes - 1, 0, 2, 1]
    for plane in order:
        to_core(plane, 1 - x).start()
    for plane in order:
        to_core(plane, x).start()
    out_y = send_to(other_ref, y_ref, y_send.at[0], y_recv.at[0], partner)
    out_y.start()

    def joined(plane, line):
        to_core(plane, line).wait_recv()
        return wide(big_ref[plane * 4 + line * 2 + core]) + wide(core_ref[plane * 2 + line])

    for plane in order:
        sum_ref[plane] = low(joined(plane, 1 - x))
        to_side(plane).start()
    for plane in order:
        acc_ref[plane] = joined(plane, x)
    def ready(plane):
        to_side(plane).wait_recv()
        acc_ref[plane] += wide(side_ref[plane])

    def rise(plane):
        @pl.when(jnp.logical_and(z > 0, z <= plane))
        def _():
            to_up(plane).wait_recv()
            acc_ref[plane] += wide(urecv_ref[plane])

        @pl.when(z < plane)
        def _():
            usend_ref[plane] = low(acc_ref[plane])
            to_up(plane).start()

    def fall(plane):
        @pl.when(jnp.logical_and(z < planes - 1, z >= plane))
        def _():
            to_down(plane).wait_recv()
            acc_ref[plane] += wide(drecv_ref[plane])

        @pl.when(z > plane)
        def _():
            dsend_ref[plane] = low(acc_ref[plane])
            to_down(plane).start()

    ready(3)
    rise(3)
    ready(0)
    fall(0)
    ready(2)
    rise(2)
    ready(1)
    fall(1)
    rise(1)
    fall(2)
    rise(0)
    fall(3)
    values = acc_ref[z]
    red_ref[...] = values[:, : 4 * heads_width]
    share = sum(
        jnp.sum(
            values[:, part * heads_width : (part + 1) * heads_width] * wide(wqkv_ref[part]),
            axis=1,
            keepdims=True,
        )
        for part in range(3)
    )
    last = values[:, 4 * heads_width :]
    last = jnp.where(lax.broadcasted_iota(jnp.int32, last.shape, 1) == 0, share, last)
    part_rows = tail_ref.shape[0]
    tsend_ref[0] = last[:part_rows, :]
    tsend_ref[1] = last[part_rows:, :]
    tail_y = send_to(tsend_ref.at[1 - tp], trecv_ref, y_send.at[1], y_recv.at[1], partner)
    tail_y.start()
    out_y.wait()
    tail_y.wait()
    tail_ref[...] = tsend_ref[tp] + trecv_ref[...]
    for plane in range(planes):
        to_core(plane, 1 - x).wait_send()
        to_core(plane, x).wait_send()
        to_side(plane).wait_send()

        @pl.when(z < plane)
        def _():
            to_up(plane).wait_send()

        @pl.when(z > plane)
        def _():
            to_down(plane).wait_send()


def run_finish(big, wqkv, other):
    size = lax.axis_size("fsdp")
    planes = size // 4
    own_rows, width = other.shape
    columns = big.shape[1]
    shard = width // size
    vmem = pl.BlockSpec(memory_space=pltpu.VMEM)
    low_t, wide_t = jnp.bfloat16, jnp.float32
    dma = pltpu.SemaphoreType.DMA
    line = (planes, shard, columns)
    return pl.pallas_call(
        finish_kernel,
        in_specs=[vmem] * 3,
        out_specs=[vmem] * 3,
        out_shape=[
            jax.ShapeDtypeStruct((own_rows, width), low_t),
            jax.ShapeDtypeStruct((shard, columns - PAIR), wide_t),
            jax.ShapeDtypeStruct((shard // 2, PAIR), wide_t),
        ],
        scratch_shapes=[
            pltpu.VMEM(line, low_t),
            pltpu.VMEM((2 * planes, shard, columns), low_t),
            pltpu.VMEM(line, low_t),
            pltpu.VMEM(line, wide_t),
            pltpu.VMEM(line, low_t),
            pltpu.VMEM(line, low_t),
            pltpu.VMEM(line, low_t),
            pltpu.VMEM(line, low_t),
            pltpu.VMEM((2, shard // 2, PAIR), wide_t),
            pltpu.VMEM((shard // 2, PAIR), wide_t),
            dma((2 * planes,)),
            dma((2 * planes,)),
        ]
        + [dma((planes,))] * 6
        + [dma((2,))] * 2,
        compiler_params=pltpu.CompilerParams(
            collective_id=4, has_side_effects=True, vmem_limit_bytes=60 << 20
        ),
    )(big.reshape(size, shard, columns), wqkv, other)


def write_kernel(
    base_ref,
    y_ref,
    grad_ref,
    red_ref,
    tail_ref,
    gain_ref,
    expert_ref,
    out_ref,
    hidden_ref,
    qkv_ref,
    attn_ref,
    gains_ref,
    router_ref,
    mixing_ref,
    value_ref,
    in_ref,
    down_ref,
):
    hidden = down_ref.shape[2]
    heads_width = attn_ref.shape[1]
    out_ref[...] = low(base_ref[...] + wide(y_ref[...]))
    hidden_ref[...] = grad_ref[...]
    values = wide(expert_ref[0])
    in_ref[0, :, 0, :] = values[:, :hidden]
    in_ref[0, :, 1, :] = values[:, hidden : 2 * hidden]
    down_ref[0] = values[:, 2 * hidden :]

    @pl.when(pl.program_id(0) == 0)
    def _():
        for part in range(3):
            qkv_ref[part] = red_ref[:, part * heads_width : (part + 1) * heads_width]
        attn_ref[...] = red_ref[:, 3 * heads_width :]
        count = tail_ref.shape[0]
        blank = jnp.zeros((PAIR - count, PAIR), jnp.float32)
        turned = jnp.concatenate([tail_ref[...], blank], axis=0).T[:, :count]
        gains_ref[0:1, :] = turned[0:1, :] / gain_ref[0:1, :]
        gains_ref[1:2, :] = turned[1:2, :]
        router_ref[...] = turned[ROUTER:MIXING, :]
        mixing_ref[...] = turned[MIXING:VALUE, :]
        value_ref[...] = turned[VALUE : VALUE + 2, :]


def run_write(base, y, grad_hidden, red, tail, gains, arrived):
    own_rows, width = base.shape
    shard = red.shape[0]
    heads_width = red.shape[1] // 4
    count = tail.shape[0]
    experts, _, total = arrived.shape
    hidden = total // 3
    wide_t = jnp.float32
    rows = pl.BlockSpec((own_rows // experts, width), lambda e: (e, 0))

    def whole(shape):
        return pl.BlockSpec(shape, lambda e: (0,) * len(shape))

    return pl.pallas_call(
        write_kernel,
        grid=(experts,),
        in_specs=[
            rows,
            rows,
            rows,
            whole(red.shape),
            whole(tail.shape),
            whole(gains.shape),
            pl.BlockSpec((1, shard, total), lambda e: (e, 0, 0)),
        ],
        out_specs=[
            rows,
            rows,
            whole((3, shard, heads_width)),
            whole((shard, heads_width)),
            whole((2, count)),
            whole((MIXING - ROUTER, count)),
            whole((VALUE - MIXING, count)),
            whole((2, count)),
            pl.BlockSpec((1, shard, 2, hidden), lambda e: (e, 0, 0, 0)),
            pl.BlockSpec((1, shard, hidden), lambda e: (e, 0, 0)),
        ],
        out_shape=[
            jax.ShapeDtypeStruct((own_rows, width), jnp.bfloat16),
            jax.ShapeDtypeStruct((own_rows, width), wide_t),
            jax.ShapeDtypeStruct((3, shard, heads_width), wide_t),
            jax.ShapeDtypeStruct((shard, heads_width), wide_t),
            jax.ShapeDtypeStruct((2, count), wide_t),
            jax.ShapeDtypeStruct((MIXING - ROUTER, count), wide_t),
            jax.ShapeDtypeStruct((VALUE - MIXING, count), wide_t),
            jax.ShapeDtypeStruct((2, count), wide_t),
            jax.ShapeDtypeStruct((experts, shard, 2, hidden), wide_t),
            jax.ShapeDtypeStruct((experts, shard, hidden), wide_t),
        ],
    )(base, y, grad_hidden, red, tail, gains, arrived)


def expert_kernel(
    s2_ref,
    cot_ref,
    line_ref,
    slot_ref,
    weight_ref,
    res_out_ref,
    dx_out_ref,
    grads_out_ref,
    xs_ref,
    gs_ref,
    x_ref,
    g_ref,
    w_ref,
    gate_ref,
    up_ref,
    act_ref,
    xt_ref,
    gt_ref,
    acc_ref,
    grads_ref,
    sibling_ref,
    ysend_ref,
    yrecv_ref,
    w_sem,
    grad_sem,
    xs_sem,
    xr_sem,
    gs_sem,
    gr_sem,
    xfs_sem,
    xfr_sem,
    gfs_sem,
    gfr_sem,
    ys_sem,
    yr_sem,
    rs_sem,
    rr_sem,
    ds_sem,
    dr_sem,
):
    peers, rows, width = xs_ref.shape
    total = peers * rows
    hidden = gate_ref.shape[1]
    tiles = hidden // TILE
    me = lax.axis_index("fsdp")
    tp = lax.axis_index("tp")
    rank = lax.rem(me, peers)
    core = lax.rem(rank, 2)
    start = me - rank

    def peer(k):
        return {"fsdp": start + flipped(rank, k, peers)}

    partner = {"tp": 1 - tp}
    sibling = {"fsdp": start + rank + 1 - 2 * core}

    def out_x(k):
        return send_to(xs_ref.at[k], x_ref.at[0, k], xs_sem.at[k], xr_sem.at[k], peer(k))

    def out_g(k):
        return send_to(gs_ref.at[k], g_ref.at[0, k], gs_sem.at[k], gr_sem.at[k], peer(k))

    def pass_x(k):
        return send_to(x_ref.at[0, k], x_ref.at[1, k], xfs_sem.at[k], xfr_sem.at[k], partner)

    def pass_g(k):
        return send_to(g_ref.at[0, k], g_ref.at[1, k], gfs_sem.at[k], gfr_sem.at[k], partner)

    def across(index, k):
        return send_to(
            ysend_ref.at[index, k],
            yrecv_ref.at[index, k],
            ys_sem.at[index, k],
            yr_sem.at[index, k],
            partner,
        )

    def back(index, k):
        if index == 0:
            return send_to(xs_ref.at[k], res_out_ref.at[k], rs_sem.at[k], rr_sem.at[k], peer(k))
        return send_to(gs_ref.at[k], dx_out_ref.at[k], ds_sem.at[k], dr_sem.at[k], peer(k))

    def return_order(body):
        def step(j, carry):
            body(8 + 2 * j)
            body(4 + j)
            body(9 + 2 * j)
            return carry

        lax.fori_loop(0, 4, step, 0)
        for k in (2, 3, 1, 0):
            body(k)

    def join(index, k):
        across(index, k).wait_recv()
        own = xs_ref if index == 0 else gs_ref
        own[k] = low(wide(own[k]) + wide(yrecv_ref[index, k]))
        back(index, k).start()

    def join_some(index, tile):
        join(index, 8 + 2 * tile)
        join(index, 4 + tile)
        join(index, 9 + 2 * tile)

    def join_last(index):
        for k in (2, 3, 1):
            join(index, k)
        across(index, 0).wait_recv()
        own, target = (xs_ref, res_out_ref) if index == 0 else (gs_ref, dx_out_ref)
        target[0] = low(wide(own[0]) + wide(yrecv_ref[index, 0]))

    greet_group(peers)
    here = pltpu.make_async_copy(weight_ref, w_ref.at[:, core], w_sem.at[0])
    here.start()
    there = send_to(weight_ref, w_ref.at[:, core], w_sem.at[1], w_sem.at[2], sibling)
    half = total // 2
    halves = []
    for part in range(2):
        blocks = slice(part * peers // 2, (part + 1) * peers // 2)
        ids = slot_ref[part * half : (part + 1) * half, 0:1]
        hits = [line_ref[m : m + 1, :] == ids for m in range(2)]
        onehot = low(jnp.where(hits[0] | hits[1], 1.0, 0.0))
        xs_ref[blocks] = low(nn_dot(onehot, s2_ref[...])).reshape(peers // 2, rows, width)
        if part == 0:
            x_ref[0, 0] = xs_ref[0]
            pass_x(0).start()
        each(max(1, part * peers // 2), (part + 1) * peers // 2, lambda k: out_x(k).start())
        halves.append((blocks, onehot, hits))
    there.start()
    for part in range(2):
        blocks, onehot, hits = halves[part]
        gate = sum(
            jnp.sum(jnp.where(hits[m], line_ref[2 + m : 3 + m, :], 0.0), axis=1, keepdims=True)
            for m in range(2)
        )
        gs_ref[blocks] = low(nn_dot(onehot, cot_ref[...]) * gate).reshape(peers // 2, rows, width)
        if part == 0:
            g_ref[0, 0] = gs_ref[0]
        each(max(1, part * peers // 2), (part + 1) * peers // 2, lambda k: out_g(k).start())

    def forward_x(k):
        out_x(k).wait_recv()
        pass_x(k).start()

    each(1, peers, forward_x)
    pass_g(0).start()
    here.wait()
    send_to(weight_ref, w_ref.at[:, 1 - core], w_sem.at[1], w_sem.at[2], sibling).wait_recv()
    there.wait_send()
    each(0, peers, lambda k: pass_x(k).wait_recv())

    def weights(which, lanes):
        return w_ref[:, :, :, pl.ds(pl.multiple_of(which * hidden + lanes, TILE), TILE)].reshape(
            width, TILE
        )

    acc_ref[...] = jnp.zeros_like(acc_ref)

    def forward_tile(tile, carry):
        lanes = pl.multiple_of(tile * TILE, TILE)
        here_lanes = pl.ds(lanes, TILE)
        x = x_ref[...].reshape(2 * total, width)
        gate = nn_dot(x, weights(0, lanes))
        up = nn_dot(x, weights(1, lanes))
        gate_ref[:, here_lanes] = low(gate)
        up_ref[:, here_lanes] = low(up)
        act = low(gate / (1.0 + jnp.exp(-gate)) * up)
        act_ref[:, here_lanes] = act
        acc_ref[...] += nt_dot(act, weights(2, lanes))

        def forward_g(k):
            @pl.when(k > 0)
            def _():
                out_g(k).wait_recv()
                pass_g(k).start()

        each(tile * (peers // tiles), (tile + 1) * (peers // tiles), forward_g)
        return carry

    lax.fori_loop(0, tiles, forward_tile, 0)
    each(1, peers, lambda k: out_x(k).wait_send())
    xs_ref[...] = low(acc_ref[:total, :]).reshape(peers, rows, width)
    ysend_ref[0] = low(acc_ref[total:, :]).reshape(peers, rows, width)
    return_order(lambda k: across(0, k).start())
    xt_ref[...] = x_ref[...].reshape(2 * total, width).T
    acc_ref[...] = jnp.zeros_like(acc_ref)
    each(0, peers, lambda k: pass_g(k).wait_recv())

    def slope_tile(tile, carry):
        lanes = pl.multiple_of(tile * TILE, TILE)
        here_lanes = pl.ds(lanes, TILE)
        gate = wide(gate_ref[:, here_lanes])
        up = wide(up_ref[:, here_lanes])
        sig = 1.0 / (1.0 + jnp.exp(-gate))
        d_act = nn_dot(g_ref[...].reshape(2 * total, width), weights(2, lanes))
        d_up = low(d_act * gate * sig)
        d_gate = low(d_act * up * sig * (1.0 + gate * (1.0 - sig)))
        gate_ref[:, here_lanes] = d_gate
        up_ref[:, here_lanes] = d_up
        acc_ref[...] += nt_dot(d_gate, weights(0, lanes)) + nt_dot(d_up, weights(1, lanes))
        join_some(0, tile)
        return carry

    lax.fori_loop(0, tiles, slope_tile, 0)
    join_last(0)
    each(1, peers, lambda k: out_g(k).wait_send())
    gs_ref[...] = low(acc_ref[:total, :]).reshape(peers, rows, width)
    ysend_ref[1] = low(acc_ref[total:, :]).reshape(peers, rows, width)
    return_order(lambda k: across(1, k).start())
    gt_ref[...] = g_ref[...].reshape(2 * total, width).T

    def weight_tile(tile, carry):
        lanes = pl.multiple_of(tile * TILE, TILE)
        here_lanes = pl.ds(lanes, TILE)

        def keep(which, values):
            grads_ref[
                :, :, :, pl.ds(pl.multiple_of(which * hidden + lanes, TILE), TILE)
            ] = low(values).reshape(peers // 2, 2, rows, TILE)

        keep(0, nn_dot(xt_ref[...], gate_ref[:, here_lanes]))
        keep(1, nn_dot(xt_ref[...], up_ref[:, here_lanes]))
        keep(2, nn_dot(gt_ref[...], act_ref[:, here_lanes]))
        join_some(1, tile)
        return carry

    lax.fori_loop(0, tiles, weight_tile, 0)
    join_last(1)
    swap_grads = send_to(
        grads_ref.at[:, 1 - core], sibling_ref, grad_sem.at[0], grad_sem.at[1], sibling
    )
    swap_grads.start()
    each(0, peers, lambda k: pass_x(k).wait_send())
    each(0, peers, lambda k: pass_g(k).wait_send())
    for index in range(2):
        each(0, peers, lambda k: across(index, k).wait_send())
        each(1, peers, lambda k: back(index, k).wait_send())
    swap_grads.wait()
    grads_out_ref[...] = low(wide(grads_ref[:, core]) + wide(sibling_ref[...]))
    for index in range(2):
        each(1, peers, lambda k: back(index, k).wait_recv())


def run_expert(s2, cot, lines, slots, weights):
    length, width = s2.shape
    experts, shard, total = weights.shape
    peers = 2 * experts
    rows = slots.shape[0] // peers
    hidden = total // 3
    both = 2 * peers * rows
    vmem = pl.BlockSpec(memory_space=pltpu.VMEM)
    low_t, wide_t = jnp.bfloat16, jnp.float32
    dma = pltpu.SemaphoreType.DMA
    block = (peers, rows, width)
    return pl.pallas_call(
        expert_kernel,
        in_specs=[vmem] * 4 + [pl.BlockSpec(memory_space=pl.ANY)],
        out_specs=[vmem] * 3,
        out_shape=[
            jax.ShapeDtypeStruct(block, low_t),
            jax.ShapeDtypeStruct(block, low_t),
            jax.ShapeDtypeStruct(weights.shape, low_t),
        ],
        scratch_shapes=[
            pltpu.VMEM(block, low_t),
            pltpu.VMEM(block, low_t),
            pltpu.VMEM((2,) + block, low_t),
            pltpu.VMEM((2,) + block, low_t),
            pltpu.VMEM((experts, 2, shard, total), low_t),
            pltpu.VMEM((both, hidden), low_t),
            pltpu.VMEM((both, hidden), low_t),
            pltpu.VMEM((both, hidden), low_t),
            pltpu.VMEM((width, both), low_t),
            pltpu.VMEM((width, both), low_t),
            pltpu.VMEM((both, width), wide_t),
            pltpu.VMEM((experts, 2, shard, total), low_t),
            pltpu.VMEM((experts, shard, total), low_t),
            pltpu.VMEM((2,) + block, low_t),
            pltpu.VMEM((2,) + block, low_t),
            dma((3,)),
            dma((2,)),
        ]
        + [dma((peers,))] * 8
        + [dma((2, peers))] * 2
        + [dma((peers,))] * 4,
        compiler_params=pltpu.CompilerParams(
            collective_id=2, has_side_effects=True, vmem_limit_bytes=67043328
        ),
    )(s2, cot, lines, slots, weights)


def attend(
    hid_ref,
    token_block,
    weight,
    small_ref,
    gains,
    cos_ref,
    sin_ref,
    s1_ref,
    qkv_ref,
    lse_ref,
    mixed_ref,
    mid_ref,
    s2_ref,
    tok_ref,
    line_ref,
    vt_ref,
    send_ref,
    recv_ref,
    send_sem,
    recv_sem,
):
    blocks = hid_ref.shape[0] // BLOCK
    heads_width = mixed_ref.shape[1]
    pairs = heads_width // PAIR
    gain_one, gain_two = gains
    copies = []
    lse_ref[...] = jnp.zeros_like(lse_ref)
    for block in range(blocks):
        rows = block_rows(block)
        keys = (block + 1) * BLOCK
        source = wide(hid_ref[rows, :])
        s1 = low(source * lax.rsqrt(mean_last(source * source) + EPSILON) * gain_one)
        s1_ref[rows, :] = s1
        cosine, sine = cos_ref[rows, :], sin_ref[rows, :]
        for part in range(3):
            projected = nn_dot(s1, weight(part))
            for pair in range(pairs):
                chunk = projected[:, pair * PAIR : (pair + 1) * PAIR]
                if part < 2:
                    chunk = turn(chunk, cosine, sine)
                else:
                    vt_ref[pair * PAIR : (pair + 1) * PAIR, rows] = low(chunk.T)
                start = part * heads_width + pair * PAIR
                qkv_ref[rows, start : start + PAIR] = low(chunk)
        for pair in range(pairs):
            lanes = slice(pair * PAIR, (pair + 1) * PAIR)
            query = qkv_ref[rows, lanes] * jnp.bfloat16(SCALING)
            key = qkv_ref[:keys, heads_width + pair * PAIR : heads_width + (pair + 1) * PAIR]
            value_t = vt_ref[lanes, :keys]
            gathered = None
            for half in range(2):
                masked = jnp.where(head_lanes(query.shape, half, 1), query, jnp.bfloat16(0))
                scores = nt_dot(key, masked)
                highest = jnp.max(scores, axis=0, keepdims=True)
                expanded = jnp.exp(scores - highest)
                totals = jnp.sum(expanded, axis=0, keepdims=True)
                probs = low(expanded * (1.0 / totals))
                lse_ref[2 * pair + half : 2 * pair + half + 1, rows] = highest + jnp.log(totals)
                found = nn_dot(value_t, probs)
                gathered = (
                    found
                    if half == 0
                    else jnp.where(head_lanes(found.shape, 1, 0), found, gathered)
                )
            mixed_ref[rows, lanes] = low(gathered.T)
        send_ref[block] = low(nt_dot(mixed_ref[rows, :], weight(3)))
        copy = to_partner(
            send_ref.at[block], recv_ref.at[block], send_sem.at[block], recv_sem.at[block]
        )
        copy.start()
        copies.append(copy)
    for block in range(blocks):
        rows = block_rows(block)
        copies[block].wait()
        mid = wide(hid_ref[rows, :]) + (wide(send_ref[block]) + wide(recv_ref[block]))
        mid_ref[rows, :] = mid
        s2 = low(mid * lax.rsqrt(mean_last(mid * mid) + EPSILON) * gain_two)
        s2_ref[rows, :] = s2
        tok = token_block(block)
        lane = lax.broadcasted_iota(jnp.int32, tok.shape, 1)
        logits = nn_dot(s2, small_ref[...]) + tok
        picked = [
            jnp.sum(
                jnp.where(wide(lane - ROUTER) == column(tok, ROUTE + member), logits, 0.0),
                axis=1,
                keepdims=True,
            )
            for member in range(2)
        ]
        gate = [
            1.0 / (1.0 + jnp.exp(picked[1 - member] - picked[member])) for member in range(2)
        ]
        tok = jnp.where(lane == GATE, gate[0], jnp.where(lane == GATE + 1, gate[1], tok))
        tok_ref[rows, :] = tok
        line_ref[:, rows] = tok.T[TARGET : TARGET + 8, :]


def forward_plain_kernel(
    hid_ref,
    tok_in_ref,
    block_ref,
    small_ref,
    rows_ref,
    cos_ref,
    sin_ref,
    shard_ref,
    cot_own_ref,
    s1_ref,
    qkv_ref,
    lse_ref,
    mixed_ref,
    mid_ref,
    s2_ref,
    tok_ref,
    line_ref,
    expert_ref,
    cot_ref,
    vt_ref,
    send_ref,
    recv_ref,
    send_sem,
    recv_sem,
    wsend_sem,
    wrecv_sem,
    cot_sem,
):
    greet_group(2 * shard_ref.shape[0])
    own_rows = cot_own_ref.shape[0]
    heads_width = mixed_ref.shape[1]
    width = hid_ref.shape[1]
    mine = pl.ds(pl.multiple_of(lax.axis_index("tp") * own_rows, own_rows), own_rows)
    cot_copy = to_partner(cot_own_ref, cot_ref.at[mine], cot_sem.at[0], cot_sem.at[1])
    cot_copy.start()
    experts = CoreExchange(shard_ref, expert_ref, wsend_sem, wrecv_sem)
    experts.start()
    cot_ref[mine, :] = cot_own_ref[...]

    def weight(part):
        return block_ref[:, :, part * heads_width : (part + 1) * heads_width].reshape(
            width, heads_width
        )

    attend(
        hid_ref,
        lambda block: tok_in_ref[block_rows(block), :],
        weight,
        small_ref,
        (rows_ref[0:1, :], rows_ref[1:2, :]),
        cos_ref,
        sin_ref,
        s1_ref,
        qkv_ref,
        lse_ref,
        mixed_ref,
        mid_ref,
        s2_ref,
        tok_ref,
        line_ref,
        vt_ref,
        send_ref,
        recv_ref,
        send_sem,
        recv_sem,
    )
    cot_copy.wait()
    experts.wait()


def forward_kernel(
    hid_own_ref,
    cot_own_ref,
    logit_ref,
    route_ref,
    rank_ref,
    drop_ref,
    gain_ref,
    router_ref,
    mixing_ref,
    value_ref,
    wqkv_ref,
    wout_ref,
    win_ref,
    wdown_ref,
    cos_ref,
    sin_ref,
    all_ref,
    small_ref,
    rows_ref,
    s1_ref,
    qkv_ref,
    lse_ref,
    mixed_ref,
    mid_ref,
    s2_ref,
    tok_ref,
    line_ref,
    expert_ref,
    cot_ref,
    hid_ref,
    vt_ref,
    send_ref,
    recv_ref,
    shard_ref,
    stage_ref,
    small_all_ref,
    tok_all_ref,
    send_sem,
    recv_sem,
    wsend_sem,
    wrecv_sem,
    y_send,
    y_recv,
    up_send,
    up_recv,
    down_send,
    down_recv,
    x_send,
    x_recv,
    core_send,
    core_recv,
):
    size, shard, _ = all_ref.shape
    planes = size // 4
    me = lax.axis_index("fsdp")
    tp = lax.axis_index("tp")
    z, x, core = me // 4, lax.rem(me // 2, 2), lax.rem(me, 2)
    own_rows, width = hid_own_ref.shape
    heads_width = wout_ref.shape[1]
    small_rows = shard // 2
    greet_group(size)
    partner = {"tp": 1 - tp}
    mine = pl.ds(pl.multiple_of(tp * own_rows, own_rows), own_rows)
    stage_ref[...] = jnp.zeros_like(stage_ref)
    stage_ref[0:2, :small_rows] = gain_ref[...]
    stage_ref[ROUTER:MIXING, :small_rows] = wide(router_ref[...])
    stage_ref[MIXING:VALUE, :small_rows] = wide(mixing_ref[...])
    stage_ref[VALUE : VALUE + 2, :small_rows] = wide(value_ref[...])
    small_all_ref[me, tp] = stage_ref[...].T[:small_rows, :]
    small_y = send_to(
        small_all_ref.at[me, tp], small_all_ref.at[me, tp], y_send.at[0], y_recv.at[0], partner
    )
    small_y.start()
    for part in range(3):
        all_ref[me, :, part * heads_width : (part + 1) * heads_width] = wqkv_ref[part]
    all_ref[me, :, 3 * heads_width :] = wout_ref[...]
    hid_y = send_to(hid_own_ref, hid_ref.at[mine], y_send.at[1], y_recv.at[1], partner)
    tok_y = send_to(tok_all_ref.at[tp], tok_all_ref.at[tp], y_send.at[2], y_recv.at[2], partner)
    cot_y = send_to(cot_own_ref, cot_ref.at[mine], y_send.at[3], y_recv.at[3], partner)
    experts = CoreExchange(shard_ref, expert_ref, wsend_sem, wrecv_sem)
    expert_count, _, hidden = wdown_ref.shape

    def stage_tokens():
        tok_all_ref[tp] = jnp.zeros(tok_all_ref.shape[1:], jnp.float32)
        routes = route_ref[...]
        kept = jnp.logical_and(routes < expert_count, drop_ref[...] == 0)
        target = jnp.where(kept, routes * (own_rows * 2 * 9 // 48) + rank_ref[...], -1)
        tok_all_ref[tp, ROUTER:MIXING, :] = logit_ref[...]
        tok_all_ref[tp, ROUTE : ROUTE + 2, :] = wide(routes)
        tok_all_ref[tp, TARGET : TARGET + 2, :] = wide(target)

    def stage_shard():
        def one(e):
            for part in range(2):
                shard_ref[e, :, part * hidden : (part + 1) * hidden] = win_ref[e, :, part, :]
            shard_ref[e, :, 2 * hidden :] = wdown_ref[e]

        each(0, expert_count, one)

    def number(plane, line):
        return plane * 4 + line * 2 + core

    def piece(kind, number_of, send, recv, slot, device):
        array = small_all_ref if kind else all_ref
        return send_to(
            array.at[number_of],
            array.at[number_of],
            send.at[kind, slot],
            recv.at[kind, slot],
            device,
        )

    def up(kind, step, plane):
        device = {"fsdp": number(lax.min(z + 1, planes - 1), x)}
        return piece(kind, number(plane, x), up_send, up_recv, step, device)

    def down(kind, step, plane):
        device = {"fsdp": number(lax.max(z - 1, 0), x)}
        return piece(kind, number(plane, x), down_send, down_recv, step, device)

    def side(kind, plane, line):
        device = {"fsdp": number(z, 1 - x)}
        return piece(kind, number(plane, line), x_send, x_recv, plane, device)

    def sibling(kind, plane, line, parity):
        return piece(
            kind,
            plane * 4 + line * 2 + parity,
            core_send,
            core_recv,
            plane * 2 + line,
            {"fsdp": me + 1 - 2 * core},
        )

    def launch(kind):
        @pl.when(z < planes - 1)
        def _():
            up(kind, 0, z).start()

        @pl.when(z > 0)
        def _():
            down(kind, 0, z).start()

        side(kind, z, x).start()
        sibling(kind, z, x, core).start()

    launch(0)
    hid_y.start()
    stage_tokens()
    tok_y.start()
    cot_y.start()
    hid_ref[mine, :] = hid_own_ref[...]
    cot_ref[mine, :] = cot_own_ref[...]
    small_y.wait()
    launch(1)
    stage_shard()
    for step in range(1, planes):
        for kind in range(2):

            @pl.when(z >= step)
            def _():
                up(kind, step - 1, z - step).wait_recv()

                @pl.when(z < planes - 1)
                def _():
                    up(kind, step, z - step).start()

                side(kind, z - step, x).start()
                sibling(kind, z - step, x, core).start()

            @pl.when(z + step < planes)
            def _():
                down(kind, step - 1, z + step).wait_recv()

                @pl.when(z > 0)
                def _():
                    down(kind, step, z + step).start()

                side(kind, z + step, x).start()
                sibling(kind, z + step, x, core).start()

    experts.start()
    for step in range(planes):
        for kind in range(2):

            @pl.when(z >= step)
            def _():
                side(kind, z - step, 1 - x).wait_recv()
                sibling(kind, z - step, 1 - x, core).start()

            if step > 0:

                @pl.when(z + step < planes)
                def _():
                    side(kind, z + step, 1 - x).wait_recv()
                    sibling(kind, z + step, 1 - x, core).start()

    for plane in range(planes):
        for line in range(2):
            for kind in range(2):
                sibling(kind, plane, line, 1 - core).wait_recv()
    small_all = small_all_ref[...].reshape(width, PAIR)
    small_ref[...] = low(small_all)
    rows_ref[...] = small_all.T[:8, :]
    tok_y.wait()
    hid_y.wait()

    def token_block(block):
        per = own_rows // BLOCK
        part = tok_all_ref[block // per, :, (block % per) * BLOCK : (block % per + 1) * BLOCK]
        blank = jnp.zeros((PAIR - part.shape[0], BLOCK), jnp.float32)
        return jnp.concatenate([part, blank], axis=0).T

    def weight(part):
        return all_ref[:, :, part * heads_width : (part + 1) * heads_width].reshape(
            width, heads_width
        )

    attend(
        hid_ref,
        token_block,
        weight,
        small_ref,
        (rows_ref[0:1, :], rows_ref[1:2, :]),
        cos_ref,
        sin_ref,
        s1_ref,
        qkv_ref,
        lse_ref,
        mixed_ref,
        mid_ref,
        s2_ref,
        tok_ref,
        line_ref,
        vt_ref,
        send_ref,
        recv_ref,
        send_sem,
        recv_sem,
    )
    for kind in range(2):
        for step in range(planes):

            @pl.when(jnp.logical_and(z >= step, z < planes - 1))
            def _():
                up(kind, step, z - step).wait_send()

            @pl.when(jnp.logical_and(z + step < planes, z > 0))
            def _():
                down(kind, step, z + step).wait_send()

        for plane in range(planes):
            side(kind, plane, x).wait_send()
            for line in range(2):
                sibling(kind, plane, line, core).wait_send()
    cot_y.wait()
    experts.wait()


def backward_kernel(
    res_ref,
    dx_ref,
    slot_ref,
    tok_ref,
    cot_ref,
    mid_hbm,
    s1_hbm,
    qkv_hbm,
    lse_ref,
    mixed_hbm,
    block_hbm,
    small_ref,
    rows_ref,
    cos_hbm,
    sin_hbm,
    own_ref,
    egrad_ref,
    grad_ref,
    base_ref,
    other_ref,
    big_ref,
    arrived_ref,
    gsend_ref,
    grecv_ref,
    ssend_ref,
    srecv_ref,
    mid_ref,
    s1_ref,
    qkv_ref,
    mixed_ref,
    block_ref,
    cos_ref,
    sin_ref,
    hsend_ref,
    hrecv_ref,
    gmid_ref,
    gown_ref,
    kt_ref,
    gm_ref,
    dk_ref,
    dv_ref,
    gp_ref,
    acc_qkv_ref,
    acc_out_ref,
    acc_small_ref,
    acc_gain_ref,
    gsend_sem,
    grecv_sem,
    hsend_sem,
    hrecv_sem,
    esend_sem,
    erecv_sem,
    ssend_sem,
    srecv_sem,
    load_sem,
):
    loads = [
        pltpu.make_async_copy(source, target, load_sem.at[index])
        for index, (source, target) in enumerate(
            [
                (mid_hbm, mid_ref),
                (qkv_hbm, qkv_ref),
                (cos_hbm, cos_ref),
                (sin_hbm, sin_ref),
                (mixed_hbm, mixed_ref),
                (block_hbm, block_ref),
                (s1_hbm, s1_ref),
            ]
        )
    ]
    for load in loads:
        load.start()
    greet_group(2 * egrad_ref.shape[0])
    experts = CoreExchange(egrad_ref, arrived_ref, esend_sem, erecv_sem)
    tp = lax.axis_index("tp")
    width = dx_ref.shape[1]
    blocks = cot_ref.shape[0] // BLOCK
    heads_width = mixed_ref.shape[1]
    pairs = heads_width // PAIR
    gain_one = rows_ref[0:1, :]
    gain_two = rows_ref[1:2, :]
    slot_row = slot_ref[0:1, :]

    def weights(first_part, last_part):
        lanes = slice(first_part * heads_width, last_part * heads_width)
        return block_ref[:, :, lanes].reshape(width, (last_part - first_part) * heads_width)

    order = list(reversed(range(blocks)))
    first = order[0]
    gcopies = {}
    for block in order:
        rows = block_rows(block)
        tok = tok_ref[rows, :]
        onehots = [
            low(jnp.where(column(tok, TARGET + m) == slot_row, 1.0, 0.0)) for m in range(2)
        ]
        placed = [nn_dot(onehot, res_ref[...]) for onehot in onehots]
        cot_wide = wide(cot_ref[rows, :])
        shares = [
            column(tok, GATE + m) * jnp.sum(placed[m] * cot_wide, axis=1, keepdims=True)
            for m in range(2)
        ]
        gsend_ref[block] = low(nn_dot(onehots[0] + onehots[1], dx_ref[...]))
        ssend_ref[block] = lane_matrix(tok.shape, [(0, shares[0]), (1, shares[1])]).T[:8, :]
        copy = (
            to_partner(
                gsend_ref.at[block], grecv_ref.at[block], gsend_sem.at[block], grecv_sem.at[block]
            ),
            to_partner(
                ssend_ref.at[block], srecv_ref.at[block], ssend_sem.at[block], srecv_sem.at[block]
            ),
        )
        copy[0].start()
        copy[1].start()
        gcopies[block] = copy
        placed = column(tok, GATE) * placed[0] + column(tok, GATE + 1) * placed[1]
        slab = slice((block % 2) * BLOCK, (block % 2 + 1) * BLOCK)

        @pl.when(tp == block // 2)
        def _():
            base_ref[slab, :] = placed

        @pl.when(tp != block // 2)
        def _():
            other_ref[slab, :] = low(placed)

    experts.start()
    for load in loads:
        load.wait()
    kt_ref[...] = qkv_ref[:, heads_width : 2 * heads_width].T
    for block in order:
        rows = block_rows(block)
        keys = (block + 1) * BLOCK
        slab = slice((block % 2) * BLOCK, (block % 2 + 1) * BLOCK)
        mine = tp == block // 2
        mine_f = jnp.where(mine, 1.0, 0.0)
        mid = mid_ref[rows, :]
        cot = cot_ref[rows, :]
        cot_wide = wide(cot)
        tok = tok_ref[rows, :]
        scale = lax.rsqrt(mean_last(mid * mid) + EPSILON)
        unit = mid * scale
        normed = unit * gain_two
        s2 = low(normed)
        small = small_ref[...]
        mixing = nn_dot(s2, small)
        value_dot = nn_dot(cot, small)
        normed_dot = jnp.sum(normed * cot_wide, axis=1, keepdims=True)
        route = [column(tok, ROUTE + member) for member in range(2)]
        gate = [column(tok, GATE + member) for member in range(2)]

        def weight_of(expert):
            return sum(jnp.where(route[m] == expert, gate[m], 0.0) for m in range(2))

        copy_weight = weight_of(COPY)
        copy_share = [jnp.where(route[m] == COPY, normed_dot, 0.0) for m in range(2)]
        alpha = copy_weight
        columns = []
        value_columns = []
        for c in range(2):
            weight = weight_of(COPY + 1 + c)
            left = column(mixing, MIXING + 2 * c)
            right = column(mixing, MIXING + 2 * c + 1)
            a0 = 1.0 / (1.0 + jnp.exp(right - left))
            a1 = 1.0 / (1.0 + jnp.exp(left - right))
            vd = column(value_dot, VALUE + c)
            alpha = alpha + weight * a0
            for m in range(2):
                copy_share[m] = copy_share[m] + jnp.where(
                    route[m] == COPY + 1 + c, a0 * normed_dot + a1 * vd, 0.0
                )
            slope = a0 * a1 * weight * (normed_dot - vd)
            columns.append((MIXING + 2 * c, slope))
            columns.append((MIXING + 2 * c + 1, -slope))
            value_columns.append((VALUE + c, weight * a1))
        value_matrix = lane_matrix(tok.shape, value_columns)
        base = mid + alpha * normed + nt_dot(low(value_matrix), small)

        @pl.when(mine)
        def _():
            base_ref[slab, :] += base

        gcopies[block][0].wait()
        gcopies[block][1].wait()
        extra = ssend_ref[block] + srecv_ref[block]
        extra = jnp.concatenate(
            [extra, jnp.zeros((PAIR - extra.shape[0], BLOCK), jnp.float32)], axis=0
        ).T
        share = [column(extra, m) + gate[m] * copy_share[m] for m in range(2)]
        lane = lax.broadcasted_iota(jnp.int32, tok.shape, 1)
        slopes = lane_matrix(tok.shape, columns)
        for m in range(2):
            local = share[m] - gate[m] * (share[0] + share[1])
            slopes = slopes + jnp.where(wide(lane - ROUTER) == route[m], local, 0.0)
        slopes_low = low(slopes)
        grad_normed = (
            wide(gsend_ref[block])
            + wide(grecv_ref[block])
            + alpha * cot_wide
            + nt_dot(slopes_low, small)
        )
        small_grad = tn_dot(s2, low(slopes * mine_f)) + tn_dot(cot, low(value_matrix * mine_f))
        gain_grad = jnp.sum(unit * grad_normed, axis=0, keepdims=True) * mine_f
        scaled = grad_normed * gain_two
        grad_mid = cot_wide + scale * (scaled - unit * mean_last(scaled * unit))
        gmid_ref[rows, :] = grad_mid
        attended = low(grad_mid)
        out_grad = tn_dot(attended, mixed_ref[rows, :])
        gm_ref[...] = low(nn_dot(attended, weights(3, 4)))
        if block == first:
            acc_small_ref[...] = small_grad
            acc_gain_ref[...] = jnp.broadcast_to(gain_grad, acc_gain_ref.shape)
            acc_out_ref[...] = out_grad
        else:
            acc_small_ref[...] += small_grad
            acc_gain_ref[...] += jnp.broadcast_to(gain_grad, acc_gain_ref.shape)
            acc_out_ref[...] += out_grad
        cosine, sine = cos_ref[rows, :], sin_ref[rows, :]

        def one_pair(pair, carry):
            start = pl.multiple_of(pair * PAIR, PAIR)
            lanes = pl.ds(start, PAIR)
            key_lanes = pl.ds(pl.multiple_of(heads_width + start, PAIR), PAIR)
            value_lanes = pl.ds(pl.multiple_of(2 * heads_width + start, PAIR), PAIR)
            query = qkv_ref[rows, lanes] * jnp.bfloat16(SCALING)
            key = qkv_ref[:keys, key_lanes]
            value = qkv_ref[:keys, value_lanes]
            grad_out = gm_ref[:, lanes]
            key_t = kt_ref[lanes, :keys]
            grad_value = None
            for half in range(2):
                keep = head_lanes(query.shape, half, 1)
                q_half = jnp.where(keep, query, jnp.bfloat16(0))
                g_half = jnp.where(keep, grad_out, jnp.bfloat16(0))
                probs = jnp.exp(nt_dot(key, q_half) - lse_ref[pl.ds(2 * pair + half, 1), rows])
                grad_probs = nt_dot(value, g_half)
                inner = jnp.sum(probs * grad_probs, axis=0, keepdims=True)
                grad_scores = low(probs * (grad_probs - inner))
                value_part = nn_dot(low(probs), g_half)
                key_part = nn_dot(grad_scores, q_half)
                query_part = nn_dot(key_t, grad_scores)
                if half == 0:
                    grad_value, grad_key, grad_query = value_part, key_part, query_part
                else:
                    grad_value = grad_value + value_part
                    grad_key = grad_key + key_part
                    grad_query = jnp.where(
                        head_lanes(query_part.shape, 1, 0), query_part, grad_query
                    )
            if block == first:
                dv_ref[:keys, lanes] = grad_value
                dk_ref[:keys, lanes] = grad_key
            else:
                dv_ref[:keys, lanes] += grad_value
                dk_ref[:keys, lanes] += grad_key
            gp_ref[:, lanes] = low(turn(grad_query.T * SCALING, cosine, -sine))
            gp_ref[:, key_lanes] = low(turn(dk_ref[rows, lanes], cosine, -sine))
            gp_ref[:, value_lanes] = low(dv_ref[rows, lanes])
            return carry

        lax.fori_loop(0, pairs, one_pair, 0)
        gp = gp_ref[...]
        qkv_grad = tn_dot(s1_ref[rows, :], gp)
        if block == first:
            acc_qkv_ref[...] = qkv_grad
        else:
            acc_qkv_ref[...] += qkv_grad
        stream_grad = nt_dot(gp, weights(0, 3))

        @pl.when(mine)
        def _():
            gown_ref[block % 2] = stream_grad

        @pl.when(jnp.logical_not(mine))
        def _():
            hsend_ref[block % 2] = low(stream_grad)
            to_partner(
                hsend_ref.at[block % 2],
                hrecv_ref.at[block % 2],
                hsend_sem.at[block % 2],
                hrecv_sem.at[block % 2],
            ).start()

    big_ref[:, : 3 * heads_width] = low(acc_qkv_ref[...])
    big_ref[:, 3 * heads_width : 4 * heads_width] = low(acc_out_ref[...])
    gain_rows = acc_gain_ref[0:1, :]
    tall = jnp.where(
        lax.broadcasted_iota(jnp.int32, (PAIR, width), 0) == 1,
        jnp.broadcast_to(gain_rows, (PAIR, width)),
        0.0,
    )
    big_ref[:, 4 * heads_width :] = low(acc_small_ref[...] + tall.T)
    for slot in reversed(range(2)):
        slab = slice(slot * BLOCK, (slot + 1) * BLOCK)
        to_partner(
            hsend_ref.at[slot], hrecv_ref.at[slot], hsend_sem.at[slot], hrecv_sem.at[slot]
        ).wait()
        source = wide(own_ref[slab, :])
        scale = lax.rsqrt(mean_last(source * source) + EPSILON)
        unit = source * scale
        scaled = (gown_ref[slot] + wide(hrecv_ref[slot])) * gain_one
        mid_rows = pl.ds(pl.multiple_of(tp * 2 * BLOCK + slot * BLOCK, BLOCK), BLOCK)
        grad_ref[slab, :] = gmid_ref[mid_rows, :] + scale * (
            scaled - unit * mean_last(scaled * unit)
        )
    experts.wait()


def forward_results(length, width, heads_width, shard):
    low_t, wide_t = jnp.bfloat16, jnp.float32
    return [
        jax.ShapeDtypeStruct((length, width), low_t),
        jax.ShapeDtypeStruct((length, 3 * heads_width), low_t),
        jax.ShapeDtypeStruct((8, length), wide_t),
        jax.ShapeDtypeStruct((length, heads_width), low_t),
        jax.ShapeDtypeStruct((length, width), wide_t),
        jax.ShapeDtypeStruct((length, width), low_t),
        jax.ShapeDtypeStruct((length, PAIR), wide_t),
        jax.ShapeDtypeStruct((8, length), wide_t),
        jax.ShapeDtypeStruct(shard, low_t),
        jax.ShapeDtypeStruct((length, width), low_t),
    ]


def attend_scratch(length, width, heads_width):
    blocks = length // BLOCK
    return [
        pltpu.VMEM((heads_width, length), jnp.bfloat16),
        pltpu.VMEM((blocks, BLOCK, width), jnp.bfloat16),
        pltpu.VMEM((blocks, BLOCK, width), jnp.bfloat16),
    ]


def run_forward_plain(hid, tok, blocks, small, rows, cosine, sine, shard, cot):
    length, width = hid.shape
    heads_width = blocks.shape[2] // 4
    vmem = pl.BlockSpec(memory_space=pltpu.VMEM)
    dma = pltpu.SemaphoreType.DMA
    count = length // BLOCK
    return pl.pallas_call(
        forward_plain_kernel,
        in_specs=[vmem] * 9,
        out_specs=[vmem] * 10,
        out_shape=forward_results(length, width, heads_width, shard.shape),
        scratch_shapes=attend_scratch(length, width, heads_width)
        + [dma((count,)), dma((count,)), dma((shard.shape[0],)), dma((shard.shape[0],)), dma((2,))],
        compiler_params=pltpu.CompilerParams(
            collective_id=0, has_side_effects=True, vmem_limit_bytes=60 << 20
        ),
    )(hid, tok, blocks, small, rows, cosine, sine, shard, cot)


def run_forward(*operands):
    hid, wout, wdown, cosine = operands[0], operands[11], operands[13], operands[14]
    own_rows, width = hid.shape
    length = cosine.shape[0]
    shard, heads_width = wout.shape
    experts, _, hidden = wdown.shape
    size = lax.axis_size("fsdp")
    count = length // BLOCK
    vmem = pl.BlockSpec(memory_space=pltpu.VMEM)
    low_t, wide_t = jnp.bfloat16, jnp.float32
    dma = pltpu.SemaphoreType.DMA
    return pl.pallas_call(
        forward_kernel,
        in_specs=[vmem] * 16,
        out_specs=[vmem] * 11 + [pl.BlockSpec(memory_space=pl.ANY), vmem],
        out_shape=[
            jax.ShapeDtypeStruct((size, shard, 4 * heads_width), low_t),
            jax.ShapeDtypeStruct((width, PAIR), low_t),
            jax.ShapeDtypeStruct((8, width), wide_t),
        ]
        + forward_results(length, width, heads_width, (experts, shard, 3 * hidden)),
        scratch_shapes=[pltpu.VMEM((length, width), low_t)]
        + attend_scratch(length, width, heads_width)
        + [
            pltpu.VMEM((experts, shard, 3 * hidden), low_t),
            pltpu.VMEM((PAIR, PAIR), wide_t),
            pltpu.VMEM((size, 2, shard // 2, PAIR), wide_t),
            pltpu.VMEM((2, 32, own_rows), wide_t),
            dma((count,)),
            dma((count,)),
            dma((experts,)),
            dma((experts,)),
            dma((4,)),
            dma((4,)),
        ]
        + [dma((2, size // 4))] * 6
        + [dma((2, size // 2))] * 2,
        compiler_params=pltpu.CompilerParams(
            collective_id=3, has_side_effects=True, vmem_limit_bytes=60 << 20
        ),
    )(*operands)


def run_backward(*operands):
    cot, mid, s1, qkv, mixed, blocks, cosine, own, egrads = (
        operands[index] for index in (4, 5, 6, 7, 9, 10, 13, 15, 16)
    )
    length, width = cot.shape
    heads_width = mixed.shape[1]
    count = length // BLOCK
    own_rows = own.shape[0]
    vmem = pl.BlockSpec(memory_space=pltpu.VMEM)
    hbm = pl.BlockSpec(memory_space=pl.ANY)
    low_t, wide_t = jnp.bfloat16, jnp.float32
    dma = pltpu.SemaphoreType.DMA
    return pl.pallas_call(
        backward_kernel,
        in_specs=[vmem] * 5
        + [hbm] * 3
        + [vmem]
        + [hbm] * 2
        + [vmem] * 2
        + [hbm] * 2
        + [vmem, hbm],
        out_specs=[vmem] * 4 + [hbm],
        out_shape=[
            jax.ShapeDtypeStruct((own_rows, width), wide_t),
            jax.ShapeDtypeStruct((own_rows, width), wide_t),
            jax.ShapeDtypeStruct((own_rows, width), low_t),
            jax.ShapeDtypeStruct((width, 4 * heads_width + PAIR), low_t),
            jax.ShapeDtypeStruct(egrads.shape, low_t),
        ],
        scratch_shapes=[
            pltpu.VMEM((count, BLOCK, width), low_t),
            pltpu.VMEM((count, BLOCK, width), low_t),
            pltpu.VMEM((count, 8, BLOCK), wide_t),
            pltpu.VMEM((count, 8, BLOCK), wide_t),
            pltpu.VMEM(mid.shape, wide_t),
            pltpu.VMEM(s1.shape, low_t),
            pltpu.VMEM(qkv.shape, low_t),
            pltpu.VMEM(mixed.shape, low_t),
            pltpu.VMEM(blocks.shape, low_t),
            pltpu.VMEM(cosine.shape, wide_t),
            pltpu.VMEM(cosine.shape, wide_t),
            pltpu.VMEM((2, BLOCK, width), low_t),
            pltpu.VMEM((2, BLOCK, width), low_t),
            pltpu.VMEM((length, width), wide_t),
            pltpu.VMEM((2, BLOCK, width), wide_t),
            pltpu.VMEM((heads_width, length), low_t),
            pltpu.VMEM((BLOCK, heads_width), low_t),
            pltpu.VMEM((length, heads_width), wide_t),
            pltpu.VMEM((length, heads_width), wide_t),
            pltpu.VMEM((BLOCK, 3 * heads_width), low_t),
            pltpu.VMEM((width, 3 * heads_width), wide_t),
            pltpu.VMEM((width, heads_width), wide_t),
            pltpu.VMEM((width, PAIR), wide_t),
            pltpu.VMEM((8, width), wide_t),
            dma((count,)),
            dma((count,)),
            dma((2,)),
            dma((2,)),
            dma((egrads.shape[0],)),
            dma((egrads.shape[0],)),
            dma((count,)),
            dma((count,)),
            dma((7,)),
        ],
        compiler_params=pltpu.CompilerParams(
            collective_id=1, has_side_effects=True, vmem_limit_bytes=60 << 20
        ),
    )(*operands)


def shards(
    hidden,
    prev_logits,
    routes,
    slot_rank,
    dropped,
    cotangent,
    attn_norm,
    ffn_norm,
    w_qkv,
    w_attn_out,
    w_router,
    w_const_gate,
    w_const_value,
    w_expert_in,
    w_expert_out,
):
    own_rows, width = hidden.shape
    length = own_rows * lax.axis_size("tp")
    experts = w_expert_in.shape[0]
    route_count = w_router.shape[1]
    capacity = 9 * length // (4 * route_count)
    planned = lax.axis_size("fsdp") == 16
    cosine, sine = (jnp.asarray(table) for table in rotary_tables(length))
    gains = jnp.stack([wide(attn_norm), wide(ffn_norm)], axis=0)
    wqkv = w_qkv.transpose(1, 0, 2)
    operands = (
        hidden,
        cotangent,
        prev_logits.T,
        routes.T,
        slot_rank.T,
        dropped.T,
        gains,
        w_router.T,
        w_const_gate.T,
        w_const_value.T,
        wqkv,
        w_attn_out,
        w_expert_in,
        w_expert_out,
    )
    if planned:
        forward = run_forward(*operands, cosine, sine)
    else:
        forward = forward_plain(operands, cosine, sine)
    blocks, small, rows, s1, qkv, lse, mixed, mid, s2, tok, lines, gathered, cot = forward
    expert_weights = join_weights(gathered, experts)
    peers = 2 * experts
    half = capacity // 2
    block = half // 2
    place = jnp.arange(peers * block)
    owner = (lax.axis_index("fsdp") % peers) ^ (place // block)
    slot = wide(
        (owner // 2) * capacity
        + lax.axis_index("tp") * half
        + (owner % 2) * block
        + place % block
    )
    results, grad_rows, grads_exp = run_expert(
        s2, cot, lines, jnp.broadcast_to(slot[:, None], (slot.shape[0], PAIR)), expert_weights
    )
    grad_hidden, base, for_other, big, arrived = run_backward(
        results.reshape(-1, width),
        grad_rows.reshape(-1, width),
        jnp.broadcast_to(slot[None, :], (8, slot.shape[0])),
        tok,
        cot,
        mid,
        s1,
        qkv,
        lse,
        mixed,
        blocks,
        small,
        rows,
        cosine,
        sine,
        hidden,
        split_grads(grads_exp),
    )
    received, red, last = (run_finish if planned else finish_plain)(big, wqkv, for_other)
    output, grad_hidden, grad_qkv, grad_attn_out, gain_grads, grad_router, grad_mixing, grad_value, grad_in, grad_out = run_write(
        base, received, grad_hidden, red, last, gains, arrived
    )
    return (
        output,
        grad_hidden,
        gain_grads[0],
        gain_grads[1],
        grad_qkv.transpose(1, 0, 2),
        grad_attn_out,
        grad_router.T,
        grad_mixing.T,
        grad_value.T,
        grad_in,
        grad_out,
    )


def solution(mesh):
    in_specs = (
        P(("fsdp", "tp"), None),
        P(("fsdp", "tp"), None),
        P(("fsdp", "tp"), None),
        P(("fsdp", "tp"), None),
        P(("fsdp", "tp"), None),
        P(("fsdp", "tp"), None),
        P(("fsdp", "tp")),
        P(("fsdp", "tp")),
        P("fsdp", None, "tp"),
        P("fsdp", "tp"),
        P(("fsdp", "tp"), None),
        P(("fsdp", "tp"), None),
        P(("fsdp", "tp"), None),
        P(None, "fsdp", None, "tp"),
        P(None, "fsdp", "tp"),
    )
    out_specs = (
        P(("fsdp", "tp"), None),
        P(("fsdp", "tp"), None),
        P(("fsdp", "tp")),
        P(("fsdp", "tp")),
        P("fsdp", None, "tp"),
        P("fsdp", "tp"),
        P(("fsdp", "tp"), None),
        P(("fsdp", "tp"), None),
        P(("fsdp", "tp"), None),
        P(None, "fsdp", None, "tp"),
        P(None, "fsdp", "tp"),
    )
    return jax.shard_map(shards, mesh=mesh, in_specs=in_specs, out_specs=out_specs, check_vma=False)
```

```python
import functools

import jax
import jax.numpy as jnp
import numpy as np
from jax import lax
from jax.experimental import pallas as pl
from jax.experimental.pallas import tpu as pltpu
from jax.sharding import PartitionSpec as P

HD = 64
BLOCK = 256


EPSILON = 1e-06
MESH = pl.DeviceIdType.MESH
PAIR = 2 * HD
SCALING = HD ** (-0.5)
ROUTER = 2
MIXING = 14
VALUE = 18
ROUTE = 20
TARGET = 24
GATE = 26
COPY = 9


TILE = 256


def swap(values):
    return lax.ppermute(values, "tp", [(0, 1), (1, 0)])


def gather_rows(values):
    other = swap(values)
    first = lax.axis_index("tp") == 0
    return jnp.concatenate(
        [jnp.where(first, values, other), jnp.where(first, other, values)], axis=0
    )


def own_half(values):
    half = values.shape[0] // 2
    return lax.dynamic_slice_in_dim(values, lax.axis_index("tp") * half, half, 0)


def other_half(values):
    half = values.shape[0] // 2
    return lax.dynamic_slice_in_dim(values, (1 - lax.axis_index("tp")) * half, half, 0)


def member_groups(size, experts):
    span = 2 * experts
    starts = range(0, size, span)
    cores = [[start + 2 * e, start + 2 * e + 1] for start in starts for e in range(experts)]
    across = [[start + r for start in starts] for r in range(span)]
    return cores, across


def own_core(values, rows):
    parts = values.reshape(-1, 2, rows, values.shape[-1])
    return lax.dynamic_index_in_dim(parts, lax.axis_index("fsdp") % 2, 1, keepdims=False)


def join_weights(got, experts):
    size = lax.axis_size("fsdp")
    if size == 2 * experts:
        return got
    cores, across = member_groups(size, experts)
    got = lax.all_gather(got, "fsdp", axis=1, axis_index_groups=cores, tiled=True)
    got = got.reshape(-1, got.shape[-1])
    got = lax.all_gather(got, "fsdp", axis=0, axis_index_groups=across, tiled=True)
    return own_core(got, got.shape[0] // (2 * experts))


def split_grads(grads):
    experts, _, columns = grads.shape
    size = lax.axis_size("fsdp")
    if size == 2 * experts:
        return grads
    cores, across = member_groups(size, experts)
    grads = lax.all_gather(grads[:, None], "fsdp", axis=1, axis_index_groups=cores, tiled=True)
    grads = grads.reshape(-1, columns)
    grads = lax.psum_scatter(
        grads, "fsdp", scatter_dimension=0, axis_index_groups=across, tiled=True
    )
    return own_core(grads, grads.shape[0] // (2 * experts))


def finish_plain(big, wqkv, other):
    heads_width = (big.shape[1] - PAIR) // 4
    reduced = wide(lax.psum_scatter(big, "fsdp", scatter_dimension=0, tiled=True))
    parts = reduced[:, : 3 * heads_width].reshape(-1, 3, heads_width).transpose(1, 0, 2)
    share = jnp.sum(parts * wide(wqkv), axis=(0, 2))
    last = jnp.concatenate([share[:, None], reduced[:, 4 * heads_width + 1 :]], axis=1)
    return (
        swap(other),
        reduced[:, : 4 * heads_width],
        own_half(last) + swap(other_half(last)),
    )


def forward_plain(operands, table):
    (
        hidden,
        cotangent,
        logits,
        routes,
        rank,
        dropped,
        gains,
        router,
        mixing,
        value,
        wqkv,
        wout,
        w_in,
        w_down,
    ) = operands
    own_rows, width = hidden.shape
    experts, shard, units = w_down.shape
    small = jnp.concatenate([wide(v) for v in (gains, router, mixing, value)], axis=0)
    small = jnp.pad(small, ((0, PAIR - small.shape[0]), (0, 0))).T
    small = lax.all_gather(small, ("fsdp", "tp"), axis=0, tiled=True)
    capacity = own_rows * 2 * 9 // 48
    kept = (routes < experts) & (dropped == 0)
    target = jnp.where(kept, routes * capacity + rank, -1)
    blank = jnp.zeros((2, own_rows), jnp.float32)
    tok = jnp.concatenate(
        [blank, logits, blank, blank, blank, wide(routes), blank, wide(target)], axis=0
    )
    tok = lax.all_gather(tok, "tp", axis=1, tiled=True).T
    tok = jnp.pad(tok, ((0, 0), (0, PAIR - tok.shape[1])))
    blocks = jnp.concatenate([wqkv[0], wqkv[1], wqkv[2], wout], axis=1)
    blocks = lax.all_gather(blocks, "fsdp", axis=0, tiled=True).reshape(2 * experts, -1, blocks.shape[1])
    rows = small.T[:8]
    small = low(small)
    shards_flat = jnp.concatenate([w_in.reshape(experts, shard, 2 * units), w_down], axis=2)
    return (blocks, small, rows) + tuple(
        run_forward_plain(
            gather_rows(hidden), tok, blocks, small, rows, table, shards_flat, cotangent
        )
    )


def nt_dot(left, right):
    return lax.dot_general(left, right, (((1,), (1,)), ((), ())), preferred_element_type=jnp.float32)


def nn_dot(left, right):
    return jnp.dot(left, right, preferred_element_type=jnp.float32)


def tn_dot(left, right):
    return lax.dot_general(left, right, (((0,), (0,)), ((), ())), preferred_element_type=jnp.float32)


def low(values):
    return values.astype(jnp.bfloat16)


def wide(values):
    return values.astype(jnp.float32)


def rotary_table(length):
    half = HD // 2
    positions = np.arange(length, dtype=np.float32)
    inverse = np.power(np.float32(10000.0), -np.arange(half, dtype=np.float32) / np.float32(half))
    angles = (positions[:, None] * inverse[None, :].astype(np.float32)).astype(np.float32)
    cosine = np.cos(angles.astype(np.float64)).astype(np.float32)
    sine = np.sin(angles.astype(np.float64)).astype(np.float32)
    return np.concatenate([cosine, sine], axis=1)


def spread_table(table):
    quarter = HD // 2
    table = jnp.concatenate([table, jnp.zeros_like(table)], axis=1)
    lane = lax.broadcasted_iota(jnp.int32, table.shape, 1)
    cosine = jnp.where(lane < quarter, table, 0.0)
    cosine = cosine + pltpu.roll(cosine, quarter, 1)
    sine = jnp.where(lane < quarter, 0.0, table)
    sine = sine - pltpu.roll(sine, PAIR - quarter, 1)
    return cosine + pltpu.roll(cosine, HD, 1), sine + pltpu.roll(sine, HD, 1)


def turn(values, cosine, sine):
    lane = lax.broadcasted_iota(jnp.int32, values.shape, 1)
    upper = lax.rem(lane, HD) >= HD // 2
    partner = jnp.where(
        upper, pltpu.roll(values, HD // 2, 1), pltpu.roll(values, PAIR - HD // 2, 1)
    )
    return values * cosine + partner * sine


def head_lanes(shape, half, axis):
    return (lax.broadcasted_iota(jnp.int32, shape, axis) >= HD) == bool(half)


def mean_last(values):
    return jnp.mean(values, axis=-1, keepdims=True)


def to_partner(source, target, send_sem, recv_sem):
    return pltpu.make_async_remote_copy(
        src_ref=source,
        dst_ref=target,
        send_sem=send_sem,
        recv_sem=recv_sem,
        device_id={"tp": 1 - lax.axis_index("tp")},
        device_id_type=MESH,
    )


def block_rows(block):
    return pl.ds(pl.multiple_of(block * BLOCK, BLOCK), BLOCK)


def column(values, index):
    return values[:, index : index + 1]


def lane_matrix(shape, columns):
    lane = lax.broadcasted_iota(jnp.int32, shape, 1)
    total = jnp.zeros(shape, jnp.float32)
    for index, values in columns:
        total = jnp.where(lane == index, values, total)
    return total


def send_to(source, target, send_sem, recv_sem, device):
    return pltpu.make_async_remote_copy(
        src_ref=source,
        dst_ref=target,
        send_sem=send_sem,
        recv_sem=recv_sem,
        device_id=device,
        device_id_type=MESH,
    )


def greet_group(peers):
    me = lax.axis_index("fsdp")
    rank = lax.rem(me, peers)
    barrier = pltpu.get_barrier_semaphore()
    for k in range(1, peers):
        pl.semaphore_signal(
            barrier,
            inc=1,
            device_id={"fsdp": me - rank + lax.rem(rank + k, peers)},
            device_id_type=MESH,
        )
    pl.semaphore_signal(
        barrier, inc=1, device_id={"tp": 1 - lax.axis_index("tp")}, device_id_type=MESH
    )
    pl.semaphore_wait(barrier, peers)


def each(first, last, body):
    def step(k, carry):
        body(k)
        return carry

    lax.fori_loop(first, last, step, 0)


def flipped(value, k, bits):
    other = 0
    bit = 1
    while bit < bits:
        ours, theirs = lax.rem(value // bit, 2), lax.rem(k // bit, 2)
        other = other + bit * (ours + theirs - 2 * ours * theirs)
        bit *= 2
    return other


class CoreExchange:
    def __init__(self, source, target, send_sem, recv_sem):
        experts = source.shape[0]
        me = lax.axis_index("fsdp")
        rank = lax.rem(me, 2 * experts)
        core = lax.rem(rank, 2)
        mine = rank // 2

        def device(k):
            return {"fsdp": me - rank + 2 * flipped(mine, k, experts) + core}

        def copy(k):
            there = flipped(mine, k, experts)
            return send_to(
                source.at[there], target.at[mine], send_sem.at[k], recv_sem.at[k], device(k)
            )

        def arrival(k):
            there = flipped(mine, k, experts)
            return send_to(
                source.at[there], target.at[there], send_sem.at[k], recv_sem.at[k], device(k)
            )

        self.experts, self.copy, self.arrival = experts, copy, arrival
        self.local = pltpu.make_async_copy(source.at[mine], target.at[mine], send_sem.at[0])

    def start(self):
        self.local.start()
        each(1, self.experts, lambda k: self.copy(k).start())

    def wait(self):
        each(1, self.experts, lambda k: self.copy(k).wait_send())
        each(1, self.experts, lambda k: self.arrival(k).wait_recv())
        self.local.wait()


def finish_kernel(
    big_ref,
    wqkv_ref,
    other_ref,
    y_ref,
    red_ref,
    tail_ref,
    sum_ref,
    core_ref,
    side_ref,
    acc_ref,
    usend_ref,
    urecv_ref,
    dsend_ref,
    drecv_ref,
    tsend_ref,
    trecv_ref,
    core_send,
    core_recv,
    x_send,
    x_recv,
    up_send,
    up_recv,
    dn_send,
    dn_recv,
    y_send,
    y_recv,
):
    size = big_ref.shape[0]
    planes = size // 4
    me = lax.axis_index("fsdp")
    tp = lax.axis_index("tp")
    z, x, core = me // 4, lax.rem(me // 2, 2), lax.rem(me, 2)
    heads_width = wqkv_ref.shape[2]
    greet_group(size)
    partner = {"tp": 1 - tp}

    def to_core(plane, line):
        slot = plane * 2 + line
        return send_to(
            big_ref.at[plane * 4 + line * 2 + 1 - core],
            core_ref.at[slot],
            core_send.at[slot],
            core_recv.at[slot],
            {"fsdp": me + 1 - 2 * core},
        )

    def to_side(plane):
        return send_to(
            sum_ref.at[plane],
            side_ref.at[plane],
            x_send.at[plane],
            x_recv.at[plane],
            {"fsdp": z * 4 + (1 - x) * 2 + core},
        )

    def to_up(plane):
        return send_to(
            usend_ref.at[plane],
            urecv_ref.at[plane],
            up_send.at[plane],
            up_recv.at[plane],
            {"fsdp": lax.min(z + 1, planes - 1) * 4 + x * 2 + core},
        )

    def to_down(plane):
        return send_to(
            dsend_ref.at[plane],
            drecv_ref.at[plane],
            dn_send.at[plane],
            dn_recv.at[plane],
            {"fsdp": lax.max(z - 1, 0) * 4 + x * 2 + core},
        )

    order = [planes - 1, 0, 2, 1]
    for plane in order:
        to_core(plane, 1 - x).start()
    for plane in order:
        to_core(plane, x).start()
    out_y = send_to(other_ref, y_ref, y_send.at[0], y_recv.at[0], partner)
    out_y.start()

    def joined(plane, line):
        to_core(plane, line).wait_recv()
        return wide(big_ref[plane * 4 + line * 2 + core]) + wide(core_ref[plane * 2 + line])

    for plane in order:
        sum_ref[plane] = low(joined(plane, 1 - x))
        to_side(plane).start()
    for plane in order:
        acc_ref[plane] = joined(plane, x)
    def ready(plane):
        to_side(plane).wait_recv()
        acc_ref[plane] += wide(side_ref[plane])

    def rise(plane):
        @pl.when(jnp.logical_and(z > 0, z <= plane))
        def _():
            to_up(plane).wait_recv()
            acc_ref[plane] += wide(urecv_ref[plane])

        @pl.when(z < plane)
        def _():
            usend_ref[plane] = low(acc_ref[plane])
            to_up(plane).start()

    def fall(plane):
        @pl.when(jnp.logical_and(z < planes - 1, z >= plane))
        def _():
            to_down(plane).wait_recv()
            acc_ref[plane] += wide(drecv_ref[plane])

        @pl.when(z > plane)
        def _():
            dsend_ref[plane] = low(acc_ref[plane])
            to_down(plane).start()

    ready(3)
    rise(3)
    ready(0)
    fall(0)
    ready(2)
    rise(2)
    ready(1)
    fall(1)
    rise(1)
    fall(2)
    rise(0)
    fall(3)
    values = acc_ref[z]
    red_ref[...] = values[:, : 4 * heads_width]
    share = sum(
        jnp.sum(
            values[:, part * heads_width : (part + 1) * heads_width] * wide(wqkv_ref[part]),
            axis=1,
            keepdims=True,
        )
        for part in range(3)
    )
    last = values[:, 4 * heads_width :]
    last = jnp.where(lax.broadcasted_iota(jnp.int32, last.shape, 1) == 0, share, last)
    part_rows = tail_ref.shape[0]
    tsend_ref[0] = last[:part_rows, :]
    tsend_ref[1] = last[part_rows:, :]
    tail_y = send_to(tsend_ref.at[1 - tp], trecv_ref, y_send.at[1], y_recv.at[1], partner)
    tail_y.start()
    out_y.wait()
    tail_y.wait()
    tail_ref[...] = tsend_ref[tp] + trecv_ref[...]
    for plane in range(planes):
        to_core(plane, 1 - x).wait_send()
        to_core(plane, x).wait_send()
        to_side(plane).wait_send()

        @pl.when(z < plane)
        def _():
            to_up(plane).wait_send()

        @pl.when(z > plane)
        def _():
            to_down(plane).wait_send()


def run_finish(big, wqkv, other):
    size = lax.axis_size("fsdp")
    planes = size // 4
    own_rows, width = other.shape
    columns = big.shape[1]
    shard = width // size
    vmem = pl.BlockSpec(memory_space=pltpu.VMEM)
    low_t, wide_t = jnp.bfloat16, jnp.float32
    dma = pltpu.SemaphoreType.DMA
    line = (planes, shard, columns)
    return pl.pallas_call(
        finish_kernel,
        in_specs=[vmem] * 3,
        out_specs=[vmem] * 3,
        out_shape=[
            jax.ShapeDtypeStruct((own_rows, width), low_t),
            jax.ShapeDtypeStruct((shard, columns - PAIR), wide_t),
            jax.ShapeDtypeStruct((shard // 2, PAIR), wide_t),
        ],
        scratch_shapes=[
            pltpu.VMEM(line, low_t),
            pltpu.VMEM((2 * planes, shard, columns), low_t),
            pltpu.VMEM(line, low_t),
            pltpu.VMEM(line, wide_t),
            pltpu.VMEM(line, low_t),
            pltpu.VMEM(line, low_t),
            pltpu.VMEM(line, low_t),
            pltpu.VMEM(line, low_t),
            pltpu.VMEM((2, shard // 2, PAIR), wide_t),
            pltpu.VMEM((shard // 2, PAIR), wide_t),
            dma((2 * planes,)),
            dma((2 * planes,)),
        ]
        + [dma((planes,))] * 6
        + [dma((2,))] * 2,
        compiler_params=pltpu.CompilerParams(
            collective_id=4, has_side_effects=True, vmem_limit_bytes=60 << 20
        ),
    )(big.reshape(size, shard, columns), wqkv, other)


def write_kernel(
    base_ref,
    y_ref,
    grad_ref,
    red_ref,
    tail_ref,
    gain_ref,
    expert_ref,
    out_ref,
    hidden_ref,
    qkv_ref,
    attn_ref,
    gains_ref,
    router_ref,
    mixing_ref,
    value_ref,
    in_ref,
    down_ref,
):
    hidden = down_ref.shape[2]
    heads_width = attn_ref.shape[1]
    out_ref[...] = low(base_ref[...] + wide(y_ref[...]))
    hidden_ref[...] = grad_ref[...]
    values = wide(expert_ref[0])
    in_ref[0, :, 0, :] = values[:, :hidden]
    in_ref[0, :, 1, :] = values[:, hidden : 2 * hidden]
    down_ref[0] = values[:, 2 * hidden :]

    @pl.when(pl.program_id(0) == 0)
    def _():
        for part in range(3):
            qkv_ref[part] = red_ref[:, part * heads_width : (part + 1) * heads_width]
        attn_ref[...] = red_ref[:, 3 * heads_width :]
        count = tail_ref.shape[0]
        blank = jnp.zeros((PAIR - count, PAIR), jnp.float32)
        turned = jnp.concatenate([tail_ref[...], blank], axis=0).T[:, :count]
        gains_ref[0:1, :] = turned[0:1, :] / gain_ref[0:1, :]
        gains_ref[1:2, :] = turned[1:2, :]
        router_ref[...] = turned[ROUTER:MIXING, :]
        mixing_ref[...] = turned[MIXING:VALUE, :]
        value_ref[...] = turned[VALUE : VALUE + 2, :]


def run_write(base, y, grad_hidden, red, tail, gains, arrived):
    own_rows, width = base.shape
    shard = red.shape[0]
    heads_width = red.shape[1] // 4
    count = tail.shape[0]
    experts, _, total = arrived.shape
    hidden = total // 3
    wide_t = jnp.float32
    rows = pl.BlockSpec((own_rows // experts, width), lambda e: (e, 0))

    def whole(shape):
        return pl.BlockSpec(shape, lambda e: (0,) * len(shape))

    return pl.pallas_call(
        write_kernel,
        grid=(experts,),
        in_specs=[
            rows,
            rows,
            rows,
            whole(red.shape),
            whole(tail.shape),
            whole(gains.shape),
            pl.BlockSpec((1, shard, total), lambda e: (e, 0, 0)),
        ],
        out_specs=[
            rows,
            rows,
            whole((3, shard, heads_width)),
            whole((shard, heads_width)),
            whole((2, count)),
            whole((MIXING - ROUTER, count)),
            whole((VALUE - MIXING, count)),
            whole((2, count)),
            pl.BlockSpec((1, shard, 2, hidden), lambda e: (e, 0, 0, 0)),
            pl.BlockSpec((1, shard, hidden), lambda e: (e, 0, 0)),
        ],
        out_shape=[
            jax.ShapeDtypeStruct((own_rows, width), jnp.bfloat16),
            jax.ShapeDtypeStruct((own_rows, width), wide_t),
            jax.ShapeDtypeStruct((3, shard, heads_width), wide_t),
            jax.ShapeDtypeStruct((shard, heads_width), wide_t),
            jax.ShapeDtypeStruct((2, count), wide_t),
            jax.ShapeDtypeStruct((MIXING - ROUTER, count), wide_t),
            jax.ShapeDtypeStruct((VALUE - MIXING, count), wide_t),
            jax.ShapeDtypeStruct((2, count), wide_t),
            jax.ShapeDtypeStruct((experts, shard, 2, hidden), wide_t),
            jax.ShapeDtypeStruct((experts, shard, hidden), wide_t),
        ],
    )(base, y, grad_hidden, red, tail, gains, arrived)


def expert_kernel(
    s2_ref,
    cot_ref,
    line_ref,
    slot_ref,
    weight_ref,
    res_out_ref,
    dx_out_ref,
    grads_out_ref,
    xs_ref,
    gs_ref,
    x_ref,
    g_ref,
    w_ref,
    gate_ref,
    up_ref,
    act_ref,
    xt_ref,
    gt_ref,
    acc_ref,
    grads_ref,
    sibling_ref,
    ysend_ref,
    yrecv_ref,
    w_sem,
    grad_sem,
    xs_sem,
    xr_sem,
    gs_sem,
    gr_sem,
    xfs_sem,
    xfr_sem,
    gfs_sem,
    gfr_sem,
    ys_sem,
    yr_sem,
    rs_sem,
    rr_sem,
    ds_sem,
    dr_sem,
):
    peers, rows, width = xs_ref.shape
    total = peers * rows
    hidden = gate_ref.shape[1]
    tiles = hidden // TILE
    me = lax.axis_index("fsdp")
    tp = lax.axis_index("tp")
    rank = lax.rem(me, peers)
    core = lax.rem(rank, 2)
    start = me - rank

    def peer(k):
        return {"fsdp": start + flipped(rank, k, peers)}

    partner = {"tp": 1 - tp}
    sibling = {"fsdp": start + rank + 1 - 2 * core}

    def out_x(k):
        return send_to(xs_ref.at[k], x_ref.at[0, k], xs_sem.at[k], xr_sem.at[k], peer(k))

    def out_g(k):
        return send_to(gs_ref.at[k], g_ref.at[0, k], gs_sem.at[k], gr_sem.at[k], peer(k))

    def pass_x(k):
        return send_to(x_ref.at[0, k], x_ref.at[1, k], xfs_sem.at[k], xfr_sem.at[k], partner)

    def pass_g(k):
        return send_to(g_ref.at[0, k], g_ref.at[1, k], gfs_sem.at[k], gfr_sem.at[k], partner)

    def across(index, k):
        return send_to(
            ysend_ref.at[index, k],
            yrecv_ref.at[index, k],
            ys_sem.at[index, k],
            yr_sem.at[index, k],
            partner,
        )

    def back(index, k):
        if index == 0:
            return send_to(xs_ref.at[k], res_out_ref.at[k], rs_sem.at[k], rr_sem.at[k], peer(k))
        return send_to(gs_ref.at[k], dx_out_ref.at[k], ds_sem.at[k], dr_sem.at[k], peer(k))

    def return_order(body):
        def step(j, carry):
            body(8 + 2 * j)
            body(4 + j)
            body(9 + 2 * j)
            return carry

        lax.fori_loop(0, 4, step, 0)
        for k in (2, 3, 1, 0):
            body(k)

    def join(index, k):
        across(index, k).wait_recv()
        own = xs_ref if index == 0 else gs_ref
        own[k] = low(wide(own[k]) + wide(yrecv_ref[index, k]))
        back(index, k).start()

    def join_some(index, tile):
        join(index, 8 + 2 * tile)
        join(index, 4 + tile)
        join(index, 9 + 2 * tile)

    def join_last(index):
        for k in (2, 3, 1):
            join(index, k)
        across(index, 0).wait_recv()
        own, target = (xs_ref, res_out_ref) if index == 0 else (gs_ref, dx_out_ref)
        target[0] = low(wide(own[0]) + wide(yrecv_ref[index, 0]))

    greet_group(peers)
    here = pltpu.make_async_copy(weight_ref, w_ref.at[:, core], w_sem.at[0])
    here.start()
    there = send_to(weight_ref, w_ref.at[:, core], w_sem.at[1], w_sem.at[2], sibling)
    half = total // 2
    halves = []
    for part in range(2):
        blocks = slice(part * peers // 2, (part + 1) * peers // 2)
        ids = slot_ref[part * half : (part + 1) * half, 0:1]
        hits = [line_ref[m : m + 1, :] == ids for m in range(2)]
        onehot = low(jnp.where(hits[0] | hits[1], 1.0, 0.0))
        xs_ref[blocks] = low(nn_dot(onehot, s2_ref[...])).reshape(peers // 2, rows, width)
        if part == 0:
            x_ref[0, 0] = xs_ref[0]
            pass_x(0).start()
        each(max(1, part * peers // 2), (part + 1) * peers // 2, lambda k: out_x(k).start())
        halves.append((blocks, onehot, hits))
    there.start()
    for part in range(2):
        blocks, onehot, hits = halves[part]
        gate = sum(
            jnp.sum(jnp.where(hits[m], line_ref[2 + m : 3 + m, :], 0.0), axis=1, keepdims=True)
            for m in range(2)
        )
        gs_ref[blocks] = low(nn_dot(onehot, cot_ref[...]) * gate).reshape(peers // 2, rows, width)
        if part == 0:
            g_ref[0, 0] = gs_ref[0]
        each(max(1, part * peers // 2), (part + 1) * peers // 2, lambda k: out_g(k).start())

    def forward_x(k):
        out_x(k).wait_recv()
        pass_x(k).start()

    each(1, peers, forward_x)
    pass_g(0).start()
    here.wait()
    send_to(weight_ref, w_ref.at[:, 1 - core], w_sem.at[1], w_sem.at[2], sibling).wait_recv()
    there.wait_send()
    each(0, peers, lambda k: pass_x(k).wait_recv())

    def weights(which, lanes):
        return w_ref[:, :, :, pl.ds(pl.multiple_of(which * hidden + lanes, TILE), TILE)].reshape(
            width, TILE
        )

    acc_ref[...] = jnp.zeros_like(acc_ref)

    def forward_tile(tile, carry):
        lanes = pl.multiple_of(tile * TILE, TILE)
        here_lanes = pl.ds(lanes, TILE)
        x = x_ref[...].reshape(2 * total, width)
        gate = nn_dot(x, weights(0, lanes))
        up = nn_dot(x, weights(1, lanes))
        gate_ref[:, here_lanes] = low(gate)
        up_ref[:, here_lanes] = low(up)
        act = low(gate / (1.0 + jnp.exp(-gate)) * up)
        act_ref[:, here_lanes] = act
        acc_ref[...] += nt_dot(act, weights(2, lanes))

        def forward_g(k):
            @pl.when(k > 0)
            def _():
                out_g(k).wait_recv()
                pass_g(k).start()

        each(tile * (peers // tiles), (tile + 1) * (peers // tiles), forward_g)
        return carry

    lax.fori_loop(0, tiles, forward_tile, 0)
    each(1, peers, lambda k: out_x(k).wait_send())
    xs_ref[...] = low(acc_ref[:total, :]).reshape(peers, rows, width)
    ysend_ref[0] = low(acc_ref[total:, :]).reshape(peers, rows, width)
    return_order(lambda k: across(0, k).start())
    xt_ref[...] = x_ref[...].reshape(2 * total, width).T
    acc_ref[...] = jnp.zeros_like(acc_ref)
    each(0, peers, lambda k: pass_g(k).wait_recv())

    def slope_tile(tile, carry):
        lanes = pl.multiple_of(tile * TILE, TILE)
        here_lanes = pl.ds(lanes, TILE)
        gate = wide(gate_ref[:, here_lanes])
        up = wide(up_ref[:, here_lanes])
        sig = 1.0 / (1.0 + jnp.exp(-gate))
        d_act = nn_dot(g_ref[...].reshape(2 * total, width), weights(2, lanes))
        d_up = low(d_act * gate * sig)
        d_gate = low(d_act * up * sig * (1.0 + gate * (1.0 - sig)))
        gate_ref[:, here_lanes] = d_gate
        up_ref[:, here_lanes] = d_up
        acc_ref[...] += nt_dot(d_gate, weights(0, lanes)) + nt_dot(d_up, weights(1, lanes))
        join_some(0, tile)
        return carry

    lax.fori_loop(0, tiles, slope_tile, 0)
    join_last(0)
    each(1, peers, lambda k: out_g(k).wait_send())
    gs_ref[...] = low(acc_ref[:total, :]).reshape(peers, rows, width)
    ysend_ref[1] = low(acc_ref[total:, :]).reshape(peers, rows, width)
    return_order(lambda k: across(1, k).start())
    gt_ref[...] = g_ref[...].reshape(2 * total, width).T

    def weight_tile(tile, carry):
        lanes = pl.multiple_of(tile * TILE, TILE)
        here_lanes = pl.ds(lanes, TILE)

        def keep(which, values):
            grads_ref[
                :, :, :, pl.ds(pl.multiple_of(which * hidden + lanes, TILE), TILE)
            ] = low(values).reshape(peers // 2, 2, rows, TILE)

        keep(0, nn_dot(xt_ref[...], gate_ref[:, here_lanes]))
        keep(1, nn_dot(xt_ref[...], up_ref[:, here_lanes]))
        keep(2, nn_dot(gt_ref[...], act_ref[:, here_lanes]))
        join_some(1, tile)
        return carry

    lax.fori_loop(0, tiles, weight_tile, 0)
    join_last(1)
    swap_grads = send_to(
        grads_ref.at[:, 1 - core], sibling_ref, grad_sem.at[0], grad_sem.at[1], sibling
    )
    swap_grads.start()
    each(0, peers, lambda k: pass_x(k).wait_send())
    each(0, peers, lambda k: pass_g(k).wait_send())
    for index in range(2):
        each(0, peers, lambda k: across(index, k).wait_send())
        each(1, peers, lambda k: back(index, k).wait_send())
    swap_grads.wait()
    grads_out_ref[...] = low(wide(grads_ref[:, core]) + wide(sibling_ref[...]))
    for index in range(2):
        each(1, peers, lambda k: back(index, k).wait_recv())


def run_expert(s2, cot, lines, slots, weights):
    length, width = s2.shape
    experts, shard, total = weights.shape
    peers = 2 * experts
    rows = slots.shape[0] // peers
    hidden = total // 3
    both = 2 * peers * rows
    vmem = pl.BlockSpec(memory_space=pltpu.VMEM)
    low_t, wide_t = jnp.bfloat16, jnp.float32
    dma = pltpu.SemaphoreType.DMA
    block = (peers, rows, width)
    return pl.pallas_call(
        expert_kernel,
        in_specs=[vmem] * 4 + [pl.BlockSpec(memory_space=pl.ANY)],
        out_specs=[vmem] * 3,
        out_shape=[
            jax.ShapeDtypeStruct(block, low_t),
            jax.ShapeDtypeStruct(block, low_t),
            jax.ShapeDtypeStruct(weights.shape, low_t),
        ],
        scratch_shapes=[
            pltpu.VMEM(block, low_t),
            pltpu.VMEM(block, low_t),
            pltpu.VMEM((2,) + block, low_t),
            pltpu.VMEM((2,) + block, low_t),
            pltpu.VMEM((experts, 2, shard, total), low_t),
            pltpu.VMEM((both, hidden), low_t),
            pltpu.VMEM((both, hidden), low_t),
            pltpu.VMEM((both, hidden), low_t),
            pltpu.VMEM((width, both), low_t),
            pltpu.VMEM((width, both), low_t),
            pltpu.VMEM((both, width), wide_t),
            pltpu.VMEM((experts, 2, shard, total), low_t),
            pltpu.VMEM((experts, shard, total), low_t),
            pltpu.VMEM((2,) + block, low_t),
            pltpu.VMEM((2,) + block, low_t),
            dma((3,)),
            dma((2,)),
        ]
        + [dma((peers,))] * 8
        + [dma((2, peers))] * 2
        + [dma((peers,))] * 4,
        compiler_params=pltpu.CompilerParams(
            collective_id=2, has_side_effects=True, vmem_limit_bytes=67043328
        ),
    )(s2, cot, lines, slots, weights)


def attend(
    hid_ref,
    token_block,
    weight,
    small_ref,
    gains,
    table_ref,
    s1_ref,
    qkv_ref,
    lse_ref,
    mixed_ref,
    mid_ref,
    s2_ref,
    tok_ref,
    line_ref,
    vt_ref,
    send_ref,
    recv_ref,
    send_sem,
    recv_sem,
    between,
):
    blocks = hid_ref.shape[0] // BLOCK
    heads_width = mixed_ref.shape[1]
    pairs = heads_width // PAIR
    gain_one, gain_two = gains
    lse_ref[...] = jnp.zeros_like(lse_ref)

    def copy(block):
        return to_partner(
            send_ref.at[block], recv_ref.at[block], send_sem.at[block], recv_sem.at[block]
        )

    def compute(block):
        rows = block_rows(block)
        source = wide(hid_ref[rows, :])
        s1 = low(source * lax.rsqrt(mean_last(source * source) + EPSILON) * gain_one)
        s1_ref[rows, :] = s1
        cosine, sine = spread_table(table_ref[rows, :])
        for part in range(3):
            projected = nn_dot(s1, weight(part))
            for pair in range(pairs):
                chunk = projected[:, pair * PAIR : (pair + 1) * PAIR]
                if part < 2:
                    chunk = turn(chunk, cosine, sine)
                else:
                    vt_ref[pair * PAIR : (pair + 1) * PAIR, rows] = low(chunk.T)
                start = part * heads_width + pair * PAIR
                qkv_ref[rows, start : start + PAIR] = low(chunk)

        def one_pair(keys, pair):
            start = pl.multiple_of(pair * PAIR, PAIR)
            lanes = pl.ds(start, PAIR)
            key_lanes = pl.ds(pl.multiple_of(heads_width + start, PAIR), PAIR)
            query = qkv_ref[rows, lanes] * jnp.bfloat16(SCALING)
            key = qkv_ref[:keys, key_lanes]
            value_t = vt_ref[lanes, :keys]
            gathered = None
            for half in range(2):
                masked = jnp.where(head_lanes(query.shape, half, 1), query, jnp.bfloat16(0))
                scores = nt_dot(key, masked)
                highest = jnp.max(scores, axis=0, keepdims=True)
                expanded = jnp.exp(scores - highest)
                totals = jnp.sum(expanded, axis=0, keepdims=True)
                probs = low(expanded * (1.0 / totals))
                lse_ref[pl.ds(2 * pair + half, 1), rows] = highest + jnp.log(totals)
                found = nn_dot(value_t, probs)
                gathered = (
                    found
                    if half == 0
                    else jnp.where(head_lanes(found.shape, 1, 0), found, gathered)
                )
            mixed_ref[rows, lanes] = low(gathered.T)

        for static in range(blocks):

            @pl.when(block == static)
            def _():
                each(0, pairs, functools.partial(one_pair, (static + 1) * BLOCK))

        send_ref[block] = low(nt_dot(mixed_ref[rows, :], weight(3)))
        copy(block).start()

    def finish(block):
        rows = block_rows(block)
        copy(block).wait()
        mid = wide(hid_ref[rows, :]) + (wide(send_ref[block]) + wide(recv_ref[block]))
        mid_ref[rows, :] = mid
        s2 = low(mid * lax.rsqrt(mean_last(mid * mid) + EPSILON) * gain_two)
        s2_ref[rows, :] = s2
        tok = token_block(block)
        lane = lax.broadcasted_iota(jnp.int32, tok.shape, 1)
        logits = nn_dot(s2, small_ref[...]) + tok
        picked = [
            jnp.sum(
                jnp.where(wide(lane - ROUTER) == column(tok, ROUTE + member), logits, 0.0),
                axis=1,
                keepdims=True,
            )
            for member in range(2)
        ]
        gate = [
            1.0 / (1.0 + jnp.exp(picked[1 - member] - picked[member])) for member in range(2)
        ]
        tok = jnp.where(lane == GATE, gate[0], jnp.where(lane == GATE + 1, gate[1], tok))
        tok_ref[rows, :] = tok
        line_ref[:, rows] = tok.T[TARGET : TARGET + 8, :]

    each(0, blocks, compute)
    between()
    each(0, blocks, finish)


def forward_plain_kernel(
    hid_ref,
    tok_in_ref,
    block_ref,
    small_ref,
    rows_ref,
    table_ref,
    shard_ref,
    cot_own_ref,
    s1_ref,
    qkv_ref,
    lse_ref,
    mixed_ref,
    mid_ref,
    s2_ref,
    tok_ref,
    line_ref,
    expert_ref,
    cot_ref,
    vt_ref,
    send_ref,
    recv_ref,
    send_sem,
    recv_sem,
    wsend_sem,
    wrecv_sem,
    cot_sem,
):
    greet_group(2 * shard_ref.shape[0])
    own_rows = cot_own_ref.shape[0]
    heads_width = mixed_ref.shape[1]
    width = hid_ref.shape[1]
    mine = pl.ds(pl.multiple_of(lax.axis_index("tp") * own_rows, own_rows), own_rows)
    cot_copy = to_partner(cot_own_ref, cot_ref.at[mine], cot_sem.at[0], cot_sem.at[1])
    cot_copy.start()
    experts = CoreExchange(shard_ref, expert_ref, wsend_sem, wrecv_sem)
    experts.start()
    cot_ref[mine, :] = cot_own_ref[...]

    def weight(part):
        return block_ref[:, :, part * heads_width : (part + 1) * heads_width].reshape(
            width, heads_width
        )

    attend(
        hid_ref,
        lambda block: tok_in_ref[block_rows(block), :],
        weight,
        small_ref,
        (rows_ref[0:1, :], rows_ref[1:2, :]),
        table_ref,
        s1_ref,
        qkv_ref,
        lse_ref,
        mixed_ref,
        mid_ref,
        s2_ref,
        tok_ref,
        line_ref,
        vt_ref,
        send_ref,
        recv_ref,
        send_sem,
        recv_sem,
        lambda: None,
    )
    cot_copy.wait()
    experts.wait()


def forward_kernel(
    hid_own_ref,
    cot_own_ref,
    logit_ref,
    route_ref,
    rank_ref,
    drop_ref,
    gain_ref,
    router_ref,
    mixing_ref,
    value_ref,
    wqkv_ref,
    wout_ref,
    win_ref,
    wdown_ref,
    table_ref,
    all_out,
    small_ref,
    rows_ref,
    s1_out,
    qkv_out,
    lse_ref,
    mixed_out,
    mid_ref,
    s2_ref,
    tok_ref,
    line_ref,
    expert_ref,
    cot_out,
    all_ref,
    s1_ref,
    qkv_ref,
    mixed_ref,
    cot_ref,
    hid_ref,
    vt_ref,
    send_ref,
    recv_ref,
    shard_ref,
    stage_ref,
    small_all_ref,
    tok_all_ref,
    send_sem,
    recv_sem,
    wsend_sem,
    wrecv_sem,
    y_send,
    y_recv,
    up_send,
    up_recv,
    down_send,
    down_recv,
    x_send,
    x_recv,
    core_send,
    core_recv,
    store_sem,
):
    size, shard, _ = all_ref.shape
    planes = size // 4
    me = lax.axis_index("fsdp")
    tp = lax.axis_index("tp")
    z, x, core = me // 4, lax.rem(me // 2, 2), lax.rem(me, 2)
    own_rows, width = hid_own_ref.shape
    heads_width = wout_ref.shape[1]
    small_rows = shard // 2
    greet_group(size)
    partner = {"tp": 1 - tp}
    mine = pl.ds(pl.multiple_of(tp * own_rows, own_rows), own_rows)
    stage_ref[...] = jnp.zeros_like(stage_ref)
    stage_ref[0:2, :small_rows] = gain_ref[...]
    stage_ref[ROUTER:MIXING, :small_rows] = wide(router_ref[...])
    stage_ref[MIXING:VALUE, :small_rows] = wide(mixing_ref[...])
    stage_ref[VALUE : VALUE + 2, :small_rows] = wide(value_ref[...])
    small_all_ref[me, tp] = stage_ref[...].T[:small_rows, :]
    small_y = send_to(
        small_all_ref.at[me, tp], small_all_ref.at[me, tp], y_send.at[0], y_recv.at[0], partner
    )
    small_y.start()
    for part in range(3):
        all_ref[me, :, part * heads_width : (part + 1) * heads_width] = wqkv_ref[part]
    all_ref[me, :, 3 * heads_width :] = wout_ref[...]
    hid_y = send_to(hid_own_ref, hid_ref.at[mine], y_send.at[1], y_recv.at[1], partner)
    tok_y = send_to(tok_all_ref.at[tp], tok_all_ref.at[tp], y_send.at[2], y_recv.at[2], partner)
    cot_y = send_to(cot_own_ref, cot_ref.at[mine], y_send.at[3], y_recv.at[3], partner)
    experts = CoreExchange(shard_ref, expert_ref, wsend_sem, wrecv_sem)
    expert_count, _, hidden = wdown_ref.shape

    def stage_tokens():
        tok_all_ref[tp] = jnp.zeros(tok_all_ref.shape[1:], jnp.float32)
        routes = route_ref[...]
        kept = jnp.logical_and(routes < expert_count, drop_ref[...] == 0)
        target = jnp.where(kept, routes * (own_rows * 2 * 9 // 48) + rank_ref[...], -1)
        tok_all_ref[tp, ROUTER:MIXING, :] = logit_ref[...]
        tok_all_ref[tp, ROUTE : ROUTE + 2, :] = wide(routes)
        tok_all_ref[tp, TARGET : TARGET + 2, :] = wide(target)

    def stage_shard():
        def one(e):
            for part in range(2):
                shard_ref[e, :, part * hidden : (part + 1) * hidden] = win_ref[e, :, part, :]
            shard_ref[e, :, 2 * hidden :] = wdown_ref[e]

        each(0, expert_count, one)

    def number(plane, line):
        return plane * 4 + line * 2 + core

    def piece(kind, number_of, send, recv, slot, device):
        array = small_all_ref if kind else all_ref
        return send_to(
            array.at[number_of],
            array.at[number_of],
            send.at[kind, slot],
            recv.at[kind, slot],
            device,
        )

    def up(kind, step, plane):
        device = {"fsdp": number(lax.min(z + 1, planes - 1), x)}
        return piece(kind, number(plane, x), up_send, up_recv, step, device)

    def down(kind, step, plane):
        device = {"fsdp": number(lax.max(z - 1, 0), x)}
        return piece(kind, number(plane, x), down_send, down_recv, step, device)

    def side(kind, plane, line):
        device = {"fsdp": number(z, 1 - x)}
        return piece(kind, number(plane, line), x_send, x_recv, plane, device)

    def sibling(kind, plane, line, parity):
        return piece(
            kind,
            plane * 4 + line * 2 + parity,
            core_send,
            core_recv,
            plane * 2 + line,
            {"fsdp": me + 1 - 2 * core},
        )

    def launch(kind):
        @pl.when(z < planes - 1)
        def _():
            up(kind, 0, z).start()

        @pl.when(z > 0)
        def _():
            down(kind, 0, z).start()

        side(kind, z, x).start()
        sibling(kind, z, x, core).start()

    launch(0)
    hid_y.start()
    stage_tokens()
    tok_y.start()
    cot_y.start()
    hid_ref[mine, :] = hid_own_ref[...]
    cot_ref[mine, :] = cot_own_ref[...]
    small_y.wait()
    launch(1)
    stage_shard()
    for step in range(1, planes):
        for kind in range(2):

            @pl.when(z >= step)
            def _():
                up(kind, step - 1, z - step).wait_recv()

                @pl.when(z < planes - 1)
                def _():
                    up(kind, step, z - step).start()

                side(kind, z - step, x).start()
                sibling(kind, z - step, x, core).start()

            @pl.when(z + step < planes)
            def _():
                down(kind, step - 1, z + step).wait_recv()

                @pl.when(z > 0)
                def _():
                    down(kind, step, z + step).start()

                side(kind, z + step, x).start()
                sibling(kind, z + step, x, core).start()

    experts.start()
    for step in range(planes):
        for kind in range(2):

            @pl.when(z >= step)
            def _():
                side(kind, z - step, 1 - x).wait_recv()
                sibling(kind, z - step, 1 - x, core).start()

            if step > 0:

                @pl.when(z + step < planes)
                def _():
                    side(kind, z + step, 1 - x).wait_recv()
                    sibling(kind, z + step, 1 - x, core).start()

    for plane in range(planes):
        for line in range(2):
            for kind in range(2):
                sibling(kind, plane, line, 1 - core).wait_recv()
    small_all = small_all_ref[...].reshape(width, PAIR)
    small_ref[...] = low(small_all)
    rows_ref[...] = small_all.T[:8, :]
    tok_y.wait()
    hid_y.wait()

    def token_block(block):
        per = own_rows // BLOCK
        lanes = pl.ds(pl.multiple_of(lax.rem(block, per) * BLOCK, BLOCK), BLOCK)
        part = tok_all_ref[block // per, :, lanes]
        blank = jnp.zeros((PAIR - part.shape[0], BLOCK), jnp.float32)
        return jnp.concatenate([part, blank], axis=0).T

    def weight(part):
        return all_ref[:, :, part * heads_width : (part + 1) * heads_width].reshape(
            width, heads_width
        )

    stores = [
        pltpu.make_async_copy(source, target, store_sem.at[index])
        for index, (source, target) in enumerate(
            [
                (all_ref, all_out),
                (s1_ref, s1_out),
                (qkv_ref, qkv_out),
                (mixed_ref, mixed_out),
                (cot_ref, cot_out),
            ]
        )
    ]
    stores[0].start()

    def between():
        for store in stores[1:4]:
            store.start()
        cot_y.wait()
        stores[4].start()

    attend(
        hid_ref,
        token_block,
        weight,
        small_ref,
        (rows_ref[0:1, :], rows_ref[1:2, :]),
        table_ref,
        s1_ref,
        qkv_ref,
        lse_ref,
        mixed_ref,
        mid_ref,
        s2_ref,
        tok_ref,
        line_ref,
        vt_ref,
        send_ref,
        recv_ref,
        send_sem,
        recv_sem,
        between,
    )
    for kind in range(2):
        for step in range(planes):

            @pl.when(jnp.logical_and(z >= step, z < planes - 1))
            def _():
                up(kind, step, z - step).wait_send()

            @pl.when(jnp.logical_and(z + step < planes, z > 0))
            def _():
                down(kind, step, z + step).wait_send()

        for plane in range(planes):
            side(kind, plane, x).wait_send()
            for line in range(2):
                sibling(kind, plane, line, core).wait_send()
    for store in stores:
        store.wait()
    experts.wait()


def backward_kernel(
    res_ref,
    dx_ref,
    slot_ref,
    tok_ref,
    cot_ref,
    mid_hbm,
    s1_hbm,
    qkv_hbm,
    lse_ref,
    mixed_hbm,
    block_hbm,
    small_ref,
    rows_ref,
    table_ref,
    own_ref,
    egrad_ref,
    grad_ref,
    base_ref,
    other_ref,
    big_ref,
    arrived_ref,
    gsend_ref,
    grecv_ref,
    ssend_ref,
    srecv_ref,
    mid_ref,
    s1_ref,
    qkv_ref,
    mixed_ref,
    block_ref,
    hsend_ref,
    hrecv_ref,
    gmid_ref,
    gown_ref,
    kt_ref,
    gm_ref,
    dk_ref,
    dv_ref,
    gp_ref,
    att_ref,
    s2_ref,
    slope_ref,
    value_ref,
    acc_gain_ref,
    gsend_sem,
    grecv_sem,
    hsend_sem,
    hrecv_sem,
    esend_sem,
    erecv_sem,
    ssend_sem,
    srecv_sem,
    load_sem,
):
    loads = [
        pltpu.make_async_copy(source, target, load_sem.at[index])
        for index, (source, target) in enumerate(
            [
                (mid_hbm, mid_ref),
                (qkv_hbm, qkv_ref),
                (mixed_hbm, mixed_ref),
                (block_hbm, block_ref),
                (s1_hbm, s1_ref),
            ]
        )
    ]
    for load in loads:
        load.start()
    greet_group(2 * egrad_ref.shape[0])
    experts = CoreExchange(egrad_ref, arrived_ref, esend_sem, erecv_sem)
    tp = lax.axis_index("tp")
    width = dx_ref.shape[1]
    blocks = cot_ref.shape[0] // BLOCK
    heads_width = mixed_ref.shape[1]
    pairs = heads_width // PAIR
    gain_one = rows_ref[0:1, :]
    gain_two = rows_ref[1:2, :]
    slot_row = slot_ref[0:1, :]

    def weights(first_part, last_part):
        lanes = slice(first_part * heads_width, last_part * heads_width)
        return block_ref[:, :, lanes].reshape(width, (last_part - first_part) * heads_width)

    half_blocks = blocks // 2
    experts.start()

    def row_copy(block):
        return to_partner(
            gsend_ref.at[block], grecv_ref.at[block], gsend_sem.at[block], grecv_sem.at[block]
        )

    def share_copy(block):
        return to_partner(
            ssend_ref.at[block], srecv_ref.at[block], ssend_sem.at[block], srecv_sem.at[block]
        )

    def stream_copy(slot):
        return to_partner(
            hsend_ref.at[slot], hrecv_ref.at[slot], hsend_sem.at[slot], hrecv_sem.at[slot]
        )

    def slab_of(block):
        return block_rows(lax.rem(block, half_blocks))

    def backwards(body):
        each(0, blocks, lambda step: body(blocks - 1 - step))

    def send_rows(block):
        rows = block_rows(block)
        tok = tok_ref[rows, :]
        onehots = [low(jnp.where(column(tok, TARGET + m) == slot_row, 1.0, 0.0)) for m in range(2)]
        gsend_ref[block] = low(nn_dot(onehots[0] + onehots[1], dx_ref[...]))
        row_copy(block).start()
        placed = [nn_dot(onehot, res_ref[...]) for onehot in onehots]
        cot_wide = wide(cot_ref[rows, :])
        shares = [
            column(tok, GATE + m) * jnp.sum(placed[m] * cot_wide, axis=1, keepdims=True)
            for m in range(2)
        ]
        ssend_ref[block] = lane_matrix(tok.shape, [(0, shares[0]), (1, shares[1])]).T[:8, :]
        share_copy(block).start()
        mixture = column(tok, GATE) * placed[0] + column(tok, GATE + 1) * placed[1]

        @pl.when(tp == block // half_blocks)
        def _():
            base_ref[slab_of(block), :] = mixture

        @pl.when(tp != block // half_blocks)
        def _():
            other_ref[slab_of(block), :] = low(mixture)

    backwards(send_rows)
    for load in loads:
        load.wait()
    kt_ref[...] = qkv_ref[:, heads_width : 2 * heads_width].T
    dk_ref[...] = jnp.zeros_like(dk_ref)
    dv_ref[...] = jnp.zeros_like(dv_ref)
    acc_gain_ref[...] = jnp.zeros_like(acc_gain_ref)

    def main(block):
        rows = block_rows(block)
        mine = tp == block // half_blocks
        mine_f = jnp.where(mine, 1.0, 0.0)
        mid = mid_ref[rows, :]
        cot = cot_ref[rows, :]
        cot_wide = wide(cot)
        tok = tok_ref[rows, :]
        scale = lax.rsqrt(mean_last(mid * mid) + EPSILON)
        unit = mid * scale
        normed = unit * gain_two
        s2 = low(normed)
        small = small_ref[...]
        mixing = nn_dot(s2, small)
        value_dot = nn_dot(cot, small)
        normed_dot = jnp.sum(normed * cot_wide, axis=1, keepdims=True)
        route = [column(tok, ROUTE + member) for member in range(2)]
        gate = [column(tok, GATE + member) for member in range(2)]

        def weight_of(expert):
            return sum(jnp.where(route[m] == expert, gate[m], 0.0) for m in range(2))

        copy_weight = weight_of(COPY)
        copy_share = [jnp.where(route[m] == COPY, normed_dot, 0.0) for m in range(2)]
        alpha = copy_weight
        columns = []
        value_columns = []
        for c in range(2):
            weight = weight_of(COPY + 1 + c)
            left = column(mixing, MIXING + 2 * c)
            right = column(mixing, MIXING + 2 * c + 1)
            a0 = 1.0 / (1.0 + jnp.exp(right - left))
            a1 = 1.0 / (1.0 + jnp.exp(left - right))
            vd = column(value_dot, VALUE + c)
            alpha = alpha + weight * a0
            for m in range(2):
                copy_share[m] = copy_share[m] + jnp.where(
                    route[m] == COPY + 1 + c, a0 * normed_dot + a1 * vd, 0.0
                )
            slope = a0 * a1 * weight * (normed_dot - vd)
            columns.append((MIXING + 2 * c, slope))
            columns.append((MIXING + 2 * c + 1, -slope))
            value_columns.append((VALUE + c, weight * a1))
        value_matrix = lane_matrix(tok.shape, value_columns)
        base = mid + alpha * normed + nt_dot(low(value_matrix), small)

        @pl.when(mine)
        def _():
            base_ref[slab_of(block), :] += base

        row_copy(block).wait()
        share_copy(block).wait()
        extra = ssend_ref[block] + srecv_ref[block]
        extra = jnp.concatenate(
            [extra, jnp.zeros((PAIR - extra.shape[0], BLOCK), jnp.float32)], axis=0
        ).T
        share = [column(extra, m) + gate[m] * copy_share[m] for m in range(2)]
        lane = lax.broadcasted_iota(jnp.int32, tok.shape, 1)
        slopes = lane_matrix(tok.shape, columns)
        for m in range(2):
            local = share[m] - gate[m] * (share[0] + share[1])
            slopes = slopes + jnp.where(wide(lane - ROUTER) == route[m], local, 0.0)
        slopes_low = low(slopes)
        grad_normed = (
            wide(gsend_ref[block])
            + wide(grecv_ref[block])
            + alpha * cot_wide
            + nt_dot(slopes_low, small)
        )
        s2_ref[rows, :] = s2
        slope_ref[rows, :] = low(slopes * mine_f)
        value_ref[rows, :] = low(value_matrix * mine_f)
        gain_grad = jnp.sum(unit * grad_normed, axis=0, keepdims=True) * mine_f
        acc_gain_ref[...] += jnp.broadcast_to(gain_grad, acc_gain_ref.shape)
        scaled = grad_normed * gain_two
        grad_mid = cot_wide + scale * (scaled - unit * mean_last(scaled * unit))
        gmid_ref[rows, :] = grad_mid
        attended = low(grad_mid)
        att_ref[rows, :] = attended
        gm_ref[...] = low(nn_dot(attended, weights(3, 4)))
        cosine, sine = spread_table(table_ref[rows, :])

        def one_pair(keys, pair):
            start = pl.multiple_of(pair * PAIR, PAIR)
            lanes = pl.ds(start, PAIR)
            key_lanes = pl.ds(pl.multiple_of(heads_width + start, PAIR), PAIR)
            value_lanes = pl.ds(pl.multiple_of(2 * heads_width + start, PAIR), PAIR)
            query = qkv_ref[rows, lanes] * jnp.bfloat16(SCALING)
            key = qkv_ref[:keys, key_lanes]
            value = qkv_ref[:keys, value_lanes]
            grad_out = gm_ref[:, lanes]
            key_t = kt_ref[lanes, :keys]
            grad_value = None
            for half in range(2):
                keep = head_lanes(query.shape, half, 1)
                q_half = jnp.where(keep, query, jnp.bfloat16(0))
                g_half = jnp.where(keep, grad_out, jnp.bfloat16(0))
                probs = jnp.exp(nt_dot(key, q_half) - lse_ref[pl.ds(2 * pair + half, 1), rows])
                grad_probs = nt_dot(value, g_half)
                inner = jnp.sum(probs * grad_probs, axis=0, keepdims=True)
                grad_scores = low(probs * (grad_probs - inner))
                value_part = nn_dot(low(probs), g_half)
                key_part = nn_dot(grad_scores, q_half)
                query_part = nn_dot(key_t, grad_scores)
                if half == 0:
                    grad_value, grad_key, grad_query = value_part, key_part, query_part
                else:
                    grad_value = grad_value + value_part
                    grad_key = grad_key + key_part
                    grad_query = jnp.where(
                        head_lanes(query_part.shape, 1, 0), query_part, grad_query
                    )
            dv_ref[:keys, lanes] += grad_value
            dk_ref[:keys, lanes] += grad_key
            gp_ref[rows, lanes] = low(turn(grad_query.T * SCALING, cosine, -sine))
            gp_ref[rows, key_lanes] = low(turn(dk_ref[rows, lanes], cosine, -sine))
            gp_ref[rows, value_lanes] = low(dv_ref[rows, lanes])

        for static in range(blocks):

            @pl.when(block == static)
            def _():
                each(0, pairs, functools.partial(one_pair, (static + 1) * BLOCK))

        stream_grad = nt_dot(gp_ref[rows, :], weights(0, 3))
        slot = lax.rem(block, half_blocks)

        @pl.when(mine)
        def _():
            gown_ref[slot] = stream_grad

        @pl.when(jnp.logical_not(mine))
        def _():
            hsend_ref[slot] = low(stream_grad)
            stream_copy(slot).start()

    backwards(main)
    s1_turned = s1_ref[...].T
    for part in range(3):
        lanes = slice(part * heads_width, (part + 1) * heads_width)
        big_ref[:, lanes] = low(nn_dot(s1_turned, gp_ref[:, lanes]))
    big_ref[:, 3 * heads_width : 4 * heads_width] = low(tn_dot(att_ref[...], mixed_ref[...]))
    tall = jnp.where(
        lax.broadcasted_iota(jnp.int32, (PAIR, width), 0) == 1,
        jnp.broadcast_to(acc_gain_ref[0:1, :], (PAIR, width)),
        0.0,
    )
    big_ref[:, 4 * heads_width :] = low(
        tn_dot(s2_ref[...], slope_ref[...]) + tn_dot(cot_ref[...], value_ref[...]) + tall.T
    )
    for slot in reversed(range(half_blocks)):
        slab = slice(slot * BLOCK, (slot + 1) * BLOCK)
        stream_copy(slot).wait()
        source = wide(own_ref[slab, :])
        scale = lax.rsqrt(mean_last(source * source) + EPSILON)
        unit = source * scale
        scaled = (gown_ref[slot] + wide(hrecv_ref[slot])) * gain_one
        mid_rows = block_rows(tp * half_blocks + slot)
        grad_ref[slab, :] = gmid_ref[mid_rows, :] + scale * (
            scaled - unit * mean_last(scaled * unit)
        )
    experts.wait()


def forward_results(length, width, heads_width, shard):
    low_t, wide_t = jnp.bfloat16, jnp.float32
    return [
        jax.ShapeDtypeStruct((length, width), low_t),
        jax.ShapeDtypeStruct((length, 3 * heads_width), low_t),
        jax.ShapeDtypeStruct((8, length), wide_t),
        jax.ShapeDtypeStruct((length, heads_width), low_t),
        jax.ShapeDtypeStruct((length, width), wide_t),
        jax.ShapeDtypeStruct((length, width), low_t),
        jax.ShapeDtypeStruct((length, PAIR), wide_t),
        jax.ShapeDtypeStruct((8, length), wide_t),
        jax.ShapeDtypeStruct(shard, low_t),
        jax.ShapeDtypeStruct((length, width), low_t),
    ]


def attend_scratch(length, width, heads_width):
    blocks = length // BLOCK
    return [
        pltpu.VMEM((heads_width, length), jnp.bfloat16),
        pltpu.VMEM((blocks, BLOCK, width), jnp.bfloat16),
        pltpu.VMEM((blocks, BLOCK, width), jnp.bfloat16),
    ]


def run_forward_plain(hid, tok, blocks, small, rows, table, shard, cot):
    length, width = hid.shape
    heads_width = blocks.shape[2] // 4
    vmem = pl.BlockSpec(memory_space=pltpu.VMEM)
    dma = pltpu.SemaphoreType.DMA
    count = length // BLOCK
    return pl.pallas_call(
        forward_plain_kernel,
        in_specs=[vmem] * 8,
        out_specs=[vmem] * 10,
        out_shape=forward_results(length, width, heads_width, shard.shape),
        scratch_shapes=attend_scratch(length, width, heads_width)
        + [dma((count,)), dma((count,)), dma((shard.shape[0],)), dma((shard.shape[0],)), dma((2,))],
        compiler_params=pltpu.CompilerParams(
            collective_id=0, has_side_effects=True, vmem_limit_bytes=60 << 20
        ),
    )(hid, tok, blocks, small, rows, table, shard, cot)


def run_forward(*operands):
    hid, wout, wdown, table = operands[0], operands[11], operands[13], operands[14]
    own_rows, width = hid.shape
    length = table.shape[0]
    shard, heads_width = wout.shape
    experts, _, hidden = wdown.shape
    size = lax.axis_size("fsdp")
    count = length // BLOCK
    hbm = pl.BlockSpec(memory_space=pl.ANY)
    vmem = pl.BlockSpec(memory_space=pltpu.VMEM)
    low_t, wide_t = jnp.bfloat16, jnp.float32
    dma = pltpu.SemaphoreType.DMA
    return pl.pallas_call(
        forward_kernel,
        in_specs=[vmem] * 15,
        out_specs=[hbm, vmem, vmem, hbm, hbm, vmem, hbm]
        + [vmem] * 4
        + [hbm, hbm],
        out_shape=[
            jax.ShapeDtypeStruct((size, shard, 4 * heads_width), low_t),
            jax.ShapeDtypeStruct((width, PAIR), low_t),
            jax.ShapeDtypeStruct((8, width), wide_t),
        ]
        + forward_results(length, width, heads_width, (experts, shard, 3 * hidden)),
        scratch_shapes=[
            pltpu.VMEM((size, shard, 4 * heads_width), low_t),
            pltpu.VMEM((length, width), low_t),
            pltpu.VMEM((length, 3 * heads_width), low_t),
            pltpu.VMEM((length, heads_width), low_t),
            pltpu.VMEM((length, width), low_t),
            pltpu.VMEM((length, width), low_t),
        ]
        + attend_scratch(length, width, heads_width)
        + [
            pltpu.VMEM((experts, shard, 3 * hidden), low_t),
            pltpu.VMEM((PAIR, PAIR), wide_t),
            pltpu.VMEM((size, 2, shard // 2, PAIR), wide_t),
            pltpu.VMEM((2, 32, own_rows), wide_t),
            dma((count,)),
            dma((count,)),
            dma((experts,)),
            dma((experts,)),
            dma((4,)),
            dma((4,)),
        ]
        + [dma((2, size // 4))] * 6
        + [dma((2, size // 2))] * 2
        + [dma((5,))],
        compiler_params=pltpu.CompilerParams(
            collective_id=3, has_side_effects=True, vmem_limit_bytes=60 << 20
        ),
    )(*operands)


def run_backward(*operands):
    cot, mid, s1, qkv, mixed, blocks, own, egrads = (
        operands[index] for index in (4, 5, 6, 7, 9, 10, 14, 15)
    )
    length, width = cot.shape
    heads_width = mixed.shape[1]
    count = length // BLOCK
    own_rows = own.shape[0]
    vmem = pl.BlockSpec(memory_space=pltpu.VMEM)
    hbm = pl.BlockSpec(memory_space=pl.ANY)
    low_t, wide_t = jnp.bfloat16, jnp.float32
    dma = pltpu.SemaphoreType.DMA
    return pl.pallas_call(
        backward_kernel,
        in_specs=[vmem] * 5
        + [hbm] * 3
        + [vmem]
        + [hbm] * 2
        + [vmem] * 4
        + [hbm],
        out_specs=[vmem] * 4 + [hbm],
        out_shape=[
            jax.ShapeDtypeStruct((own_rows, width), wide_t),
            jax.ShapeDtypeStruct((own_rows, width), wide_t),
            jax.ShapeDtypeStruct((own_rows, width), low_t),
            jax.ShapeDtypeStruct((width, 4 * heads_width + PAIR), low_t),
            jax.ShapeDtypeStruct(egrads.shape, low_t),
        ],
        scratch_shapes=[
            pltpu.VMEM((count, BLOCK, width), low_t),
            pltpu.VMEM((count, BLOCK, width), low_t),
            pltpu.VMEM((count, 8, BLOCK), wide_t),
            pltpu.VMEM((count, 8, BLOCK), wide_t),
            pltpu.VMEM(mid.shape, wide_t),
            pltpu.VMEM(s1.shape, low_t),
            pltpu.VMEM(qkv.shape, low_t),
            pltpu.VMEM(mixed.shape, low_t),
            pltpu.VMEM(blocks.shape, low_t),
            pltpu.VMEM((2, BLOCK, width), low_t),
            pltpu.VMEM((2, BLOCK, width), low_t),
            pltpu.VMEM((length, width), wide_t),
            pltpu.VMEM((2, BLOCK, width), wide_t),
            pltpu.VMEM((heads_width, length), low_t),
            pltpu.VMEM((BLOCK, heads_width), low_t),
            pltpu.VMEM((length, heads_width), wide_t),
            pltpu.VMEM((length, heads_width), wide_t),
            pltpu.VMEM((length, 3 * heads_width), low_t),
            pltpu.VMEM((length, width), low_t),
            pltpu.VMEM((length, width), low_t),
            pltpu.VMEM((length, PAIR), low_t),
            pltpu.VMEM((length, PAIR), low_t),
            pltpu.VMEM((8, width), wide_t),
            dma((count,)),
            dma((count,)),
            dma((2,)),
            dma((2,)),
            dma((egrads.shape[0],)),
            dma((egrads.shape[0],)),
            dma((count,)),
            dma((count,)),
            dma((5,)),
        ],
        compiler_params=pltpu.CompilerParams(
            collective_id=1, has_side_effects=True, vmem_limit_bytes=60 << 20
        ),
    )(*operands)


def shards(
    hidden,
    prev_logits,
    routes,
    slot_rank,
    dropped,
    cotangent,
    attn_norm,
    ffn_norm,
    w_qkv,
    w_attn_out,
    w_router,
    w_const_gate,
    w_const_value,
    w_expert_in,
    w_expert_out,
):
    own_rows, width = hidden.shape
    length = own_rows * lax.axis_size("tp")
    experts = w_expert_in.shape[0]
    route_count = w_router.shape[1]
    capacity = 9 * length // (4 * route_count)
    planned = lax.axis_size("fsdp") == 16
    table = jnp.asarray(rotary_table(length))
    gains = jnp.stack([wide(attn_norm), wide(ffn_norm)], axis=0)
    wqkv = w_qkv.transpose(1, 0, 2)
    operands = (
        hidden,
        cotangent,
        prev_logits.T,
        routes.T,
        slot_rank.T,
        dropped.T,
        gains,
        w_router.T,
        w_const_gate.T,
        w_const_value.T,
        wqkv,
        w_attn_out,
        w_expert_in,
        w_expert_out,
    )
    if planned:
        forward = run_forward(*operands, table)
    else:
        forward = forward_plain(operands, table)
    blocks, small, rows, s1, qkv, lse, mixed, mid, s2, tok, lines, gathered, cot = forward
    expert_weights = join_weights(gathered, experts)
    peers = 2 * experts
    half = capacity // 2
    block = half // 2
    place = jnp.arange(peers * block)
    owner = (lax.axis_index("fsdp") % peers) ^ (place // block)
    slot = wide(
        (owner // 2) * capacity
        + lax.axis_index("tp") * half
        + (owner % 2) * block
        + place % block
    )
    results, grad_rows, grads_exp = run_expert(
        s2, cot, lines, jnp.broadcast_to(slot[:, None], (slot.shape[0], PAIR)), expert_weights
    )
    grad_hidden, base, for_other, big, arrived = run_backward(
        results.reshape(-1, width),
        grad_rows.reshape(-1, width),
        jnp.broadcast_to(slot[None, :], (8, slot.shape[0])),
        tok,
        cot,
        mid,
        s1,
        qkv,
        lse,
        mixed,
        blocks,
        small,
        rows,
        table,
        hidden,
        split_grads(grads_exp),
    )
    received, red, last = (run_finish if planned else finish_plain)(big, wqkv, for_other)
    output, grad_hidden, grad_qkv, grad_attn_out, gain_grads, grad_router, grad_mixing, grad_value, grad_in, grad_out = run_write(
        base, received, grad_hidden, red, last, gains, arrived
    )
    return (
        output,
        grad_hidden,
        gain_grads[0],
        gain_grads[1],
        grad_qkv.transpose(1, 0, 2),
        grad_attn_out,
        grad_router.T,
        grad_mixing.T,
        grad_value.T,
        grad_in,
        grad_out,
    )


def solution(mesh):
    in_specs = (
        P(("fsdp", "tp"), None),
        P(("fsdp", "tp"), None),
        P(("fsdp", "tp"), None),
        P(("fsdp", "tp"), None),
        P(("fsdp", "tp"), None),
        P(("fsdp", "tp"), None),
        P(("fsdp", "tp")),
        P(("fsdp", "tp")),
        P("fsdp", None, "tp"),
        P("fsdp", "tp"),
        P(("fsdp", "tp"), None),
        P(("fsdp", "tp"), None),
        P(("fsdp", "tp"), None),
        P(None, "fsdp", None, "tp"),
        P(None, "fsdp", "tp"),
    )
    out_specs = (
        P(("fsdp", "tp"), None),
        P(("fsdp", "tp"), None),
        P(("fsdp", "tp")),
        P(("fsdp", "tp")),
        P("fsdp", None, "tp"),
        P("fsdp", "tp"),
        P(("fsdp", "tp"), None),
        P(("fsdp", "tp"), None),
        P(("fsdp", "tp"), None),
        P(None, "fsdp", None, "tp"),
        P(None, "fsdp", "tp"),
    )
    return jax.shard_map(shards, mesh=mesh, in_specs=in_specs, out_specs=out_specs, check_vma=False)
```

```python
import functools

import jax
import jax.numpy as jnp
import numpy as np
from jax import lax
from jax.experimental import pallas as pl
from jax.experimental.pallas import tpu as pltpu
from jax.sharding import PartitionSpec as P

HD = 64
BLOCK = 256


EPSILON = 1e-06
MESH = pl.DeviceIdType.MESH
PAIR = 2 * HD
SCALING = HD ** (-0.5)
ROUTER = 2
MIXING = 14
VALUE = 18
ROUTE = 20
TARGET = 24
GATE = 26
COPY = 9


TILE = 256


def swap(values):
    return lax.ppermute(values, "tp", [(0, 1), (1, 0)])


def gather_rows(values):
    other = swap(values)
    first = lax.axis_index("tp") == 0
    return jnp.concatenate(
        [jnp.where(first, values, other), jnp.where(first, other, values)], axis=0
    )


def own_half(values):
    half = values.shape[0] // 2
    return lax.dynamic_slice_in_dim(values, lax.axis_index("tp") * half, half, 0)


def other_half(values):
    half = values.shape[0] // 2
    return lax.dynamic_slice_in_dim(values, (1 - lax.axis_index("tp")) * half, half, 0)


def member_groups(size, experts):
    span = 2 * experts
    starts = range(0, size, span)
    cores = [[start + 2 * e, start + 2 * e + 1] for start in starts for e in range(experts)]
    across = [[start + r for start in starts] for r in range(span)]
    return cores, across


def own_core(values, rows):
    parts = values.reshape(-1, 2, rows, values.shape[-1])
    return lax.dynamic_index_in_dim(parts, lax.axis_index("fsdp") % 2, 1, keepdims=False)


def join_weights(got, experts):
    size = lax.axis_size("fsdp")
    if size == 2 * experts:
        return got
    cores, across = member_groups(size, experts)
    got = lax.all_gather(got, "fsdp", axis=1, axis_index_groups=cores, tiled=True)
    got = got.reshape(-1, got.shape[-1])
    got = lax.all_gather(got, "fsdp", axis=0, axis_index_groups=across, tiled=True)
    return own_core(got, got.shape[0] // (2 * experts))


def split_grads(grads):
    experts, _, columns = grads.shape
    size = lax.axis_size("fsdp")
    if size == 2 * experts:
        return grads
    cores, across = member_groups(size, experts)
    grads = lax.all_gather(grads[:, None], "fsdp", axis=1, axis_index_groups=cores, tiled=True)
    grads = grads.reshape(-1, columns)
    grads = lax.psum_scatter(
        grads, "fsdp", scatter_dimension=0, axis_index_groups=across, tiled=True
    )
    return own_core(grads, grads.shape[0] // (2 * experts))


def finish_plain(big, wqkv, other):
    heads_width = (big.shape[1] - PAIR) // 4
    reduced = wide(lax.psum_scatter(big, "fsdp", scatter_dimension=0, tiled=True))
    parts = reduced[:, : 3 * heads_width].reshape(-1, 3, heads_width).transpose(1, 0, 2)
    share = jnp.sum(parts * wide(wqkv), axis=(0, 2))
    last = jnp.concatenate([share[:, None], reduced[:, 4 * heads_width + 1 :]], axis=1)
    return (
        swap(other),
        reduced[:, : 4 * heads_width],
        own_half(last) + swap(other_half(last)),
    )


def forward_plain(operands, table):
    (
        hidden,
        cotangent,
        logits,
        routes,
        rank,
        dropped,
        gains,
        router,
        mixing,
        value,
        wqkv,
        wout,
        w_in,
        w_down,
    ) = operands
    own_rows, width = hidden.shape
    experts, shard, units = w_down.shape
    small = jnp.concatenate([wide(v) for v in (gains, router, mixing, value)], axis=0)
    small = jnp.pad(small, ((0, PAIR - small.shape[0]), (0, 0))).T
    small = lax.all_gather(small, ("fsdp", "tp"), axis=0, tiled=True)
    capacity = own_rows * 2 * 9 // 48
    kept = (routes < experts) & (dropped == 0)
    target = jnp.where(kept, routes * capacity + rank, -1)
    blank = jnp.zeros((2, own_rows), jnp.float32)
    tok = jnp.concatenate(
        [blank, logits, blank, blank, blank, wide(routes), blank, wide(target)], axis=0
    )
    tok = lax.all_gather(tok, "tp", axis=1, tiled=True).T
    tok = jnp.pad(tok, ((0, 0), (0, PAIR - tok.shape[1])))
    blocks = jnp.concatenate([wqkv[0], wqkv[1], wqkv[2], wout], axis=1)
    blocks = lax.all_gather(blocks, "fsdp", axis=0, tiled=True).reshape(2 * experts, -1, blocks.shape[1])
    rows = small.T[:8]
    small = low(small)
    shards_flat = jnp.concatenate([w_in.reshape(experts, shard, 2 * units), w_down], axis=2)
    return (blocks, small, rows) + tuple(
        run_forward_plain(
            gather_rows(hidden), tok, blocks, small, rows, table, shards_flat, cotangent
        )
    )


def nt_dot(left, right):
    return lax.dot_general(left, right, (((1,), (1,)), ((), ())), preferred_element_type=jnp.float32)


def nn_dot(left, right):
    return jnp.dot(left, right, preferred_element_type=jnp.float32)


def tn_dot(left, right):
    return lax.dot_general(left, right, (((0,), (0,)), ((), ())), preferred_element_type=jnp.float32)


def low(values):
    return values.astype(jnp.bfloat16)


def wide(values):
    return values.astype(jnp.float32)


def rotary_table(length):
    half = HD // 2
    positions = np.arange(length, dtype=np.float32)
    inverse = np.power(np.float32(10000.0), -np.arange(half, dtype=np.float32) / np.float32(half))
    angles = (positions[:, None] * inverse[None, :].astype(np.float32)).astype(np.float32)
    cosine = np.cos(angles.astype(np.float64)).astype(np.float32)
    sine = np.sin(angles.astype(np.float64)).astype(np.float32)
    both = np.concatenate([cosine, sine], axis=1)
    return np.concatenate([both[: length // 2], both[length // 2 :]], axis=1)


def spread_table(table_ref, block):
    quarter = HD // 2
    blocks = table_ref.shape[0] // BLOCK
    table = table_ref[block_rows(lax.rem(block, blocks)), :]
    table = jnp.where(block >= blocks, pltpu.roll(table, HD, 1), table)
    lane = lax.broadcasted_iota(jnp.int32, table.shape, 1)
    cosine = jnp.where(lane < quarter, table, 0.0)
    cosine = cosine + pltpu.roll(cosine, quarter, 1)
    sine = jnp.where(jnp.logical_and(lane >= quarter, lane < HD), table, 0.0)
    sine = sine - pltpu.roll(sine, PAIR - quarter, 1)
    return cosine + pltpu.roll(cosine, HD, 1), sine + pltpu.roll(sine, HD, 1)


def turn(values, cosine, sine):
    lane = lax.broadcasted_iota(jnp.int32, values.shape, 1)
    upper = lax.rem(lane, HD) >= HD // 2
    partner = jnp.where(
        upper, pltpu.roll(values, HD // 2, 1), pltpu.roll(values, PAIR - HD // 2, 1)
    )
    return values * cosine + partner * sine


def head_lanes(shape, half, axis):
    return (lax.broadcasted_iota(jnp.int32, shape, axis) >= HD) == bool(half)


def mean_last(values):
    return jnp.mean(values, axis=-1, keepdims=True)


def to_partner(source, target, send_sem, recv_sem):
    return pltpu.make_async_remote_copy(
        src_ref=source,
        dst_ref=target,
        send_sem=send_sem,
        recv_sem=recv_sem,
        device_id={"tp": 1 - lax.axis_index("tp")},
        device_id_type=MESH,
    )


def block_rows(block):
    return pl.ds(pl.multiple_of(block * BLOCK, BLOCK), BLOCK)


def column(values, index):
    return values[:, index : index + 1]


def lane_matrix(shape, columns):
    lane = lax.broadcasted_iota(jnp.int32, shape, 1)
    total = jnp.zeros(shape, jnp.float32)
    for index, values in columns:
        total = jnp.where(lane == index, values, total)
    return total


def send_to(source, target, send_sem, recv_sem, device):
    return pltpu.make_async_remote_copy(
        src_ref=source,
        dst_ref=target,
        send_sem=send_sem,
        recv_sem=recv_sem,
        device_id=device,
        device_id_type=MESH,
    )


def greet_group(peers):
    me = lax.axis_index("fsdp")
    rank = lax.rem(me, peers)
    barrier = pltpu.get_barrier_semaphore()
    for k in range(1, peers):
        pl.semaphore_signal(
            barrier,
            inc=1,
            device_id={"fsdp": me - rank + lax.rem(rank + k, peers)},
            device_id_type=MESH,
        )
    pl.semaphore_signal(
        barrier, inc=1, device_id={"tp": 1 - lax.axis_index("tp")}, device_id_type=MESH
    )
    pl.semaphore_wait(barrier, peers)


def each(first, last, body):
    def step(k, carry):
        body(k)
        return carry

    lax.fori_loop(first, last, step, 0)


def flipped(value, k, bits):
    other = 0
    bit = 1
    while bit < bits:
        ours, theirs = lax.rem(value // bit, 2), lax.rem(k // bit, 2)
        other = other + bit * (ours + theirs - 2 * ours * theirs)
        bit *= 2
    return other


class CoreExchange:
    def __init__(self, source, target, send_sem, recv_sem):
        experts = source.shape[0]
        me = lax.axis_index("fsdp")
        rank = lax.rem(me, 2 * experts)
        core = lax.rem(rank, 2)
        mine = rank // 2

        def device(k):
            return {"fsdp": me - rank + 2 * flipped(mine, k, experts) + core}

        def copy(k):
            there = flipped(mine, k, experts)
            return send_to(
                source.at[there], target.at[mine], send_sem.at[k], recv_sem.at[k], device(k)
            )

        def arrival(k):
            there = flipped(mine, k, experts)
            return send_to(
                source.at[there], target.at[there], send_sem.at[k], recv_sem.at[k], device(k)
            )

        self.experts, self.copy, self.arrival = experts, copy, arrival
        self.local = pltpu.make_async_copy(source.at[mine], target.at[mine], send_sem.at[0])

    def start(self):
        self.local.start()
        each(1, self.experts, lambda k: self.copy(k).start())

    def wait(self):
        each(1, self.experts, lambda k: self.copy(k).wait_send())
        each(1, self.experts, lambda k: self.arrival(k).wait_recv())
        self.local.wait()


def finish_kernel(
    big_ref,
    wqkv_ref,
    other_ref,
    y_ref,
    red_ref,
    tail_ref,
    sum_ref,
    core_ref,
    side_ref,
    acc_ref,
    usend_ref,
    urecv_ref,
    dsend_ref,
    drecv_ref,
    tsend_ref,
    trecv_ref,
    core_send,
    core_recv,
    x_send,
    x_recv,
    up_send,
    up_recv,
    dn_send,
    dn_recv,
    y_send,
    y_recv,
):
    size = big_ref.shape[0]
    planes = size // 4
    me = lax.axis_index("fsdp")
    tp = lax.axis_index("tp")
    z, x, core = me // 4, lax.rem(me // 2, 2), lax.rem(me, 2)
    heads_width = wqkv_ref.shape[2]
    greet_group(size)
    partner = {"tp": 1 - tp}

    def to_core(plane, line):
        slot = plane * 2 + line
        return send_to(
            big_ref.at[plane * 4 + line * 2 + 1 - core],
            core_ref.at[slot],
            core_send.at[slot],
            core_recv.at[slot],
            {"fsdp": me + 1 - 2 * core},
        )

    def to_side(plane):
        return send_to(
            sum_ref.at[plane],
            side_ref.at[plane],
            x_send.at[plane],
            x_recv.at[plane],
            {"fsdp": z * 4 + (1 - x) * 2 + core},
        )

    def to_up(plane):
        return send_to(
            usend_ref.at[plane],
            urecv_ref.at[plane],
            up_send.at[plane],
            up_recv.at[plane],
            {"fsdp": lax.min(z + 1, planes - 1) * 4 + x * 2 + core},
        )

    def to_down(plane):
        return send_to(
            dsend_ref.at[plane],
            drecv_ref.at[plane],
            dn_send.at[plane],
            dn_recv.at[plane],
            {"fsdp": lax.max(z - 1, 0) * 4 + x * 2 + core},
        )

    lower = z < planes // 2
    order = [jnp.where(lower, planes - 1 - step, step) for step in range(planes)]
    for plane in order:
        to_core(plane, 1 - x).start()
    for plane in order:
        to_core(plane, x).start()
    out_y = send_to(other_ref, y_ref, y_send.at[0], y_recv.at[0], partner)
    out_y.start()

    def joined(plane, line):
        to_core(plane, line).wait_recv()
        return wide(big_ref[plane * 4 + line * 2 + core]) + wide(core_ref[plane * 2 + line])

    for plane in order:
        sum_ref[plane] = low(joined(plane, 1 - x))
        to_side(plane).start()
    for plane in order:
        acc_ref[plane] = joined(plane, x)

    def rise(plane):
        @pl.when(z < plane)
        def _():
            @pl.when(z > 0)
            def _():
                to_up(plane).wait_recv()
                acc_ref[plane] += wide(urecv_ref[plane])

            usend_ref[plane] = low(acc_ref[plane])
            to_up(plane).start()

    def fall(plane):
        @pl.when(z > plane)
        def _():
            @pl.when(z < planes - 1)
            def _():
                to_down(plane).wait_recv()
                acc_ref[plane] += wide(drecv_ref[plane])

            dsend_ref[plane] = low(acc_ref[plane])
            to_down(plane).start()

    for step, plane in enumerate(order):
        to_side(plane).wait_recv()
        acc_ref[plane] += wide(side_ref[plane])
        last_step = step == planes - 1

        @pl.when(lower)
        def _():
            (fall if last_step else rise)(plane)

        @pl.when(jnp.logical_not(lower))
        def _():
            (rise if last_step else fall)(plane)

    @pl.when(z > 0)
    def _():
        to_up(z).wait_recv()
        acc_ref[z] += wide(urecv_ref[z])

    @pl.when(z < planes - 1)
    def _():
        to_down(z).wait_recv()
        acc_ref[z] += wide(drecv_ref[z])

    values = acc_ref[z]
    red_ref[...] = values[:, : 4 * heads_width]
    share = sum(
        jnp.sum(
            values[:, part * heads_width : (part + 1) * heads_width] * wide(wqkv_ref[part]),
            axis=1,
            keepdims=True,
        )
        for part in range(3)
    )
    last = values[:, 4 * heads_width :]
    last = jnp.where(lax.broadcasted_iota(jnp.int32, last.shape, 1) == 0, share, last)
    part_rows = tail_ref.shape[0]
    tsend_ref[0] = last[:part_rows, :]
    tsend_ref[1] = last[part_rows:, :]
    tail_y = send_to(tsend_ref.at[1 - tp], trecv_ref, y_send.at[1], y_recv.at[1], partner)
    tail_y.start()
    out_y.wait()
    tail_y.wait()
    tail_ref[...] = tsend_ref[tp] + trecv_ref[...]
    for plane in range(planes):
        to_core(plane, 1 - x).wait_send()
        to_core(plane, x).wait_send()
        to_side(plane).wait_send()

        @pl.when(z < plane)
        def _():
            to_up(plane).wait_send()

        @pl.when(z > plane)
        def _():
            to_down(plane).wait_send()


def run_finish(big, wqkv, other):
    size = lax.axis_size("fsdp")
    planes = size // 4
    own_rows, width = other.shape
    columns = big.shape[1]
    shard = width // size
    vmem = pl.BlockSpec(memory_space=pltpu.VMEM)
    low_t, wide_t = jnp.bfloat16, jnp.float32
    dma = pltpu.SemaphoreType.DMA
    line = (planes, shard, columns)
    return pl.pallas_call(
        finish_kernel,
        in_specs=[vmem] * 3,
        out_specs=[vmem] * 3,
        out_shape=[
            jax.ShapeDtypeStruct((own_rows, width), low_t),
            jax.ShapeDtypeStruct((shard, columns - PAIR), wide_t),
            jax.ShapeDtypeStruct((shard // 2, PAIR), wide_t),
        ],
        scratch_shapes=[
            pltpu.VMEM(line, low_t),
            pltpu.VMEM((2 * planes, shard, columns), low_t),
            pltpu.VMEM(line, low_t),
            pltpu.VMEM(line, wide_t),
            pltpu.VMEM(line, low_t),
            pltpu.VMEM(line, low_t),
            pltpu.VMEM(line, low_t),
            pltpu.VMEM(line, low_t),
            pltpu.VMEM((2, shard // 2, PAIR), wide_t),
            pltpu.VMEM((shard // 2, PAIR), wide_t),
            dma((2 * planes,)),
            dma((2 * planes,)),
        ]
        + [dma((planes,))] * 6
        + [dma((2,))] * 2,
        compiler_params=pltpu.CompilerParams(
            collective_id=4, has_side_effects=True, vmem_limit_bytes=60 << 20
        ),
    )(big.reshape(size, shard, columns), wqkv, other)


def write_kernel(
    base_ref,
    y_ref,
    grad_ref,
    red_ref,
    tail_ref,
    gain_ref,
    expert_ref,
    out_ref,
    hidden_ref,
    qkv_ref,
    attn_ref,
    gains_ref,
    router_ref,
    mixing_ref,
    value_ref,
    in_ref,
    down_ref,
):
    hidden = down_ref.shape[2]
    heads_width = attn_ref.shape[1]
    out_ref[...] = low(base_ref[...] + wide(y_ref[...]))
    hidden_ref[...] = grad_ref[...]
    values = wide(expert_ref[0])
    in_ref[0, :, 0, :] = values[:, :hidden]
    in_ref[0, :, 1, :] = values[:, hidden : 2 * hidden]
    down_ref[0] = values[:, 2 * hidden :]

    @pl.when(pl.program_id(0) == 0)
    def _():
        for part in range(3):
            qkv_ref[part] = red_ref[:, part * heads_width : (part + 1) * heads_width]
        attn_ref[...] = red_ref[:, 3 * heads_width :]
        count = tail_ref.shape[0]
        blank = jnp.zeros((PAIR - count, PAIR), jnp.float32)
        turned = jnp.concatenate([tail_ref[...], blank], axis=0).T[:, :count]
        gains_ref[0:1, :] = turned[0:1, :] / gain_ref[0:1, :]
        gains_ref[1:2, :] = turned[1:2, :]
        router_ref[...] = turned[ROUTER:MIXING, :]
        mixing_ref[...] = turned[MIXING:VALUE, :]
        value_ref[...] = turned[VALUE : VALUE + 2, :]


def run_write(base, y, grad_hidden, red, tail, gains, arrived):
    own_rows, width = base.shape
    shard = red.shape[0]
    heads_width = red.shape[1] // 4
    count = tail.shape[0]
    experts, _, total = arrived.shape
    hidden = total // 3
    wide_t = jnp.float32
    rows = pl.BlockSpec((own_rows // experts, width), lambda e: (e, 0))

    def whole(shape):
        return pl.BlockSpec(shape, lambda e: (0,) * len(shape))

    return pl.pallas_call(
        write_kernel,
        grid=(experts,),
        in_specs=[
            rows,
            rows,
            rows,
            whole(red.shape),
            whole(tail.shape),
            whole(gains.shape),
            pl.BlockSpec((1, shard, total), lambda e: (e, 0, 0)),
        ],
        out_specs=[
            rows,
            rows,
            whole((3, shard, heads_width)),
            whole((shard, heads_width)),
            whole((2, count)),
            whole((MIXING - ROUTER, count)),
            whole((VALUE - MIXING, count)),
            whole((2, count)),
            pl.BlockSpec((1, shard, 2, hidden), lambda e: (e, 0, 0, 0)),
            pl.BlockSpec((1, shard, hidden), lambda e: (e, 0, 0)),
        ],
        out_shape=[
            jax.ShapeDtypeStruct((own_rows, width), jnp.bfloat16),
            jax.ShapeDtypeStruct((own_rows, width), wide_t),
            jax.ShapeDtypeStruct((3, shard, heads_width), wide_t),
            jax.ShapeDtypeStruct((shard, heads_width), wide_t),
            jax.ShapeDtypeStruct((2, count), wide_t),
            jax.ShapeDtypeStruct((MIXING - ROUTER, count), wide_t),
            jax.ShapeDtypeStruct((VALUE - MIXING, count), wide_t),
            jax.ShapeDtypeStruct((2, count), wide_t),
            jax.ShapeDtypeStruct((experts, shard, 2, hidden), wide_t),
            jax.ShapeDtypeStruct((experts, shard, hidden), wide_t),
        ],
    )(base, y, grad_hidden, red, tail, gains, arrived)


def expert_kernel(
    s2_ref,
    cot_ref,
    line_ref,
    slot_ref,
    weight_ref,
    res_out_ref,
    dx_out_ref,
    grads_out_ref,
    xs_ref,
    gs_ref,
    x_ref,
    g_ref,
    w_ref,
    gate_ref,
    up_ref,
    act_ref,
    xt_ref,
    gt_ref,
    acc_ref,
    grads_ref,
    sibling_ref,
    ysend_ref,
    yrecv_ref,
    w_sem,
    grad_sem,
    xs_sem,
    xr_sem,
    gs_sem,
    gr_sem,
    xfs_sem,
    xfr_sem,
    gfs_sem,
    gfr_sem,
    ys_sem,
    yr_sem,
    rs_sem,
    rr_sem,
    ds_sem,
    dr_sem,
):
    peers, rows, width = xs_ref.shape
    total = peers * rows
    hidden = gate_ref.shape[1]
    tiles = hidden // TILE
    me = lax.axis_index("fsdp")
    tp = lax.axis_index("tp")
    rank = lax.rem(me, peers)
    core = lax.rem(rank, 2)
    start = me - rank

    def peer(k):
        return {"fsdp": start + flipped(rank, k, peers)}

    partner = {"tp": 1 - tp}
    sibling = {"fsdp": start + rank + 1 - 2 * core}

    def out_x(k):
        return send_to(xs_ref.at[k], x_ref.at[0, k], xs_sem.at[k], xr_sem.at[k], peer(k))

    def out_g(k):
        return send_to(gs_ref.at[k], g_ref.at[0, k], gs_sem.at[k], gr_sem.at[k], peer(k))

    def pass_x(k):
        return send_to(x_ref.at[0, k], x_ref.at[1, k], xfs_sem.at[k], xfr_sem.at[k], partner)

    def pass_g(k):
        return send_to(g_ref.at[0, k], g_ref.at[1, k], gfs_sem.at[k], gfr_sem.at[k], partner)

    def across(index, k):
        return send_to(
            ysend_ref.at[index, k],
            yrecv_ref.at[index, k],
            ys_sem.at[index, k],
            yr_sem.at[index, k],
            partner,
        )

    def back(index, k):
        if index == 0:
            return send_to(xs_ref.at[k], res_out_ref.at[k], rs_sem.at[k], rr_sem.at[k], peer(k))
        return send_to(gs_ref.at[k], dx_out_ref.at[k], ds_sem.at[k], dr_sem.at[k], peer(k))

    def return_order(body):
        def step(j, carry):
            body(8 + 2 * j)
            body(4 + j)
            body(9 + 2 * j)
            return carry

        lax.fori_loop(0, 4, step, 0)
        for k in (2, 3, 1, 0):
            body(k)

    def turn_rows(source, target, m):
        target[:, pl.ds(pl.multiple_of(m * total, total), total)] = (
            source[m].reshape(total, width).T
        )

    def join(index, k):
        across(index, k).wait_recv()
        own = xs_ref if index == 0 else gs_ref
        own[k] = low(wide(own[k]) + wide(yrecv_ref[index, k]))
        back(index, k).start()

    def join_some(index, tile):
        join(index, 8 + 2 * tile)
        join(index, 4 + tile)
        join(index, 9 + 2 * tile)

    def join_last(index):
        for k in (2, 3, 1):
            join(index, k)
        across(index, 0).wait_recv()
        own, target = (xs_ref, res_out_ref) if index == 0 else (gs_ref, dx_out_ref)
        target[0] = low(wide(own[0]) + wide(yrecv_ref[index, 0]))

    greet_group(peers)
    here = pltpu.make_async_copy(weight_ref, w_ref.at[:, core], w_sem.at[0])
    here.start()
    there = send_to(weight_ref, w_ref.at[:, core], w_sem.at[1], w_sem.at[2], sibling)
    half = total // 2
    group = peers // 2

    def hits_of(part):
        ids = slot_ref[pl.ds(pl.multiple_of(part * half, half), half), 0:1]
        return [line_ref[m : m + 1, :] == ids for m in range(2)]

    def pack_x(part):
        hits = hits_of(part)
        onehot = low(jnp.where(hits[0] | hits[1], 1.0, 0.0))
        xs_ref[pl.ds(part * group, group)] = low(nn_dot(onehot, s2_ref[...])).reshape(
            group, rows, width
        )

        @pl.when(part == 0)
        def _():
            x_ref[0, 0] = xs_ref[0]
            pass_x(0).start()

        def launch(k):
            @pl.when(k > 0)
            def _():
                out_x(k).start()

        each(part * group, (part + 1) * group, launch)

    def pack_g(part):
        hits = hits_of(part)
        onehot = low(jnp.where(hits[0] | hits[1], 1.0, 0.0))
        gate = sum(
            jnp.sum(jnp.where(hits[m], line_ref[2 + m : 3 + m, :], 0.0), axis=1, keepdims=True)
            for m in range(2)
        )
        gs_ref[pl.ds(part * group, group)] = low(nn_dot(onehot, cot_ref[...]) * gate).reshape(
            group, rows, width
        )

        @pl.when(part == 0)
        def _():
            g_ref[0, 0] = gs_ref[0]

        def launch(k):
            @pl.when(k > 0)
            def _():
                out_g(k).start()

        each(part * group, (part + 1) * group, launch)

    each(0, 2, pack_x)
    there.start()
    each(0, 2, pack_g)

    def forward_x(k):
        out_x(k).wait_recv()
        pass_x(k).start()

    each(1, peers, forward_x)
    pass_g(0).start()
    here.wait()
    send_to(weight_ref, w_ref.at[:, 1 - core], w_sem.at[1], w_sem.at[2], sibling).wait_recv()
    there.wait_send()
    each(0, peers, lambda k: pass_x(k).wait_recv())

    def weights(which, lanes):
        return w_ref[:, :, :, pl.ds(pl.multiple_of(which * hidden + lanes, TILE), TILE)].reshape(
            width, TILE
        )

    acc_ref[...] = jnp.zeros_like(acc_ref)

    def forward_tile(tile, carry):
        lanes = pl.multiple_of(tile * TILE, TILE)
        here_lanes = pl.ds(lanes, TILE)

        def one_half(m):
            band = pl.ds(pl.multiple_of(m * total, total), total)
            x = x_ref[m].reshape(total, width)
            gate = nn_dot(x, weights(0, lanes))
            up = nn_dot(x, weights(1, lanes))
            gate_ref[band, here_lanes] = low(gate)
            up_ref[band, here_lanes] = low(up)
            act = low(gate / (1.0 + jnp.exp(-gate)) * up)
            act_ref[band, here_lanes] = act
            acc_ref[band, :] += nt_dot(act, weights(2, lanes))

        each(0, 2, one_half)

        def forward_g(k):
            @pl.when(k > 0)
            def _():
                out_g(k).wait_recv()
                pass_g(k).start()

        each(tile * (peers // tiles), (tile + 1) * (peers // tiles), forward_g)
        return carry

    lax.fori_loop(0, tiles, forward_tile, 0)
    each(1, peers, lambda k: out_x(k).wait_send())
    xs_ref[...] = low(acc_ref[:total, :]).reshape(peers, rows, width)
    ysend_ref[0] = low(acc_ref[total:, :]).reshape(peers, rows, width)
    return_order(lambda k: across(0, k).start())
    each(0, 2, lambda m: turn_rows(x_ref, xt_ref, m))
    acc_ref[...] = jnp.zeros_like(acc_ref)
    each(0, peers, lambda k: pass_g(k).wait_recv())

    def slope_tile(tile, carry):
        lanes = pl.multiple_of(tile * TILE, TILE)
        here_lanes = pl.ds(lanes, TILE)

        def one_half(m):
            band = pl.ds(pl.multiple_of(m * total, total), total)
            gate = wide(gate_ref[band, here_lanes])
            up = wide(up_ref[band, here_lanes])
            sig = 1.0 / (1.0 + jnp.exp(-gate))
            d_act = nn_dot(g_ref[m].reshape(total, width), weights(2, lanes))
            d_up = low(d_act * gate * sig)
            d_gate = low(d_act * up * sig * (1.0 + gate * (1.0 - sig)))
            gate_ref[band, here_lanes] = d_gate
            up_ref[band, here_lanes] = d_up
            acc_ref[band, :] += nt_dot(d_gate, weights(0, lanes)) + nt_dot(
                d_up, weights(1, lanes)
            )

        each(0, 2, one_half)
        join_some(0, tile)
        return carry

    lax.fori_loop(0, tiles, slope_tile, 0)
    join_last(0)
    each(1, peers, lambda k: out_g(k).wait_send())
    gs_ref[...] = low(acc_ref[:total, :]).reshape(peers, rows, width)
    ysend_ref[1] = low(acc_ref[total:, :]).reshape(peers, rows, width)
    return_order(lambda k: across(1, k).start())
    each(0, 2, lambda m: turn_rows(g_ref, gt_ref, m))

    def weight_tile(tile, carry):
        lanes = pl.multiple_of(tile * TILE, TILE)
        here_lanes = pl.ds(lanes, TILE)

        def keep(which, values):
            grads_ref[
                :, :, :, pl.ds(pl.multiple_of(which * hidden + lanes, TILE), TILE)
            ] = low(values).reshape(peers // 2, 2, rows, TILE)

        keep(0, nn_dot(xt_ref[...], gate_ref[:, here_lanes]))
        keep(1, nn_dot(xt_ref[...], up_ref[:, here_lanes]))
        keep(2, nn_dot(gt_ref[...], act_ref[:, here_lanes]))
        join_some(1, tile)
        return carry

    lax.fori_loop(0, tiles, weight_tile, 0)
    swap_grads = send_to(
        grads_ref.at[:, 1 - core], sibling_ref, grad_sem.at[0], grad_sem.at[1], sibling
    )
    swap_grads.start()
    join_last(1)
    each(0, peers, lambda k: pass_x(k).wait_send())
    each(0, peers, lambda k: pass_g(k).wait_send())
    for index in range(2):
        each(0, peers, lambda k: across(index, k).wait_send())
        each(1, peers, lambda k: back(index, k).wait_send())
    swap_grads.wait()
    grads_out_ref[...] = low(wide(grads_ref[:, core]) + wide(sibling_ref[...]))
    for index in range(2):
        each(1, peers, lambda k: back(index, k).wait_recv())


def run_expert(s2, cot, lines, slots, weights):
    length, width = s2.shape
    experts, shard, total = weights.shape
    peers = 2 * experts
    rows = slots.shape[0] // peers
    hidden = total // 3
    both = 2 * peers * rows
    vmem = pl.BlockSpec(memory_space=pltpu.VMEM)
    low_t, wide_t = jnp.bfloat16, jnp.float32
    dma = pltpu.SemaphoreType.DMA
    block = (peers, rows, width)
    return pl.pallas_call(
        expert_kernel,
        in_specs=[vmem] * 4 + [pl.BlockSpec(memory_space=pl.ANY)],
        out_specs=[vmem] * 3,
        out_shape=[
            jax.ShapeDtypeStruct(block, low_t),
            jax.ShapeDtypeStruct(block, low_t),
            jax.ShapeDtypeStruct(weights.shape, low_t),
        ],
        scratch_shapes=[
            pltpu.VMEM(block, low_t),
            pltpu.VMEM(block, low_t),
            pltpu.VMEM((2,) + block, low_t),
            pltpu.VMEM((2,) + block, low_t),
            pltpu.VMEM((experts, 2, shard, total), low_t),
            pltpu.VMEM((both, hidden), low_t),
            pltpu.VMEM((both, hidden), low_t),
            pltpu.VMEM((both, hidden), low_t),
            pltpu.VMEM((width, both), low_t),
            pltpu.VMEM((width, both), low_t),
            pltpu.VMEM((both, width), wide_t),
            pltpu.VMEM((experts, 2, shard, total), low_t),
            pltpu.VMEM((experts, shard, total), low_t),
            pltpu.VMEM((2,) + block, low_t),
            pltpu.VMEM((2,) + block, low_t),
            dma((3,)),
            dma((2,)),
        ]
        + [dma((peers,))] * 8
        + [dma((2, peers))] * 2
        + [dma((peers,))] * 4,
        compiler_params=pltpu.CompilerParams(
            collective_id=2, has_side_effects=True, vmem_limit_bytes=67043328
        ),
    )(s2, cot, lines, slots, weights)


def attend(
    hid_ref,
    token_block,
    weight,
    small_ref,
    gains,
    table_ref,
    s1_ref,
    qkv_ref,
    lse_ref,
    mixed_ref,
    mid_ref,
    s2_ref,
    tok_ref,
    line_ref,
    vt_ref,
    send_ref,
    recv_ref,
    send_sem,
    recv_sem,
    between,
):
    blocks = hid_ref.shape[0] // BLOCK
    heads_width = mixed_ref.shape[1]
    pairs = heads_width // PAIR
    gain_one, gain_two = gains
    lse_ref[...] = jnp.zeros_like(lse_ref)

    def copy(block):
        return to_partner(
            send_ref.at[block], recv_ref.at[block], send_sem.at[block], recv_sem.at[block]
        )

    def compute(block):
        rows = block_rows(block)
        source = wide(hid_ref[rows, :])
        s1 = low(source * lax.rsqrt(mean_last(source * source) + EPSILON) * gain_one)
        s1_ref[rows, :] = s1
        cosine, sine = spread_table(table_ref, block)
        for part in range(3):
            projected = nn_dot(s1, weight(part))
            for pair in range(pairs):
                chunk = projected[:, pair * PAIR : (pair + 1) * PAIR]
                if part < 2:
                    chunk = turn(chunk, cosine, sine)
                else:
                    vt_ref[pair * PAIR : (pair + 1) * PAIR, rows] = low(chunk.T)
                start = part * heads_width + pair * PAIR
                qkv_ref[rows, start : start + PAIR] = low(chunk)

        def one_pair(keys, pair):
            start = pl.multiple_of(pair * PAIR, PAIR)
            lanes = pl.ds(start, PAIR)
            key_lanes = pl.ds(pl.multiple_of(heads_width + start, PAIR), PAIR)
            query = qkv_ref[rows, lanes] * jnp.bfloat16(SCALING)
            key = qkv_ref[:keys, key_lanes]
            value_t = vt_ref[lanes, :keys]
            gathered = None
            for half in range(2):
                masked = jnp.where(head_lanes(query.shape, half, 1), query, jnp.bfloat16(0))
                scores = nt_dot(key, masked)
                highest = jnp.max(scores, axis=0, keepdims=True)
                expanded = jnp.exp(scores - highest)
                totals = jnp.sum(expanded, axis=0, keepdims=True)
                probs = low(expanded * (1.0 / totals))
                lse_ref[pl.ds(2 * pair + half, 1), rows] = highest + jnp.log(totals)
                found = nn_dot(value_t, probs)
                gathered = (
                    found
                    if half == 0
                    else jnp.where(head_lanes(found.shape, 1, 0), found, gathered)
                )
            mixed_ref[rows, lanes] = low(gathered.T)

        for static in range(blocks):

            @pl.when(block == static)
            def _():
                each(0, pairs, functools.partial(one_pair, (static + 1) * BLOCK))

        send_ref[block] = low(nt_dot(mixed_ref[rows, :], weight(3)))
        copy(block).start()

    def finish(block):
        rows = block_rows(block)
        copy(block).wait()
        mid = wide(hid_ref[rows, :]) + (wide(send_ref[block]) + wide(recv_ref[block]))
        mid_ref[rows, :] = mid
        s2 = low(mid * lax.rsqrt(mean_last(mid * mid) + EPSILON) * gain_two)
        s2_ref[rows, :] = s2
        tok = token_block(block)
        lane = lax.broadcasted_iota(jnp.int32, tok.shape, 1)
        logits = nn_dot(s2, small_ref[...]) + tok
        picked = [
            jnp.sum(
                jnp.where(wide(lane - ROUTER) == column(tok, ROUTE + member), logits, 0.0),
                axis=1,
                keepdims=True,
            )
            for member in range(2)
        ]
        gate = [
            1.0 / (1.0 + jnp.exp(picked[1 - member] - picked[member])) for member in range(2)
        ]
        tok = jnp.where(lane == GATE, gate[0], jnp.where(lane == GATE + 1, gate[1], tok))
        tok_ref[rows, :] = tok
        line_ref[:, rows] = tok.T[TARGET : TARGET + 8, :]

    each(0, blocks, compute)
    between()
    each(0, blocks, finish)


def forward_plain_kernel(
    hid_ref,
    tok_in_ref,
    block_ref,
    small_ref,
    rows_ref,
    table_ref,
    shard_ref,
    cot_own_ref,
    s1_ref,
    qkv_ref,
    lse_ref,
    mixed_ref,
    mid_ref,
    s2_ref,
    tok_ref,
    line_ref,
    expert_ref,
    cot_ref,
    vt_ref,
    send_ref,
    recv_ref,
    send_sem,
    recv_sem,
    wsend_sem,
    wrecv_sem,
    cot_sem,
):
    greet_group(2 * shard_ref.shape[0])
    own_rows = cot_own_ref.shape[0]
    heads_width = mixed_ref.shape[1]
    width = hid_ref.shape[1]
    mine = pl.ds(pl.multiple_of(lax.axis_index("tp") * own_rows, own_rows), own_rows)
    cot_copy = to_partner(cot_own_ref, cot_ref.at[mine], cot_sem.at[0], cot_sem.at[1])
    cot_copy.start()
    experts = CoreExchange(shard_ref, expert_ref, wsend_sem, wrecv_sem)
    experts.start()
    cot_ref[mine, :] = cot_own_ref[...]

    def weight(part):
        return block_ref[:, :, part * heads_width : (part + 1) * heads_width].reshape(
            width, heads_width
        )

    attend(
        hid_ref,
        lambda block: tok_in_ref[block_rows(block), :],
        weight,
        small_ref,
        (rows_ref[0:1, :], rows_ref[1:2, :]),
        table_ref,
        s1_ref,
        qkv_ref,
        lse_ref,
        mixed_ref,
        mid_ref,
        s2_ref,
        tok_ref,
        line_ref,
        vt_ref,
        send_ref,
        recv_ref,
        send_sem,
        recv_sem,
        lambda: None,
    )
    cot_copy.wait()
    experts.wait()


def forward_kernel(
    hid_own_ref,
    cot_own_ref,
    logit_ref,
    route_ref,
    rank_ref,
    drop_ref,
    gain_ref,
    router_ref,
    mixing_ref,
    value_ref,
    wqkv_ref,
    wout_ref,
    win_ref,
    wdown_ref,
    table_ref,
    all_out,
    small_ref,
    rows_ref,
    s1_out,
    qkv_out,
    lse_ref,
    mixed_out,
    mid_ref,
    s2_ref,
    tok_ref,
    line_ref,
    expert_ref,
    cot_out,
    all_ref,
    s1_ref,
    qkv_ref,
    mixed_ref,
    cot_ref,
    hid_ref,
    vt_ref,
    send_ref,
    recv_ref,
    shard_ref,
    stage_ref,
    small_all_ref,
    tok_all_ref,
    send_sem,
    recv_sem,
    wsend_sem,
    wrecv_sem,
    y_send,
    y_recv,
    up_send,
    up_recv,
    down_send,
    down_recv,
    x_send,
    x_recv,
    core_send,
    core_recv,
    store_sem,
):
    size, shard, _ = all_ref.shape
    planes = size // 4
    me = lax.axis_index("fsdp")
    tp = lax.axis_index("tp")
    z, x, core = me // 4, lax.rem(me // 2, 2), lax.rem(me, 2)
    own_rows, width = hid_own_ref.shape
    heads_width = wout_ref.shape[1]
    small_rows = shard // 2
    greet_group(size)
    partner = {"tp": 1 - tp}
    mine = pl.ds(pl.multiple_of(tp * own_rows, own_rows), own_rows)
    stage_ref[...] = jnp.zeros_like(stage_ref)
    stage_ref[0:2, :small_rows] = gain_ref[...]
    stage_ref[ROUTER:MIXING, :small_rows] = wide(router_ref[...])
    stage_ref[MIXING:VALUE, :small_rows] = wide(mixing_ref[...])
    stage_ref[VALUE : VALUE + 2, :small_rows] = wide(value_ref[...])
    small_all_ref[me, tp] = stage_ref[...].T[:small_rows, :]
    small_y = send_to(
        small_all_ref.at[me, tp], small_all_ref.at[me, tp], y_send.at[0], y_recv.at[0], partner
    )
    small_y.start()
    for part in range(3):
        all_ref[me, :, part * heads_width : (part + 1) * heads_width] = wqkv_ref[part]
    all_ref[me, :, 3 * heads_width :] = wout_ref[...]
    hid_y = send_to(hid_own_ref, hid_ref.at[mine], y_send.at[1], y_recv.at[1], partner)
    tok_y = send_to(tok_all_ref.at[tp], tok_all_ref.at[tp], y_send.at[2], y_recv.at[2], partner)
    cot_y = send_to(cot_own_ref, cot_ref.at[mine], y_send.at[3], y_recv.at[3], partner)
    experts = CoreExchange(shard_ref, expert_ref, wsend_sem, wrecv_sem)
    expert_count, _, hidden = wdown_ref.shape

    def stage_tokens():
        tok_all_ref[tp] = jnp.zeros(tok_all_ref.shape[1:], jnp.float32)
        routes = route_ref[...]
        kept = jnp.logical_and(routes < expert_count, drop_ref[...] == 0)
        target = jnp.where(kept, routes * (own_rows * 2 * 9 // 48) + rank_ref[...], -1)
        tok_all_ref[tp, ROUTER:MIXING, :] = logit_ref[...]
        tok_all_ref[tp, ROUTE : ROUTE + 2, :] = wide(routes)
        tok_all_ref[tp, TARGET : TARGET + 2, :] = wide(target)

    def stage_shard():
        def one(e):
            for part in range(2):
                shard_ref[e, :, part * hidden : (part + 1) * hidden] = win_ref[e, :, part, :]
            shard_ref[e, :, 2 * hidden :] = wdown_ref[e]

        each(0, expert_count, one)

    def number(plane, line):
        return plane * 4 + line * 2 + core

    def piece(kind, number_of, send, recv, slot, device):
        array = small_all_ref if kind else all_ref
        return send_to(
            array.at[number_of],
            array.at[number_of],
            send.at[kind, slot],
            recv.at[kind, slot],
            device,
        )

    def up(kind, step, plane):
        device = {"fsdp": number(lax.min(z + 1, planes - 1), x)}
        return piece(kind, number(plane, x), up_send, up_recv, step, device)

    def down(kind, step, plane):
        device = {"fsdp": number(lax.max(z - 1, 0), x)}
        return piece(kind, number(plane, x), down_send, down_recv, step, device)

    def side(kind, plane, line):
        device = {"fsdp": number(z, 1 - x)}
        return piece(kind, number(plane, line), x_send, x_recv, plane, device)

    def sibling(kind, plane, line, parity):
        return piece(
            kind,
            plane * 4 + line * 2 + parity,
            core_send,
            core_recv,
            plane * 2 + line,
            {"fsdp": me + 1 - 2 * core},
        )

    def launch(kind):
        @pl.when(z < planes - 1)
        def _():
            up(kind, 0, z).start()

        @pl.when(z > 0)
        def _():
            down(kind, 0, z).start()

        side(kind, z, x).start()
        sibling(kind, z, x, core).start()

    launch(0)
    hid_y.start()
    stage_tokens()
    tok_y.start()
    cot_y.start()
    hid_ref[mine, :] = hid_own_ref[...]
    cot_ref[mine, :] = cot_own_ref[...]
    small_y.wait()
    launch(1)
    stage_shard()
    for step in range(1, planes):
        for kind in range(2):

            @pl.when(z >= step)
            def _():
                up(kind, step - 1, z - step).wait_recv()

                @pl.when(z < planes - 1)
                def _():
                    up(kind, step, z - step).start()

                side(kind, z - step, x).start()
                sibling(kind, z - step, x, core).start()

            @pl.when(z + step < planes)
            def _():
                down(kind, step - 1, z + step).wait_recv()

                @pl.when(z > 0)
                def _():
                    down(kind, step, z + step).start()

                side(kind, z + step, x).start()
                sibling(kind, z + step, x, core).start()

    experts.start()
    for step in range(planes):
        for kind in range(2):

            @pl.when(z >= step)
            def _():
                side(kind, z - step, 1 - x).wait_recv()
                sibling(kind, z - step, 1 - x, core).start()

            if step > 0:

                @pl.when(z + step < planes)
                def _():
                    side(kind, z + step, 1 - x).wait_recv()
                    sibling(kind, z + step, 1 - x, core).start()

    for plane in range(planes):
        for line in range(2):
            for kind in range(2):
                sibling(kind, plane, line, 1 - core).wait_recv()
    small_all = small_all_ref[...].reshape(width, PAIR)
    small_ref[...] = low(small_all)
    rows_ref[...] = small_all.T[:8, :]
    tok_y.wait()
    hid_y.wait()

    def token_block(block):
        per = own_rows // BLOCK
        lanes = pl.ds(pl.multiple_of(lax.rem(block, per) * BLOCK, BLOCK), BLOCK)
        part = tok_all_ref[block // per, :, lanes]
        blank = jnp.zeros((PAIR - part.shape[0], BLOCK), jnp.float32)
        return jnp.concatenate([part, blank], axis=0).T

    def weight(part):
        return all_ref[:, :, part * heads_width : (part + 1) * heads_width].reshape(
            width, heads_width
        )

    stores = [
        pltpu.make_async_copy(source, target, store_sem.at[index])
        for index, (source, target) in enumerate(
            [
                (all_ref, all_out),
                (s1_ref, s1_out),
                (qkv_ref, qkv_out),
                (mixed_ref, mixed_out),
                (cot_ref, cot_out),
            ]
        )
    ]
    stores[0].start()

    def between():
        for store in stores[1:4]:
            store.start()
        cot_y.wait()
        stores[4].start()

    attend(
        hid_ref,
        token_block,
        weight,
        small_ref,
        (rows_ref[0:1, :], rows_ref[1:2, :]),
        table_ref,
        s1_ref,
        qkv_ref,
        lse_ref,
        mixed_ref,
        mid_ref,
        s2_ref,
        tok_ref,
        line_ref,
        vt_ref,
        send_ref,
        recv_ref,
        send_sem,
        recv_sem,
        between,
    )
    for kind in range(2):
        for step in range(planes):

            @pl.when(jnp.logical_and(z >= step, z < planes - 1))
            def _():
                up(kind, step, z - step).wait_send()

            @pl.when(jnp.logical_and(z + step < planes, z > 0))
            def _():
                down(kind, step, z + step).wait_send()

        for plane in range(planes):
            side(kind, plane, x).wait_send()
            for line in range(2):
                sibling(kind, plane, line, core).wait_send()
    for store in stores:
        store.wait()
    experts.wait()


def backward_kernel(
    res_ref,
    dx_ref,
    slot_ref,
    tok_ref,
    cot_ref,
    mid_hbm,
    s1_hbm,
    qkv_hbm,
    lse_ref,
    mixed_hbm,
    block_hbm,
    small_ref,
    rows_ref,
    table_ref,
    own_ref,
    egrad_ref,
    grad_ref,
    base_ref,
    other_ref,
    big_ref,
    arrived_ref,
    gsend_ref,
    grecv_ref,
    ssend_ref,
    srecv_ref,
    mid_ref,
    s1_ref,
    qkv_ref,
    mixed_ref,
    block_ref,
    hsend_ref,
    hrecv_ref,
    gmid_ref,
    gown_ref,
    kt_ref,
    gm_ref,
    dk_ref,
    dv_ref,
    gp_ref,
    att_ref,
    s2_ref,
    slope_ref,
    value_ref,
    acc_gain_ref,
    gsend_sem,
    grecv_sem,
    hsend_sem,
    hrecv_sem,
    esend_sem,
    erecv_sem,
    ssend_sem,
    srecv_sem,
    load_sem,
):
    loads = [
        pltpu.make_async_copy(source, target, load_sem.at[index])
        for index, (source, target) in enumerate(
            [
                (mid_hbm, mid_ref),
                (qkv_hbm, qkv_ref),
                (mixed_hbm, mixed_ref),
                (block_hbm, block_ref),
                (s1_hbm, s1_ref),
            ]
        )
    ]
    for load in loads:
        load.start()
    greet_group(2 * egrad_ref.shape[0])
    experts = CoreExchange(egrad_ref, arrived_ref, esend_sem, erecv_sem)
    tp = lax.axis_index("tp")
    width = dx_ref.shape[1]
    blocks = cot_ref.shape[0] // BLOCK
    heads_width = mixed_ref.shape[1]
    pairs = heads_width // PAIR
    gain_one = rows_ref[0:1, :]
    gain_two = rows_ref[1:2, :]
    slot_row = slot_ref[0:1, :]

    def weights(first_part, last_part):
        lanes = slice(first_part * heads_width, last_part * heads_width)
        return block_ref[:, :, lanes].reshape(width, (last_part - first_part) * heads_width)

    half_blocks = blocks // 2
    experts.start()

    def row_copy(block):
        return to_partner(
            gsend_ref.at[block], grecv_ref.at[block], gsend_sem.at[block], grecv_sem.at[block]
        )

    def share_copy(block):
        return to_partner(
            ssend_ref.at[block], srecv_ref.at[block], ssend_sem.at[block], srecv_sem.at[block]
        )

    def stream_copy(slot):
        return to_partner(
            hsend_ref.at[slot], hrecv_ref.at[slot], hsend_sem.at[slot], hrecv_sem.at[slot]
        )

    def slab_of(block):
        return block_rows(lax.rem(block, half_blocks))

    def backwards(body):
        each(0, blocks, lambda step: body(blocks - 1 - step))

    def send_rows(block):
        rows = block_rows(block)
        tok = tok_ref[rows, :]
        onehots = [low(jnp.where(column(tok, TARGET + m) == slot_row, 1.0, 0.0)) for m in range(2)]
        gsend_ref[block] = low(nn_dot(onehots[0] + onehots[1], dx_ref[...]))
        row_copy(block).start()
        placed = [nn_dot(onehot, res_ref[...]) for onehot in onehots]
        cot_wide = wide(cot_ref[rows, :])
        shares = [
            column(tok, GATE + m) * jnp.sum(placed[m] * cot_wide, axis=1, keepdims=True)
            for m in range(2)
        ]
        ssend_ref[block] = lane_matrix(tok.shape, [(0, shares[0]), (1, shares[1])]).T[:8, :]
        share_copy(block).start()
        mixture = column(tok, GATE) * placed[0] + column(tok, GATE + 1) * placed[1]

        @pl.when(tp == block // half_blocks)
        def _():
            base_ref[slab_of(block), :] = mixture

        @pl.when(tp != block // half_blocks)
        def _():
            other_ref[slab_of(block), :] = low(mixture)

    backwards(send_rows)
    for load in loads:
        load.wait()
    kt_ref[...] = qkv_ref[:, heads_width : 2 * heads_width].T
    dk_ref[...] = jnp.zeros_like(dk_ref)
    dv_ref[...] = jnp.zeros_like(dv_ref)
    acc_gain_ref[...] = jnp.zeros_like(acc_gain_ref)

    def main(block):
        rows = block_rows(block)
        mine = tp == block // half_blocks
        mine_f = jnp.where(mine, 1.0, 0.0)
        mid = mid_ref[rows, :]
        cot = cot_ref[rows, :]
        cot_wide = wide(cot)
        tok = tok_ref[rows, :]
        scale = lax.rsqrt(mean_last(mid * mid) + EPSILON)
        unit = mid * scale
        normed = unit * gain_two
        s2 = low(normed)
        small = small_ref[...]
        mixing = nn_dot(s2, small)
        value_dot = nn_dot(cot, small)
        normed_dot = jnp.sum(normed * cot_wide, axis=1, keepdims=True)
        route = [column(tok, ROUTE + member) for member in range(2)]
        gate = [column(tok, GATE + member) for member in range(2)]

        def weight_of(expert):
            return sum(jnp.where(route[m] == expert, gate[m], 0.0) for m in range(2))

        copy_weight = weight_of(COPY)
        copy_share = [jnp.where(route[m] == COPY, normed_dot, 0.0) for m in range(2)]
        alpha = copy_weight
        columns = []
        value_columns = []
        for c in range(2):
            weight = weight_of(COPY + 1 + c)
            left = column(mixing, MIXING + 2 * c)
            right = column(mixing, MIXING + 2 * c + 1)
            a0 = 1.0 / (1.0 + jnp.exp(right - left))
            a1 = 1.0 / (1.0 + jnp.exp(left - right))
            vd = column(value_dot, VALUE + c)
            alpha = alpha + weight * a0
            for m in range(2):
                copy_share[m] = copy_share[m] + jnp.where(
                    route[m] == COPY + 1 + c, a0 * normed_dot + a1 * vd, 0.0
                )
            slope = a0 * a1 * weight * (normed_dot - vd)
            columns.append((MIXING + 2 * c, slope))
            columns.append((MIXING + 2 * c + 1, -slope))
            value_columns.append((VALUE + c, weight * a1))
        value_matrix = lane_matrix(tok.shape, value_columns)
        base = mid + alpha * normed + nt_dot(low(value_matrix), small)

        @pl.when(mine)
        def _():
            base_ref[slab_of(block), :] += base

        row_copy(block).wait()
        share_copy(block).wait()
        extra = ssend_ref[block] + srecv_ref[block]
        extra = jnp.concatenate(
            [extra, jnp.zeros((PAIR - extra.shape[0], BLOCK), jnp.float32)], axis=0
        ).T
        share = [column(extra, m) + gate[m] * copy_share[m] for m in range(2)]
        lane = lax.broadcasted_iota(jnp.int32, tok.shape, 1)
        slopes = lane_matrix(tok.shape, columns)
        for m in range(2):
            local = share[m] - gate[m] * (share[0] + share[1])
            slopes = slopes + jnp.where(wide(lane - ROUTER) == route[m], local, 0.0)
        slopes_low = low(slopes)
        grad_normed = (
            wide(gsend_ref[block])
            + wide(grecv_ref[block])
            + alpha * cot_wide
            + nt_dot(slopes_low, small)
        )
        s2_ref[rows, :] = s2
        slope_ref[rows, :] = low(slopes * mine_f)
        value_ref[rows, :] = low(value_matrix * mine_f)
        gain_grad = jnp.sum(unit * grad_normed, axis=0, keepdims=True) * mine_f
        acc_gain_ref[...] += jnp.broadcast_to(gain_grad, acc_gain_ref.shape)
        scaled = grad_normed * gain_two
        grad_mid = cot_wide + scale * (scaled - unit * mean_last(scaled * unit))
        gmid_ref[rows, :] = grad_mid
        attended = low(grad_mid)
        att_ref[rows, :] = attended
        gm_ref[...] = low(nn_dot(attended, weights(3, 4)))
        cosine, sine = spread_table(table_ref, block)

        def one_pair(keys, pair):
            start = pl.multiple_of(pair * PAIR, PAIR)
            lanes = pl.ds(start, PAIR)
            key_lanes = pl.ds(pl.multiple_of(heads_width + start, PAIR), PAIR)
            value_lanes = pl.ds(pl.multiple_of(2 * heads_width + start, PAIR), PAIR)
            query = qkv_ref[rows, lanes] * jnp.bfloat16(SCALING)
            key = qkv_ref[:keys, key_lanes]
            value = qkv_ref[:keys, value_lanes]
            grad_out = gm_ref[:, lanes]
            key_t = kt_ref[lanes, :keys]
            grad_value = None
            for half in range(2):
                keep = head_lanes(query.shape, half, 1)
                q_half = jnp.where(keep, query, jnp.bfloat16(0))
                g_half = jnp.where(keep, grad_out, jnp.bfloat16(0))
                probs = jnp.exp(nt_dot(key, q_half) - lse_ref[pl.ds(2 * pair + half, 1), rows])
                grad_probs = nt_dot(value, g_half)
                inner = jnp.sum(probs * grad_probs, axis=0, keepdims=True)
                grad_scores = low(probs * (grad_probs - inner))
                value_part = nn_dot(low(probs), g_half)
                key_part = nn_dot(grad_scores, q_half)
                query_part = nn_dot(key_t, grad_scores)
                if half == 0:
                    grad_value, grad_key, grad_query = value_part, key_part, query_part
                else:
                    grad_value = grad_value + value_part
                    grad_key = grad_key + key_part
                    grad_query = jnp.where(
                        head_lanes(query_part.shape, 1, 0), query_part, grad_query
                    )
            dv_ref[:keys, lanes] += grad_value
            dk_ref[:keys, lanes] += grad_key
            gp_ref[rows, lanes] = low(turn(grad_query.T * SCALING, cosine, -sine))
            gp_ref[rows, key_lanes] = low(turn(dk_ref[rows, lanes], cosine, -sine))
            gp_ref[rows, value_lanes] = low(dv_ref[rows, lanes])

        for static in range(blocks):

            @pl.when(block == static)
            def _():
                each(0, pairs, functools.partial(one_pair, (static + 1) * BLOCK))

        stream_grad = nt_dot(gp_ref[rows, :], weights(0, 3))
        slot = lax.rem(block, half_blocks)

        @pl.when(mine)
        def _():
            gown_ref[slot] = stream_grad

        @pl.when(jnp.logical_not(mine))
        def _():
            hsend_ref[slot] = low(stream_grad)
            stream_copy(slot).start()

    backwards(main)
    s1_turned = s1_ref[...].T
    for part in range(3):
        lanes = slice(part * heads_width, (part + 1) * heads_width)
        big_ref[:, lanes] = low(nn_dot(s1_turned, gp_ref[:, lanes]))
    big_ref[:, 3 * heads_width : 4 * heads_width] = low(tn_dot(att_ref[...], mixed_ref[...]))
    tall = jnp.where(
        lax.broadcasted_iota(jnp.int32, (PAIR, width), 0) == 1,
        jnp.broadcast_to(acc_gain_ref[0:1, :], (PAIR, width)),
        0.0,
    )
    big_ref[:, 4 * heads_width :] = low(
        tn_dot(s2_ref[...], slope_ref[...]) + tn_dot(cot_ref[...], value_ref[...]) + tall.T
    )
    for slot in reversed(range(half_blocks)):
        slab = slice(slot * BLOCK, (slot + 1) * BLOCK)
        stream_copy(slot).wait()
        source = wide(own_ref[slab, :])
        scale = lax.rsqrt(mean_last(source * source) + EPSILON)
        unit = source * scale
        scaled = (gown_ref[slot] + wide(hrecv_ref[slot])) * gain_one
        mid_rows = block_rows(tp * half_blocks + slot)
        grad_ref[slab, :] = gmid_ref[mid_rows, :] + scale * (
            scaled - unit * mean_last(scaled * unit)
        )
    experts.wait()


def forward_results(length, width, heads_width, shard):
    low_t, wide_t = jnp.bfloat16, jnp.float32
    return [
        jax.ShapeDtypeStruct((length, width), low_t),
        jax.ShapeDtypeStruct((length, 3 * heads_width), low_t),
        jax.ShapeDtypeStruct((8, length), wide_t),
        jax.ShapeDtypeStruct((length, heads_width), low_t),
        jax.ShapeDtypeStruct((length, width), wide_t),
        jax.ShapeDtypeStruct((length, width), low_t),
        jax.ShapeDtypeStruct((length, PAIR), wide_t),
        jax.ShapeDtypeStruct((8, length), wide_t),
        jax.ShapeDtypeStruct(shard, low_t),
        jax.ShapeDtypeStruct((length, width), low_t),
    ]


def attend_scratch(length, width, heads_width):
    blocks = length // BLOCK
    return [
        pltpu.VMEM((heads_width, length), jnp.bfloat16),
        pltpu.VMEM((blocks, BLOCK, width), jnp.bfloat16),
        pltpu.VMEM((blocks, BLOCK, width), jnp.bfloat16),
    ]


def run_forward_plain(hid, tok, blocks, small, rows, table, shard, cot):
    length, width = hid.shape
    heads_width = blocks.shape[2] // 4
    vmem = pl.BlockSpec(memory_space=pltpu.VMEM)
    dma = pltpu.SemaphoreType.DMA
    count = length // BLOCK
    return pl.pallas_call(
        forward_plain_kernel,
        in_specs=[vmem] * 8,
        out_specs=[vmem] * 10,
        out_shape=forward_results(length, width, heads_width, shard.shape),
        scratch_shapes=attend_scratch(length, width, heads_width)
        + [dma((count,)), dma((count,)), dma((shard.shape[0],)), dma((shard.shape[0],)), dma((2,))],
        compiler_params=pltpu.CompilerParams(
            collective_id=0, has_side_effects=True, vmem_limit_bytes=60 << 20
        ),
    )(hid, tok, blocks, small, rows, table, shard, cot)


def run_forward(*operands):
    hid, wout, wdown, table = operands[0], operands[11], operands[13], operands[14]
    own_rows, width = hid.shape
    length = 2 * table.shape[0]
    shard, heads_width = wout.shape
    experts, _, hidden = wdown.shape
    size = lax.axis_size("fsdp")
    count = length // BLOCK
    hbm = pl.BlockSpec(memory_space=pl.ANY)
    vmem = pl.BlockSpec(memory_space=pltpu.VMEM)
    low_t, wide_t = jnp.bfloat16, jnp.float32
    dma = pltpu.SemaphoreType.DMA
    return pl.pallas_call(
        forward_kernel,
        in_specs=[vmem] * 15,
        out_specs=[hbm, vmem, vmem, hbm, hbm, vmem, hbm]
        + [vmem] * 4
        + [hbm, hbm],
        out_shape=[
            jax.ShapeDtypeStruct((size, shard, 4 * heads_width), low_t),
            jax.ShapeDtypeStruct((width, PAIR), low_t),
            jax.ShapeDtypeStruct((8, width), wide_t),
        ]
        + forward_results(length, width, heads_width, (experts, shard, 3 * hidden)),
        scratch_shapes=[
            pltpu.VMEM((size, shard, 4 * heads_width), low_t),
            pltpu.VMEM((length, width), low_t),
            pltpu.VMEM((length, 3 * heads_width), low_t),
            pltpu.VMEM((length, heads_width), low_t),
            pltpu.VMEM((length, width), low_t),
            pltpu.VMEM((length, width), low_t),
        ]
        + attend_scratch(length, width, heads_width)
        + [
            pltpu.VMEM((experts, shard, 3 * hidden), low_t),
            pltpu.VMEM((PAIR, PAIR), wide_t),
            pltpu.VMEM((size, 2, shard // 2, PAIR), wide_t),
            pltpu.VMEM((2, 32, own_rows), wide_t),
            dma((count,)),
            dma((count,)),
            dma((experts,)),
            dma((experts,)),
            dma((4,)),
            dma((4,)),
        ]
        + [dma((2, size // 4))] * 6
        + [dma((2, size // 2))] * 2
        + [dma((5,))],
        compiler_params=pltpu.CompilerParams(
            collective_id=3, has_side_effects=True, vmem_limit_bytes=60 << 20
        ),
    )(*operands)


def run_backward(*operands):
    cot, mid, s1, qkv, mixed, blocks, own, egrads = (
        operands[index] for index in (4, 5, 6, 7, 9, 10, 14, 15)
    )
    length, width = cot.shape
    heads_width = mixed.shape[1]
    count = length // BLOCK
    own_rows = own.shape[0]
    vmem = pl.BlockSpec(memory_space=pltpu.VMEM)
    hbm = pl.BlockSpec(memory_space=pl.ANY)
    low_t, wide_t = jnp.bfloat16, jnp.float32
    dma = pltpu.SemaphoreType.DMA
    return pl.pallas_call(
        backward_kernel,
        in_specs=[vmem] * 5
        + [hbm] * 3
        + [vmem]
        + [hbm] * 2
        + [vmem] * 4
        + [hbm],
        out_specs=[vmem] * 4 + [hbm],
        out_shape=[
            jax.ShapeDtypeStruct((own_rows, width), wide_t),
            jax.ShapeDtypeStruct((own_rows, width), wide_t),
            jax.ShapeDtypeStruct((own_rows, width), low_t),
            jax.ShapeDtypeStruct((width, 4 * heads_width + PAIR), low_t),
            jax.ShapeDtypeStruct(egrads.shape, low_t),
        ],
        scratch_shapes=[
            pltpu.VMEM((count, BLOCK, width), low_t),
            pltpu.VMEM((count, BLOCK, width), low_t),
            pltpu.VMEM((count, 8, BLOCK), wide_t),
            pltpu.VMEM((count, 8, BLOCK), wide_t),
            pltpu.VMEM(mid.shape, wide_t),
            pltpu.VMEM(s1.shape, low_t),
            pltpu.VMEM(qkv.shape, low_t),
            pltpu.VMEM(mixed.shape, low_t),
            pltpu.VMEM(blocks.shape, low_t),
            pltpu.VMEM((2, BLOCK, width), low_t),
            pltpu.VMEM((2, BLOCK, width), low_t),
            pltpu.VMEM((length, width), wide_t),
            pltpu.VMEM((2, BLOCK, width), wide_t),
            pltpu.VMEM((heads_width, length), low_t),
            pltpu.VMEM((BLOCK, heads_width), low_t),
            pltpu.VMEM((length, heads_width), wide_t),
            pltpu.VMEM((length, heads_width), wide_t),
            pltpu.VMEM((length, 3 * heads_width), low_t),
            pltpu.VMEM((length, width), low_t),
            pltpu.VMEM((length, width), low_t),
            pltpu.VMEM((length, PAIR), low_t),
            pltpu.VMEM((length, PAIR), low_t),
            pltpu.VMEM((8, width), wide_t),
            dma((count,)),
            dma((count,)),
            dma((2,)),
            dma((2,)),
            dma((egrads.shape[0],)),
            dma((egrads.shape[0],)),
            dma((count,)),
            dma((count,)),
            dma((5,)),
        ],
        compiler_params=pltpu.CompilerParams(
            collective_id=1, has_side_effects=True, vmem_limit_bytes=60 << 20
        ),
    )(*operands)


def shards(
    hidden,
    prev_logits,
    routes,
    slot_rank,
    dropped,
    cotangent,
    attn_norm,
    ffn_norm,
    w_qkv,
    w_attn_out,
    w_router,
    w_const_gate,
    w_const_value,
    w_expert_in,
    w_expert_out,
):
    own_rows, width = hidden.shape
    length = own_rows * lax.axis_size("tp")
    experts = w_expert_in.shape[0]
    route_count = w_router.shape[1]
    capacity = 9 * length // (4 * route_count)
    planned = lax.axis_size("fsdp") == 16
    table = jnp.asarray(rotary_table(length))
    gains = jnp.stack([wide(attn_norm), wide(ffn_norm)], axis=0)
    wqkv = w_qkv.transpose(1, 0, 2)
    operands = (
        hidden,
        cotangent,
        prev_logits.T,
        routes.T,
        slot_rank.T,
        dropped.T,
        gains,
        w_router.T,
        w_const_gate.T,
        w_const_value.T,
        wqkv,
        w_attn_out,
        w_expert_in,
        w_expert_out,
    )
    if planned:
        forward = run_forward(*operands, table)
    else:
        forward = forward_plain(operands, table)
    blocks, small, rows, s1, qkv, lse, mixed, mid, s2, tok, lines, gathered, cot = forward
    expert_weights = join_weights(gathered, experts)
    peers = 2 * experts
    half = capacity // 2
    block = half // 2
    place = jnp.arange(peers * block)
    owner = (lax.axis_index("fsdp") % peers) ^ (place // block)
    slot = wide(
        (owner // 2) * capacity
        + lax.axis_index("tp") * half
        + (owner % 2) * block
        + place % block
    )
    results, grad_rows, grads_exp = run_expert(
        s2, cot, lines, jnp.broadcast_to(slot[:, None], (slot.shape[0], PAIR)), expert_weights
    )
    grad_hidden, base, for_other, big, arrived = run_backward(
        results.reshape(-1, width),
        grad_rows.reshape(-1, width),
        jnp.broadcast_to(slot[None, :], (8, slot.shape[0])),
        tok,
        cot,
        mid,
        s1,
        qkv,
        lse,
        mixed,
        blocks,
        small,
        rows,
        table,
        hidden,
        split_grads(grads_exp),
    )
    received, red, last = (run_finish if planned else finish_plain)(big, wqkv, for_other)
    output, grad_hidden, grad_qkv, grad_attn_out, gain_grads, grad_router, grad_mixing, grad_value, grad_in, grad_out = run_write(
        base, received, grad_hidden, red, last, gains, arrived
    )
    return (
        output,
        grad_hidden,
        gain_grads[0],
        gain_grads[1],
        grad_qkv.transpose(1, 0, 2),
        grad_attn_out,
        grad_router.T,
        grad_mixing.T,
        grad_value.T,
        grad_in,
        grad_out,
    )


def solution(mesh):
    in_specs = (
        P(("fsdp", "tp"), None),
        P(("fsdp", "tp"), None),
        P(("fsdp", "tp"), None),
        P(("fsdp", "tp"), None),
        P(("fsdp", "tp"), None),
        P(("fsdp", "tp"), None),
        P(("fsdp", "tp")),
        P(("fsdp", "tp")),
        P("fsdp", None, "tp"),
        P("fsdp", "tp"),
        P(("fsdp", "tp"), None),
        P(("fsdp", "tp"), None),
        P(("fsdp", "tp"), None),
        P(None, "fsdp", None, "tp"),
        P(None, "fsdp", "tp"),
    )
    out_specs = (
        P(("fsdp", "tp"), None),
        P(("fsdp", "tp"), None),
        P(("fsdp", "tp")),
        P(("fsdp", "tp")),
        P("fsdp", None, "tp"),
        P("fsdp", "tp"),
        P(("fsdp", "tp"), None),
        P(("fsdp", "tp"), None),
        P(("fsdp", "tp"), None),
        P(None, "fsdp", None, "tp"),
        P(None, "fsdp", "tp"),
    )
    return jax.shard_map(shards, mesh=mesh, in_specs=in_specs, out_specs=out_specs, check_vma=False)
```

```python
import functools

import jax
import jax.numpy as jnp
import numpy as np
from jax import lax
from jax.experimental import pallas as pl
from jax.experimental.pallas import tpu as pltpu
from jax.sharding import PartitionSpec as P

HD = 64
BLOCK = 256


EPSILON = 1e-06
MESH = pl.DeviceIdType.MESH
PAIR = 2 * HD
SCALING = HD ** (-0.5)
ROUTER = 2
MIXING = 14
VALUE = 18
ROUTE = 20
TARGET = 24
GATE = 26
COPY = 9


TILE = 256
SUB = 16


def swap(values):
    return lax.ppermute(values, "tp", [(0, 1), (1, 0)])


def gather_rows(values):
    other = swap(values)
    first = lax.axis_index("tp") == 0
    return jnp.concatenate(
        [jnp.where(first, values, other), jnp.where(first, other, values)], axis=0
    )


def own_half(values):
    half = values.shape[0] // 2
    return lax.dynamic_slice_in_dim(values, lax.axis_index("tp") * half, half, 0)


def other_half(values):
    half = values.shape[0] // 2
    return lax.dynamic_slice_in_dim(values, (1 - lax.axis_index("tp")) * half, half, 0)


def member_groups(size, experts):
    span = 2 * experts
    starts = range(0, size, span)
    cores = [[start + 2 * e, start + 2 * e + 1] for start in starts for e in range(experts)]
    across = [[start + r for start in starts] for r in range(span)]
    return cores, across


def own_core(values, rows):
    parts = values.reshape(-1, 2, rows, values.shape[-1])
    return lax.dynamic_index_in_dim(parts, lax.axis_index("fsdp") % 2, 1, keepdims=False)


def join_weights(got, experts):
    size = lax.axis_size("fsdp")
    if size == 2 * experts:
        return got
    cores, across = member_groups(size, experts)
    got = lax.all_gather(got, "fsdp", axis=1, axis_index_groups=cores, tiled=True)
    got = got.reshape(-1, got.shape[-1])
    got = lax.all_gather(got, "fsdp", axis=0, axis_index_groups=across, tiled=True)
    return own_core(got, got.shape[0] // (2 * experts))


def split_grads(grads):
    experts, _, columns = grads.shape
    size = lax.axis_size("fsdp")
    if size == 2 * experts:
        return grads
    cores, across = member_groups(size, experts)
    grads = lax.all_gather(grads[:, None], "fsdp", axis=1, axis_index_groups=cores, tiled=True)
    grads = grads.reshape(-1, columns)
    grads = lax.psum_scatter(
        grads, "fsdp", scatter_dimension=0, axis_index_groups=across, tiled=True
    )
    return own_core(grads, grads.shape[0] // (2 * experts))


def finish_plain(big, wqkv, other):
    heads_width = (big.shape[1] - PAIR) // 4
    reduced = wide(lax.psum_scatter(big, "fsdp", scatter_dimension=0, tiled=True))
    parts = reduced[:, : 3 * heads_width].reshape(-1, 3, heads_width).transpose(1, 0, 2)
    share = jnp.sum(parts * wide(wqkv), axis=(0, 2))
    last = jnp.concatenate([share[:, None], reduced[:, 4 * heads_width + 1 :]], axis=1)
    return (
        swap(other),
        reduced[:, : 4 * heads_width],
        own_half(last) + swap(other_half(last)),
    )


def forward_plain(operands, table):
    (
        hidden,
        cotangent,
        logits,
        routes,
        rank,
        dropped,
        gains,
        router,
        mixing,
        value,
        wqkv,
        wout,
        w_in,
        w_down,
    ) = operands
    own_rows, width = hidden.shape
    experts, shard, units = w_down.shape
    small = jnp.concatenate([wide(v) for v in (gains, router, mixing, value)], axis=0)
    small = jnp.pad(small, ((0, PAIR - small.shape[0]), (0, 0))).T
    small = lax.all_gather(small, ("fsdp", "tp"), axis=0, tiled=True)
    capacity = own_rows * 2 * 9 // 48
    kept = (routes < experts) & (dropped == 0)
    target = jnp.where(kept, routes * capacity + rank, -1)
    blank = jnp.zeros((2, own_rows), jnp.float32)
    tok = jnp.concatenate(
        [blank, logits, blank, blank, blank, wide(routes), blank, wide(target)], axis=0
    )
    tok = lax.all_gather(tok, "tp", axis=1, tiled=True).T
    tok = jnp.pad(tok, ((0, 0), (0, PAIR - tok.shape[1])))
    blocks = jnp.concatenate([wqkv[0], wqkv[1], wqkv[2], wout], axis=1)
    blocks = lax.all_gather(blocks, "fsdp", axis=0, tiled=True).reshape(2 * experts, -1, blocks.shape[1])
    rows = small.T[:8]
    small = low(small)
    shards_flat = jnp.concatenate([w_in.reshape(experts, shard, 2 * units), w_down], axis=2)
    return (blocks, small, rows) + tuple(
        run_forward_plain(
            gather_rows(hidden), tok, blocks, small, rows, table, shards_flat, cotangent
        )
    )


def nt_dot(left, right):
    return lax.dot_general(left, right, (((1,), (1,)), ((), ())), preferred_element_type=jnp.float32)


def nn_dot(left, right):
    return jnp.dot(left, right, preferred_element_type=jnp.float32)


def tn_dot(left, right):
    return lax.dot_general(left, right, (((0,), (0,)), ((), ())), preferred_element_type=jnp.float32)


def low(values):
    return values.astype(jnp.bfloat16)


def wide(values):
    return values.astype(jnp.float32)


def rotary_table(length):
    half = HD // 2
    positions = np.arange(length, dtype=np.float32)
    inverse = np.power(np.float32(10000.0), -np.arange(half, dtype=np.float32) / np.float32(half))
    angles = (positions[:, None] * inverse[None, :].astype(np.float32)).astype(np.float32)
    cosine = np.cos(angles.astype(np.float64)).astype(np.float32)
    sine = np.sin(angles.astype(np.float64)).astype(np.float32)
    both = np.concatenate([cosine, sine], axis=1)
    return np.concatenate([both[: length // 2], both[length // 2 :]], axis=1)


def spread_table(table_ref, block):
    quarter = HD // 2
    blocks = table_ref.shape[0] // BLOCK
    table = table_ref[block_rows(lax.rem(block, blocks)), :]
    table = jnp.where(block >= blocks, pltpu.roll(table, HD, 1), table)
    lane = lax.broadcasted_iota(jnp.int32, table.shape, 1)
    cosine = jnp.where(lane < quarter, table, 0.0)
    cosine = cosine + pltpu.roll(cosine, quarter, 1)
    sine = jnp.where(jnp.logical_and(lane >= quarter, lane < HD), table, 0.0)
    sine = sine - pltpu.roll(sine, PAIR - quarter, 1)
    return cosine + pltpu.roll(cosine, HD, 1), sine + pltpu.roll(sine, HD, 1)


def turn(values, cosine, sine):
    lane = lax.broadcasted_iota(jnp.int32, values.shape, 1)
    upper = lax.rem(lane, HD) >= HD // 2
    partner = jnp.where(
        upper, pltpu.roll(values, HD // 2, 1), pltpu.roll(values, PAIR - HD // 2, 1)
    )
    return values * cosine + partner * sine


def head_lanes(shape, half, axis):
    return (lax.broadcasted_iota(jnp.int32, shape, axis) >= HD) == bool(half)


def mean_last(values):
    return jnp.mean(values, axis=-1, keepdims=True)


def to_partner(source, target, send_sem, recv_sem):
    return pltpu.make_async_remote_copy(
        src_ref=source,
        dst_ref=target,
        send_sem=send_sem,
        recv_sem=recv_sem,
        device_id={"tp": 1 - lax.axis_index("tp")},
        device_id_type=MESH,
    )


def block_rows(block):
    return pl.ds(pl.multiple_of(block * BLOCK, BLOCK), BLOCK)


def column(values, index):
    return values[:, index : index + 1]


def lane_matrix(shape, columns):
    lane = lax.broadcasted_iota(jnp.int32, shape, 1)
    total = jnp.zeros(shape, jnp.float32)
    for index, values in columns:
        total = jnp.where(lane == index, values, total)
    return total


def send_to(source, target, send_sem, recv_sem, device):
    return pltpu.make_async_remote_copy(
        src_ref=source,
        dst_ref=target,
        send_sem=send_sem,
        recv_sem=recv_sem,
        device_id=device,
        device_id_type=MESH,
    )


def greet_group(peers):
    me = lax.axis_index("fsdp")
    rank = lax.rem(me, peers)
    barrier = pltpu.get_barrier_semaphore()
    for k in range(1, peers):
        pl.semaphore_signal(
            barrier,
            inc=1,
            device_id={"fsdp": me - rank + lax.rem(rank + k, peers)},
            device_id_type=MESH,
        )
    pl.semaphore_signal(
        barrier, inc=1, device_id={"tp": 1 - lax.axis_index("tp")}, device_id_type=MESH
    )
    pl.semaphore_wait(barrier, peers)


def each(first, last, body):
    def step(k, carry):
        body(k)
        return carry

    lax.fori_loop(first, last, step, 0)


def flipped(value, k, bits):
    other = 0
    bit = 1
    while bit < bits:
        ours, theirs = lax.rem(value // bit, 2), lax.rem(k // bit, 2)
        other = other + bit * (ours + theirs - 2 * ours * theirs)
        bit *= 2
    return other


class CoreExchange:
    def __init__(self, source, target, send_sem, recv_sem):
        experts = source.shape[0]
        me = lax.axis_index("fsdp")
        rank = lax.rem(me, 2 * experts)
        core = lax.rem(rank, 2)
        mine = rank // 2

        def device(k):
            return {"fsdp": me - rank + 2 * flipped(mine, k, experts) + core}

        def copy(k):
            there = flipped(mine, k, experts)
            return send_to(
                source.at[there], target.at[mine], send_sem.at[k], recv_sem.at[k], device(k)
            )

        def arrival(k):
            there = flipped(mine, k, experts)
            return send_to(
                source.at[there], target.at[there], send_sem.at[k], recv_sem.at[k], device(k)
            )

        self.experts, self.copy, self.arrival = experts, copy, arrival
        self.local = pltpu.make_async_copy(source.at[mine], target.at[mine], send_sem.at[0])

    def start(self, done=()):
        self.local.start()
        for k in range(1, self.experts):
            if k not in done:
                self.copy(k).start()

    def wait(self):
        each(1, self.experts, lambda k: self.copy(k).wait_send())
        each(1, self.experts, lambda k: self.arrival(k).wait_recv())
        self.local.wait()


def sum_stages(
    big_ref,
    wqkv_ref,
    other_ref,
    y_ref,
    red_ref,
    tail_ref,
    sum_ref,
    core_ref,
    side_ref,
    acc_ref,
    usend_ref,
    urecv_ref,
    dsend_ref,
    drecv_ref,
    tsend_ref,
    trecv_ref,
    core_send,
    core_recv,
    x_send,
    x_recv,
    up_send,
    up_recv,
    dn_send,
    dn_recv,
    y_send,
    y_recv,
):
    size = big_ref.shape[0]
    subs = big_ref.shape[1] // SUB
    planes = size // 4
    me = lax.axis_index("fsdp")
    tp = lax.axis_index("tp")
    z, x, core = me // 4, lax.rem(me // 2, 2), lax.rem(me, 2)
    heads_width = wqkv_ref.shape[2]
    partner = {"tp": 1 - tp}

    def to_core(plane, line):
        slot = plane * 2 + line
        return send_to(
            big_ref.at[plane * 4 + line * 2 + 1 - core],
            core_ref.at[slot],
            core_send.at[slot],
            core_recv.at[slot],
            {"fsdp": me + 1 - 2 * core},
        )

    def band(sub):
        return pl.ds(pl.multiple_of(sub * SUB, SUB), SUB)

    def to_side(plane, sub):
        slot = plane * subs + sub
        return send_to(
            sum_ref.at[plane, band(sub)],
            side_ref.at[plane, band(sub)],
            x_send.at[slot],
            x_recv.at[slot],
            {"fsdp": z * 4 + (1 - x) * 2 + core},
        )

    def to_up(plane, sub):
        slot = plane * subs + sub
        return send_to(
            usend_ref.at[plane, band(sub)],
            urecv_ref.at[plane, band(sub)],
            up_send.at[slot],
            up_recv.at[slot],
            {"fsdp": lax.min(z + 1, planes - 1) * 4 + x * 2 + core},
        )

    def to_down(plane, sub):
        slot = plane * subs + sub
        return send_to(
            dsend_ref.at[plane, band(sub)],
            drecv_ref.at[plane, band(sub)],
            dn_send.at[slot],
            dn_recv.at[slot],
            {"fsdp": lax.max(z - 1, 0) * 4 + x * 2 + core},
        )

    lower = z < planes // 2
    order = [jnp.where(lower, planes - 1 - step, step) for step in range(planes)]
    out_y = send_to(other_ref, y_ref, y_send.at[0], y_recv.at[0], partner)
    def joined(plane, line):
        to_core(plane, line).wait_recv()
        return wide(big_ref[plane * 4 + line * 2 + core]) + wide(core_ref[plane * 2 + line])

    def rise(plane, sub):
        @pl.when(z < plane)
        def _():
            @pl.when(z > 0)
            def _():
                to_up(plane, sub).wait_recv()
                acc_ref[plane, band(sub)] += wide(urecv_ref[plane, band(sub)])

            usend_ref[plane, band(sub)] = low(acc_ref[plane, band(sub)])
            to_up(plane, sub).start()

    def fall(plane, sub):
        @pl.when(z > plane)
        def _():
            @pl.when(z < planes - 1)
            def _():
                to_down(plane, sub).wait_recv()
                acc_ref[plane, band(sub)] += wide(drecv_ref[plane, band(sub)])

            dsend_ref[plane, band(sub)] = low(acc_ref[plane, band(sub)])
            to_down(plane, sub).start()

    def begin():
        for plane in order:
            to_core(plane, 1 - x).start()
        for plane in order:
            to_core(plane, x).start()
        out_y.start()

        for plane in order:
            sum_ref[plane] = low(joined(plane, 1 - x))
            each(0, subs, lambda sub: to_side(plane, sub).start())
        for plane in order:
            acc_ref[plane] = joined(plane, x)

    def end():
        for step, plane in enumerate(order):
            last_step = step == planes - 1

            def advance(sub):
                to_side(plane, sub).wait_recv()
                acc_ref[plane, band(sub)] += wide(side_ref[plane, band(sub)])

                @pl.when(lower)
                def _():
                    (fall if last_step else rise)(plane, sub)

                @pl.when(jnp.logical_not(lower))
                def _():
                    (rise if last_step else fall)(plane, sub)

            each(0, subs, advance)

        @pl.when(z > 0)
        def _():
            each(0, subs, lambda sub: to_up(z, sub).wait_recv())
            acc_ref[z] += wide(urecv_ref[z])

        @pl.when(z < planes - 1)
        def _():
            each(0, subs, lambda sub: to_down(z, sub).wait_recv())
            acc_ref[z] += wide(drecv_ref[z])

        values = acc_ref[z]
        red_ref[...] = values[:, : 4 * heads_width]
        share = sum(
            jnp.sum(
                values[:, part * heads_width : (part + 1) * heads_width] * wide(wqkv_ref[part]),
                axis=1,
                keepdims=True,
            )
            for part in range(3)
        )
        last = values[:, 4 * heads_width :]
        last = jnp.where(lax.broadcasted_iota(jnp.int32, last.shape, 1) == 0, share, last)
        part_rows = tail_ref.shape[0]
        tsend_ref[0] = last[:part_rows, :]
        tsend_ref[1] = last[part_rows:, :]
        tail_y = send_to(tsend_ref.at[1 - tp], trecv_ref, y_send.at[1], y_recv.at[1], partner)
        tail_y.start()
        out_y.wait()
        tail_y.wait()
        tail_ref[...] = tsend_ref[tp] + trecv_ref[...]
        for plane in range(planes):
            to_core(plane, 1 - x).wait_send()
            to_core(plane, x).wait_send()

            def drain(sub):
                to_side(plane, sub).wait_send()

                @pl.when(z < plane)
                def _():
                    to_up(plane, sub).wait_send()

                @pl.when(z > plane)
                def _():
                    to_down(plane, sub).wait_send()

            each(0, subs, drain)

    return begin, end


def sum_scratch(planes, shard, columns):
    low_t, wide_t = jnp.bfloat16, jnp.float32
    dma = pltpu.SemaphoreType.DMA
    line = (planes, shard, columns)
    return (
        [
            pltpu.VMEM(line, low_t),
            pltpu.VMEM((2 * planes, shard, columns), low_t),
            pltpu.VMEM(line, low_t),
            pltpu.VMEM(line, wide_t),
            pltpu.VMEM(line, low_t),
            pltpu.VMEM(line, low_t),
            pltpu.VMEM(line, low_t),
            pltpu.VMEM(line, low_t),
            pltpu.VMEM((2, shard // 2, PAIR), wide_t),
            pltpu.VMEM((shard // 2, PAIR), wide_t),
            dma((2 * planes,)),
            dma((2 * planes,)),
        ]
        + [dma((planes * (shard // SUB),))] * 6
        + [dma((2,))] * 2
    )


def write_kernel(
    base_ref,
    y_ref,
    grad_ref,
    red_ref,
    tail_ref,
    gain_ref,
    expert_ref,
    out_ref,
    hidden_ref,
    qkv_ref,
    attn_ref,
    gains_ref,
    router_ref,
    mixing_ref,
    value_ref,
    in_ref,
    down_ref,
):
    hidden = down_ref.shape[2]
    heads_width = attn_ref.shape[1]
    out_ref[...] = low(base_ref[...] + wide(y_ref[...]))
    hidden_ref[...] = grad_ref[...]

    def lay_out(e):
        values = wide(expert_ref[e])
        in_ref[e, :, 0, :] = values[:, :hidden]
        in_ref[e, :, 1, :] = values[:, hidden : 2 * hidden]
        down_ref[e] = values[:, 2 * hidden :]

    each(0, expert_ref.shape[0], lay_out)

    @pl.when(pl.program_id(0) == 0)
    def _():
        for part in range(3):
            qkv_ref[part] = red_ref[:, part * heads_width : (part + 1) * heads_width]
        attn_ref[...] = red_ref[:, 3 * heads_width :]
        count = tail_ref.shape[0]
        blank = jnp.zeros((PAIR - count, PAIR), jnp.float32)
        turned = jnp.concatenate([tail_ref[...], blank], axis=0).T[:, :count]
        gains_ref[0:1, :] = turned[0:1, :] / gain_ref[0:1, :]
        gains_ref[1:2, :] = turned[1:2, :]
        router_ref[...] = turned[ROUTER:MIXING, :]
        mixing_ref[...] = turned[MIXING:VALUE, :]
        value_ref[...] = turned[VALUE : VALUE + 2, :]


def run_write(base, y, grad_hidden, red, tail, gains, arrived):
    own_rows, width = base.shape
    shard = red.shape[0]
    heads_width = red.shape[1] // 4
    count = tail.shape[0]
    experts, _, total = arrived.shape
    hidden = total // 3
    wide_t = jnp.float32
    steps = experts // 2
    rows = pl.BlockSpec((own_rows // steps, width), lambda e: (e, 0))

    def whole(shape):
        return pl.BlockSpec(shape, lambda e: (0,) * len(shape))

    return pl.pallas_call(
        write_kernel,
        grid=(steps,),
        in_specs=[
            rows,
            rows,
            rows,
            whole(red.shape),
            whole(tail.shape),
            whole(gains.shape),
            pl.BlockSpec((2, shard, total), lambda e: (e, 0, 0)),
        ],
        out_specs=[
            rows,
            rows,
            whole((3, shard, heads_width)),
            whole((shard, heads_width)),
            whole((2, count)),
            whole((MIXING - ROUTER, count)),
            whole((VALUE - MIXING, count)),
            whole((2, count)),
            pl.BlockSpec((2, shard, 2, hidden), lambda e: (e, 0, 0, 0)),
            pl.BlockSpec((2, shard, hidden), lambda e: (e, 0, 0)),
        ],
        out_shape=[
            jax.ShapeDtypeStruct((own_rows, width), jnp.bfloat16),
            jax.ShapeDtypeStruct((own_rows, width), wide_t),
            jax.ShapeDtypeStruct((3, shard, heads_width), wide_t),
            jax.ShapeDtypeStruct((shard, heads_width), wide_t),
            jax.ShapeDtypeStruct((2, count), wide_t),
            jax.ShapeDtypeStruct((MIXING - ROUTER, count), wide_t),
            jax.ShapeDtypeStruct((VALUE - MIXING, count), wide_t),
            jax.ShapeDtypeStruct((2, count), wide_t),
            jax.ShapeDtypeStruct((experts, shard, 2, hidden), wide_t),
            jax.ShapeDtypeStruct((experts, shard, hidden), wide_t),
        ],
    )(base, y, grad_hidden, red, tail, gains, arrived)


def expert_kernel(
    s2_ref,
    cot_ref,
    line_ref,
    slot_ref,
    weight_ref,
    res_out_ref,
    dx_out_ref,
    grads_out_ref,
    xs_ref,
    gs_ref,
    x_ref,
    g_ref,
    w_ref,
    gate_ref,
    up_ref,
    act_ref,
    xt_ref,
    gt_ref,
    acc_ref,
    grads_ref,
    sibling_ref,
    ysend_ref,
    yrecv_ref,
    w_sem,
    grad_sem,
    xs_sem,
    xr_sem,
    gs_sem,
    gr_sem,
    xfs_sem,
    xfr_sem,
    gfs_sem,
    gfr_sem,
    ys_sem,
    yr_sem,
    rs_sem,
    rr_sem,
    ds_sem,
    dr_sem,
):
    peers, rows, width = xs_ref.shape
    total = peers * rows
    hidden = gate_ref.shape[1]
    tiles = hidden // TILE
    me = lax.axis_index("fsdp")
    tp = lax.axis_index("tp")
    rank = lax.rem(me, peers)
    core = lax.rem(rank, 2)
    start = me - rank

    def peer(k):
        return {"fsdp": start + flipped(rank, k, peers)}

    partner = {"tp": 1 - tp}
    sibling = {"fsdp": start + rank + 1 - 2 * core}

    def out_x(k):
        return send_to(xs_ref.at[k], x_ref.at[0, k], xs_sem.at[k], xr_sem.at[k], peer(k))

    def out_g(k):
        return send_to(gs_ref.at[k], g_ref.at[0, k], gs_sem.at[k], gr_sem.at[k], peer(k))

    def pass_x(k):
        return send_to(x_ref.at[0, k], x_ref.at[1, k], xfs_sem.at[k], xfr_sem.at[k], partner)

    def pass_g(k):
        return send_to(g_ref.at[0, k], g_ref.at[1, k], gfs_sem.at[k], gfr_sem.at[k], partner)

    def across(index, k):
        return send_to(
            ysend_ref.at[index, k],
            yrecv_ref.at[index, k],
            ys_sem.at[index, k],
            yr_sem.at[index, k],
            partner,
        )

    def back(index, k):
        if index == 0:
            return send_to(xs_ref.at[k], res_out_ref.at[k], rs_sem.at[k], rr_sem.at[k], peer(k))
        return send_to(gs_ref.at[k], dx_out_ref.at[k], ds_sem.at[k], dr_sem.at[k], peer(k))

    def return_order(body):
        def step(j, carry):
            body(8 + 2 * j)
            body(4 + j)
            body(9 + 2 * j)
            return carry

        lax.fori_loop(0, 4, step, 0)
        for k in (2, 3, 1, 0):
            body(k)

    def turn_rows(source, target, m):
        target[:, pl.ds(pl.multiple_of(m * total, total), total)] = (
            source[m].reshape(total, width).T
        )

    def join(index, k):
        across(index, k).wait_recv()
        own = xs_ref if index == 0 else gs_ref
        own[k] = low(wide(own[k]) + wide(yrecv_ref[index, k]))
        back(index, k).start()

    def join_some(index, tile):
        join(index, 8 + 2 * tile)
        join(index, 4 + tile)
        join(index, 9 + 2 * tile)

    def join_last(index):
        for k in (2, 3, 1):
            join(index, k)
        across(index, 0).wait_recv()
        own, target = (xs_ref, res_out_ref) if index == 0 else (gs_ref, dx_out_ref)
        target[0] = low(wide(own[0]) + wide(yrecv_ref[index, 0]))

    greet_group(peers)
    here = pltpu.make_async_copy(weight_ref, w_ref.at[:, core], w_sem.at[0])
    here.start()
    there = send_to(weight_ref, w_ref.at[:, core], w_sem.at[1], w_sem.at[2], sibling)
    half = total // 2
    group = peers // 2

    def hits_of(part):
        ids = slot_ref[pl.ds(pl.multiple_of(part * half, half), half), 0:1]
        return [line_ref[m : m + 1, :] == ids for m in range(2)]

    def pack_x(part):
        hits = hits_of(part)
        onehot = low(jnp.where(hits[0] | hits[1], 1.0, 0.0))
        xs_ref[pl.ds(part * group, group)] = low(nn_dot(onehot, s2_ref[...])).reshape(
            group, rows, width
        )

        @pl.when(part == 0)
        def _():
            x_ref[0, 0] = xs_ref[0]
            pass_x(0).start()

        def launch(k):
            @pl.when(k > 0)
            def _():
                out_x(k).start()

        each(part * group, (part + 1) * group, launch)

    def pack_g(part):
        hits = hits_of(part)
        onehot = low(jnp.where(hits[0] | hits[1], 1.0, 0.0))
        gate = sum(
            jnp.sum(jnp.where(hits[m], line_ref[2 + m : 3 + m, :], 0.0), axis=1, keepdims=True)
            for m in range(2)
        )
        gs_ref[pl.ds(part * group, group)] = low(nn_dot(onehot, cot_ref[...]) * gate).reshape(
            group, rows, width
        )

        @pl.when(part == 0)
        def _():
            g_ref[0, 0] = gs_ref[0]

        def launch(k):
            @pl.when(k > 0)
            def _():
                out_g(k).start()

        each(part * group, (part + 1) * group, launch)

    each(0, 2, pack_x)
    there.start()
    each(0, 2, pack_g)

    def forward_x(k):
        out_x(k).wait_recv()
        pass_x(k).start()

    each(1, peers, forward_x)
    pass_g(0).start()
    here.wait()
    send_to(weight_ref, w_ref.at[:, 1 - core], w_sem.at[1], w_sem.at[2], sibling).wait_recv()
    there.wait_send()
    each(0, peers, lambda k: pass_x(k).wait_recv())

    def weights(which, lanes):
        return w_ref[:, :, :, pl.ds(pl.multiple_of(which * hidden + lanes, TILE), TILE)].reshape(
            width, TILE
        )

    acc_ref[...] = jnp.zeros_like(acc_ref)

    def forward_tile(tile, carry):
        lanes = pl.multiple_of(tile * TILE, TILE)
        here_lanes = pl.ds(lanes, TILE)

        def one_half(m):
            band = pl.ds(pl.multiple_of(m * total, total), total)
            x = x_ref[m].reshape(total, width)
            gate = nn_dot(x, weights(0, lanes))
            up = nn_dot(x, weights(1, lanes))
            gate_ref[band, here_lanes] = low(gate)
            up_ref[band, here_lanes] = low(up)
            act = low(gate / (1.0 + jnp.exp(-gate)) * up)
            act_ref[band, here_lanes] = act
            acc_ref[band, :] += nt_dot(act, weights(2, lanes))

        each(0, 2, one_half)

        def forward_g(k):
            @pl.when(k > 0)
            def _():
                out_g(k).wait_recv()
                pass_g(k).start()

        each(tile * (peers // tiles), (tile + 1) * (peers // tiles), forward_g)
        return carry

    lax.fori_loop(0, tiles, forward_tile, 0)
    each(1, peers, lambda k: out_x(k).wait_send())
    xs_ref[...] = low(acc_ref[:total, :]).reshape(peers, rows, width)
    ysend_ref[0] = low(acc_ref[total:, :]).reshape(peers, rows, width)
    return_order(lambda k: across(0, k).start())
    each(0, 2, lambda m: turn_rows(x_ref, xt_ref, m))
    acc_ref[...] = jnp.zeros_like(acc_ref)
    each(0, peers, lambda k: pass_g(k).wait_recv())

    def slope_tile(tile, carry):
        lanes = pl.multiple_of(tile * TILE, TILE)
        here_lanes = pl.ds(lanes, TILE)

        def one_half(m):
            band = pl.ds(pl.multiple_of(m * total, total), total)
            gate = wide(gate_ref[band, here_lanes])
            up = wide(up_ref[band, here_lanes])
            sig = 1.0 / (1.0 + jnp.exp(-gate))
            d_act = nn_dot(g_ref[m].reshape(total, width), weights(2, lanes))
            d_up = low(d_act * gate * sig)
            d_gate = low(d_act * up * sig * (1.0 + gate * (1.0 - sig)))
            gate_ref[band, here_lanes] = d_gate
            up_ref[band, here_lanes] = d_up
            acc_ref[band, :] += nt_dot(d_gate, weights(0, lanes)) + nt_dot(
                d_up, weights(1, lanes)
            )

        each(0, 2, one_half)
        join_some(0, tile)
        return carry

    lax.fori_loop(0, tiles, slope_tile, 0)
    join_last(0)
    each(1, peers, lambda k: out_g(k).wait_send())
    gs_ref[...] = low(acc_ref[:total, :]).reshape(peers, rows, width)
    ysend_ref[1] = low(acc_ref[total:, :]).reshape(peers, rows, width)
    return_order(lambda k: across(1, k).start())
    each(0, 2, lambda m: turn_rows(g_ref, gt_ref, m))

    def weight_tile(tile, carry):
        lanes = pl.multiple_of(tile * TILE, TILE)
        here_lanes = pl.ds(lanes, TILE)

        def keep(which, values):
            grads_ref[
                :, :, :, pl.ds(pl.multiple_of(which * hidden + lanes, TILE), TILE)
            ] = low(values).reshape(peers // 2, 2, rows, TILE)

        keep(0, nn_dot(xt_ref[...], gate_ref[:, here_lanes]))
        keep(1, nn_dot(xt_ref[...], up_ref[:, here_lanes]))
        keep(2, nn_dot(gt_ref[...], act_ref[:, here_lanes]))
        join_some(1, tile)
        return carry

    lax.fori_loop(0, tiles, weight_tile, 0)
    swap_grads = send_to(
        grads_ref.at[:, 1 - core], sibling_ref, grad_sem.at[0], grad_sem.at[1], sibling
    )
    swap_grads.start()
    join_last(1)
    each(0, peers, lambda k: pass_x(k).wait_send())
    each(0, peers, lambda k: pass_g(k).wait_send())
    for index in range(2):
        each(0, peers, lambda k: across(index, k).wait_send())
        each(1, peers, lambda k: back(index, k).wait_send())
    swap_grads.wait()
    grads_out_ref[...] = low(wide(grads_ref[:, core]) + wide(sibling_ref[...]))
    for index in range(2):
        each(1, peers, lambda k: back(index, k).wait_recv())


def run_expert(s2, cot, lines, slots, weights):
    length, width = s2.shape
    experts, shard, total = weights.shape
    peers = 2 * experts
    rows = slots.shape[0] // peers
    hidden = total // 3
    both = 2 * peers * rows
    vmem = pl.BlockSpec(memory_space=pltpu.VMEM)
    low_t, wide_t = jnp.bfloat16, jnp.float32
    dma = pltpu.SemaphoreType.DMA
    block = (peers, rows, width)
    return pl.pallas_call(
        expert_kernel,
        in_specs=[vmem] * 4 + [pl.BlockSpec(memory_space=pl.ANY)],
        out_specs=[vmem] * 3,
        out_shape=[
            jax.ShapeDtypeStruct(block, low_t),
            jax.ShapeDtypeStruct(block, low_t),
            jax.ShapeDtypeStruct(weights.shape, low_t),
        ],
        scratch_shapes=[
            pltpu.VMEM(block, low_t),
            pltpu.VMEM(block, low_t),
            pltpu.VMEM((2,) + block, low_t),
            pltpu.VMEM((2,) + block, low_t),
            pltpu.VMEM((experts, 2, shard, total), low_t),
            pltpu.VMEM((both, hidden), low_t),
            pltpu.VMEM((both, hidden), low_t),
            pltpu.VMEM((both, hidden), low_t),
            pltpu.VMEM((width, both), low_t),
            pltpu.VMEM((width, both), low_t),
            pltpu.VMEM((both, width), wide_t),
            pltpu.VMEM((experts, 2, shard, total), low_t),
            pltpu.VMEM((experts, shard, total), low_t),
            pltpu.VMEM((2,) + block, low_t),
            pltpu.VMEM((2,) + block, low_t),
            dma((3,)),
            dma((2,)),
        ]
        + [dma((peers,))] * 8
        + [dma((2, peers))] * 2
        + [dma((peers,))] * 4,
        compiler_params=pltpu.CompilerParams(
            collective_id=2, has_side_effects=True, vmem_limit_bytes=67043328
        ),
    )(s2, cot, lines, slots, weights)


def attend(
    hid_ref,
    token_block,
    weight,
    small_ref,
    gains,
    table_ref,
    s1_ref,
    qkv_ref,
    lse_ref,
    mixed_ref,
    mid_ref,
    s2_ref,
    tok_ref,
    line_ref,
    vt_ref,
    send_ref,
    recv_ref,
    send_sem,
    recv_sem,
    between,
):
    blocks = hid_ref.shape[0] // BLOCK
    heads_width = mixed_ref.shape[1]
    pairs = heads_width // PAIR
    gain_one, gain_two = gains
    lse_ref[...] = jnp.zeros_like(lse_ref)

    def copy(block):
        return to_partner(
            send_ref.at[block], recv_ref.at[block], send_sem.at[block], recv_sem.at[block]
        )

    def compute(block):
        rows = block_rows(block)
        source = wide(hid_ref[rows, :])
        s1 = low(source * lax.rsqrt(mean_last(source * source) + EPSILON) * gain_one)
        s1_ref[rows, :] = s1
        cosine, sine = spread_table(table_ref, block)
        for part in range(3):
            projected = nn_dot(s1, weight(part))
            for pair in range(pairs):
                chunk = projected[:, pair * PAIR : (pair + 1) * PAIR]
                if part < 2:
                    chunk = turn(chunk, cosine, sine)
                else:
                    vt_ref[pair * PAIR : (pair + 1) * PAIR, rows] = low(chunk.T)
                start = part * heads_width + pair * PAIR
                qkv_ref[rows, start : start + PAIR] = low(chunk)

        def one_pair(keys, pair):
            start = pl.multiple_of(pair * PAIR, PAIR)
            lanes = pl.ds(start, PAIR)
            key_lanes = pl.ds(pl.multiple_of(heads_width + start, PAIR), PAIR)
            query = qkv_ref[rows, lanes] * jnp.bfloat16(SCALING)
            key = qkv_ref[:keys, key_lanes]
            value_t = vt_ref[lanes, :keys]
            gathered = None
            for half in range(2):
                masked = jnp.where(head_lanes(query.shape, half, 1), query, jnp.bfloat16(0))
                scores = nt_dot(key, masked)
                highest = jnp.max(scores, axis=0, keepdims=True)
                expanded = jnp.exp(scores - highest)
                totals = jnp.sum(expanded, axis=0, keepdims=True)
                probs = low(expanded * (1.0 / totals))
                lse_ref[pl.ds(2 * pair + half, 1), rows] = highest + jnp.log(totals)
                found = nn_dot(value_t, probs)
                gathered = (
                    found
                    if half == 0
                    else jnp.where(head_lanes(found.shape, 1, 0), found, gathered)
                )
            mixed_ref[rows, lanes] = low(gathered.T)

        for static in range(blocks):

            @pl.when(block == static)
            def _():
                each(0, pairs, functools.partial(one_pair, (static + 1) * BLOCK))

        send_ref[block] = low(nt_dot(mixed_ref[rows, :], weight(3)))
        copy(block).start()

    def finish(block):
        rows = block_rows(block)
        copy(block).wait()
        mid = wide(hid_ref[rows, :]) + (wide(send_ref[block]) + wide(recv_ref[block]))
        mid_ref[rows, :] = mid
        s2 = low(mid * lax.rsqrt(mean_last(mid * mid) + EPSILON) * gain_two)
        s2_ref[rows, :] = s2
        tok = token_block(block)
        lane = lax.broadcasted_iota(jnp.int32, tok.shape, 1)
        logits = nn_dot(s2, small_ref[...]) + tok
        picked = [
            jnp.sum(
                jnp.where(wide(lane - ROUTER) == column(tok, ROUTE + member), logits, 0.0),
                axis=1,
                keepdims=True,
            )
            for member in range(2)
        ]
        gate = [
            1.0 / (1.0 + jnp.exp(picked[1 - member] - picked[member])) for member in range(2)
        ]
        tok = jnp.where(lane == GATE, gate[0], jnp.where(lane == GATE + 1, gate[1], tok))
        tok_ref[rows, :] = tok
        line_ref[:, rows] = tok.T[TARGET : TARGET + 8, :]

    each(0, blocks, compute)
    between()
    each(0, blocks, finish)


def forward_plain_kernel(
    hid_ref,
    tok_in_ref,
    block_ref,
    small_ref,
    rows_ref,
    table_ref,
    shard_ref,
    cot_own_ref,
    s1_ref,
    qkv_ref,
    lse_ref,
    mixed_ref,
    mid_ref,
    s2_ref,
    tok_ref,
    line_ref,
    expert_ref,
    cot_ref,
    vt_ref,
    send_ref,
    recv_ref,
    send_sem,
    recv_sem,
    wsend_sem,
    wrecv_sem,
    cot_sem,
):
    greet_group(2 * shard_ref.shape[0])
    own_rows = cot_own_ref.shape[0]
    heads_width = mixed_ref.shape[1]
    width = hid_ref.shape[1]
    mine = pl.ds(pl.multiple_of(lax.axis_index("tp") * own_rows, own_rows), own_rows)
    cot_copy = to_partner(cot_own_ref, cot_ref.at[mine], cot_sem.at[0], cot_sem.at[1])
    cot_copy.start()
    experts = CoreExchange(shard_ref, expert_ref, wsend_sem, wrecv_sem)
    experts.start()
    cot_ref[mine, :] = cot_own_ref[...]

    def weight(part):
        return block_ref[:, :, part * heads_width : (part + 1) * heads_width].reshape(
            width, heads_width
        )

    attend(
        hid_ref,
        lambda block: tok_in_ref[block_rows(block), :],
        weight,
        small_ref,
        (rows_ref[0:1, :], rows_ref[1:2, :]),
        table_ref,
        s1_ref,
        qkv_ref,
        lse_ref,
        mixed_ref,
        mid_ref,
        s2_ref,
        tok_ref,
        line_ref,
        vt_ref,
        send_ref,
        recv_ref,
        send_sem,
        recv_sem,
        lambda: None,
    )
    cot_copy.wait()
    experts.wait()


def forward_kernel(
    hid_own_ref,
    cot_own_ref,
    logit_ref,
    route_ref,
    rank_ref,
    drop_ref,
    gain_ref,
    router_ref,
    mixing_ref,
    value_ref,
    wqkv_ref,
    wout_ref,
    win_ref,
    wdown_ref,
    table_ref,
    all_out,
    small_ref,
    rows_ref,
    s1_out,
    qkv_out,
    lse_ref,
    mixed_out,
    mid_ref,
    s2_ref,
    tok_ref,
    line_ref,
    expert_ref,
    cot_out,
    all_ref,
    s1_ref,
    qkv_ref,
    mixed_ref,
    cot_ref,
    hid_ref,
    vt_ref,
    send_ref,
    recv_ref,
    shard_ref,
    stage_ref,
    small_all_ref,
    tok_all_ref,
    send_sem,
    recv_sem,
    wsend_sem,
    wrecv_sem,
    y_send,
    y_recv,
    up_send,
    up_recv,
    down_send,
    down_recv,
    x_send,
    x_recv,
    core_send,
    core_recv,
    store_sem,
):
    size, shard, _ = all_ref.shape
    planes = size // 4
    me = lax.axis_index("fsdp")
    tp = lax.axis_index("tp")
    z, x, core = me // 4, lax.rem(me // 2, 2), lax.rem(me, 2)
    own_rows, width = hid_own_ref.shape
    heads_width = wout_ref.shape[1]
    small_rows = shard // 2
    greet_group(size)
    partner = {"tp": 1 - tp}
    mine = pl.ds(pl.multiple_of(tp * own_rows, own_rows), own_rows)
    hid_y = send_to(hid_own_ref, hid_ref.at[mine], y_send.at[1], y_recv.at[1], partner)
    stage_ref[...] = jnp.zeros_like(stage_ref)
    stage_ref[0:2, :small_rows] = gain_ref[...]
    stage_ref[ROUTER:MIXING, :small_rows] = wide(router_ref[...])
    stage_ref[MIXING:VALUE, :small_rows] = wide(mixing_ref[...])
    stage_ref[VALUE : VALUE + 2, :small_rows] = wide(value_ref[...])
    small_all_ref[me, tp] = stage_ref[...].T[:small_rows, :]
    small_y = send_to(
        small_all_ref.at[me, tp], small_all_ref.at[me, tp], y_send.at[0], y_recv.at[0], partner
    )
    small_y.start()
    hid_y.start()
    for part in range(3):
        all_ref[me, :, part * heads_width : (part + 1) * heads_width] = wqkv_ref[part]
    all_ref[me, :, 3 * heads_width :] = wout_ref[...]
    tok_y = send_to(tok_all_ref.at[tp], tok_all_ref.at[tp], y_send.at[2], y_recv.at[2], partner)

    def cot_copy(part):
        count = own_rows // 4
        near = pl.ds(part * count, count)
        far = pl.ds(pl.multiple_of(tp * own_rows + part * count, count), count)
        return send_to(
            cot_own_ref.at[near], cot_ref.at[far], y_send.at[3 + part], y_recv.at[3 + part], partner
        )

    experts = CoreExchange(shard_ref, expert_ref, wsend_sem, wrecv_sem)
    expert_count, _, hidden = wdown_ref.shape

    def stage_tokens():
        tok_all_ref[tp] = jnp.zeros(tok_all_ref.shape[1:], jnp.float32)
        routes = route_ref[...]
        kept = jnp.logical_and(routes < expert_count, drop_ref[...] == 0)
        target = jnp.where(kept, routes * (own_rows * 2 * 9 // 48) + rank_ref[...], -1)
        tok_all_ref[tp, ROUTER:MIXING, :] = logit_ref[...]
        tok_all_ref[tp, ROUTE : ROUTE + 2, :] = wide(routes)
        tok_all_ref[tp, TARGET : TARGET + 2, :] = wide(target)

    def stage_shard():
        def one(e):
            for part in range(2):
                shard_ref[e, :, part * hidden : (part + 1) * hidden] = win_ref[e, :, part, :]
            shard_ref[e, :, 2 * hidden :] = wdown_ref[e]

        each(0, expert_count, one)

    def number(plane, line):
        return plane * 4 + line * 2 + core

    def piece(kind, number_of, send, recv, slot, device):
        array = small_all_ref if kind else all_ref
        return send_to(
            array.at[number_of],
            array.at[number_of],
            send.at[kind, slot],
            recv.at[kind, slot],
            device,
        )

    def up(kind, step, plane):
        device = {"fsdp": number(lax.min(z + 1, planes - 1), x)}
        return piece(kind, number(plane, x), up_send, up_recv, step, device)

    def down(kind, step, plane):
        device = {"fsdp": number(lax.max(z - 1, 0), x)}
        return piece(kind, number(plane, x), down_send, down_recv, step, device)

    def side(kind, plane, line):
        device = {"fsdp": number(z, 1 - x)}
        return piece(kind, number(plane, line), x_send, x_recv, plane, device)

    def sibling(kind, plane, line, parity):
        return piece(
            kind,
            plane * 4 + line * 2 + parity,
            core_send,
            core_recv,
            plane * 2 + line,
            {"fsdp": me + 1 - 2 * core},
        )

    def launch(kind):
        @pl.when(z < planes - 1)
        def _():
            up(kind, 0, z).start()

        @pl.when(z > 0)
        def _():
            down(kind, 0, z).start()

        side(kind, z, x).start()
        sibling(kind, z, x, core).start()

    launch(0)
    stage_tokens()
    tok_y.start()
    for part in range(4):
        cot_copy(part).start()
    hid_ref[mine, :] = hid_own_ref[...]
    cot_ref[mine, :] = cot_own_ref[...]
    small_y.wait()
    launch(1)
    stage_shard()
    for step in range(1, planes):
        for kind in range(2):

            @pl.when(z >= step)
            def _():
                up(kind, step - 1, z - step).wait_recv()

                @pl.when(z < planes - 1)
                def _():
                    up(kind, step, z - step).start()

                side(kind, z - step, x).start()
                sibling(kind, z - step, x, core).start()

            @pl.when(z + step < planes)
            def _():
                down(kind, step - 1, z + step).wait_recv()

                @pl.when(z > 0)
                def _():
                    down(kind, step, z + step).start()

                side(kind, z + step, x).start()
                sibling(kind, z + step, x, core).start()

    experts.start()
    for step in range(planes):
        for kind in range(2):

            @pl.when(z >= step)
            def _():
                side(kind, z - step, 1 - x).wait_recv()
                sibling(kind, z - step, 1 - x, core).start()

            if step > 0:

                @pl.when(z + step < planes)
                def _():
                    side(kind, z + step, 1 - x).wait_recv()
                    sibling(kind, z + step, 1 - x, core).start()

    for plane in range(planes):
        for line in range(2):
            for kind in range(2):
                sibling(kind, plane, line, 1 - core).wait_recv()
    small_all = small_all_ref[...].reshape(width, PAIR)
    small_ref[...] = low(small_all)
    rows_ref[...] = small_all.T[:8, :]
    tok_y.wait()
    hid_y.wait()

    def token_block(block):
        per = own_rows // BLOCK
        lanes = pl.ds(pl.multiple_of(lax.rem(block, per) * BLOCK, BLOCK), BLOCK)
        part = tok_all_ref[block // per, :, lanes]
        blank = jnp.zeros((PAIR - part.shape[0], BLOCK), jnp.float32)
        return jnp.concatenate([part, blank], axis=0).T

    def weight(part):
        return all_ref[:, :, part * heads_width : (part + 1) * heads_width].reshape(
            width, heads_width
        )

    stores = [
        pltpu.make_async_copy(source, target, store_sem.at[index])
        for index, (source, target) in enumerate(
            [
                (all_ref, all_out),
                (s1_ref, s1_out),
                (qkv_ref, qkv_out),
                (mixed_ref, mixed_out),
                (cot_ref, cot_out),
            ]
        )
    ]
    stores[0].start()

    def between():
        for store in stores[1:4]:
            store.start()
        for part in range(4):
            cot_copy(part).wait()
        stores[4].start()

    attend(
        hid_ref,
        token_block,
        weight,
        small_ref,
        (rows_ref[0:1, :], rows_ref[1:2, :]),
        table_ref,
        s1_ref,
        qkv_ref,
        lse_ref,
        mixed_ref,
        mid_ref,
        s2_ref,
        tok_ref,
        line_ref,
        vt_ref,
        send_ref,
        recv_ref,
        send_sem,
        recv_sem,
        between,
    )
    for kind in range(2):
        for step in range(planes):

            @pl.when(jnp.logical_and(z >= step, z < planes - 1))
            def _():
                up(kind, step, z - step).wait_send()

            @pl.when(jnp.logical_and(z + step < planes, z > 0))
            def _():
                down(kind, step, z + step).wait_send()

        for plane in range(planes):
            side(kind, plane, x).wait_send()
            for line in range(2):
                sibling(kind, plane, line, core).wait_send()
    for store in stores:
        store.wait()
    experts.wait()


def backward_body(
    begin,
    end,
    res_ref,
    dx_ref,
    slot_ref,
    tok_ref,
    cot_ref,
    mid_hbm,
    s1_hbm,
    qkv_hbm,
    lse_ref,
    mixed_hbm,
    block_hbm,
    small_ref,
    rows_ref,
    table_ref,
    own_ref,
    egrad_ref,
    grad_ref,
    base_ref,
    other_ref,
    big_ref,
    arrived_ref,
    gsend_ref,
    grecv_ref,
    ssend_ref,
    srecv_ref,
    mid_ref,
    s1_ref,
    qkv_ref,
    mixed_ref,
    block_ref,
    hsend_ref,
    hrecv_ref,
    gmid_ref,
    gown_ref,
    kt_ref,
    gm_ref,
    dk_ref,
    dv_ref,
    gp_ref,
    att_ref,
    s2_ref,
    slope_ref,
    value_ref,
    acc_gain_ref,
    gsend_sem,
    grecv_sem,
    hsend_sem,
    hrecv_sem,
    esend_sem,
    erecv_sem,
    ssend_sem,
    srecv_sem,
    load_sem,
):
    loads = [
        pltpu.make_async_copy(source, target, load_sem.at[index])
        for index, (source, target) in enumerate(
            [
                (mid_hbm, mid_ref),
                (qkv_hbm, qkv_ref),
                (mixed_hbm, mixed_ref),
                (block_hbm, block_ref),
                (s1_hbm, s1_ref),
            ]
        )
    ]
    for load in loads:
        load.start()
    greet_group(2 * egrad_ref.shape[0])
    experts = CoreExchange(egrad_ref, arrived_ref, esend_sem, erecv_sem)
    tp = lax.axis_index("tp")
    width = dx_ref.shape[1]
    blocks = cot_ref.shape[0] // BLOCK
    heads_width = mixed_ref.shape[1]
    pairs = heads_width // PAIR
    gain_one = rows_ref[0:1, :]
    gain_two = rows_ref[1:2, :]
    slot_row = slot_ref[0:1, :]

    def weights(first_part, last_part):
        lanes = slice(first_part * heads_width, last_part * heads_width)
        return block_ref[:, :, lanes].reshape(width, (last_part - first_part) * heads_width)

    half_blocks = blocks // 2
    experts.start()

    def row_copy(block):
        return to_partner(
            gsend_ref.at[block], grecv_ref.at[block], gsend_sem.at[block], grecv_sem.at[block]
        )

    def share_copy(block):
        return to_partner(
            ssend_ref.at[block], srecv_ref.at[block], ssend_sem.at[block], srecv_sem.at[block]
        )

    def stream_copy(slot):
        return to_partner(
            hsend_ref.at[slot], hrecv_ref.at[slot], hsend_sem.at[slot], hrecv_sem.at[slot]
        )

    def slab_of(block):
        return block_rows(lax.rem(block, half_blocks))

    def backwards(body):
        each(0, blocks, lambda step: body(blocks - 1 - step))

    def send_rows(block):
        rows = block_rows(block)
        tok = tok_ref[rows, :]
        onehots = [low(jnp.where(column(tok, TARGET + m) == slot_row, 1.0, 0.0)) for m in range(2)]
        gsend_ref[block] = low(nn_dot(onehots[0] + onehots[1], dx_ref[...]))
        row_copy(block).start()
        placed = [nn_dot(onehot, res_ref[...]) for onehot in onehots]
        cot_wide = wide(cot_ref[rows, :])
        shares = [
            column(tok, GATE + m) * jnp.sum(placed[m] * cot_wide, axis=1, keepdims=True)
            for m in range(2)
        ]
        ssend_ref[block] = lane_matrix(tok.shape, [(0, shares[0]), (1, shares[1])]).T[:8, :]
        share_copy(block).start()
        mixture = column(tok, GATE) * placed[0] + column(tok, GATE + 1) * placed[1]

        @pl.when(tp == block // half_blocks)
        def _():
            base_ref[slab_of(block), :] = mixture

        @pl.when(tp != block // half_blocks)
        def _():
            other_ref[slab_of(block), :] = low(mixture)

    backwards(send_rows)
    for load in loads:
        load.wait()
    kt_ref[...] = qkv_ref[:, heads_width : 2 * heads_width].T
    dk_ref[...] = jnp.zeros_like(dk_ref)
    dv_ref[...] = jnp.zeros_like(dv_ref)
    acc_gain_ref[...] = jnp.zeros_like(acc_gain_ref)

    def main(block):
        rows = block_rows(block)
        mine = tp == block // half_blocks
        mine_f = jnp.where(mine, 1.0, 0.0)
        mid = mid_ref[rows, :]
        cot = cot_ref[rows, :]
        cot_wide = wide(cot)
        tok = tok_ref[rows, :]
        scale = lax.rsqrt(mean_last(mid * mid) + EPSILON)
        unit = mid * scale
        normed = unit * gain_two
        s2 = low(normed)
        small = small_ref[...]
        mixing = nn_dot(s2, small)
        value_dot = nn_dot(cot, small)
        normed_dot = jnp.sum(normed * cot_wide, axis=1, keepdims=True)
        route = [column(tok, ROUTE + member) for member in range(2)]
        gate = [column(tok, GATE + member) for member in range(2)]

        def weight_of(expert):
            return sum(jnp.where(route[m] == expert, gate[m], 0.0) for m in range(2))

        copy_weight = weight_of(COPY)
        copy_share = [jnp.where(route[m] == COPY, normed_dot, 0.0) for m in range(2)]
        alpha = copy_weight
        columns = []
        value_columns = []
        for c in range(2):
            weight = weight_of(COPY + 1 + c)
            left = column(mixing, MIXING + 2 * c)
            right = column(mixing, MIXING + 2 * c + 1)
            a0 = 1.0 / (1.0 + jnp.exp(right - left))
            a1 = 1.0 / (1.0 + jnp.exp(left - right))
            vd = column(value_dot, VALUE + c)
            alpha = alpha + weight * a0
            for m in range(2):
                copy_share[m] = copy_share[m] + jnp.where(
                    route[m] == COPY + 1 + c, a0 * normed_dot + a1 * vd, 0.0
                )
            slope = a0 * a1 * weight * (normed_dot - vd)
            columns.append((MIXING + 2 * c, slope))
            columns.append((MIXING + 2 * c + 1, -slope))
            value_columns.append((VALUE + c, weight * a1))
        value_matrix = lane_matrix(tok.shape, value_columns)

        @pl.when(mine)
        def _():
            base_ref[slab_of(block), :] += (
                mid + alpha * normed + nt_dot(low(value_matrix), small)
            )

        row_copy(block).wait()
        share_copy(block).wait()
        extra = ssend_ref[block] + srecv_ref[block]
        extra = jnp.concatenate(
            [extra, jnp.zeros((PAIR - extra.shape[0], BLOCK), jnp.float32)], axis=0
        ).T
        share = [column(extra, m) + gate[m] * copy_share[m] for m in range(2)]
        lane = lax.broadcasted_iota(jnp.int32, tok.shape, 1)
        slopes = lane_matrix(tok.shape, columns)
        for m in range(2):
            local = share[m] - gate[m] * (share[0] + share[1])
            slopes = slopes + jnp.where(wide(lane - ROUTER) == route[m], local, 0.0)
        slopes_low = low(slopes)
        grad_normed = (
            wide(gsend_ref[block])
            + wide(grecv_ref[block])
            + alpha * cot_wide
            + nt_dot(slopes_low, small)
        )
        s2_ref[rows, :] = s2
        slope_ref[rows, :] = low(slopes * mine_f)
        value_ref[rows, :] = low(value_matrix * mine_f)
        gain_grad = jnp.sum(unit * grad_normed, axis=0, keepdims=True) * mine_f
        acc_gain_ref[...] += jnp.broadcast_to(gain_grad, acc_gain_ref.shape)
        scaled = grad_normed * gain_two
        grad_mid = cot_wide + scale * (scaled - unit * mean_last(scaled * unit))
        gmid_ref[rows, :] = grad_mid
        attended = low(grad_mid)
        att_ref[rows, :] = attended
        gm_ref[...] = low(nn_dot(attended, weights(3, 4)))
        cosine, sine = spread_table(table_ref, block)

        def one_pair(keys, pair):
            start = pl.multiple_of(pair * PAIR, PAIR)
            lanes = pl.ds(start, PAIR)
            key_lanes = pl.ds(pl.multiple_of(heads_width + start, PAIR), PAIR)
            value_lanes = pl.ds(pl.multiple_of(2 * heads_width + start, PAIR), PAIR)
            query = qkv_ref[rows, lanes] * jnp.bfloat16(SCALING)
            key = qkv_ref[:keys, key_lanes]
            value = qkv_ref[:keys, value_lanes]
            grad_out = gm_ref[:, lanes]
            key_t = kt_ref[lanes, :keys]
            grad_value = None
            for half in range(2):
                keep = head_lanes(query.shape, half, 1)
                q_half = jnp.where(keep, query, jnp.bfloat16(0))
                g_half = jnp.where(keep, grad_out, jnp.bfloat16(0))
                probs = jnp.exp(nt_dot(key, q_half) - lse_ref[pl.ds(2 * pair + half, 1), rows])
                grad_probs = nt_dot(value, g_half)
                inner = jnp.sum(probs * grad_probs, axis=0, keepdims=True)
                grad_scores = low(probs * (grad_probs - inner))
                value_part = nn_dot(low(probs), g_half)
                key_part = nn_dot(grad_scores, q_half)
                query_part = nn_dot(key_t, grad_scores)
                if half == 0:
                    grad_value, grad_key, grad_query = value_part, key_part, query_part
                else:
                    grad_value = grad_value + value_part
                    grad_key = grad_key + key_part
                    grad_query = jnp.where(
                        head_lanes(query_part.shape, 1, 0), query_part, grad_query
                    )
            dv_ref[:keys, lanes] += grad_value
            dk_ref[:keys, lanes] += grad_key
            gp_ref[rows, lanes] = low(turn(grad_query.T * SCALING, cosine, -sine))
            gp_ref[rows, key_lanes] = low(turn(dk_ref[rows, lanes], cosine, -sine))
            gp_ref[rows, value_lanes] = low(dv_ref[rows, lanes])

        for static in range(blocks):

            @pl.when(block == static)
            def _():
                each(0, pairs, functools.partial(one_pair, (static + 1) * BLOCK))

        stream_grad = nt_dot(gp_ref[rows, :], weights(0, 3))
        slot = lax.rem(block, half_blocks)

        @pl.when(mine)
        def _():
            gown_ref[slot] = stream_grad

        @pl.when(jnp.logical_not(mine))
        def _():
            hsend_ref[slot] = low(stream_grad)
            stream_copy(slot).start()

    backwards(main)
    s1_turned = s1_ref[...].T
    for part in range(3):
        lanes = slice(part * heads_width, (part + 1) * heads_width)
        big_ref[:, :, lanes] = low(nn_dot(s1_turned, gp_ref[:, lanes])).reshape(
            big_ref.shape[:2] + (heads_width,)
        )
    big_ref[:, :, 3 * heads_width : 4 * heads_width] = low(
        tn_dot(att_ref[...], mixed_ref[...])
    ).reshape(big_ref.shape[:2] + (heads_width,))
    tall = jnp.where(
        lax.broadcasted_iota(jnp.int32, (PAIR, width), 0) == 1,
        jnp.broadcast_to(acc_gain_ref[0:1, :], (PAIR, width)),
        0.0,
    )
    big_ref[:, :, 4 * heads_width :] = low(
        tn_dot(s2_ref[...], slope_ref[...]) + tn_dot(cot_ref[...], value_ref[...]) + tall.T
    ).reshape(big_ref.shape[:2] + (PAIR,))
    begin()
    for slot in reversed(range(half_blocks)):
        slab = slice(slot * BLOCK, (slot + 1) * BLOCK)
        stream_copy(slot).wait()
        source = wide(own_ref[slab, :])
        scale = lax.rsqrt(mean_last(source * source) + EPSILON)
        unit = source * scale
        scaled = (gown_ref[slot] + wide(hrecv_ref[slot])) * gain_one
        mid_rows = block_rows(tp * half_blocks + slot)
        grad_ref[slab, :] = gmid_ref[mid_rows, :] + scale * (
            scaled - unit * mean_last(scaled * unit)
        )
    end()
    experts.wait()


def backward_plain_kernel(*refs):
    backward_body(lambda: None, lambda: None, *refs)


def backward_kernel(body_count, *refs):
    operands, wqkv_ref = refs[:16], refs[16]
    grad_ref, base_ref, arrived_ref, y_ref, red_ref, tail_ref = refs[17:23]
    other_ref, big_ref = refs[23:25]
    body, sums = refs[25 : 25 + body_count], refs[25 + body_count :]
    begin, end = sum_stages(big_ref, wqkv_ref, other_ref, y_ref, red_ref, tail_ref, *sums)
    backward_body(
        begin, end, *operands, grad_ref, base_ref, other_ref, big_ref, arrived_ref, *body
    )


def forward_results(length, width, heads_width, shard):
    low_t, wide_t = jnp.bfloat16, jnp.float32
    return [
        jax.ShapeDtypeStruct((length, width), low_t),
        jax.ShapeDtypeStruct((length, 3 * heads_width), low_t),
        jax.ShapeDtypeStruct((8, length), wide_t),
        jax.ShapeDtypeStruct((length, heads_width), low_t),
        jax.ShapeDtypeStruct((length, width), wide_t),
        jax.ShapeDtypeStruct((length, width), low_t),
        jax.ShapeDtypeStruct((length, PAIR), wide_t),
        jax.ShapeDtypeStruct((8, length), wide_t),
        jax.ShapeDtypeStruct(shard, low_t),
        jax.ShapeDtypeStruct((length, width), low_t),
    ]


def attend_scratch(length, width, heads_width):
    blocks = length // BLOCK
    return [
        pltpu.VMEM((heads_width, length), jnp.bfloat16),
        pltpu.VMEM((blocks, BLOCK, width), jnp.bfloat16),
        pltpu.VMEM((blocks, BLOCK, width), jnp.bfloat16),
    ]


def run_forward_plain(hid, tok, blocks, small, rows, table, shard, cot):
    length, width = hid.shape
    heads_width = blocks.shape[2] // 4
    vmem = pl.BlockSpec(memory_space=pltpu.VMEM)
    dma = pltpu.SemaphoreType.DMA
    count = length // BLOCK
    return pl.pallas_call(
        forward_plain_kernel,
        in_specs=[vmem] * 8,
        out_specs=[vmem] * 10,
        out_shape=forward_results(length, width, heads_width, shard.shape),
        scratch_shapes=attend_scratch(length, width, heads_width)
        + [dma((count,)), dma((count,)), dma((shard.shape[0],)), dma((shard.shape[0],)), dma((2,))],
        compiler_params=pltpu.CompilerParams(
            collective_id=0, has_side_effects=True, vmem_limit_bytes=60 << 20
        ),
    )(hid, tok, blocks, small, rows, table, shard, cot)


def run_forward(*operands):
    hid, wout, wdown, table = operands[0], operands[11], operands[13], operands[14]
    own_rows, width = hid.shape
    length = 2 * table.shape[0]
    shard, heads_width = wout.shape
    experts, _, hidden = wdown.shape
    size = lax.axis_size("fsdp")
    count = length // BLOCK
    hbm = pl.BlockSpec(memory_space=pl.ANY)
    vmem = pl.BlockSpec(memory_space=pltpu.VMEM)
    low_t, wide_t = jnp.bfloat16, jnp.float32
    dma = pltpu.SemaphoreType.DMA
    return pl.pallas_call(
        forward_kernel,
        in_specs=[vmem] * 15,
        out_specs=[hbm, vmem, vmem, hbm, hbm, vmem, hbm]
        + [vmem] * 4
        + [hbm, hbm],
        out_shape=[
            jax.ShapeDtypeStruct((size, shard, 4 * heads_width), low_t),
            jax.ShapeDtypeStruct((width, PAIR), low_t),
            jax.ShapeDtypeStruct((8, width), wide_t),
        ]
        + forward_results(length, width, heads_width, (experts, shard, 3 * hidden)),
        scratch_shapes=[
            pltpu.VMEM((size, shard, 4 * heads_width), low_t),
            pltpu.VMEM((length, width), low_t),
            pltpu.VMEM((length, 3 * heads_width), low_t),
            pltpu.VMEM((length, heads_width), low_t),
            pltpu.VMEM((length, width), low_t),
            pltpu.VMEM((length, width), low_t),
        ]
        + attend_scratch(length, width, heads_width)
        + [
            pltpu.VMEM((experts, shard, 3 * hidden), low_t),
            pltpu.VMEM((PAIR, PAIR), wide_t),
            pltpu.VMEM((size, 2, shard // 2, PAIR), wide_t),
            pltpu.VMEM((2, 32, own_rows), wide_t),
            dma((count,)),
            dma((count,)),
            dma((experts,)),
            dma((experts,)),
            dma((7,)),
            dma((7,)),
        ]
        + [dma((2, size // 4))] * 6
        + [dma((2, size // 2))] * 2
        + [dma((5,))],
        compiler_params=pltpu.CompilerParams(
            collective_id=3, has_side_effects=True, vmem_limit_bytes=60 << 20
        ),
    )(*operands)


def run_backward(wqkv, *operands):
    cot, mid, s1, qkv, mixed, blocks, own, egrads = (
        operands[index] for index in (4, 5, 6, 7, 9, 10, 14, 15)
    )
    length, width = cot.shape
    heads_width = mixed.shape[1]
    count = length // BLOCK
    own_rows = own.shape[0]
    parts, shard = blocks.shape[:2]
    columns = 4 * heads_width + PAIR
    vmem = pl.BlockSpec(memory_space=pltpu.VMEM)
    hbm = pl.BlockSpec(memory_space=pl.ANY)
    low_t, wide_t = jnp.bfloat16, jnp.float32
    dma = pltpu.SemaphoreType.DMA
    in_specs = [vmem] * 5 + [hbm] * 3 + [vmem] + [hbm] * 2 + [vmem] * 4 + [hbm]
    body = [
        pltpu.VMEM((count, BLOCK, width), low_t),
        pltpu.VMEM((count, BLOCK, width), low_t),
        pltpu.VMEM((count, 8, BLOCK), wide_t),
        pltpu.VMEM((count, 8, BLOCK), wide_t),
        pltpu.VMEM(mid.shape, wide_t),
        pltpu.VMEM(s1.shape, low_t),
        pltpu.VMEM(qkv.shape, low_t),
        pltpu.VMEM(mixed.shape, low_t),
        pltpu.VMEM(blocks.shape, low_t),
        pltpu.VMEM((2, BLOCK, width), low_t),
        pltpu.VMEM((2, BLOCK, width), low_t),
        pltpu.VMEM((length, width), wide_t),
        pltpu.VMEM((2, BLOCK, width), wide_t),
        pltpu.VMEM((heads_width, length), low_t),
        pltpu.VMEM((BLOCK, heads_width), low_t),
        pltpu.VMEM((length, heads_width), wide_t),
        pltpu.VMEM((length, heads_width), wide_t),
        pltpu.VMEM((length, 3 * heads_width), low_t),
        pltpu.VMEM((length, width), low_t),
        pltpu.VMEM((length, width), low_t),
        pltpu.VMEM((length, PAIR), low_t),
        pltpu.VMEM((length, PAIR), low_t),
        pltpu.VMEM((8, width), wide_t),
        dma((count,)),
        dma((count,)),
        dma((2,)),
        dma((2,)),
        dma((egrads.shape[0],)),
        dma((egrads.shape[0],)),
        dma((count,)),
        dma((count,)),
        dma((5,)),
    ]
    own_wide = jax.ShapeDtypeStruct((own_rows, width), wide_t)
    own_low = jax.ShapeDtypeStruct((own_rows, width), low_t)
    arrived = jax.ShapeDtypeStruct(egrads.shape, low_t)
    params = pltpu.CompilerParams(
        collective_id=1, has_side_effects=True, vmem_limit_bytes=67043328
    )
    if wqkv is None:
        return pl.pallas_call(
            backward_plain_kernel,
            in_specs=in_specs,
            out_specs=[vmem] * 4 + [hbm],
            out_shape=[
                own_wide,
                own_wide,
                own_low,
                jax.ShapeDtypeStruct((parts, shard, columns), low_t),
                arrived,
            ],
            scratch_shapes=body,
            compiler_params=params,
        )(*operands)
    return pl.pallas_call(
        functools.partial(backward_kernel, len(body)),
        in_specs=in_specs + [vmem],
        out_specs=[vmem] * 2 + [hbm] + [vmem] * 3,
        out_shape=[
            own_wide,
            own_wide,
            arrived,
            own_low,
            jax.ShapeDtypeStruct((shard, columns - PAIR), wide_t),
            jax.ShapeDtypeStruct((shard // 2, PAIR), wide_t),
        ],
        scratch_shapes=[
            pltpu.VMEM((own_rows, width), low_t),
            pltpu.VMEM((parts, shard, columns), low_t),
        ]
        + body
        + sum_scratch(parts // 4, shard, columns),
        compiler_params=params,
    )(*operands, wqkv)


def shards(
    hidden,
    prev_logits,
    routes,
    slot_rank,
    dropped,
    cotangent,
    attn_norm,
    ffn_norm,
    w_qkv,
    w_attn_out,
    w_router,
    w_const_gate,
    w_const_value,
    w_expert_in,
    w_expert_out,
):
    own_rows, width = hidden.shape
    length = own_rows * lax.axis_size("tp")
    experts = w_expert_in.shape[0]
    route_count = w_router.shape[1]
    capacity = 9 * length // (4 * route_count)
    planned = lax.axis_size("fsdp") == 16
    table = jnp.asarray(rotary_table(length))
    gains = jnp.stack([wide(attn_norm), wide(ffn_norm)], axis=0)
    wqkv = w_qkv.transpose(1, 0, 2)
    operands = (
        hidden,
        cotangent,
        prev_logits.T,
        routes.T,
        slot_rank.T,
        dropped.T,
        gains,
        w_router.T,
        w_const_gate.T,
        w_const_value.T,
        wqkv,
        w_attn_out,
        w_expert_in,
        w_expert_out,
    )
    if planned:
        forward = run_forward(*operands, table)
    else:
        forward = forward_plain(operands, table)
    blocks, small, rows, s1, qkv, lse, mixed, mid, s2, tok, lines, gathered, cot = forward
    expert_weights = join_weights(gathered, experts)
    peers = 2 * experts
    half = capacity // 2
    block = half // 2
    place = jnp.arange(peers * block)
    owner = (lax.axis_index("fsdp") % peers) ^ (place // block)
    slot = wide(
        (owner // 2) * capacity
        + lax.axis_index("tp") * half
        + (owner % 2) * block
        + place % block
    )
    results, grad_rows, grads_exp = run_expert(
        s2, cot, lines, jnp.broadcast_to(slot[:, None], (slot.shape[0], PAIR)), expert_weights
    )
    backward = run_backward(
        wqkv if planned else None,
        results.reshape(-1, width),
        grad_rows.reshape(-1, width),
        jnp.broadcast_to(slot[None, :], (8, slot.shape[0])),
        tok,
        cot,
        mid,
        s1,
        qkv,
        lse,
        mixed,
        blocks,
        small,
        rows,
        table,
        hidden,
        split_grads(grads_exp),
    )
    if planned:
        grad_hidden, base, arrived, received, red, last = backward
    else:
        grad_hidden, base, for_other, big, arrived = backward
        received, red, last = finish_plain(big.reshape(width, -1), wqkv, for_other)
    output, grad_hidden, grad_qkv, grad_attn_out, gain_grads, grad_router, grad_mixing, grad_value, grad_in, grad_out = run_write(
        base, received, grad_hidden, red, last, gains, arrived
    )
    return (
        output,
        grad_hidden,
        gain_grads[0],
        gain_grads[1],
        grad_qkv.transpose(1, 0, 2),
        grad_attn_out,
        grad_router.T,
        grad_mixing.T,
        grad_value.T,
        grad_in,
        grad_out,
    )


def solution(mesh):
    in_specs = (
        P(("fsdp", "tp"), None),
        P(("fsdp", "tp"), None),
        P(("fsdp", "tp"), None),
        P(("fsdp", "tp"), None),
        P(("fsdp", "tp"), None),
        P(("fsdp", "tp"), None),
        P(("fsdp", "tp")),
        P(("fsdp", "tp")),
        P("fsdp", None, "tp"),
        P("fsdp", "tp"),
        P(("fsdp", "tp"), None),
        P(("fsdp", "tp"), None),
        P(("fsdp", "tp"), None),
        P(None, "fsdp", None, "tp"),
        P(None, "fsdp", "tp"),
    )
    out_specs = (
        P(("fsdp", "tp"), None),
        P(("fsdp", "tp"), None),
        P(("fsdp", "tp")),
        P(("fsdp", "tp")),
        P("fsdp", None, "tp"),
        P("fsdp", "tp"),
        P(("fsdp", "tp"), None),
        P(("fsdp", "tp"), None),
        P(("fsdp", "tp"), None),
        P(None, "fsdp", None, "tp"),
        P(None, "fsdp", "tp"),
    )
    return jax.shard_map(shards, mesh=mesh, in_specs=in_specs, out_specs=out_specs, check_vma=False)
```

```python
import functools

import jax
import jax.numpy as jnp
import numpy as np
from jax import lax
from jax.experimental import pallas as pl
from jax.experimental.pallas import tpu as pltpu
from jax.sharding import PartitionSpec as P

HD = 64
BLOCK = 256


EPSILON = 1e-06
MESH = pl.DeviceIdType.MESH
PAIR = 2 * HD
SCALING = HD ** (-0.5)
ROUTER = 2
MIXING = 14
VALUE = 18
ROUTE = 20
TARGET = 24
GATE = 26
COPY = 9


TILE = 256
SUB = 16


def swap(values):
    return lax.ppermute(values, "tp", [(0, 1), (1, 0)])


def gather_rows(values):
    other = swap(values)
    first = lax.axis_index("tp") == 0
    return jnp.concatenate(
        [jnp.where(first, values, other), jnp.where(first, other, values)], axis=0
    )


def own_half(values):
    half = values.shape[0] // 2
    return lax.dynamic_slice_in_dim(values, lax.axis_index("tp") * half, half, 0)


def other_half(values):
    half = values.shape[0] // 2
    return lax.dynamic_slice_in_dim(values, (1 - lax.axis_index("tp")) * half, half, 0)


def member_groups(size, experts):
    span = 2 * experts
    starts = range(0, size, span)
    cores = [[start + 2 * e, start + 2 * e + 1] for start in starts for e in range(experts)]
    across = [[start + r for start in starts] for r in range(span)]
    return cores, across


def own_core(values, rows):
    parts = values.reshape(-1, 2, rows, values.shape[-1])
    return lax.dynamic_index_in_dim(parts, lax.axis_index("fsdp") % 2, 1, keepdims=False)


def join_weights(got, experts):
    size = lax.axis_size("fsdp")
    if size == 2 * experts:
        return got
    cores, across = member_groups(size, experts)
    got = lax.all_gather(got, "fsdp", axis=1, axis_index_groups=cores, tiled=True)
    got = got.reshape(-1, got.shape[-1])
    got = lax.all_gather(got, "fsdp", axis=0, axis_index_groups=across, tiled=True)
    return own_core(got, got.shape[0] // (2 * experts))


def split_grads(grads):
    experts, _, columns = grads.shape
    size = lax.axis_size("fsdp")
    if size == 2 * experts:
        return grads
    cores, across = member_groups(size, experts)
    grads = lax.all_gather(grads[:, None], "fsdp", axis=1, axis_index_groups=cores, tiled=True)
    grads = grads.reshape(-1, columns)
    grads = lax.psum_scatter(
        grads, "fsdp", scatter_dimension=0, axis_index_groups=across, tiled=True
    )
    return own_core(grads, grads.shape[0] // (2 * experts))


def finish_plain(big, wqkv, other):
    heads_width = (big.shape[1] - PAIR) // 4
    reduced = wide(lax.psum_scatter(big, "fsdp", scatter_dimension=0, tiled=True))
    parts = reduced[:, : 3 * heads_width].reshape(-1, 3, heads_width).transpose(1, 0, 2)
    share = jnp.sum(parts * wide(wqkv), axis=(0, 2))
    last = jnp.concatenate([share[:, None], reduced[:, 4 * heads_width + 1 :]], axis=1)
    return (
        swap(other),
        reduced[:, : 4 * heads_width],
        own_half(last) + swap(other_half(last)),
    )


def forward_plain(operands, table):
    (
        hidden,
        cotangent,
        logits,
        routes,
        rank,
        dropped,
        gains,
        router,
        mixing,
        value,
        wqkv,
        wout,
        w_in,
        w_down,
    ) = operands
    own_rows, width = hidden.shape
    experts, shard, units = w_down.shape
    small = jnp.concatenate([wide(v) for v in (gains, router, mixing, value)], axis=0)
    small = jnp.pad(small, ((0, PAIR - small.shape[0]), (0, 0))).T
    small = lax.all_gather(small, ("fsdp", "tp"), axis=0, tiled=True)
    capacity = own_rows * 2 * 9 // 48
    kept = (routes < experts) & (dropped == 0)
    target = jnp.where(kept, routes * capacity + rank, -1)
    blank = jnp.zeros((2, own_rows), jnp.float32)
    tok = jnp.concatenate(
        [blank, logits, blank, blank, blank, wide(routes), blank, wide(target)], axis=0
    )
    tok = lax.all_gather(tok, "tp", axis=1, tiled=True).T
    tok = jnp.pad(tok, ((0, 0), (0, PAIR - tok.shape[1])))
    blocks = jnp.concatenate([wqkv[0], wqkv[1], wqkv[2], wout], axis=1)
    blocks = lax.all_gather(blocks, "fsdp", axis=0, tiled=True).reshape(2 * experts, -1, blocks.shape[1])
    rows = small.T[:8]
    small = low(small)
    shards_flat = jnp.concatenate([w_in.reshape(experts, shard, 2 * units), w_down], axis=2)
    return (blocks, small, rows) + tuple(
        run_forward_plain(
            gather_rows(hidden), tok, blocks, small, rows, table, shards_flat, cotangent
        )
    )


def nt_dot(left, right):
    return lax.dot_general(left, right, (((1,), (1,)), ((), ())), preferred_element_type=jnp.float32)


def nn_dot(left, right):
    return jnp.dot(left, right, preferred_element_type=jnp.float32)


def tn_dot(left, right):
    return lax.dot_general(left, right, (((0,), (0,)), ((), ())), preferred_element_type=jnp.float32)


def low(values):
    return values.astype(jnp.bfloat16)


def wide(values):
    return values.astype(jnp.float32)


def rotary_table(length):
    half = HD // 2
    positions = np.arange(length, dtype=np.float32)
    inverse = np.power(np.float32(10000.0), -np.arange(half, dtype=np.float32) / np.float32(half))
    angles = (positions[:, None] * inverse[None, :].astype(np.float32)).astype(np.float32)
    cosine = np.cos(angles.astype(np.float64)).astype(np.float32)
    sine = np.sin(angles.astype(np.float64)).astype(np.float32)
    both = np.concatenate([cosine, sine], axis=1)
    return np.concatenate([both[: length // 2], both[length // 2 :]], axis=1)


def spread_table(table_ref, block):
    quarter = HD // 2
    blocks = table_ref.shape[0] // BLOCK
    table = table_ref[block_rows(lax.rem(block, blocks)), :]
    table = jnp.where(block >= blocks, pltpu.roll(table, HD, 1), table)
    lane = lax.broadcasted_iota(jnp.int32, table.shape, 1)
    cosine = jnp.where(lane < quarter, table, 0.0)
    cosine = cosine + pltpu.roll(cosine, quarter, 1)
    sine = jnp.where(jnp.logical_and(lane >= quarter, lane < HD), table, 0.0)
    sine = sine - pltpu.roll(sine, PAIR - quarter, 1)
    return cosine + pltpu.roll(cosine, HD, 1), sine + pltpu.roll(sine, HD, 1)


def turn(values, cosine, sine):
    lane = lax.broadcasted_iota(jnp.int32, values.shape, 1)
    upper = lax.rem(lane, HD) >= HD // 2
    partner = jnp.where(
        upper, pltpu.roll(values, HD // 2, 1), pltpu.roll(values, PAIR - HD // 2, 1)
    )
    return values * cosine + partner * sine


def head_lanes(shape, half, axis):
    return (lax.broadcasted_iota(jnp.int32, shape, axis) >= HD) == bool(half)


def mean_last(values):
    return jnp.mean(values, axis=-1, keepdims=True)


def to_partner(source, target, send_sem, recv_sem):
    return pltpu.make_async_remote_copy(
        src_ref=source,
        dst_ref=target,
        send_sem=send_sem,
        recv_sem=recv_sem,
        device_id={"tp": 1 - lax.axis_index("tp")},
        device_id_type=MESH,
    )


def block_rows(block):
    return pl.ds(pl.multiple_of(block * BLOCK, BLOCK), BLOCK)


def column(values, index):
    return values[:, index : index + 1]


def lane_matrix(shape, columns):
    lane = lax.broadcasted_iota(jnp.int32, shape, 1)
    total = jnp.zeros(shape, jnp.float32)
    for index, values in columns:
        total = jnp.where(lane == index, values, total)
    return total


def send_to(source, target, send_sem, recv_sem, device):
    return pltpu.make_async_remote_copy(
        src_ref=source,
        dst_ref=target,
        send_sem=send_sem,
        recv_sem=recv_sem,
        device_id=device,
        device_id_type=MESH,
    )


def greet_group(peers):
    me = lax.axis_index("fsdp")
    rank = lax.rem(me, peers)
    barrier = pltpu.get_barrier_semaphore()
    for k in range(1, peers):
        pl.semaphore_signal(
            barrier,
            inc=1,
            device_id={"fsdp": me - rank + lax.rem(rank + k, peers)},
            device_id_type=MESH,
        )
    pl.semaphore_signal(
        barrier, inc=1, device_id={"tp": 1 - lax.axis_index("tp")}, device_id_type=MESH
    )
    pl.semaphore_wait(barrier, peers)


def each(first, last, body):
    def step(k, carry):
        body(k)
        return carry

    lax.fori_loop(first, last, step, 0)


def flipped(value, k, bits):
    other = 0
    bit = 1
    while bit < bits:
        ours, theirs = lax.rem(value // bit, 2), lax.rem(k // bit, 2)
        other = other + bit * (ours + theirs - 2 * ours * theirs)
        bit *= 2
    return other


class CoreExchange:
    def __init__(self, source, target, send_sem, recv_sem):
        experts = source.shape[0]
        me = lax.axis_index("fsdp")
        rank = lax.rem(me, 2 * experts)
        core = lax.rem(rank, 2)
        mine = rank // 2

        def device(k):
            return {"fsdp": me - rank + 2 * flipped(mine, k, experts) + core}

        def copy(k):
            there = flipped(mine, k, experts)
            return send_to(
                source.at[there], target.at[mine], send_sem.at[k], recv_sem.at[k], device(k)
            )

        def arrival(k):
            there = flipped(mine, k, experts)
            return send_to(
                source.at[there], target.at[there], send_sem.at[k], recv_sem.at[k], device(k)
            )

        self.experts, self.copy, self.arrival = experts, copy, arrival
        self.local = pltpu.make_async_copy(source.at[mine], target.at[mine], send_sem.at[0])

    def start(self, order=(1, 2, 3, 4, 5, 6, 7)):
        self.local.start()
        for k in order:
            self.copy(k).start()

    def wait(self):
        each(1, self.experts, lambda k: self.copy(k).wait_send())
        each(1, self.experts, lambda k: self.arrival(k).wait_recv())
        self.local.wait()


def sum_stages(
    big_ref,
    wqkv_ref,
    other_ref,
    y_ref,
    red_ref,
    tail_ref,
    sum_ref,
    core_ref,
    side_ref,
    acc_ref,
    usend_ref,
    urecv_ref,
    dsend_ref,
    drecv_ref,
    tsend_ref,
    trecv_ref,
    core_send,
    core_recv,
    x_send,
    x_recv,
    up_send,
    up_recv,
    dn_send,
    dn_recv,
    y_send,
    y_recv,
):
    size = big_ref.shape[0]
    subs = big_ref.shape[1] // SUB
    planes = size // 4
    me = lax.axis_index("fsdp")
    tp = lax.axis_index("tp")
    z, x, core = me // 4, lax.rem(me // 2, 2), lax.rem(me, 2)
    heads_width = wqkv_ref.shape[2]
    partner = {"tp": 1 - tp}

    def to_core(plane, line):
        slot = plane * 2 + line
        return send_to(
            big_ref.at[plane * 4 + line * 2 + 1 - core],
            core_ref.at[slot],
            core_send.at[slot],
            core_recv.at[slot],
            {"fsdp": me + 1 - 2 * core},
        )

    def band(sub):
        return pl.ds(pl.multiple_of(sub * SUB, SUB), SUB)

    def to_side(plane, sub):
        slot = plane * subs + sub
        return send_to(
            sum_ref.at[plane, band(sub)],
            side_ref.at[plane, band(sub)],
            x_send.at[slot],
            x_recv.at[slot],
            {"fsdp": z * 4 + (1 - x) * 2 + core},
        )

    def to_up(plane, sub):
        slot = plane * subs + sub
        return send_to(
            usend_ref.at[plane, band(sub)],
            urecv_ref.at[plane, band(sub)],
            up_send.at[slot],
            up_recv.at[slot],
            {"fsdp": lax.min(z + 1, planes - 1) * 4 + x * 2 + core},
        )

    def to_down(plane, sub):
        slot = plane * subs + sub
        return send_to(
            dsend_ref.at[plane, band(sub)],
            drecv_ref.at[plane, band(sub)],
            dn_send.at[slot],
            dn_recv.at[slot],
            {"fsdp": lax.max(z - 1, 0) * 4 + x * 2 + core},
        )

    lower = z < planes // 2
    order = [jnp.where(lower, planes - 1 - step, step) for step in range(planes)]
    half_rows = other_ref.shape[0] // 2

    def out_y(part):
        rows = pl.ds(part * half_rows, half_rows)
        return send_to(
            other_ref.at[rows], y_ref.at[rows], y_send.at[2 * part], y_recv.at[2 * part], partner
        )

    def joined(plane, line):
        to_core(plane, line).wait_recv()
        return wide(big_ref[plane * 4 + line * 2 + core]) + wide(core_ref[plane * 2 + line])

    def rise(plane, sub):
        @pl.when(z < plane)
        def _():
            @pl.when(z > 0)
            def _():
                to_up(plane, sub).wait_recv()
                acc_ref[plane, band(sub)] += wide(urecv_ref[plane, band(sub)])

            usend_ref[plane, band(sub)] = low(acc_ref[plane, band(sub)])
            to_up(plane, sub).start()

    def fall(plane, sub):
        @pl.when(z > plane)
        def _():
            @pl.when(z < planes - 1)
            def _():
                to_down(plane, sub).wait_recv()
                acc_ref[plane, band(sub)] += wide(drecv_ref[plane, band(sub)])

            dsend_ref[plane, band(sub)] = low(acc_ref[plane, band(sub)])
            to_down(plane, sub).start()

    def begin():
        for plane in order:
            to_core(plane, 1 - x).start()
        for plane in order:
            to_core(plane, x).start()
        out_y(1).start()

        for plane in order:
            sum_ref[plane] = low(joined(plane, 1 - x))
            each(0, subs, lambda sub: to_side(plane, sub).start())
        for plane in order:
            acc_ref[plane] = joined(plane, x)

    def middle():
        for step, plane in enumerate(order):
            last_step = step == planes - 1

            def advance(sub):
                to_side(plane, sub).wait_recv()
                acc_ref[plane, band(sub)] += wide(side_ref[plane, band(sub)])

                @pl.when(lower)
                def _():
                    (fall if last_step else rise)(plane, sub)

                @pl.when(jnp.logical_not(lower))
                def _():
                    (rise if last_step else fall)(plane, sub)

            each(0, subs, advance)

    def end():
        @pl.when(z > 0)
        def _():
            each(0, subs, lambda sub: to_up(z, sub).wait_recv())
            acc_ref[z] += wide(urecv_ref[z])

        @pl.when(z < planes - 1)
        def _():
            each(0, subs, lambda sub: to_down(z, sub).wait_recv())
            acc_ref[z] += wide(drecv_ref[z])

        values = acc_ref[z]
        red_ref[...] = values[:, : 4 * heads_width]
        share = sum(
            jnp.sum(
                values[:, part * heads_width : (part + 1) * heads_width] * wide(wqkv_ref[part]),
                axis=1,
                keepdims=True,
            )
            for part in range(3)
        )
        last = values[:, 4 * heads_width :]
        last = jnp.where(lax.broadcasted_iota(jnp.int32, last.shape, 1) == 0, share, last)
        part_rows = tail_ref.shape[0]
        tsend_ref[0] = last[:part_rows, :]
        tsend_ref[1] = last[part_rows:, :]
        tail_y = send_to(tsend_ref.at[1 - tp], trecv_ref, y_send.at[1], y_recv.at[1], partner)
        tail_y.start()
        out_y(0).wait()
        out_y(1).wait()
        tail_y.wait()
        tail_ref[...] = tsend_ref[tp] + trecv_ref[...]
        for plane in range(planes):
            to_core(plane, 1 - x).wait_send()
            to_core(plane, x).wait_send()

            def drain(sub):
                to_side(plane, sub).wait_send()

                @pl.when(z < plane)
                def _():
                    to_up(plane, sub).wait_send()

                @pl.when(z > plane)
                def _():
                    to_down(plane, sub).wait_send()

            each(0, subs, drain)

    return lambda: out_y(0).start(), begin, middle, end


def sum_scratch(planes, shard, columns):
    low_t, wide_t = jnp.bfloat16, jnp.float32
    dma = pltpu.SemaphoreType.DMA
    line = (planes, shard, columns)
    return (
        [
            pltpu.VMEM(line, low_t),
            pltpu.VMEM((2 * planes, shard, columns), low_t),
            pltpu.VMEM(line, low_t),
            pltpu.VMEM(line, wide_t),
            pltpu.VMEM(line, low_t),
            pltpu.VMEM(line, low_t),
            pltpu.VMEM(line, low_t),
            pltpu.VMEM(line, low_t),
            pltpu.VMEM((2, shard // 2, PAIR), wide_t),
            pltpu.VMEM((shard // 2, PAIR), wide_t),
            dma((2 * planes,)),
            dma((2 * planes,)),
        ]
        + [dma((planes * (shard // SUB),))] * 6
        + [dma((3,))] * 2
    )


def write_kernel(
    base_ref,
    y_ref,
    grad_ref,
    red_ref,
    tail_ref,
    gain_ref,
    expert_ref,
    out_ref,
    hidden_ref,
    qkv_ref,
    attn_ref,
    gains_ref,
    router_ref,
    mixing_ref,
    value_ref,
    in_ref,
    down_ref,
):
    hidden = down_ref.shape[2]
    heads_width = attn_ref.shape[1]
    out_ref[...] = low(base_ref[...] + wide(y_ref[...]))
    hidden_ref[...] = grad_ref[...]

    def lay_out(e):
        values = wide(expert_ref[e])
        in_ref[e, :, 0, :] = values[:, :hidden]
        in_ref[e, :, 1, :] = values[:, hidden : 2 * hidden]
        down_ref[e] = values[:, 2 * hidden :]

    each(0, expert_ref.shape[0], lay_out)

    @pl.when(pl.program_id(0) == 0)
    def _():
        for part in range(3):
            qkv_ref[part] = red_ref[:, part * heads_width : (part + 1) * heads_width]
        attn_ref[...] = red_ref[:, 3 * heads_width :]
        count = tail_ref.shape[0]
        blank = jnp.zeros((PAIR - count, PAIR), jnp.float32)
        turned = jnp.concatenate([tail_ref[...], blank], axis=0).T[:, :count]
        gains_ref[0:1, :] = turned[0:1, :] / gain_ref[0:1, :]
        gains_ref[1:2, :] = turned[1:2, :]
        router_ref[...] = turned[ROUTER:MIXING, :]
        mixing_ref[...] = turned[MIXING:VALUE, :]
        value_ref[...] = turned[VALUE : VALUE + 2, :]


def run_write(base, y, grad_hidden, red, tail, gains, arrived):
    own_rows, width = base.shape
    shard = red.shape[0]
    heads_width = red.shape[1] // 4
    count = tail.shape[0]
    experts, _, total = arrived.shape
    hidden = total // 3
    wide_t = jnp.float32
    steps = experts // 2
    rows = pl.BlockSpec((own_rows // steps, width), lambda e: (e, 0))

    def whole(shape):
        return pl.BlockSpec(shape, lambda e: (0,) * len(shape))

    return pl.pallas_call(
        write_kernel,
        grid=(steps,),
        in_specs=[
            rows,
            rows,
            rows,
            whole(red.shape),
            whole(tail.shape),
            whole(gains.shape),
            pl.BlockSpec((2, shard, total), lambda e: (e, 0, 0)),
        ],
        out_specs=[
            rows,
            rows,
            whole((3, shard, heads_width)),
            whole((shard, heads_width)),
            whole((2, count)),
            whole((MIXING - ROUTER, count)),
            whole((VALUE - MIXING, count)),
            whole((2, count)),
            pl.BlockSpec((2, shard, 2, hidden), lambda e: (e, 0, 0, 0)),
            pl.BlockSpec((2, shard, hidden), lambda e: (e, 0, 0)),
        ],
        out_shape=[
            jax.ShapeDtypeStruct((own_rows, width), jnp.bfloat16),
            jax.ShapeDtypeStruct((own_rows, width), wide_t),
            jax.ShapeDtypeStruct((3, shard, heads_width), wide_t),
            jax.ShapeDtypeStruct((shard, heads_width), wide_t),
            jax.ShapeDtypeStruct((2, count), wide_t),
            jax.ShapeDtypeStruct((MIXING - ROUTER, count), wide_t),
            jax.ShapeDtypeStruct((VALUE - MIXING, count), wide_t),
            jax.ShapeDtypeStruct((2, count), wide_t),
            jax.ShapeDtypeStruct((experts, shard, 2, hidden), wide_t),
            jax.ShapeDtypeStruct((experts, shard, hidden), wide_t),
        ],
    )(base, y, grad_hidden, red, tail, gains, arrived)


def expert_kernel(
    s2_ref,
    cot_ref,
    line_ref,
    slot_ref,
    weight_ref,
    res_out_ref,
    dx_out_ref,
    grads_out_ref,
    xs_ref,
    gs_ref,
    x_ref,
    g_ref,
    w_ref,
    gate_ref,
    up_ref,
    act_ref,
    xt_ref,
    gt_ref,
    acc_ref,
    grads_ref,
    sibling_ref,
    ysend_ref,
    yrecv_ref,
    w_sem,
    grad_sem,
    xs_sem,
    xr_sem,
    gs_sem,
    gr_sem,
    xfs_sem,
    xfr_sem,
    gfs_sem,
    gfr_sem,
    ys_sem,
    yr_sem,
    rs_sem,
    rr_sem,
    ds_sem,
    dr_sem,
):
    peers, rows, width = xs_ref.shape
    total = peers * rows
    hidden = gate_ref.shape[1]
    tiles = hidden // TILE
    me = lax.axis_index("fsdp")
    tp = lax.axis_index("tp")
    rank = lax.rem(me, peers)
    core = lax.rem(rank, 2)
    start = me - rank

    def peer(k):
        return {"fsdp": start + flipped(rank, k, peers)}

    partner = {"tp": 1 - tp}
    sibling = {"fsdp": start + rank + 1 - 2 * core}

    def out_x(k):
        return send_to(xs_ref.at[k], x_ref.at[0, k], xs_sem.at[k], xr_sem.at[k], peer(k))

    def out_g(k):
        return send_to(gs_ref.at[k], g_ref.at[0, k], gs_sem.at[k], gr_sem.at[k], peer(k))

    def pass_x(k):
        return send_to(x_ref.at[0, k], x_ref.at[1, k], xfs_sem.at[k], xfr_sem.at[k], partner)

    def pass_g(k):
        return send_to(g_ref.at[0, k], g_ref.at[1, k], gfs_sem.at[k], gfr_sem.at[k], partner)

    def across(index, k):
        return send_to(
            ysend_ref.at[index, k],
            yrecv_ref.at[index, k],
            ys_sem.at[index, k],
            yr_sem.at[index, k],
            partner,
        )

    def back(index, k):
        if index == 0:
            return send_to(xs_ref.at[k], res_out_ref.at[k], rs_sem.at[k], rr_sem.at[k], peer(k))
        return send_to(gs_ref.at[k], dx_out_ref.at[k], ds_sem.at[k], dr_sem.at[k], peer(k))

    def return_order(body):
        def step(j, carry):
            body(8 + 2 * j)
            body(4 + j)
            body(9 + 2 * j)
            return carry

        lax.fori_loop(0, 4, step, 0)
        for k in (2, 3, 1, 0):
            body(k)

    def turn_rows(source, target, m):
        target[:, pl.ds(pl.multiple_of(m * total, total), total)] = (
            source[m].reshape(total, width).T
        )

    def join(index, k):
        across(index, k).wait_recv()
        own = xs_ref if index == 0 else gs_ref
        own[k] = low(wide(own[k]) + wide(yrecv_ref[index, k]))
        back(index, k).start()

    def join_some(index, tile):
        join(index, 8 + 2 * tile)
        join(index, 4 + tile)
        join(index, 9 + 2 * tile)

    def join_last(index):
        for k in (2, 3, 1):
            join(index, k)
        across(index, 0).wait_recv()
        own, target = (xs_ref, res_out_ref) if index == 0 else (gs_ref, dx_out_ref)
        target[0] = low(wide(own[0]) + wide(yrecv_ref[index, 0]))

    greet_group(peers)
    here = pltpu.make_async_copy(weight_ref, w_ref.at[:, core], w_sem.at[0])
    here.start()
    there = send_to(weight_ref, w_ref.at[:, core], w_sem.at[1], w_sem.at[2], sibling)
    half = total // 2
    group = peers // 2

    def hits_of(part):
        ids = slot_ref[pl.ds(pl.multiple_of(part * half, half), half), 0:1]
        return [line_ref[m : m + 1, :] == ids for m in range(2)]

    def pack_x(part):
        hits = hits_of(part)
        onehot = low(jnp.where(hits[0] | hits[1], 1.0, 0.0))
        xs_ref[pl.ds(part * group, group)] = low(nn_dot(onehot, s2_ref[...])).reshape(
            group, rows, width
        )

        @pl.when(part == 0)
        def _():
            x_ref[0, 0] = xs_ref[0]
            pass_x(0).start()

        def launch(k):
            @pl.when(k > 0)
            def _():
                out_x(k).start()

        each(part * group, (part + 1) * group, launch)

    def pack_g(part):
        hits = hits_of(part)
        onehot = low(jnp.where(hits[0] | hits[1], 1.0, 0.0))
        gate = sum(
            jnp.sum(jnp.where(hits[m], line_ref[2 + m : 3 + m, :], 0.0), axis=1, keepdims=True)
            for m in range(2)
        )
        gs_ref[pl.ds(part * group, group)] = low(nn_dot(onehot, cot_ref[...]) * gate).reshape(
            group, rows, width
        )

        @pl.when(part == 0)
        def _():
            g_ref[0, 0] = gs_ref[0]

        def launch(k):
            @pl.when(k > 0)
            def _():
                out_g(k).start()

        each(part * group, (part + 1) * group, launch)

    each(0, 2, pack_x)
    there.start()
    each(0, 2, pack_g)

    def forward_x(k):
        out_x(k).wait_recv()
        pass_x(k).start()

    each(1, peers, forward_x)
    pass_g(0).start()
    here.wait()
    send_to(weight_ref, w_ref.at[:, 1 - core], w_sem.at[1], w_sem.at[2], sibling).wait_recv()
    there.wait_send()
    each(0, peers, lambda k: pass_x(k).wait_recv())

    def weights(which, lanes):
        return w_ref[:, :, :, pl.ds(pl.multiple_of(which * hidden + lanes, TILE), TILE)].reshape(
            width, TILE
        )

    acc_ref[...] = jnp.zeros_like(acc_ref)

    def forward_tile(tile, carry):
        lanes = pl.multiple_of(tile * TILE, TILE)
        here_lanes = pl.ds(lanes, TILE)

        def one_half(m):
            band = pl.ds(pl.multiple_of(m * total, total), total)
            x = x_ref[m].reshape(total, width)
            gate = nn_dot(x, weights(0, lanes))
            up = nn_dot(x, weights(1, lanes))
            gate_ref[band, here_lanes] = low(gate)
            up_ref[band, here_lanes] = low(up)
            act = low(gate / (1.0 + jnp.exp(-gate)) * up)
            act_ref[band, here_lanes] = act
            acc_ref[band, :] += nt_dot(act, weights(2, lanes))

        each(0, 2, one_half)

        def forward_g(k):
            @pl.when(k > 0)
            def _():
                out_g(k).wait_recv()
                pass_g(k).start()

        each(tile * (peers // tiles), (tile + 1) * (peers // tiles), forward_g)
        return carry

    lax.fori_loop(0, tiles, forward_tile, 0)
    each(1, peers, lambda k: out_x(k).wait_send())
    xs_ref[...] = low(acc_ref[:total, :]).reshape(peers, rows, width)
    ysend_ref[0] = low(acc_ref[total:, :]).reshape(peers, rows, width)
    return_order(lambda k: across(0, k).start())
    each(0, 2, lambda m: turn_rows(x_ref, xt_ref, m))
    acc_ref[...] = jnp.zeros_like(acc_ref)
    each(0, peers, lambda k: pass_g(k).wait_recv())

    def slope_tile(tile, carry):
        lanes = pl.multiple_of(tile * TILE, TILE)
        here_lanes = pl.ds(lanes, TILE)

        def one_half(m):
            band = pl.ds(pl.multiple_of(m * total, total), total)
            gate = wide(gate_ref[band, here_lanes])
            up = wide(up_ref[band, here_lanes])
            sig = 1.0 / (1.0 + jnp.exp(-gate))
            d_act = nn_dot(g_ref[m].reshape(total, width), weights(2, lanes))
            d_up = low(d_act * gate * sig)
            d_gate = low(d_act * up * sig * (1.0 + gate * (1.0 - sig)))
            gate_ref[band, here_lanes] = d_gate
            up_ref[band, here_lanes] = d_up
            acc_ref[band, :] += nt_dot(d_gate, weights(0, lanes)) + nt_dot(
                d_up, weights(1, lanes)
            )

        each(0, 2, one_half)
        join_some(0, tile)
        return carry

    lax.fori_loop(0, tiles, slope_tile, 0)
    join_last(0)
    each(1, peers, lambda k: out_g(k).wait_send())
    gs_ref[...] = low(acc_ref[:total, :]).reshape(peers, rows, width)
    ysend_ref[1] = low(acc_ref[total:, :]).reshape(peers, rows, width)
    return_order(lambda k: across(1, k).start())
    each(0, 2, lambda m: turn_rows(g_ref, gt_ref, m))

    def weight_tile(tile, carry):
        lanes = pl.multiple_of(tile * TILE, TILE)
        here_lanes = pl.ds(lanes, TILE)

        def keep(which, values):
            grads_ref[
                :, :, :, pl.ds(pl.multiple_of(which * hidden + lanes, TILE), TILE)
            ] = low(values).reshape(peers // 2, 2, rows, TILE)

        keep(0, nn_dot(xt_ref[...], gate_ref[:, here_lanes]))
        keep(1, nn_dot(xt_ref[...], up_ref[:, here_lanes]))
        keep(2, nn_dot(gt_ref[...], act_ref[:, here_lanes]))
        join_some(1, tile)
        return carry

    lax.fori_loop(0, tiles, weight_tile, 0)
    swap_grads = send_to(
        grads_ref.at[:, 1 - core], sibling_ref, grad_sem.at[0], grad_sem.at[1], sibling
    )
    swap_grads.start()
    join_last(1)
    each(0, peers, lambda k: pass_x(k).wait_send())
    each(0, peers, lambda k: pass_g(k).wait_send())
    for index in range(2):
        each(0, peers, lambda k: across(index, k).wait_send())
        each(1, peers, lambda k: back(index, k).wait_send())
    swap_grads.wait()
    grads_out_ref[...] = low(wide(grads_ref[:, core]) + wide(sibling_ref[...]))
    for index in range(2):
        each(1, peers, lambda k: back(index, k).wait_recv())


def run_expert(s2, cot, lines, slots, weights):
    length, width = s2.shape
    experts, shard, total = weights.shape
    peers = 2 * experts
    rows = slots.shape[0] // peers
    hidden = total // 3
    both = 2 * peers * rows
    vmem = pl.BlockSpec(memory_space=pltpu.VMEM)
    low_t, wide_t = jnp.bfloat16, jnp.float32
    dma = pltpu.SemaphoreType.DMA
    block = (peers, rows, width)
    return pl.pallas_call(
        expert_kernel,
        in_specs=[vmem] * 4 + [pl.BlockSpec(memory_space=pl.ANY)],
        out_specs=[vmem] * 3,
        out_shape=[
            jax.ShapeDtypeStruct(block, low_t),
            jax.ShapeDtypeStruct(block, low_t),
            jax.ShapeDtypeStruct(weights.shape, low_t),
        ],
        scratch_shapes=[
            pltpu.VMEM(block, low_t),
            pltpu.VMEM(block, low_t),
            pltpu.VMEM((2,) + block, low_t),
            pltpu.VMEM((2,) + block, low_t),
            pltpu.VMEM((experts, 2, shard, total), low_t),
            pltpu.VMEM((both, hidden), low_t),
            pltpu.VMEM((both, hidden), low_t),
            pltpu.VMEM((both, hidden), low_t),
            pltpu.VMEM((width, both), low_t),
            pltpu.VMEM((width, both), low_t),
            pltpu.VMEM((both, width), wide_t),
            pltpu.VMEM((experts, 2, shard, total), low_t),
            pltpu.VMEM((experts, shard, total), low_t),
            pltpu.VMEM((2,) + block, low_t),
            pltpu.VMEM((2,) + block, low_t),
            dma((3,)),
            dma((2,)),
        ]
        + [dma((peers,))] * 8
        + [dma((2, peers))] * 2
        + [dma((peers,))] * 4,
        compiler_params=pltpu.CompilerParams(
            collective_id=2, has_side_effects=True, vmem_limit_bytes=67043328
        ),
    )(s2, cot, lines, slots, weights)


def attend(
    hid_ref,
    token_block,
    weight,
    small_ref,
    gains,
    table_ref,
    s1_ref,
    qkv_ref,
    lse_ref,
    mixed_ref,
    mid_ref,
    s2_ref,
    tok_ref,
    line_ref,
    vt_ref,
    send_ref,
    recv_ref,
    send_sem,
    recv_sem,
    between,
):
    blocks = hid_ref.shape[0] // BLOCK
    heads_width = mixed_ref.shape[1]
    pairs = heads_width // PAIR
    gain_one, gain_two = gains
    lse_ref[...] = jnp.zeros_like(lse_ref)

    def copy(block):
        return to_partner(
            send_ref.at[block], recv_ref.at[block], send_sem.at[block], recv_sem.at[block]
        )

    def compute(block):
        rows = block_rows(block)
        source = wide(hid_ref[rows, :])
        s1 = low(source * lax.rsqrt(mean_last(source * source) + EPSILON) * gain_one)
        s1_ref[:, rows] = s1.T
        cosine, sine = spread_table(table_ref, block)
        for part in range(3):
            projected = nn_dot(s1, weight(part))
            for pair in range(pairs):
                chunk = projected[:, pair * PAIR : (pair + 1) * PAIR]
                if part < 2:
                    chunk = turn(chunk, cosine, sine)
                else:
                    vt_ref[pair * PAIR : (pair + 1) * PAIR, rows] = low(chunk.T)
                start = part * heads_width + pair * PAIR
                qkv_ref[rows, start : start + PAIR] = low(chunk)

        def one_pair(keys, pair):
            start = pl.multiple_of(pair * PAIR, PAIR)
            lanes = pl.ds(start, PAIR)
            key_lanes = pl.ds(pl.multiple_of(heads_width + start, PAIR), PAIR)
            query = qkv_ref[rows, lanes] * jnp.bfloat16(SCALING)
            key = qkv_ref[:keys, key_lanes]
            value_t = vt_ref[lanes, :keys]
            gathered = None
            for half in range(2):
                masked = jnp.where(head_lanes(query.shape, half, 1), query, jnp.bfloat16(0))
                scores = nt_dot(key, masked)
                highest = jnp.max(scores, axis=0, keepdims=True)
                expanded = jnp.exp(scores - highest)
                totals = jnp.sum(expanded, axis=0, keepdims=True)
                probs = low(expanded * (1.0 / totals))
                lse_ref[pl.ds(2 * pair + half, 1), rows] = highest + jnp.log(totals)
                found = nn_dot(value_t, probs)
                gathered = (
                    found
                    if half == 0
                    else jnp.where(head_lanes(found.shape, 1, 0), found, gathered)
                )
            mixed_ref[rows, lanes] = low(gathered.T)

        for static in range(blocks):

            @pl.when(block == static)
            def _():
                each(0, pairs, functools.partial(one_pair, (static + 1) * BLOCK))

        send_ref[block] = low(nt_dot(mixed_ref[rows, :], weight(3)))
        copy(block).start()

    def finish(block):
        rows = block_rows(block)
        copy(block).wait()
        mid = wide(hid_ref[rows, :]) + (wide(send_ref[block]) + wide(recv_ref[block]))
        mid_ref[rows, :] = mid
        s2 = low(mid * lax.rsqrt(mean_last(mid * mid) + EPSILON) * gain_two)
        s2_ref[rows, :] = s2
        tok = token_block(block)
        lane = lax.broadcasted_iota(jnp.int32, tok.shape, 1)
        logits = nn_dot(s2, small_ref[...]) + tok
        picked = [
            jnp.sum(
                jnp.where(wide(lane - ROUTER) == column(tok, ROUTE + member), logits, 0.0),
                axis=1,
                keepdims=True,
            )
            for member in range(2)
        ]
        gate = [
            1.0 / (1.0 + jnp.exp(picked[1 - member] - picked[member])) for member in range(2)
        ]
        tok = jnp.where(lane == GATE, gate[0], jnp.where(lane == GATE + 1, gate[1], tok))
        tok_ref[rows, :] = tok
        line_ref[:, rows] = tok.T[TARGET : TARGET + 8, :]

    each(0, blocks, compute)
    between()
    each(0, blocks, finish)


def forward_plain_kernel(
    hid_ref,
    tok_in_ref,
    block_ref,
    small_ref,
    rows_ref,
    table_ref,
    shard_ref,
    cot_own_ref,
    s1_ref,
    qkv_ref,
    lse_ref,
    mixed_ref,
    mid_ref,
    s2_ref,
    tok_ref,
    line_ref,
    expert_ref,
    cot_ref,
    vt_ref,
    send_ref,
    recv_ref,
    send_sem,
    recv_sem,
    wsend_sem,
    wrecv_sem,
    cot_sem,
):
    greet_group(2 * shard_ref.shape[0])
    own_rows = cot_own_ref.shape[0]
    heads_width = mixed_ref.shape[1]
    width = hid_ref.shape[1]
    mine = pl.ds(pl.multiple_of(lax.axis_index("tp") * own_rows, own_rows), own_rows)
    cot_copy = to_partner(cot_own_ref, cot_ref.at[mine], cot_sem.at[0], cot_sem.at[1])
    cot_copy.start()
    experts = CoreExchange(shard_ref, expert_ref, wsend_sem, wrecv_sem)
    experts.start()
    cot_ref[mine, :] = cot_own_ref[...]

    def weight(part):
        return block_ref[:, :, part * heads_width : (part + 1) * heads_width].reshape(
            width, heads_width
        )

    attend(
        hid_ref,
        lambda block: tok_in_ref[block_rows(block), :],
        weight,
        small_ref,
        (rows_ref[0:1, :], rows_ref[1:2, :]),
        table_ref,
        s1_ref,
        qkv_ref,
        lse_ref,
        mixed_ref,
        mid_ref,
        s2_ref,
        tok_ref,
        line_ref,
        vt_ref,
        send_ref,
        recv_ref,
        send_sem,
        recv_sem,
        lambda: None,
    )
    cot_copy.wait()
    experts.wait()


def forward_kernel(
    hid_own_ref,
    cot_own_ref,
    logit_ref,
    route_ref,
    rank_ref,
    drop_ref,
    gain_ref,
    router_ref,
    mixing_ref,
    value_ref,
    wqkv_ref,
    wout_ref,
    win_ref,
    wdown_ref,
    table_ref,
    all_out,
    small_ref,
    rows_ref,
    s1_out,
    qkv_out,
    lse_ref,
    mixed_out,
    mid_ref,
    s2_ref,
    tok_ref,
    line_ref,
    expert_ref,
    cot_out,
    all_ref,
    s1_ref,
    qkv_ref,
    mixed_ref,
    cot_ref,
    hid_ref,
    vt_ref,
    send_ref,
    recv_ref,
    shard_ref,
    stage_ref,
    small_all_ref,
    tok_all_ref,
    send_sem,
    recv_sem,
    wsend_sem,
    wrecv_sem,
    y_send,
    y_recv,
    up_send,
    up_recv,
    down_send,
    down_recv,
    x_send,
    x_recv,
    core_send,
    core_recv,
    store_sem,
):
    size, shard, _ = all_ref.shape
    planes = size // 4
    me = lax.axis_index("fsdp")
    tp = lax.axis_index("tp")
    z, x, core = me // 4, lax.rem(me // 2, 2), lax.rem(me, 2)
    own_rows, width = hid_own_ref.shape
    heads_width = wout_ref.shape[1]
    small_rows = shard // 2
    greet_group(size)
    partner = {"tp": 1 - tp}
    mine = pl.ds(pl.multiple_of(tp * own_rows, own_rows), own_rows)
    hid_y = send_to(hid_own_ref, hid_ref.at[mine], y_send.at[1], y_recv.at[1], partner)
    stage_ref[...] = jnp.zeros_like(stage_ref)
    stage_ref[0:2, :small_rows] = gain_ref[...]
    stage_ref[ROUTER:MIXING, :small_rows] = wide(router_ref[...])
    stage_ref[MIXING:VALUE, :small_rows] = wide(mixing_ref[...])
    stage_ref[VALUE : VALUE + 2, :small_rows] = wide(value_ref[...])
    small_all_ref[me, tp] = stage_ref[...].T[:small_rows, :]
    small_y = send_to(
        small_all_ref.at[me, tp], small_all_ref.at[me, tp], y_send.at[0], y_recv.at[0], partner
    )
    small_y.start()
    hid_y.start()
    for part in range(3):
        all_ref[me, :, part * heads_width : (part + 1) * heads_width] = wqkv_ref[part]
    all_ref[me, :, 3 * heads_width :] = wout_ref[...]
    tok_y = send_to(tok_all_ref.at[tp], tok_all_ref.at[tp], y_send.at[2], y_recv.at[2], partner)

    def cot_copy(part):
        count = own_rows // 4
        near = pl.ds(part * count, count)
        far = pl.ds(pl.multiple_of(tp * own_rows + part * count, count), count)
        return send_to(
            cot_own_ref.at[near], cot_ref.at[far], y_send.at[3 + part], y_recv.at[3 + part], partner
        )

    experts = CoreExchange(shard_ref, expert_ref, wsend_sem, wrecv_sem)
    expert_count, _, hidden = wdown_ref.shape

    def stage_tokens():
        tok_all_ref[tp] = jnp.zeros(tok_all_ref.shape[1:], jnp.float32)
        routes = route_ref[...]
        kept = jnp.logical_and(routes < expert_count, drop_ref[...] == 0)
        target = jnp.where(kept, routes * (own_rows * 2 * 9 // 48) + rank_ref[...], -1)
        tok_all_ref[tp, ROUTER:MIXING, :] = logit_ref[...]
        tok_all_ref[tp, ROUTE : ROUTE + 2, :] = wide(routes)
        tok_all_ref[tp, TARGET : TARGET + 2, :] = wide(target)

    def stage_shard():
        def one(e):
            for part in range(2):
                shard_ref[e, :, part * hidden : (part + 1) * hidden] = win_ref[e, :, part, :]
            shard_ref[e, :, 2 * hidden :] = wdown_ref[e]

        each(0, expert_count, one)

    def number(plane, line):
        return plane * 4 + line * 2 + core

    def piece(kind, number_of, send, recv, slot, device):
        array = small_all_ref if kind else all_ref
        return send_to(
            array.at[number_of],
            array.at[number_of],
            send.at[kind, slot],
            recv.at[kind, slot],
            device,
        )

    def up(kind, step, plane):
        device = {"fsdp": number(lax.min(z + 1, planes - 1), x)}
        return piece(kind, number(plane, x), up_send, up_recv, step, device)

    def down(kind, step, plane):
        device = {"fsdp": number(lax.max(z - 1, 0), x)}
        return piece(kind, number(plane, x), down_send, down_recv, step, device)

    def side(kind, plane, line):
        device = {"fsdp": number(z, 1 - x)}
        return piece(kind, number(plane, line), x_send, x_recv, plane, device)

    def sibling(kind, plane, line, parity):
        return piece(
            kind,
            plane * 4 + line * 2 + parity,
            core_send,
            core_recv,
            plane * 2 + line,
            {"fsdp": me + 1 - 2 * core},
        )

    def launch(kind):
        @pl.when(z < planes - 1)
        def _():
            up(kind, 0, z).start()

        @pl.when(z > 0)
        def _():
            down(kind, 0, z).start()

        side(kind, z, x).start()
        sibling(kind, z, x, core).start()

    launch(0)
    stage_tokens()
    tok_y.start()
    for part in range(4):
        cot_copy(part).start()
    hid_ref[mine, :] = hid_own_ref[...]
    cot_ref[mine, :] = cot_own_ref[...]
    small_y.wait()
    launch(1)
    stage_shard()
    for step in range(1, planes):
        for kind in range(2):

            @pl.when(z >= step)
            def _():
                up(kind, step - 1, z - step).wait_recv()

                @pl.when(z < planes - 1)
                def _():
                    up(kind, step, z - step).start()

                side(kind, z - step, x).start()
                sibling(kind, z - step, x, core).start()

            @pl.when(z + step < planes)
            def _():
                down(kind, step - 1, z + step).wait_recv()

                @pl.when(z > 0)
                def _():
                    down(kind, step, z + step).start()

                side(kind, z + step, x).start()
                sibling(kind, z + step, x, core).start()

    experts.start()
    for step in range(planes):
        for kind in range(2):

            @pl.when(z >= step)
            def _():
                side(kind, z - step, 1 - x).wait_recv()
                sibling(kind, z - step, 1 - x, core).start()

            if step > 0:

                @pl.when(z + step < planes)
                def _():
                    side(kind, z + step, 1 - x).wait_recv()
                    sibling(kind, z + step, 1 - x, core).start()

    for plane in range(planes):
        for line in range(2):
            for kind in range(2):
                sibling(kind, plane, line, 1 - core).wait_recv()
    small_all = small_all_ref[...].reshape(width, PAIR)
    small_ref[...] = low(small_all)
    rows_ref[...] = small_all.T[:8, :]
    tok_y.wait()
    hid_y.wait()

    def token_block(block):
        per = own_rows // BLOCK
        lanes = pl.ds(pl.multiple_of(lax.rem(block, per) * BLOCK, BLOCK), BLOCK)
        part = tok_all_ref[block // per, :, lanes]
        blank = jnp.zeros((PAIR - part.shape[0], BLOCK), jnp.float32)
        return jnp.concatenate([part, blank], axis=0).T

    def weight(part):
        return all_ref[:, :, part * heads_width : (part + 1) * heads_width].reshape(
            width, heads_width
        )

    stores = [
        pltpu.make_async_copy(source, target, store_sem.at[index])
        for index, (source, target) in enumerate(
            [
                (all_ref, all_out),
                (s1_ref, s1_out),
                (qkv_ref, qkv_out),
                (mixed_ref, mixed_out),
                (cot_ref, cot_out),
            ]
        )
    ]
    stores[0].start()

    def between():
        for store in stores[1:4]:
            store.start()
        for part in range(4):
            cot_copy(part).wait()
        stores[4].start()

    attend(
        hid_ref,
        token_block,
        weight,
        small_ref,
        (rows_ref[0:1, :], rows_ref[1:2, :]),
        table_ref,
        s1_ref,
        qkv_ref,
        lse_ref,
        mixed_ref,
        mid_ref,
        s2_ref,
        tok_ref,
        line_ref,
        vt_ref,
        send_ref,
        recv_ref,
        send_sem,
        recv_sem,
        between,
    )
    for kind in range(2):
        for step in range(planes):

            @pl.when(jnp.logical_and(z >= step, z < planes - 1))
            def _():
                up(kind, step, z - step).wait_send()

            @pl.when(jnp.logical_and(z + step < planes, z > 0))
            def _():
                down(kind, step, z + step).wait_send()

        for plane in range(planes):
            side(kind, plane, x).wait_send()
            for line in range(2):
                sibling(kind, plane, line, core).wait_send()
    for store in stores:
        store.wait()
    experts.wait()


def backward_body(
    stages,
    res_ref,
    dx_ref,
    slot_ref,
    tok_ref,
    cot_ref,
    mid_hbm,
    s1_hbm,
    qkv_hbm,
    lse_ref,
    mixed_hbm,
    block_hbm,
    small_ref,
    rows_ref,
    table_ref,
    own_ref,
    egrad_ref,
    grad_ref,
    base_ref,
    other_ref,
    big_ref,
    arrived_ref,
    gsend_ref,
    grecv_ref,
    ssend_ref,
    srecv_ref,
    mid_ref,
    s1_ref,
    qkv_ref,
    mixed_ref,
    block_ref,
    hsend_ref,
    hrecv_ref,
    gmid_ref,
    gown_ref,
    kt_ref,
    gm_ref,
    dk_ref,
    dv_ref,
    gp_ref,
    att_ref,
    s2_ref,
    slope_ref,
    value_ref,
    acc_gain_ref,
    gsend_sem,
    grecv_sem,
    hsend_sem,
    hrecv_sem,
    esend_sem,
    erecv_sem,
    ssend_sem,
    srecv_sem,
    load_sem,
):
    loads = [
        pltpu.make_async_copy(source, target, load_sem.at[index])
        for index, (source, target) in enumerate(
            [
                (mid_hbm, mid_ref),
                (qkv_hbm, qkv_ref),
                (mixed_hbm, mixed_ref),
                (block_hbm, block_ref),
                (s1_hbm, s1_ref),
            ]
        )
    ]
    for load in loads:
        load.start()
    greet_group(2 * egrad_ref.shape[0])
    experts = CoreExchange(egrad_ref, arrived_ref, esend_sem, erecv_sem)
    tp = lax.axis_index("tp")
    width = dx_ref.shape[1]
    blocks = cot_ref.shape[0] // BLOCK
    heads_width = mixed_ref.shape[1]
    pairs = heads_width // PAIR
    gain_one = rows_ref[0:1, :]
    gain_two = rows_ref[1:2, :]
    slot_row = slot_ref[0:1, :]

    def weights(first_part, last_part):
        lanes = slice(first_part * heads_width, last_part * heads_width)
        return block_ref[:, :, lanes].reshape(width, (last_part - first_part) * heads_width)

    half_blocks = blocks // 2
    experts.start()

    def row_copy(block):
        return to_partner(
            gsend_ref.at[block], grecv_ref.at[block], gsend_sem.at[block], grecv_sem.at[block]
        )

    def share_copy(block):
        return to_partner(
            ssend_ref.at[block], srecv_ref.at[block], ssend_sem.at[block], srecv_sem.at[block]
        )

    def stream_copy(slot):
        return to_partner(
            hsend_ref.at[slot], hrecv_ref.at[slot], hsend_sem.at[slot], hrecv_sem.at[slot]
        )

    def slab_of(block):
        return block_rows(lax.rem(block, half_blocks))

    def backwards(body):
        each(0, blocks, lambda step: body(blocks - 1 - step))

    def send_rows(block):
        rows = block_rows(block)
        tok = tok_ref[rows, :]
        onehots = [low(jnp.where(column(tok, TARGET + m) == slot_row, 1.0, 0.0)) for m in range(2)]
        gsend_ref[block] = low(nn_dot(onehots[0] + onehots[1], dx_ref[...]))
        row_copy(block).start()
        both = nn_dot(jnp.concatenate(onehots, axis=0), res_ref[...])
        placed = [both[:BLOCK], both[BLOCK:]]
        cot_wide = wide(cot_ref[rows, :])
        shares = [
            column(tok, GATE + m) * jnp.sum(placed[m] * cot_wide, axis=1, keepdims=True)
            for m in range(2)
        ]
        ssend_ref[block] = lane_matrix(tok.shape, [(0, shares[0]), (1, shares[1])]).T[:8, :]
        share_copy(block).start()
        mixture = column(tok, GATE) * placed[0] + column(tok, GATE + 1) * placed[1]

        @pl.when(tp == block // half_blocks)
        def _():
            base_ref[slab_of(block), :] = mixture

        @pl.when(tp != block // half_blocks)
        def _():
            other_ref[slab_of(block), :] = low(mixture)

    early, begin, middle, end = stages
    backwards(send_rows)
    early()
    for load in loads:
        load.wait()
    kt_ref[...] = qkv_ref[:, heads_width : 2 * heads_width].T
    dk_ref[...] = jnp.zeros_like(dk_ref)
    dv_ref[...] = jnp.zeros_like(dv_ref)
    acc_gain_ref[...] = jnp.zeros_like(acc_gain_ref)

    def main(block):
        rows = block_rows(block)
        mine = tp == block // half_blocks
        mine_f = jnp.where(mine, 1.0, 0.0)
        mid = mid_ref[rows, :]
        cot = cot_ref[rows, :]
        cot_wide = wide(cot)
        tok = tok_ref[rows, :]
        scale = lax.rsqrt(mean_last(mid * mid) + EPSILON)
        unit = mid * scale
        normed = unit * gain_two
        s2 = low(normed)
        small = small_ref[...]
        mixing = nn_dot(s2, small)
        value_dot = nn_dot(cot, small)
        normed_dot = jnp.sum(normed * cot_wide, axis=1, keepdims=True)
        route = [column(tok, ROUTE + member) for member in range(2)]
        gate = [column(tok, GATE + member) for member in range(2)]

        def weight_of(expert):
            return sum(jnp.where(route[m] == expert, gate[m], 0.0) for m in range(2))

        copy_weight = weight_of(COPY)
        copy_share = [jnp.where(route[m] == COPY, normed_dot, 0.0) for m in range(2)]
        alpha = copy_weight
        columns = []
        value_columns = []
        for c in range(2):
            weight = weight_of(COPY + 1 + c)
            left = column(mixing, MIXING + 2 * c)
            right = column(mixing, MIXING + 2 * c + 1)
            a0 = 1.0 / (1.0 + jnp.exp(right - left))
            a1 = 1.0 / (1.0 + jnp.exp(left - right))
            vd = column(value_dot, VALUE + c)
            alpha = alpha + weight * a0
            for m in range(2):
                copy_share[m] = copy_share[m] + jnp.where(
                    route[m] == COPY + 1 + c, a0 * normed_dot + a1 * vd, 0.0
                )
            slope = a0 * a1 * weight * (normed_dot - vd)
            columns.append((MIXING + 2 * c, slope))
            columns.append((MIXING + 2 * c + 1, -slope))
            value_columns.append((VALUE + c, weight * a1))
        value_matrix = lane_matrix(tok.shape, value_columns)

        @pl.when(mine)
        def _():
            base_ref[slab_of(block), :] += (
                mid + alpha * normed + nt_dot(low(value_matrix), small)
            )

        row_copy(block).wait()
        share_copy(block).wait()
        extra = ssend_ref[block] + srecv_ref[block]
        extra = jnp.concatenate(
            [extra, jnp.zeros((PAIR - extra.shape[0], BLOCK), jnp.float32)], axis=0
        ).T
        share = [column(extra, m) + gate[m] * copy_share[m] for m in range(2)]
        lane = lax.broadcasted_iota(jnp.int32, tok.shape, 1)
        slopes = lane_matrix(tok.shape, columns)
        for m in range(2):
            local = share[m] - gate[m] * (share[0] + share[1])
            slopes = slopes + jnp.where(wide(lane - ROUTER) == route[m], local, 0.0)
        slopes_low = low(slopes)
        grad_normed = (
            wide(gsend_ref[block])
            + wide(grecv_ref[block])
            + alpha * cot_wide
            + nt_dot(slopes_low, small)
        )
        s2_ref[rows, :] = s2
        slope_ref[rows, :] = low(slopes * mine_f)
        value_ref[rows, :] = low(value_matrix * mine_f)
        gain_grad = jnp.sum(unit * grad_normed, axis=0, keepdims=True) * mine_f
        acc_gain_ref[...] += jnp.broadcast_to(gain_grad, acc_gain_ref.shape)
        scaled = grad_normed * gain_two
        grad_mid = cot_wide + scale * (scaled - unit * mean_last(scaled * unit))
        gmid_ref[rows, :] = grad_mid
        attended = low(grad_mid)
        att_ref[rows, :] = attended
        gm_ref[...] = low(nn_dot(attended, weights(3, 4)))
        cosine, sine = spread_table(table_ref, block)

        def one_pair(keys, pair):
            start = pl.multiple_of(pair * PAIR, PAIR)
            lanes = pl.ds(start, PAIR)
            key_lanes = pl.ds(pl.multiple_of(heads_width + start, PAIR), PAIR)
            value_lanes = pl.ds(pl.multiple_of(2 * heads_width + start, PAIR), PAIR)
            query = qkv_ref[rows, lanes] * jnp.bfloat16(SCALING)
            key = qkv_ref[:keys, key_lanes]
            value = qkv_ref[:keys, value_lanes]
            grad_out = gm_ref[:, lanes]
            key_t = kt_ref[lanes, :keys]
            grad_value = None
            for half in range(2):
                keep = head_lanes(query.shape, half, 1)
                q_half = jnp.where(keep, query, jnp.bfloat16(0))
                g_half = jnp.where(keep, grad_out, jnp.bfloat16(0))
                probs = jnp.exp(nt_dot(key, q_half) - lse_ref[pl.ds(2 * pair + half, 1), rows])
                grad_probs = nt_dot(value, g_half)
                inner = jnp.sum(probs * grad_probs, axis=0, keepdims=True)
                grad_scores = low(probs * (grad_probs - inner))
                value_part = nn_dot(low(probs), g_half)
                key_part = nn_dot(grad_scores, q_half)
                query_part = nn_dot(key_t, grad_scores)
                if half == 0:
                    grad_value, grad_key, grad_query = value_part, key_part, query_part
                else:
                    grad_value = grad_value + value_part
                    grad_key = grad_key + key_part
                    grad_query = jnp.where(
                        head_lanes(query_part.shape, 1, 0), query_part, grad_query
                    )
            dv_ref[:keys, lanes] += grad_value
            dk_ref[:keys, lanes] += grad_key
            gp_ref[rows, lanes] = low(turn(grad_query.T * SCALING, cosine, -sine))
            gp_ref[rows, key_lanes] = low(turn(dk_ref[rows, lanes], cosine, -sine))
            gp_ref[rows, value_lanes] = low(dv_ref[rows, lanes])

        for static in range(blocks):

            @pl.when(block == static)
            def _():
                each(0, pairs, functools.partial(one_pair, (static + 1) * BLOCK))

        stream_grad = nt_dot(gp_ref[rows, :], weights(0, 3))
        slot = lax.rem(block, half_blocks)

        @pl.when(mine)
        def _():
            gown_ref[slot] = stream_grad

        @pl.when(jnp.logical_not(mine))
        def _():
            hsend_ref[slot] = low(stream_grad)
            stream_copy(slot).start()

    backwards(main)
    for part in range(3):
        lanes = slice(part * heads_width, (part + 1) * heads_width)
        big_ref[:, :, lanes] = low(nn_dot(s1_ref[...], gp_ref[:, lanes])).reshape(
            big_ref.shape[:2] + (heads_width,)
        )
    big_ref[:, :, 3 * heads_width : 4 * heads_width] = low(
        tn_dot(att_ref[...], mixed_ref[...])
    ).reshape(big_ref.shape[:2] + (heads_width,))
    tall = jnp.where(
        lax.broadcasted_iota(jnp.int32, (PAIR, width), 0) == 1,
        jnp.broadcast_to(acc_gain_ref[0:1, :], (PAIR, width)),
        0.0,
    )
    big_ref[:, :, 4 * heads_width :] = low(
        tn_dot(s2_ref[...], slope_ref[...]) + tn_dot(cot_ref[...], value_ref[...]) + tall.T
    ).reshape(big_ref.shape[:2] + (PAIR,))
    begin()
    middle()
    for slot in reversed(range(half_blocks)):
        slab = slice(slot * BLOCK, (slot + 1) * BLOCK)
        stream_copy(slot).wait()
        source = wide(own_ref[slab, :])
        scale = lax.rsqrt(mean_last(source * source) + EPSILON)
        unit = source * scale
        scaled = (gown_ref[slot] + wide(hrecv_ref[slot])) * gain_one
        mid_rows = block_rows(tp * half_blocks + slot)
        grad_ref[slab, :] = gmid_ref[mid_rows, :] + scale * (
            scaled - unit * mean_last(scaled * unit)
        )
    end()
    experts.wait()


def backward_plain_kernel(*refs):
    backward_body([lambda: None] * 4, *refs)


def backward_kernel(body_count, *refs):
    operands, wqkv_ref = refs[:16], refs[16]
    grad_ref, base_ref, arrived_ref, y_ref, red_ref, tail_ref = refs[17:23]
    other_ref, big_ref = refs[23:25]
    body, sums = refs[25 : 25 + body_count], refs[25 + body_count :]
    stages = sum_stages(big_ref, wqkv_ref, other_ref, y_ref, red_ref, tail_ref, *sums)
    backward_body(stages, *operands, grad_ref, base_ref, other_ref, big_ref, arrived_ref, *body)


def forward_results(length, width, heads_width, shard):
    low_t, wide_t = jnp.bfloat16, jnp.float32
    return [
        jax.ShapeDtypeStruct((width, length), low_t),
        jax.ShapeDtypeStruct((length, 3 * heads_width), low_t),
        jax.ShapeDtypeStruct((8, length), wide_t),
        jax.ShapeDtypeStruct((length, heads_width), low_t),
        jax.ShapeDtypeStruct((length, width), wide_t),
        jax.ShapeDtypeStruct((length, width), low_t),
        jax.ShapeDtypeStruct((length, PAIR), wide_t),
        jax.ShapeDtypeStruct((8, length), wide_t),
        jax.ShapeDtypeStruct(shard, low_t),
        jax.ShapeDtypeStruct((length, width), low_t),
    ]


def attend_scratch(length, width, heads_width):
    blocks = length // BLOCK
    return [
        pltpu.VMEM((heads_width, length), jnp.bfloat16),
        pltpu.VMEM((blocks, BLOCK, width), jnp.bfloat16),
        pltpu.VMEM((blocks, BLOCK, width), jnp.bfloat16),
    ]


def run_forward_plain(hid, tok, blocks, small, rows, table, shard, cot):
    length, width = hid.shape
    heads_width = blocks.shape[2] // 4
    vmem = pl.BlockSpec(memory_space=pltpu.VMEM)
    dma = pltpu.SemaphoreType.DMA
    count = length // BLOCK
    return pl.pallas_call(
        forward_plain_kernel,
        in_specs=[vmem] * 8,
        out_specs=[vmem] * 10,
        out_shape=forward_results(length, width, heads_width, shard.shape),
        scratch_shapes=attend_scratch(length, width, heads_width)
        + [dma((count,)), dma((count,)), dma((shard.shape[0],)), dma((shard.shape[0],)), dma((2,))],
        compiler_params=pltpu.CompilerParams(
            collective_id=0, has_side_effects=True, vmem_limit_bytes=60 << 20
        ),
    )(hid, tok, blocks, small, rows, table, shard, cot)


def run_forward(*operands):
    hid, wout, wdown, table = operands[0], operands[11], operands[13], operands[14]
    own_rows, width = hid.shape
    length = 2 * table.shape[0]
    shard, heads_width = wout.shape
    experts, _, hidden = wdown.shape
    size = lax.axis_size("fsdp")
    count = length // BLOCK
    hbm = pl.BlockSpec(memory_space=pl.ANY)
    vmem = pl.BlockSpec(memory_space=pltpu.VMEM)
    low_t, wide_t = jnp.bfloat16, jnp.float32
    dma = pltpu.SemaphoreType.DMA
    return pl.pallas_call(
        forward_kernel,
        in_specs=[vmem] * 15,
        out_specs=[hbm, vmem, vmem, hbm, hbm, vmem, hbm]
        + [vmem] * 4
        + [hbm, hbm],
        out_shape=[
            jax.ShapeDtypeStruct((size, shard, 4 * heads_width), low_t),
            jax.ShapeDtypeStruct((width, PAIR), low_t),
            jax.ShapeDtypeStruct((8, width), wide_t),
        ]
        + forward_results(length, width, heads_width, (experts, shard, 3 * hidden)),
        scratch_shapes=[
            pltpu.VMEM((size, shard, 4 * heads_width), low_t),
            pltpu.VMEM((width, length), low_t),
            pltpu.VMEM((length, 3 * heads_width), low_t),
            pltpu.VMEM((length, heads_width), low_t),
            pltpu.VMEM((length, width), low_t),
            pltpu.VMEM((length, width), low_t),
        ]
        + attend_scratch(length, width, heads_width)
        + [
            pltpu.VMEM((experts, shard, 3 * hidden), low_t),
            pltpu.VMEM((PAIR, PAIR), wide_t),
            pltpu.VMEM((size, 2, shard // 2, PAIR), wide_t),
            pltpu.VMEM((2, 32, own_rows), wide_t),
            dma((count,)),
            dma((count,)),
            dma((experts,)),
            dma((experts,)),
            dma((7,)),
            dma((7,)),
        ]
        + [dma((2, size // 4))] * 6
        + [dma((2, size // 2))] * 2
        + [dma((5,))],
        compiler_params=pltpu.CompilerParams(
            collective_id=3, has_side_effects=True, vmem_limit_bytes=60 << 20
        ),
    )(*operands)


def run_backward(wqkv, *operands):
    cot, mid, s1, qkv, mixed, blocks, own, egrads = (
        operands[index] for index in (4, 5, 6, 7, 9, 10, 14, 15)
    )
    length, width = cot.shape
    heads_width = mixed.shape[1]
    count = length // BLOCK
    own_rows = own.shape[0]
    parts, shard = blocks.shape[:2]
    columns = 4 * heads_width + PAIR
    vmem = pl.BlockSpec(memory_space=pltpu.VMEM)
    hbm = pl.BlockSpec(memory_space=pl.ANY)
    low_t, wide_t = jnp.bfloat16, jnp.float32
    dma = pltpu.SemaphoreType.DMA
    in_specs = [vmem] * 5 + [hbm] * 3 + [vmem] + [hbm] * 2 + [vmem] * 4 + [hbm]
    body = [
        pltpu.VMEM((count, BLOCK, width), low_t),
        pltpu.VMEM((count, BLOCK, width), low_t),
        pltpu.VMEM((count, 8, BLOCK), wide_t),
        pltpu.VMEM((count, 8, BLOCK), wide_t),
        pltpu.VMEM(mid.shape, wide_t),
        pltpu.VMEM(s1.shape, low_t),
        pltpu.VMEM(qkv.shape, low_t),
        pltpu.VMEM(mixed.shape, low_t),
        pltpu.VMEM(blocks.shape, low_t),
        pltpu.VMEM((2, BLOCK, width), low_t),
        pltpu.VMEM((2, BLOCK, width), low_t),
        pltpu.VMEM((length, width), wide_t),
        pltpu.VMEM((2, BLOCK, width), wide_t),
        pltpu.VMEM((heads_width, length), low_t),
        pltpu.VMEM((BLOCK, heads_width), low_t),
        pltpu.VMEM((length, heads_width), wide_t),
        pltpu.VMEM((length, heads_width), wide_t),
        pltpu.VMEM((length, 3 * heads_width), low_t),
        pltpu.VMEM((length, width), low_t),
        pltpu.VMEM((length, width), low_t),
        pltpu.VMEM((length, PAIR), low_t),
        pltpu.VMEM((length, PAIR), low_t),
        pltpu.VMEM((8, width), wide_t),
        dma((count,)),
        dma((count,)),
        dma((2,)),
        dma((2,)),
        dma((egrads.shape[0],)),
        dma((egrads.shape[0],)),
        dma((count,)),
        dma((count,)),
        dma((5,)),
    ]
    own_wide = jax.ShapeDtypeStruct((own_rows, width), wide_t)
    own_low = jax.ShapeDtypeStruct((own_rows, width), low_t)
    arrived = jax.ShapeDtypeStruct(egrads.shape, low_t)
    params = pltpu.CompilerParams(
        collective_id=1, has_side_effects=True, vmem_limit_bytes=67043328
    )
    if wqkv is None:
        return pl.pallas_call(
            backward_plain_kernel,
            in_specs=in_specs,
            out_specs=[vmem] * 4 + [hbm],
            out_shape=[
                own_wide,
                own_wide,
                own_low,
                jax.ShapeDtypeStruct((parts, shard, columns), low_t),
                arrived,
            ],
            scratch_shapes=body,
            compiler_params=params,
        )(*operands)
    return pl.pallas_call(
        functools.partial(backward_kernel, len(body)),
        in_specs=in_specs + [vmem],
        out_specs=[vmem] * 2 + [hbm] + [vmem] * 3,
        out_shape=[
            own_wide,
            own_wide,
            arrived,
            own_low,
            jax.ShapeDtypeStruct((shard, columns - PAIR), wide_t),
            jax.ShapeDtypeStruct((shard // 2, PAIR), wide_t),
        ],
        scratch_shapes=[
            pltpu.VMEM((own_rows, width), low_t),
            pltpu.VMEM((parts, shard, columns), low_t),
        ]
        + body
        + sum_scratch(parts // 4, shard, columns),
        compiler_params=params,
    )(*operands, wqkv)


def shards(
    hidden,
    prev_logits,
    routes,
    slot_rank,
    dropped,
    cotangent,
    attn_norm,
    ffn_norm,
    w_qkv,
    w_attn_out,
    w_router,
    w_const_gate,
    w_const_value,
    w_expert_in,
    w_expert_out,
):
    own_rows, width = hidden.shape
    length = own_rows * lax.axis_size("tp")
    experts = w_expert_in.shape[0]
    route_count = w_router.shape[1]
    capacity = 9 * length // (4 * route_count)
    planned = lax.axis_size("fsdp") == 16
    table = jnp.asarray(rotary_table(length))
    gains = jnp.stack([wide(attn_norm), wide(ffn_norm)], axis=0)
    wqkv = w_qkv.transpose(1, 0, 2)
    operands = (
        hidden,
        cotangent,
        prev_logits.T,
        routes.T,
        slot_rank.T,
        dropped.T,
        gains,
        w_router.T,
        w_const_gate.T,
        w_const_value.T,
        wqkv,
        w_attn_out,
        w_expert_in,
        w_expert_out,
    )
    if planned:
        forward = run_forward(*operands, table)
    else:
        forward = forward_plain(operands, table)
    blocks, small, rows, s1, qkv, lse, mixed, mid, s2, tok, lines, gathered, cot = forward
    expert_weights = join_weights(gathered, experts)
    peers = 2 * experts
    half = capacity // 2
    block = half // 2
    place = jnp.arange(peers * block)
    owner = (lax.axis_index("fsdp") % peers) ^ (place // block)
    slot = wide(
        (owner // 2) * capacity
        + lax.axis_index("tp") * half
        + (owner % 2) * block
        + place % block
    )
    results, grad_rows, grads_exp = run_expert(
        s2, cot, lines, jnp.broadcast_to(slot[:, None], (slot.shape[0], PAIR)), expert_weights
    )
    backward = run_backward(
        wqkv if planned else None,
        results.reshape(-1, width),
        grad_rows.reshape(-1, width),
        jnp.broadcast_to(slot[None, :], (8, slot.shape[0])),
        tok,
        cot,
        mid,
        s1,
        qkv,
        lse,
        mixed,
        blocks,
        small,
        rows,
        table,
        hidden,
        split_grads(grads_exp),
    )
    if planned:
        grad_hidden, base, arrived, received, red, last = backward
    else:
        grad_hidden, base, for_other, big, arrived = backward
        received, red, last = finish_plain(big.reshape(width, -1), wqkv, for_other)
    output, grad_hidden, grad_qkv, grad_attn_out, gain_grads, grad_router, grad_mixing, grad_value, grad_in, grad_out = run_write(
        base, received, grad_hidden, red, last, gains, arrived
    )
    return (
        output,
        grad_hidden,
        gain_grads[0],
        gain_grads[1],
        grad_qkv.transpose(1, 0, 2),
        grad_attn_out,
        grad_router.T,
        grad_mixing.T,
        grad_value.T,
        grad_in,
        grad_out,
    )


def solution(mesh):
    in_specs = (
        P(("fsdp", "tp"), None),
        P(("fsdp", "tp"), None),
        P(("fsdp", "tp"), None),
        P(("fsdp", "tp"), None),
        P(("fsdp", "tp"), None),
        P(("fsdp", "tp"), None),
        P(("fsdp", "tp")),
        P(("fsdp", "tp")),
        P("fsdp", None, "tp"),
        P("fsdp", "tp"),
        P(("fsdp", "tp"), None),
        P(("fsdp", "tp"), None),
        P(("fsdp", "tp"), None),
        P(None, "fsdp", None, "tp"),
        P(None, "fsdp", "tp"),
    )
    out_specs = (
        P(("fsdp", "tp"), None),
        P(("fsdp", "tp"), None),
        P(("fsdp", "tp")),
        P(("fsdp", "tp")),
        P("fsdp", None, "tp"),
        P("fsdp", "tp"),
        P(("fsdp", "tp"), None),
        P(("fsdp", "tp"), None),
        P(("fsdp", "tp"), None),
        P(None, "fsdp", None, "tp"),
        P(None, "fsdp", "tp"),
    )
    return jax.shard_map(shards, mesh=mesh, in_specs=in_specs, out_specs=out_specs, check_vma=False)
```

```python
import functools

import jax
import jax.numpy as jnp
import numpy as np
from jax import lax
from jax.experimental import pallas as pl
from jax.experimental.pallas import tpu as pltpu
from jax.sharding import PartitionSpec as P

HD = 64
BLOCK = 256


EPSILON = 1e-06
MESH = pl.DeviceIdType.MESH
PAIR = 2 * HD
SCALING = HD ** (-0.5)
ROUTER = 2
MIXING = 14
VALUE = 18
ROUTE = 20
TARGET = 24
GATE = 26
COPY = 9


TILE = 256
SUB = 16


def swap(values):
    return lax.ppermute(values, "tp", [(0, 1), (1, 0)])


def gather_rows(values):
    other = swap(values)
    first = lax.axis_index("tp") == 0
    return jnp.concatenate(
        [jnp.where(first, values, other), jnp.where(first, other, values)], axis=0
    )


def own_half(values):
    half = values.shape[0] // 2
    return lax.dynamic_slice_in_dim(values, lax.axis_index("tp") * half, half, 0)


def other_half(values):
    half = values.shape[0] // 2
    return lax.dynamic_slice_in_dim(values, (1 - lax.axis_index("tp")) * half, half, 0)


def member_groups(size, experts):
    span = 2 * experts
    starts = range(0, size, span)
    cores = [[start + 2 * e, start + 2 * e + 1] for start in starts for e in range(experts)]
    across = [[start + r for start in starts] for r in range(span)]
    return cores, across


def own_core(values, rows):
    parts = values.reshape(-1, 2, rows, values.shape[-1])
    return lax.dynamic_index_in_dim(parts, lax.axis_index("fsdp") % 2, 1, keepdims=False)


def join_weights(got, experts):
    size = lax.axis_size("fsdp")
    if size == 2 * experts:
        return got
    cores, across = member_groups(size, experts)
    got = lax.all_gather(got, "fsdp", axis=1, axis_index_groups=cores, tiled=True)
    got = got.reshape(-1, got.shape[-1])
    got = lax.all_gather(got, "fsdp", axis=0, axis_index_groups=across, tiled=True)
    return own_core(got, got.shape[0] // (2 * experts))


def split_grads(grads):
    experts, _, columns = grads.shape
    size = lax.axis_size("fsdp")
    if size == 2 * experts:
        return grads
    cores, across = member_groups(size, experts)
    grads = lax.all_gather(grads[:, None], "fsdp", axis=1, axis_index_groups=cores, tiled=True)
    grads = grads.reshape(-1, columns)
    grads = lax.psum_scatter(
        grads, "fsdp", scatter_dimension=0, axis_index_groups=across, tiled=True
    )
    return own_core(grads, grads.shape[0] // (2 * experts))


def finish_plain(big, wqkv, other):
    heads_width = (big.shape[1] - PAIR) // 4
    reduced = wide(lax.psum_scatter(big, "fsdp", scatter_dimension=0, tiled=True))
    parts = reduced[:, : 3 * heads_width].reshape(-1, 3, heads_width).transpose(1, 0, 2)
    share = jnp.sum(parts * wide(wqkv), axis=(0, 2))
    last = jnp.concatenate([share[:, None], reduced[:, 4 * heads_width + 1 :]], axis=1)
    return (
        swap(other),
        reduced[:, : 4 * heads_width],
        own_half(last) + swap(other_half(last)),
    )


def forward_plain(operands, table):
    (
        hidden,
        cotangent,
        logits,
        routes,
        rank,
        dropped,
        gains,
        router,
        mixing,
        value,
        wqkv,
        wout,
        w_in,
        w_down,
    ) = operands
    own_rows, width = hidden.shape
    experts, shard, units = w_down.shape
    small = jnp.concatenate([wide(v) for v in (gains, router, mixing, value)], axis=0)
    small = jnp.pad(small, ((0, PAIR - small.shape[0]), (0, 0))).T
    small = lax.all_gather(small, ("fsdp", "tp"), axis=0, tiled=True)
    capacity = own_rows * 2 * 9 // 48
    kept = (routes < experts) & (dropped == 0)
    target = jnp.where(kept, routes * capacity + rank, -1)
    blank = jnp.zeros((2, own_rows), jnp.float32)
    tok = jnp.concatenate(
        [blank, logits, blank, blank, blank, wide(routes), blank, wide(target)], axis=0
    )
    tok = lax.all_gather(tok, "tp", axis=1, tiled=True).T
    tok = jnp.pad(tok, ((0, 0), (0, PAIR - tok.shape[1])))
    blocks = jnp.concatenate([wqkv[0], wqkv[1], wqkv[2], wout], axis=1)
    blocks = lax.all_gather(blocks, "fsdp", axis=0, tiled=True).reshape(2 * experts, -1, blocks.shape[1])
    rows = small.T[:8]
    small = low(small)
    shards_flat = jnp.concatenate([w_in.reshape(experts, shard, 2 * units), w_down], axis=2)
    return (blocks, small, rows) + tuple(
        run_forward_plain(
            gather_rows(hidden), tok, blocks, small, rows, table, shards_flat, cotangent
        )
    )


def nt_dot(left, right):
    return lax.dot_general(left, right, (((1,), (1,)), ((), ())), preferred_element_type=jnp.float32)


def nn_dot(left, right):
    return jnp.dot(left, right, preferred_element_type=jnp.float32)


def tn_dot(left, right):
    return lax.dot_general(left, right, (((0,), (0,)), ((), ())), preferred_element_type=jnp.float32)


def low(values):
    return values.astype(jnp.bfloat16)


def wide(values):
    return values.astype(jnp.float32)


def rotary_table(length):
    half = HD // 2
    positions = np.arange(length, dtype=np.float32)
    inverse = np.power(np.float32(10000.0), -np.arange(half, dtype=np.float32) / np.float32(half))
    angles = (positions[:, None] * inverse[None, :].astype(np.float32)).astype(np.float32)
    cosine = np.cos(angles.astype(np.float64)).astype(np.float32)
    sine = np.sin(angles.astype(np.float64)).astype(np.float32)
    both = np.concatenate([cosine, sine], axis=1)
    return np.concatenate([both[: length // 2], both[length // 2 :]], axis=1)


def spread_table(table_ref, block):
    quarter = HD // 2
    blocks = table_ref.shape[0] // BLOCK
    table = table_ref[block_rows(lax.rem(block, blocks)), :]
    table = jnp.where(block >= blocks, pltpu.roll(table, HD, 1), table)
    lane = lax.broadcasted_iota(jnp.int32, table.shape, 1)
    cosine = jnp.where(lane < quarter, table, 0.0)
    cosine = cosine + pltpu.roll(cosine, quarter, 1)
    sine = jnp.where(jnp.logical_and(lane >= quarter, lane < HD), table, 0.0)
    sine = sine - pltpu.roll(sine, PAIR - quarter, 1)
    return cosine + pltpu.roll(cosine, HD, 1), sine + pltpu.roll(sine, HD, 1)


def turn(values, cosine, sine):
    lane = lax.broadcasted_iota(jnp.int32, values.shape, 1)
    upper = lax.rem(lane, HD) >= HD // 2
    partner = jnp.where(
        upper, pltpu.roll(values, HD // 2, 1), pltpu.roll(values, PAIR - HD // 2, 1)
    )
    return values * cosine + partner * sine


def head_lanes(shape, half, axis):
    return (lax.broadcasted_iota(jnp.int32, shape, axis) >= HD) == bool(half)


def mean_last(values):
    return jnp.mean(values, axis=-1, keepdims=True)


def to_partner(source, target, send_sem, recv_sem):
    return pltpu.make_async_remote_copy(
        src_ref=source,
        dst_ref=target,
        send_sem=send_sem,
        recv_sem=recv_sem,
        device_id={"tp": 1 - lax.axis_index("tp")},
        device_id_type=MESH,
    )


def block_rows(block):
    return pl.ds(pl.multiple_of(block * BLOCK, BLOCK), BLOCK)


def column(values, index):
    return values[:, index : index + 1]


def lane_matrix(shape, columns):
    lane = lax.broadcasted_iota(jnp.int32, shape, 1)
    total = jnp.zeros(shape, jnp.float32)
    for index, values in columns:
        total = jnp.where(lane == index, values, total)
    return total


def send_to(source, target, send_sem, recv_sem, device):
    return pltpu.make_async_remote_copy(
        src_ref=source,
        dst_ref=target,
        send_sem=send_sem,
        recv_sem=recv_sem,
        device_id=device,
        device_id_type=MESH,
    )


def greet_group(peers):
    me = lax.axis_index("fsdp")
    rank = lax.rem(me, peers)
    barrier = pltpu.get_barrier_semaphore()
    for k in range(1, peers):
        pl.semaphore_signal(
            barrier,
            inc=1,
            device_id={"fsdp": me - rank + lax.rem(rank + k, peers)},
            device_id_type=MESH,
        )
    pl.semaphore_signal(
        barrier, inc=1, device_id={"tp": 1 - lax.axis_index("tp")}, device_id_type=MESH
    )
    pl.semaphore_wait(barrier, peers)


def each(first, last, body):
    def step(k, carry):
        body(k)
        return carry

    lax.fori_loop(first, last, step, 0)


def flipped(value, k, bits):
    other = 0
    bit = 1
    while bit < bits:
        ours, theirs = lax.rem(value // bit, 2), lax.rem(k // bit, 2)
        other = other + bit * (ours + theirs - 2 * ours * theirs)
        bit *= 2
    return other


class CoreExchange:
    def __init__(self, source, target, send_sem, recv_sem):
        experts = source.shape[0]
        me = lax.axis_index("fsdp")
        rank = lax.rem(me, 2 * experts)
        core = lax.rem(rank, 2)
        mine = rank // 2

        def device(k):
            return {"fsdp": me - rank + 2 * flipped(mine, k, experts) + core}

        def copy(k):
            there = flipped(mine, k, experts)
            return send_to(
                source.at[there], target.at[mine], send_sem.at[k], recv_sem.at[k], device(k)
            )

        def arrival(k):
            there = flipped(mine, k, experts)
            return send_to(
                source.at[there], target.at[there], send_sem.at[k], recv_sem.at[k], device(k)
            )

        self.experts, self.copy, self.arrival = experts, copy, arrival
        self.local = pltpu.make_async_copy(source.at[mine], target.at[mine], send_sem.at[0])

    def start(self, done=()):
        self.local.start()
        for k in range(1, self.experts):
            if k not in done:
                self.copy(k).start()

    def wait(self):
        each(1, self.experts, lambda k: self.copy(k).wait_send())
        each(1, self.experts, lambda k: self.arrival(k).wait_recv())
        self.local.wait()


def sum_stages(
    big_ref,
    wqkv_ref,
    other_ref,
    y_ref,
    red_ref,
    tail_ref,
    sum_ref,
    core_ref,
    side_ref,
    acc_ref,
    usend_ref,
    urecv_ref,
    dsend_ref,
    drecv_ref,
    tsend_ref,
    trecv_ref,
    core_send,
    core_recv,
    x_send,
    x_recv,
    up_send,
    up_recv,
    dn_send,
    dn_recv,
    y_send,
    y_recv,
):
    size = big_ref.shape[0]
    subs = big_ref.shape[1] // SUB
    planes = size // 4
    me = lax.axis_index("fsdp")
    tp = lax.axis_index("tp")
    z, x, core = me // 4, lax.rem(me // 2, 2), lax.rem(me, 2)
    heads_width = wqkv_ref.shape[2]
    partner = {"tp": 1 - tp}

    def to_core(plane, line):
        slot = plane * 2 + line
        return send_to(
            big_ref.at[plane * 4 + line * 2 + 1 - core],
            core_ref.at[slot],
            core_send.at[slot],
            core_recv.at[slot],
            {"fsdp": me + 1 - 2 * core},
        )

    def band(sub):
        return pl.ds(pl.multiple_of(sub * SUB, SUB), SUB)

    def to_side(plane, sub):
        slot = plane * subs + sub
        return send_to(
            sum_ref.at[plane, band(sub)],
            side_ref.at[plane, band(sub)],
            x_send.at[slot],
            x_recv.at[slot],
            {"fsdp": z * 4 + (1 - x) * 2 + core},
        )

    def to_up(plane, sub):
        slot = plane * subs + sub
        return send_to(
            usend_ref.at[plane, band(sub)],
            urecv_ref.at[plane, band(sub)],
            up_send.at[slot],
            up_recv.at[slot],
            {"fsdp": lax.min(z + 1, planes - 1) * 4 + x * 2 + core},
        )

    def to_down(plane, sub):
        slot = plane * subs + sub
        return send_to(
            dsend_ref.at[plane, band(sub)],
            drecv_ref.at[plane, band(sub)],
            dn_send.at[slot],
            dn_recv.at[slot],
            {"fsdp": lax.max(z - 1, 0) * 4 + x * 2 + core},
        )

    lower = z < planes // 2
    order = [jnp.where(lower, planes - 1 - step, step) for step in range(planes)]
    out_y = send_to(other_ref, y_ref, y_send.at[0], y_recv.at[0], partner)
    def joined(plane, line):
        to_core(plane, line).wait_recv()
        return wide(big_ref[plane * 4 + line * 2 + core]) + wide(core_ref[plane * 2 + line])

    def rise(plane, sub):
        @pl.when(z < plane)
        def _():
            @pl.when(z > 0)
            def _():
                to_up(plane, sub).wait_recv()
                acc_ref[plane, band(sub)] += wide(urecv_ref[plane, band(sub)])

            usend_ref[plane, band(sub)] = low(acc_ref[plane, band(sub)])
            to_up(plane, sub).start()

    def fall(plane, sub):
        @pl.when(z > plane)
        def _():
            @pl.when(z < planes - 1)
            def _():
                to_down(plane, sub).wait_recv()
                acc_ref[plane, band(sub)] += wide(drecv_ref[plane, band(sub)])

            dsend_ref[plane, band(sub)] = low(acc_ref[plane, band(sub)])
            to_down(plane, sub).start()

    def begin():
        for plane in order:
            to_core(plane, 1 - x).start()
        for plane in order:
            to_core(plane, x).start()
        out_y.start()

        for plane in order:
            sum_ref[plane] = low(joined(plane, 1 - x))
            each(0, subs, lambda sub: to_side(plane, sub).start())
        for plane in order:
            acc_ref[plane] = joined(plane, x)

    def end():
        for step, plane in enumerate(order):
            last_step = step == planes - 1

            def advance(sub):
                to_side(plane, sub).wait_recv()
                acc_ref[plane, band(sub)] += wide(side_ref[plane, band(sub)])

                @pl.when(lower)
                def _():
                    (fall if last_step else rise)(plane, sub)

                @pl.when(jnp.logical_not(lower))
                def _():
                    (rise if last_step else fall)(plane, sub)

            each(0, subs, advance)

        @pl.when(z > 0)
        def _():
            each(0, subs, lambda sub: to_up(z, sub).wait_recv())
            acc_ref[z] += wide(urecv_ref[z])

        @pl.when(z < planes - 1)
        def _():
            each(0, subs, lambda sub: to_down(z, sub).wait_recv())
            acc_ref[z] += wide(drecv_ref[z])

        values = acc_ref[z]
        red_ref[...] = values[:, : 4 * heads_width]
        share = sum(
            jnp.sum(
                values[:, part * heads_width : (part + 1) * heads_width] * wide(wqkv_ref[part]),
                axis=1,
                keepdims=True,
            )
            for part in range(3)
        )
        last = values[:, 4 * heads_width :]
        last = jnp.where(lax.broadcasted_iota(jnp.int32, last.shape, 1) == 0, share, last)
        part_rows = tail_ref.shape[0]
        tsend_ref[0] = last[:part_rows, :]
        tsend_ref[1] = last[part_rows:, :]
        tail_y = send_to(tsend_ref.at[1 - tp], trecv_ref, y_send.at[1], y_recv.at[1], partner)
        tail_y.start()
        out_y.wait()
        tail_y.wait()
        tail_ref[...] = tsend_ref[tp] + trecv_ref[...]
        for plane in range(planes):
            to_core(plane, 1 - x).wait_send()
            to_core(plane, x).wait_send()

            def drain(sub):
                to_side(plane, sub).wait_send()

                @pl.when(z < plane)
                def _():
                    to_up(plane, sub).wait_send()

                @pl.when(z > plane)
                def _():
                    to_down(plane, sub).wait_send()

            each(0, subs, drain)

    return begin, end


def sum_scratch(planes, shard, columns):
    low_t, wide_t = jnp.bfloat16, jnp.float32
    dma = pltpu.SemaphoreType.DMA
    line = (planes, shard, columns)
    return (
        [
            pltpu.VMEM(line, low_t),
            pltpu.VMEM((2 * planes, shard, columns), low_t),
            pltpu.VMEM(line, low_t),
            pltpu.VMEM(line, wide_t),
            pltpu.VMEM(line, low_t),
            pltpu.VMEM(line, low_t),
            pltpu.VMEM(line, low_t),
            pltpu.VMEM(line, low_t),
            pltpu.VMEM((2, shard // 2, PAIR), wide_t),
            pltpu.VMEM((shard // 2, PAIR), wide_t),
            dma((2 * planes,)),
            dma((2 * planes,)),
        ]
        + [dma((planes * (shard // SUB),))] * 6
        + [dma((2,))] * 2
    )


def write_kernel(
    base_ref,
    y_ref,
    grad_ref,
    red_ref,
    tail_ref,
    gain_ref,
    expert_ref,
    out_ref,
    hidden_ref,
    qkv_ref,
    attn_ref,
    gains_ref,
    router_ref,
    mixing_ref,
    value_ref,
    in_ref,
    down_ref,
):
    hidden = down_ref.shape[2]
    heads_width = attn_ref.shape[1]
    out_ref[...] = low(base_ref[...] + wide(y_ref[...]))
    hidden_ref[...] = grad_ref[...]

    def lay_out(e):
        values = wide(expert_ref[e])
        in_ref[e, :, 0, :] = values[:, :hidden]
        in_ref[e, :, 1, :] = values[:, hidden : 2 * hidden]
        down_ref[e] = values[:, 2 * hidden :]

    each(0, expert_ref.shape[0], lay_out)

    @pl.when(pl.program_id(0) == 0)
    def _():
        for part in range(3):
            qkv_ref[part] = red_ref[:, part * heads_width : (part + 1) * heads_width]
        attn_ref[...] = red_ref[:, 3 * heads_width :]
        count = tail_ref.shape[0]
        blank = jnp.zeros((PAIR - count, PAIR), jnp.float32)
        turned = jnp.concatenate([tail_ref[...], blank], axis=0).T[:, :count]
        gains_ref[0:1, :] = turned[0:1, :] / gain_ref[0:1, :]
        gains_ref[1:2, :] = turned[1:2, :]
        router_ref[...] = turned[ROUTER:MIXING, :]
        mixing_ref[...] = turned[MIXING:VALUE, :]
        value_ref[...] = turned[VALUE : VALUE + 2, :]


def run_write(base, y, grad_hidden, red, tail, gains, arrived):
    own_rows, width = base.shape
    shard = red.shape[0]
    heads_width = red.shape[1] // 4
    count = tail.shape[0]
    experts, _, total = arrived.shape
    hidden = total // 3
    wide_t = jnp.float32
    steps = experts // 2
    rows = pl.BlockSpec((own_rows // steps, width), lambda e: (e, 0))

    def whole(shape):
        return pl.BlockSpec(shape, lambda e: (0,) * len(shape))

    return pl.pallas_call(
        write_kernel,
        grid=(steps,),
        in_specs=[
            rows,
            rows,
            rows,
            whole(red.shape),
            whole(tail.shape),
            whole(gains.shape),
            pl.BlockSpec((2, shard, total), lambda e: (e, 0, 0)),
        ],
        out_specs=[
            rows,
            rows,
            whole((3, shard, heads_width)),
            whole((shard, heads_width)),
            whole((2, count)),
            whole((MIXING - ROUTER, count)),
            whole((VALUE - MIXING, count)),
            whole((2, count)),
            pl.BlockSpec((2, shard, 2, hidden), lambda e: (e, 0, 0, 0)),
            pl.BlockSpec((2, shard, hidden), lambda e: (e, 0, 0)),
        ],
        out_shape=[
            jax.ShapeDtypeStruct((own_rows, width), jnp.bfloat16),
            jax.ShapeDtypeStruct((own_rows, width), wide_t),
            jax.ShapeDtypeStruct((3, shard, heads_width), wide_t),
            jax.ShapeDtypeStruct((shard, heads_width), wide_t),
            jax.ShapeDtypeStruct((2, count), wide_t),
            jax.ShapeDtypeStruct((MIXING - ROUTER, count), wide_t),
            jax.ShapeDtypeStruct((VALUE - MIXING, count), wide_t),
            jax.ShapeDtypeStruct((2, count), wide_t),
            jax.ShapeDtypeStruct((experts, shard, 2, hidden), wide_t),
            jax.ShapeDtypeStruct((experts, shard, hidden), wide_t),
        ],
    )(base, y, grad_hidden, red, tail, gains, arrived)


def expert_kernel(
    s2_ref,
    cot_hbm,
    line_ref,
    slot_ref,
    weight_ref,
    res_out_ref,
    dx_out_ref,
    grads_out_ref,
    xs_ref,
    gs_ref,
    x_ref,
    g_ref,
    w_ref,
    gate_ref,
    up_ref,
    act_ref,
    xt_ref,
    gt_ref,
    acc_ref,
    grads_ref,
    sibling_ref,
    ysend_ref,
    yrecv_ref,
    w_sem,
    grad_sem,
    xs_sem,
    xr_sem,
    gs_sem,
    gr_sem,
    xfs_sem,
    xfr_sem,
    gfs_sem,
    gfr_sem,
    ys_sem,
    yr_sem,
    rs_sem,
    rr_sem,
    ds_sem,
    dr_sem,
    cot_ref,
    cot_sem,
):
    cot_load = pltpu.make_async_copy(cot_hbm, cot_ref, cot_sem.at[0])
    cot_load.start()
    peers, rows, width = xs_ref.shape
    total = peers * rows
    hidden = gate_ref.shape[1]
    tiles = hidden // TILE
    me = lax.axis_index("fsdp")
    tp = lax.axis_index("tp")
    rank = lax.rem(me, peers)
    core = lax.rem(rank, 2)
    start = me - rank

    def peer(k):
        return {"fsdp": start + flipped(rank, k, peers)}

    partner = {"tp": 1 - tp}
    sibling = {"fsdp": start + rank + 1 - 2 * core}

    def out_x(k):
        return send_to(xs_ref.at[k], x_ref.at[0, k], xs_sem.at[k], xr_sem.at[k], peer(k))

    def out_g(k):
        return send_to(gs_ref.at[k], g_ref.at[0, k], gs_sem.at[k], gr_sem.at[k], peer(k))

    def pass_x(k):
        return send_to(x_ref.at[0, k], x_ref.at[1, k], xfs_sem.at[k], xfr_sem.at[k], partner)

    def pass_g(k):
        return send_to(g_ref.at[0, k], g_ref.at[1, k], gfs_sem.at[k], gfr_sem.at[k], partner)

    def across(index, k):
        return send_to(
            ysend_ref.at[index, k],
            yrecv_ref.at[index, k],
            ys_sem.at[index, k],
            yr_sem.at[index, k],
            partner,
        )

    def back(index, k):
        if index == 0:
            return send_to(xs_ref.at[k], res_out_ref.at[k], rs_sem.at[k], rr_sem.at[k], peer(k))
        return send_to(gs_ref.at[k], dx_out_ref.at[k], ds_sem.at[k], dr_sem.at[k], peer(k))

    def return_order(body):
        def step(j, carry):
            body(8 + 2 * j)
            body(4 + j)
            body(9 + 2 * j)
            return carry

        lax.fori_loop(0, 4, step, 0)
        for k in (2, 3, 1, 0):
            body(k)

    def turn_rows(source, target, m):
        target[:, pl.ds(pl.multiple_of(m * total, total), total)] = (
            source[m].reshape(total, width).T
        )

    def join(index, k):
        across(index, k).wait_recv()
        own = xs_ref if index == 0 else gs_ref
        own[k] = low(wide(own[k]) + wide(yrecv_ref[index, k]))
        back(index, k).start()

    def join_some(index, tile):
        join(index, 8 + 2 * tile)
        join(index, 4 + tile)
        join(index, 9 + 2 * tile)

    def join_last(index):
        for k in (2, 3, 1):
            join(index, k)
        across(index, 0).wait_recv()
        own, target = (xs_ref, res_out_ref) if index == 0 else (gs_ref, dx_out_ref)
        target[0] = low(wide(own[0]) + wide(yrecv_ref[index, 0]))

    greet_group(peers)
    here = pltpu.make_async_copy(weight_ref, w_ref.at[:, core], w_sem.at[0])
    here.start()
    there = send_to(weight_ref, w_ref.at[:, core], w_sem.at[1], w_sem.at[2], sibling)
    half = total // 2
    group = peers // 2

    def hits_of(part):
        ids = slot_ref[pl.ds(pl.multiple_of(part * half, half), half), 0:1]
        return [line_ref[m : m + 1, :] == ids for m in range(2)]

    def pack_x(part):
        hits = hits_of(part)
        onehot = low(jnp.where(hits[0] | hits[1], 1.0, 0.0))
        xs_ref[pl.ds(part * group, group)] = low(nn_dot(onehot, s2_ref[...])).reshape(
            group, rows, width
        )

        @pl.when(part == 0)
        def _():
            x_ref[0, 0] = xs_ref[0]
            pass_x(0).start()

        def launch(k):
            @pl.when(k > 0)
            def _():
                out_x(k).start()

        each(part * group, (part + 1) * group, launch)

    def pack_g(part):
        hits = hits_of(part)
        onehot = low(jnp.where(hits[0] | hits[1], 1.0, 0.0))
        gate = sum(
            jnp.sum(jnp.where(hits[m], line_ref[2 + m : 3 + m, :], 0.0), axis=1, keepdims=True)
            for m in range(2)
        )
        gs_ref[pl.ds(part * group, group)] = low(nn_dot(onehot, cot_ref[...]) * gate).reshape(
            group, rows, width
        )

        @pl.when(part == 0)
        def _():
            g_ref[0, 0] = gs_ref[0]

        def launch(k):
            @pl.when(k > 0)
            def _():
                out_g(k).start()

        each(part * group, (part + 1) * group, launch)

    each(0, 2, pack_x)
    there.start()
    cot_load.wait()
    each(0, 2, pack_g)

    def forward_x(k):
        out_x(k).wait_recv()
        pass_x(k).start()

    each(1, peers, forward_x)
    pass_g(0).start()
    here.wait()
    send_to(weight_ref, w_ref.at[:, 1 - core], w_sem.at[1], w_sem.at[2], sibling).wait_recv()
    there.wait_send()
    each(0, peers, lambda k: pass_x(k).wait_recv())

    def weights(which, lanes):
        return w_ref[:, :, :, pl.ds(pl.multiple_of(which * hidden + lanes, TILE), TILE)].reshape(
            width, TILE
        )

    acc_ref[...] = jnp.zeros_like(acc_ref)

    def forward_tile(tile, carry):
        lanes = pl.multiple_of(tile * TILE, TILE)
        here_lanes = pl.ds(lanes, TILE)

        def one_half(m):
            band = pl.ds(pl.multiple_of(m * total, total), total)
            x = x_ref[m].reshape(total, width)
            gate = nn_dot(x, weights(0, lanes))
            up = nn_dot(x, weights(1, lanes))
            gate_ref[band, here_lanes] = low(gate)
            up_ref[band, here_lanes] = low(up)
            act = low(gate / (1.0 + jnp.exp(-gate)) * up)
            act_ref[band, here_lanes] = act
            acc_ref[band, :] += nt_dot(act, weights(2, lanes))

        each(0, 2, one_half)

        def forward_g(k):
            @pl.when(k > 0)
            def _():
                out_g(k).wait_recv()
                pass_g(k).start()

        each(tile * (peers // tiles), (tile + 1) * (peers // tiles), forward_g)
        return carry

    lax.fori_loop(0, tiles, forward_tile, 0)
    each(1, peers, lambda k: out_x(k).wait_send())
    xs_ref[...] = low(acc_ref[:total, :]).reshape(peers, rows, width)
    ysend_ref[0] = low(acc_ref[total:, :]).reshape(peers, rows, width)
    return_order(lambda k: across(0, k).start())
    each(0, 2, lambda m: turn_rows(x_ref, xt_ref, m))
    acc_ref[...] = jnp.zeros_like(acc_ref)
    each(0, peers, lambda k: pass_g(k).wait_recv())

    def slope_tile(tile, carry):
        lanes = pl.multiple_of(tile * TILE, TILE)
        here_lanes = pl.ds(lanes, TILE)

        def one_half(m):
            band = pl.ds(pl.multiple_of(m * total, total), total)
            gate = wide(gate_ref[band, here_lanes])
            up = wide(up_ref[band, here_lanes])
            sig = 1.0 / (1.0 + jnp.exp(-gate))
            d_act = nn_dot(g_ref[m].reshape(total, width), weights(2, lanes))
            d_up = low(d_act * gate * sig)
            d_gate = low(d_act * up * sig * (1.0 + gate * (1.0 - sig)))
            gate_ref[band, here_lanes] = d_gate
            up_ref[band, here_lanes] = d_up
            acc_ref[band, :] += nt_dot(d_gate, weights(0, lanes)) + nt_dot(
                d_up, weights(1, lanes)
            )

        each(0, 2, one_half)
        join_some(0, tile)
        return carry

    lax.fori_loop(0, tiles, slope_tile, 0)
    join_last(0)
    each(1, peers, lambda k: out_g(k).wait_send())
    gs_ref[...] = low(acc_ref[:total, :]).reshape(peers, rows, width)
    ysend_ref[1] = low(acc_ref[total:, :]).reshape(peers, rows, width)
    return_order(lambda k: across(1, k).start())
    each(0, 2, lambda m: turn_rows(g_ref, gt_ref, m))

    def weight_tile(tile, carry):
        lanes = pl.multiple_of(tile * TILE, TILE)
        here_lanes = pl.ds(lanes, TILE)

        def keep(which, values):
            grads_ref[
                :, :, :, pl.ds(pl.multiple_of(which * hidden + lanes, TILE), TILE)
            ] = low(values).reshape(peers // 2, 2, rows, TILE)

        keep(0, nn_dot(xt_ref[...], gate_ref[:, here_lanes]))
        keep(1, nn_dot(xt_ref[...], up_ref[:, here_lanes]))
        keep(2, nn_dot(gt_ref[...], act_ref[:, here_lanes]))
        join_some(1, tile)
        return carry

    lax.fori_loop(0, tiles, weight_tile, 0)
    swap_grads = send_to(
        grads_ref.at[:, 1 - core], sibling_ref, grad_sem.at[0], grad_sem.at[1], sibling
    )
    swap_grads.start()
    join_last(1)
    each(0, peers, lambda k: pass_x(k).wait_send())
    each(0, peers, lambda k: pass_g(k).wait_send())
    for index in range(2):
        each(0, peers, lambda k: across(index, k).wait_send())
        each(1, peers, lambda k: back(index, k).wait_send())
    swap_grads.wait()
    grads_out_ref[...] = low(wide(grads_ref[:, core]) + wide(sibling_ref[...]))
    for index in range(2):
        each(1, peers, lambda k: back(index, k).wait_recv())


def run_expert(s2, cot, lines, slots, weights):
    length, width = s2.shape
    experts, shard, total = weights.shape
    peers = 2 * experts
    rows = slots.shape[0] // peers
    hidden = total // 3
    both = 2 * peers * rows
    vmem = pl.BlockSpec(memory_space=pltpu.VMEM)
    low_t, wide_t = jnp.bfloat16, jnp.float32
    dma = pltpu.SemaphoreType.DMA
    block = (peers, rows, width)
    return pl.pallas_call(
        expert_kernel,
        in_specs=[vmem, pl.BlockSpec(memory_space=pl.ANY), vmem, vmem]
        + [pl.BlockSpec(memory_space=pl.ANY)],
        out_specs=[vmem] * 3,
        out_shape=[
            jax.ShapeDtypeStruct(block, low_t),
            jax.ShapeDtypeStruct(block, low_t),
            jax.ShapeDtypeStruct(weights.shape, low_t),
        ],
        scratch_shapes=[
            pltpu.VMEM(block, low_t),
            pltpu.VMEM(block, low_t),
            pltpu.VMEM((2,) + block, low_t),
            pltpu.VMEM((2,) + block, low_t),
            pltpu.VMEM((experts, 2, shard, total), low_t),
            pltpu.VMEM((both, hidden), low_t),
            pltpu.VMEM((both, hidden), low_t),
            pltpu.VMEM((both, hidden), low_t),
            pltpu.VMEM((width, both), low_t),
            pltpu.VMEM((width, both), low_t),
            pltpu.VMEM((both, width), wide_t),
            pltpu.VMEM((experts, 2, shard, total), low_t),
            pltpu.VMEM((experts, shard, total), low_t),
            pltpu.VMEM((2,) + block, low_t),
            pltpu.VMEM((2,) + block, low_t),
            dma((3,)),
            dma((2,)),
        ]
        + [dma((peers,))] * 8
        + [dma((2, peers))] * 2
        + [dma((peers,))] * 4
        + [pltpu.VMEM(cot.shape, low_t), dma((1,))],
        compiler_params=pltpu.CompilerParams(
            collective_id=2, has_side_effects=True, vmem_limit_bytes=67043328
        ),
    )(s2, cot, lines, slots, weights)


def attend(
    hid_ref,
    token_block,
    weight,
    small_ref,
    gains,
    table_ref,
    s1_ref,
    qkv_ref,
    lse_ref,
    mixed_ref,
    mid_ref,
    s2_ref,
    tok_ref,
    line_ref,
    vt_ref,
    send_ref,
    recv_ref,
    send_sem,
    recv_sem,
    between,
):
    blocks = hid_ref.shape[0] // BLOCK
    heads_width = mixed_ref.shape[1]
    pairs = heads_width // PAIR
    gain_one, gain_two = gains
    lse_ref[...] = jnp.zeros_like(lse_ref)

    def copy(block):
        return to_partner(
            send_ref.at[block], recv_ref.at[block], send_sem.at[block], recv_sem.at[block]
        )

    def compute(block):
        rows = block_rows(block)
        source = wide(hid_ref[rows, :])
        s1 = low(source * lax.rsqrt(mean_last(source * source) + EPSILON) * gain_one)
        s1_ref[rows, :] = s1
        cosine, sine = spread_table(table_ref, block)
        for part in range(3):
            projected = nn_dot(s1, weight(part))
            for pair in range(pairs):
                chunk = projected[:, pair * PAIR : (pair + 1) * PAIR]
                if part < 2:
                    chunk = turn(chunk, cosine, sine)
                else:
                    vt_ref[pair * PAIR : (pair + 1) * PAIR, rows] = low(chunk.T)
                start = part * heads_width + pair * PAIR
                qkv_ref[rows, start : start + PAIR] = low(chunk)

        def one_pair(keys, pair):
            start = pl.multiple_of(pair * PAIR, PAIR)
            lanes = pl.ds(start, PAIR)
            key_lanes = pl.ds(pl.multiple_of(heads_width + start, PAIR), PAIR)
            query = qkv_ref[rows, lanes] * jnp.bfloat16(SCALING)
            key = qkv_ref[:keys, key_lanes]
            value_t = vt_ref[lanes, :keys]
            gathered = None
            for half in range(2):
                masked = jnp.where(head_lanes(query.shape, half, 1), query, jnp.bfloat16(0))
                scores = nt_dot(key, masked)
                highest = jnp.max(scores, axis=0, keepdims=True)
                expanded = jnp.exp(scores - highest)
                totals = jnp.sum(expanded, axis=0, keepdims=True)
                probs = low(expanded * (1.0 / totals))
                lse_ref[pl.ds(2 * pair + half, 1), rows] = highest + jnp.log(totals)
                found = nn_dot(value_t, probs)
                gathered = (
                    found
                    if half == 0
                    else jnp.where(head_lanes(found.shape, 1, 0), found, gathered)
                )
            mixed_ref[rows, lanes] = low(gathered.T)

        for static in range(blocks):

            @pl.when(block == static)
            def _():
                each(0, pairs, functools.partial(one_pair, (static + 1) * BLOCK))

        send_ref[block] = low(nt_dot(mixed_ref[rows, :], weight(3)))
        copy(block).start()

    def finish(block):
        rows = block_rows(block)
        copy(block).wait()
        mid = wide(hid_ref[rows, :]) + (wide(send_ref[block]) + wide(recv_ref[block]))
        mid_ref[rows, :] = mid
        s2 = low(mid * lax.rsqrt(mean_last(mid * mid) + EPSILON) * gain_two)
        s2_ref[rows, :] = s2
        tok = token_block(block)
        lane = lax.broadcasted_iota(jnp.int32, tok.shape, 1)
        logits = nn_dot(s2, small_ref[...]) + tok
        picked = [
            jnp.sum(
                jnp.where(wide(lane - ROUTER) == column(tok, ROUTE + member), logits, 0.0),
                axis=1,
                keepdims=True,
            )
            for member in range(2)
        ]
        gate = [
            1.0 / (1.0 + jnp.exp(picked[1 - member] - picked[member])) for member in range(2)
        ]
        tok = jnp.where(lane == GATE, gate[0], jnp.where(lane == GATE + 1, gate[1], tok))
        tok_ref[rows, :] = tok
        line_ref[:, rows] = tok.T[TARGET : TARGET + 8, :]

    each(0, blocks, compute)
    between()
    each(0, blocks, finish)


def forward_plain_kernel(
    hid_ref,
    tok_in_ref,
    block_ref,
    small_ref,
    rows_ref,
    table_ref,
    shard_ref,
    cot_own_ref,
    s1_ref,
    qkv_ref,
    lse_ref,
    mixed_ref,
    mid_ref,
    s2_ref,
    tok_ref,
    line_ref,
    expert_ref,
    cot_ref,
    vt_ref,
    send_ref,
    recv_ref,
    send_sem,
    recv_sem,
    wsend_sem,
    wrecv_sem,
    cot_sem,
):
    greet_group(2 * shard_ref.shape[0])
    own_rows = cot_own_ref.shape[0]
    heads_width = mixed_ref.shape[1]
    width = hid_ref.shape[1]
    mine = pl.ds(pl.multiple_of(lax.axis_index("tp") * own_rows, own_rows), own_rows)
    cot_copy = to_partner(cot_own_ref, cot_ref.at[mine], cot_sem.at[0], cot_sem.at[1])
    cot_copy.start()
    experts = CoreExchange(shard_ref, expert_ref, wsend_sem, wrecv_sem)
    experts.start()
    cot_ref[mine, :] = cot_own_ref[...]

    def weight(part):
        return block_ref[:, :, part * heads_width : (part + 1) * heads_width].reshape(
            width, heads_width
        )

    attend(
        hid_ref,
        lambda block: tok_in_ref[block_rows(block), :],
        weight,
        small_ref,
        (rows_ref[0:1, :], rows_ref[1:2, :]),
        table_ref,
        s1_ref,
        qkv_ref,
        lse_ref,
        mixed_ref,
        mid_ref,
        s2_ref,
        tok_ref,
        line_ref,
        vt_ref,
        send_ref,
        recv_ref,
        send_sem,
        recv_sem,
        lambda: None,
    )
    cot_copy.wait()
    experts.wait()


def forward_kernel(
    hid_own_ref,
    cot_own_ref,
    logit_ref,
    route_ref,
    rank_ref,
    drop_ref,
    gain_ref,
    router_ref,
    mixing_ref,
    value_ref,
    wqkv_ref,
    wout_ref,
    win_ref,
    wdown_ref,
    table_ref,
    all_out,
    small_ref,
    rows_ref,
    s1_out,
    qkv_out,
    lse_ref,
    mixed_out,
    mid_ref,
    s2_ref,
    tok_ref,
    line_ref,
    expert_ref,
    cot_out,
    all_ref,
    s1_ref,
    qkv_ref,
    mixed_ref,
    cot_ref,
    hid_ref,
    vt_ref,
    send_ref,
    recv_ref,
    shard_ref,
    stage_ref,
    small_all_ref,
    tok_all_ref,
    send_sem,
    recv_sem,
    wsend_sem,
    wrecv_sem,
    y_send,
    y_recv,
    up_send,
    up_recv,
    down_send,
    down_recv,
    x_send,
    x_recv,
    core_send,
    core_recv,
    store_sem,
):
    size, shard, _ = all_ref.shape
    planes = size // 4
    me = lax.axis_index("fsdp")
    tp = lax.axis_index("tp")
    z, x, core = me // 4, lax.rem(me // 2, 2), lax.rem(me, 2)
    own_rows, width = hid_own_ref.shape
    heads_width = wout_ref.shape[1]
    small_rows = shard // 2
    greet_group(size)
    partner = {"tp": 1 - tp}
    mine = pl.ds(pl.multiple_of(tp * own_rows, own_rows), own_rows)
    hid_y = send_to(hid_own_ref, hid_ref.at[mine], y_send.at[1], y_recv.at[1], partner)
    stage_ref[...] = jnp.zeros_like(stage_ref)
    stage_ref[0:2, :small_rows] = gain_ref[...]
    stage_ref[ROUTER:MIXING, :small_rows] = wide(router_ref[...])
    stage_ref[MIXING:VALUE, :small_rows] = wide(mixing_ref[...])
    stage_ref[VALUE : VALUE + 2, :small_rows] = wide(value_ref[...])
    small_all_ref[me, tp] = stage_ref[...].T[:small_rows, :]
    small_y = send_to(
        small_all_ref.at[me, tp], small_all_ref.at[me, tp], y_send.at[0], y_recv.at[0], partner
    )
    small_y.start()
    hid_y.start()
    for part in range(3):
        all_ref[me, :, part * heads_width : (part + 1) * heads_width] = wqkv_ref[part]
    all_ref[me, :, 3 * heads_width :] = wout_ref[...]
    tok_y = send_to(tok_all_ref.at[tp], tok_all_ref.at[tp], y_send.at[2], y_recv.at[2], partner)

    def cot_copy(part):
        count = own_rows // 4
        near = pl.ds(part * count, count)
        far = pl.ds(pl.multiple_of(tp * own_rows + part * count, count), count)
        return send_to(
            cot_own_ref.at[near], cot_ref.at[far], y_send.at[3 + part], y_recv.at[3 + part], partner
        )

    experts = CoreExchange(shard_ref, expert_ref, wsend_sem, wrecv_sem)
    expert_count, _, hidden = wdown_ref.shape

    def stage_tokens():
        tok_all_ref[tp] = jnp.zeros(tok_all_ref.shape[1:], jnp.float32)
        routes = route_ref[...]
        kept = jnp.logical_and(routes < expert_count, drop_ref[...] == 0)
        target = jnp.where(kept, routes * (own_rows * 2 * 9 // 48) + rank_ref[...], -1)
        tok_all_ref[tp, ROUTER:MIXING, :] = logit_ref[...]
        tok_all_ref[tp, ROUTE : ROUTE + 2, :] = wide(routes)
        tok_all_ref[tp, TARGET : TARGET + 2, :] = wide(target)

    def stage_shard():
        def one(e):
            for part in range(2):
                shard_ref[e, :, part * hidden : (part + 1) * hidden] = win_ref[e, :, part, :]
            shard_ref[e, :, 2 * hidden :] = wdown_ref[e]

        each(0, expert_count, one)

    def number(plane, line):
        return plane * 4 + line * 2 + core

    def piece(kind, number_of, send, recv, slot, device):
        array = small_all_ref if kind else all_ref
        return send_to(
            array.at[number_of],
            array.at[number_of],
            send.at[kind, slot],
            recv.at[kind, slot],
            device,
        )

    def up(kind, step, plane):
        device = {"fsdp": number(lax.min(z + 1, planes - 1), x)}
        return piece(kind, number(plane, x), up_send, up_recv, step, device)

    def down(kind, step, plane):
        device = {"fsdp": number(lax.max(z - 1, 0), x)}
        return piece(kind, number(plane, x), down_send, down_recv, step, device)

    def side(kind, plane, line):
        device = {"fsdp": number(z, 1 - x)}
        return piece(kind, number(plane, line), x_send, x_recv, plane, device)

    def sibling(kind, plane, line, parity):
        return piece(
            kind,
            plane * 4 + line * 2 + parity,
            core_send,
            core_recv,
            plane * 2 + line,
            {"fsdp": me + 1 - 2 * core},
        )

    def launch(kind):
        @pl.when(z < planes - 1)
        def _():
            up(kind, 0, z).start()

        @pl.when(z > 0)
        def _():
            down(kind, 0, z).start()

        side(kind, z, x).start()
        sibling(kind, z, x, core).start()

    launch(0)
    stage_tokens()
    tok_y.start()
    for part in range(4):
        cot_copy(part).start()
    hid_ref[mine, :] = hid_own_ref[...]
    cot_ref[mine, :] = cot_own_ref[...]
    small_y.wait()
    launch(1)
    stage_shard()
    for step in range(1, planes):
        for kind in range(2):

            @pl.when(z >= step)
            def _():
                up(kind, step - 1, z - step).wait_recv()

                @pl.when(z < planes - 1)
                def _():
                    up(kind, step, z - step).start()

                side(kind, z - step, x).start()
                sibling(kind, z - step, x, core).start()

            @pl.when(z + step < planes)
            def _():
                down(kind, step - 1, z + step).wait_recv()

                @pl.when(z > 0)
                def _():
                    down(kind, step, z + step).start()

                side(kind, z + step, x).start()
                sibling(kind, z + step, x, core).start()

    experts.start()
    for step in range(planes):
        for kind in range(2):

            @pl.when(z >= step)
            def _():
                side(kind, z - step, 1 - x).wait_recv()
                sibling(kind, z - step, 1 - x, core).start()

            if step > 0:

                @pl.when(z + step < planes)
                def _():
                    side(kind, z + step, 1 - x).wait_recv()
                    sibling(kind, z + step, 1 - x, core).start()

    for plane in range(planes):
        for line in range(2):
            for kind in range(2):
                sibling(kind, plane, line, 1 - core).wait_recv()
    small_all = small_all_ref[...].reshape(width, PAIR)
    small_ref[...] = low(small_all)
    rows_ref[...] = small_all.T[:8, :]
    tok_y.wait()
    hid_y.wait()

    def token_block(block):
        per = own_rows // BLOCK
        lanes = pl.ds(pl.multiple_of(lax.rem(block, per) * BLOCK, BLOCK), BLOCK)
        part = tok_all_ref[block // per, :, lanes]
        blank = jnp.zeros((PAIR - part.shape[0], BLOCK), jnp.float32)
        return jnp.concatenate([part, blank], axis=0).T

    def weight(part):
        return all_ref[:, :, part * heads_width : (part + 1) * heads_width].reshape(
            width, heads_width
        )

    stores = [
        pltpu.make_async_copy(source, target, store_sem.at[index])
        for index, (source, target) in enumerate(
            [
                (all_ref, all_out),
                (s1_ref, s1_out),
                (qkv_ref, qkv_out),
                (mixed_ref, mixed_out),
                (cot_ref, cot_out),
            ]
        )
    ]
    stores[0].start()

    def between():
        for store in stores[1:4]:
            store.start()
        for part in range(4):
            cot_copy(part).wait()
        stores[4].start()

    attend(
        hid_ref,
        token_block,
        weight,
        small_ref,
        (rows_ref[0:1, :], rows_ref[1:2, :]),
        table_ref,
        s1_ref,
        qkv_ref,
        lse_ref,
        mixed_ref,
        mid_ref,
        s2_ref,
        tok_ref,
        line_ref,
        vt_ref,
        send_ref,
        recv_ref,
        send_sem,
        recv_sem,
        between,
    )
    for kind in range(2):
        for step in range(planes):

            @pl.when(jnp.logical_and(z >= step, z < planes - 1))
            def _():
                up(kind, step, z - step).wait_send()

            @pl.when(jnp.logical_and(z + step < planes, z > 0))
            def _():
                down(kind, step, z + step).wait_send()

        for plane in range(planes):
            side(kind, plane, x).wait_send()
            for line in range(2):
                sibling(kind, plane, line, core).wait_send()
    for store in stores:
        store.wait()
    experts.wait()


def backward_body(
    begin,
    end,
    res_hbm,
    dx_ref,
    slot_ref,
    tok_ref,
    cot_hbm,
    mid_hbm,
    s1_hbm,
    qkv_hbm,
    lse_ref,
    mixed_hbm,
    block_hbm,
    small_ref,
    rows_ref,
    table_ref,
    own_ref,
    egrad_ref,
    grad_ref,
    base_ref,
    other_ref,
    big_ref,
    arrived_ref,
    gsend_ref,
    grecv_ref,
    ssend_ref,
    srecv_ref,
    mid_ref,
    s1_ref,
    qkv_ref,
    mixed_ref,
    block_ref,
    hsend_ref,
    hrecv_ref,
    gmid_ref,
    gown_ref,
    kt_ref,
    gm_ref,
    dk_ref,
    dv_ref,
    gp_ref,
    att_ref,
    s2_ref,
    slope_ref,
    value_ref,
    acc_gain_ref,
    gsend_sem,
    grecv_sem,
    hsend_sem,
    hrecv_sem,
    esend_sem,
    erecv_sem,
    ssend_sem,
    srecv_sem,
    load_sem,
    res_ref,
    cot_ref,
    first_sem,
):
    first = [
        pltpu.make_async_copy(res_hbm, res_ref, first_sem.at[0]),
        pltpu.make_async_copy(cot_hbm, cot_ref, first_sem.at[1]),
    ]
    for load in first:
        load.start()
    loads = [
        pltpu.make_async_copy(source, target, load_sem.at[index])
        for index, (source, target) in enumerate(
            [
                (mid_hbm, mid_ref),
                (qkv_hbm, qkv_ref),
                (mixed_hbm, mixed_ref),
                (block_hbm, block_ref),
                (s1_hbm, s1_ref),
            ]
        )
    ]
    for load in loads:
        load.start()
    greet_group(2 * egrad_ref.shape[0])
    experts = CoreExchange(egrad_ref, arrived_ref, esend_sem, erecv_sem)
    tp = lax.axis_index("tp")
    width = dx_ref.shape[1]
    blocks = cot_ref.shape[0] // BLOCK
    heads_width = mixed_ref.shape[1]
    pairs = heads_width // PAIR
    gain_one = rows_ref[0:1, :]
    gain_two = rows_ref[1:2, :]
    slot_row = slot_ref[0:1, :]

    def weights(first_part, last_part):
        lanes = slice(first_part * heads_width, last_part * heads_width)
        return block_ref[:, :, lanes].reshape(width, (last_part - first_part) * heads_width)

    half_blocks = blocks // 2
    experts.start()

    def row_copy(block):
        return to_partner(
            gsend_ref.at[block], grecv_ref.at[block], gsend_sem.at[block], grecv_sem.at[block]
        )

    def share_copy(block):
        return to_partner(
            ssend_ref.at[block], srecv_ref.at[block], ssend_sem.at[block], srecv_sem.at[block]
        )

    def stream_copy(slot):
        return to_partner(
            hsend_ref.at[slot], hrecv_ref.at[slot], hsend_sem.at[slot], hrecv_sem.at[slot]
        )

    def slab_of(block):
        return block_rows(lax.rem(block, half_blocks))

    def backwards(body):
        each(0, blocks, lambda step: body(blocks - 1 - step))

    def send_rows(block):
        rows = block_rows(block)
        tok = tok_ref[rows, :]
        onehots = [low(jnp.where(column(tok, TARGET + m) == slot_row, 1.0, 0.0)) for m in range(2)]
        gsend_ref[block] = low(nn_dot(onehots[0] + onehots[1], dx_ref[...]))
        row_copy(block).start()

        @pl.when(block == blocks - 1)
        def _():
            for load in first:
                load.wait()

        placed = [nn_dot(onehot, res_ref[...]) for onehot in onehots]
        cot_wide = wide(cot_ref[rows, :])
        shares = [
            column(tok, GATE + m) * jnp.sum(placed[m] * cot_wide, axis=1, keepdims=True)
            for m in range(2)
        ]
        ssend_ref[block] = lane_matrix(tok.shape, [(0, shares[0]), (1, shares[1])]).T[:8, :]
        share_copy(block).start()
        mixture = column(tok, GATE) * placed[0] + column(tok, GATE + 1) * placed[1]

        @pl.when(tp == block // half_blocks)
        def _():
            base_ref[slab_of(block), :] = mixture

        @pl.when(tp != block // half_blocks)
        def _():
            other_ref[slab_of(block), :] = low(mixture)

    backwards(send_rows)
    for load in loads:
        load.wait()
    kt_ref[...] = qkv_ref[:, heads_width : 2 * heads_width].T
    dk_ref[...] = jnp.zeros_like(dk_ref)
    dv_ref[...] = jnp.zeros_like(dv_ref)
    acc_gain_ref[...] = jnp.zeros_like(acc_gain_ref)

    def main(block):
        rows = block_rows(block)
        mine = tp == block // half_blocks
        mine_f = jnp.where(mine, 1.0, 0.0)
        mid = mid_ref[rows, :]
        cot = cot_ref[rows, :]
        cot_wide = wide(cot)
        tok = tok_ref[rows, :]
        scale = lax.rsqrt(mean_last(mid * mid) + EPSILON)
        unit = mid * scale
        normed = unit * gain_two
        s2 = low(normed)
        small = small_ref[...]
        mixing = nn_dot(s2, small)
        value_dot = nn_dot(cot, small)
        normed_dot = jnp.sum(normed * cot_wide, axis=1, keepdims=True)
        route = [column(tok, ROUTE + member) for member in range(2)]
        gate = [column(tok, GATE + member) for member in range(2)]

        def weight_of(expert):
            return sum(jnp.where(route[m] == expert, gate[m], 0.0) for m in range(2))

        copy_weight = weight_of(COPY)
        copy_share = [jnp.where(route[m] == COPY, normed_dot, 0.0) for m in range(2)]
        alpha = copy_weight
        columns = []
        value_columns = []
        for c in range(2):
            weight = weight_of(COPY + 1 + c)
            left = column(mixing, MIXING + 2 * c)
            right = column(mixing, MIXING + 2 * c + 1)
            a0 = 1.0 / (1.0 + jnp.exp(right - left))
            a1 = 1.0 / (1.0 + jnp.exp(left - right))
            vd = column(value_dot, VALUE + c)
            alpha = alpha + weight * a0
            for m in range(2):
                copy_share[m] = copy_share[m] + jnp.where(
                    route[m] == COPY + 1 + c, a0 * normed_dot + a1 * vd, 0.0
                )
            slope = a0 * a1 * weight * (normed_dot - vd)
            columns.append((MIXING + 2 * c, slope))
            columns.append((MIXING + 2 * c + 1, -slope))
            value_columns.append((VALUE + c, weight * a1))
        value_matrix = lane_matrix(tok.shape, value_columns)

        @pl.when(mine)
        def _():
            base_ref[slab_of(block), :] += (
                mid + alpha * normed + nt_dot(low(value_matrix), small)
            )

        row_copy(block).wait()
        share_copy(block).wait()
        extra = ssend_ref[block] + srecv_ref[block]
        extra = jnp.concatenate(
            [extra, jnp.zeros((PAIR - extra.shape[0], BLOCK), jnp.float32)], axis=0
        ).T
        share = [column(extra, m) + gate[m] * copy_share[m] for m in range(2)]
        lane = lax.broadcasted_iota(jnp.int32, tok.shape, 1)
        slopes = lane_matrix(tok.shape, columns)
        for m in range(2):
            local = share[m] - gate[m] * (share[0] + share[1])
            slopes = slopes + jnp.where(wide(lane - ROUTER) == route[m], local, 0.0)
        slopes_low = low(slopes)
        grad_normed = (
            wide(gsend_ref[block])
            + wide(grecv_ref[block])
            + alpha * cot_wide
            + nt_dot(slopes_low, small)
        )
        s2_ref[rows, :] = s2
        slope_ref[rows, :] = low(slopes * mine_f)
        value_ref[rows, :] = low(value_matrix * mine_f)
        gain_grad = jnp.sum(unit * grad_normed, axis=0, keepdims=True) * mine_f
        acc_gain_ref[...] += jnp.broadcast_to(gain_grad, acc_gain_ref.shape)
        scaled = grad_normed * gain_two
        grad_mid = cot_wide + scale * (scaled - unit * mean_last(scaled * unit))
        gmid_ref[rows, :] = grad_mid
        attended = low(grad_mid)
        att_ref[rows, :] = attended
        gm_ref[...] = low(nn_dot(attended, weights(3, 4)))
        cosine, sine = spread_table(table_ref, block)

        def one_pair(keys, pair):
            start = pl.multiple_of(pair * PAIR, PAIR)
            lanes = pl.ds(start, PAIR)
            key_lanes = pl.ds(pl.multiple_of(heads_width + start, PAIR), PAIR)
            value_lanes = pl.ds(pl.multiple_of(2 * heads_width + start, PAIR), PAIR)
            query = qkv_ref[rows, lanes] * jnp.bfloat16(SCALING)
            key = qkv_ref[:keys, key_lanes]
            value = qkv_ref[:keys, value_lanes]
            grad_out = gm_ref[:, lanes]
            key_t = kt_ref[lanes, :keys]
            grad_value = None
            for half in range(2):
                keep = head_lanes(query.shape, half, 1)
                q_half = jnp.where(keep, query, jnp.bfloat16(0))
                g_half = jnp.where(keep, grad_out, jnp.bfloat16(0))
                probs = jnp.exp(nt_dot(key, q_half) - lse_ref[pl.ds(2 * pair + half, 1), rows])
                grad_probs = nt_dot(value, g_half)
                inner = jnp.sum(probs * grad_probs, axis=0, keepdims=True)
                grad_scores = low(probs * (grad_probs - inner))
                value_part = nn_dot(low(probs), g_half)
                key_part = nn_dot(grad_scores, q_half)
                query_part = nn_dot(key_t, grad_scores)
                if half == 0:
                    grad_value, grad_key, grad_query = value_part, key_part, query_part
                else:
                    grad_value = grad_value + value_part
                    grad_key = grad_key + key_part
                    grad_query = jnp.where(
                        head_lanes(query_part.shape, 1, 0), query_part, grad_query
                    )
            dv_ref[:keys, lanes] += grad_value
            dk_ref[:keys, lanes] += grad_key
            gp_ref[rows, lanes] = low(turn(grad_query.T * SCALING, cosine, -sine))
            gp_ref[rows, key_lanes] = low(turn(dk_ref[rows, lanes], cosine, -sine))
            gp_ref[rows, value_lanes] = low(dv_ref[rows, lanes])

        for static in range(blocks):

            @pl.when(block == static)
            def _():
                each(0, pairs, functools.partial(one_pair, (static + 1) * BLOCK))

        stream_grad = nt_dot(gp_ref[rows, :], weights(0, 3))
        slot = lax.rem(block, half_blocks)

        @pl.when(mine)
        def _():
            gown_ref[slot] = stream_grad

        @pl.when(jnp.logical_not(mine))
        def _():
            hsend_ref[slot] = low(stream_grad)
            stream_copy(slot).start()

    backwards(main)
    s1_turned = s1_ref[...].T
    for part in range(3):
        lanes = slice(part * heads_width, (part + 1) * heads_width)
        big_ref[:, :, lanes] = low(nn_dot(s1_turned, gp_ref[:, lanes])).reshape(
            big_ref.shape[:2] + (heads_width,)
        )
    big_ref[:, :, 3 * heads_width : 4 * heads_width] = low(
        tn_dot(att_ref[...], mixed_ref[...])
    ).reshape(big_ref.shape[:2] + (heads_width,))
    tall = jnp.where(
        lax.broadcasted_iota(jnp.int32, (PAIR, width), 0) == 1,
        jnp.broadcast_to(acc_gain_ref[0:1, :], (PAIR, width)),
        0.0,
    )
    big_ref[:, :, 4 * heads_width :] = low(
        tn_dot(s2_ref[...], slope_ref[...]) + tn_dot(cot_ref[...], value_ref[...]) + tall.T
    ).reshape(big_ref.shape[:2] + (PAIR,))
    begin()
    for slot in reversed(range(half_blocks)):
        slab = slice(slot * BLOCK, (slot + 1) * BLOCK)
        stream_copy(slot).wait()
        source = wide(own_ref[slab, :])
        scale = lax.rsqrt(mean_last(source * source) + EPSILON)
        unit = source * scale
        scaled = (gown_ref[slot] + wide(hrecv_ref[slot])) * gain_one
        mid_rows = block_rows(tp * half_blocks + slot)
        grad_ref[slab, :] = gmid_ref[mid_rows, :] + scale * (
            scaled - unit * mean_last(scaled * unit)
        )
    end()
    experts.wait()


def backward_plain_kernel(*refs):
    backward_body(lambda: None, lambda: None, *refs)


def backward_kernel(body_count, *refs):
    operands, wqkv_ref = refs[:16], refs[16]
    grad_ref, base_ref, arrived_ref, y_ref, red_ref, tail_ref = refs[17:23]
    other_ref, big_ref = refs[23:25]
    body, sums = refs[25 : 25 + body_count], refs[25 + body_count :]
    begin, end = sum_stages(big_ref, wqkv_ref, other_ref, y_ref, red_ref, tail_ref, *sums)
    backward_body(
        begin, end, *operands, grad_ref, base_ref, other_ref, big_ref, arrived_ref, *body
    )


def forward_results(length, width, heads_width, shard):
    low_t, wide_t = jnp.bfloat16, jnp.float32
    return [
        jax.ShapeDtypeStruct((length, width), low_t),
        jax.ShapeDtypeStruct((length, 3 * heads_width), low_t),
        jax.ShapeDtypeStruct((8, length), wide_t),
        jax.ShapeDtypeStruct((length, heads_width), low_t),
        jax.ShapeDtypeStruct((length, width), wide_t),
        jax.ShapeDtypeStruct((length, width), low_t),
        jax.ShapeDtypeStruct((length, PAIR), wide_t),
        jax.ShapeDtypeStruct((8, length), wide_t),
        jax.ShapeDtypeStruct(shard, low_t),
        jax.ShapeDtypeStruct((length, width), low_t),
    ]


def attend_scratch(length, width, heads_width):
    blocks = length // BLOCK
    return [
        pltpu.VMEM((heads_width, length), jnp.bfloat16),
        pltpu.VMEM((blocks, BLOCK, width), jnp.bfloat16),
        pltpu.VMEM((blocks, BLOCK, width), jnp.bfloat16),
    ]


def run_forward_plain(hid, tok, blocks, small, rows, table, shard, cot):
    length, width = hid.shape
    heads_width = blocks.shape[2] // 4
    vmem = pl.BlockSpec(memory_space=pltpu.VMEM)
    dma = pltpu.SemaphoreType.DMA
    count = length // BLOCK
    return pl.pallas_call(
        forward_plain_kernel,
        in_specs=[vmem] * 8,
        out_specs=[vmem] * 10,
        out_shape=forward_results(length, width, heads_width, shard.shape),
        scratch_shapes=attend_scratch(length, width, heads_width)
        + [dma((count,)), dma((count,)), dma((shard.shape[0],)), dma((shard.shape[0],)), dma((2,))],
        compiler_params=pltpu.CompilerParams(
            collective_id=0, has_side_effects=True, vmem_limit_bytes=60 << 20
        ),
    )(hid, tok, blocks, small, rows, table, shard, cot)


def run_forward(*operands):
    hid, wout, wdown, table = operands[0], operands[11], operands[13], operands[14]
    own_rows, width = hid.shape
    length = 2 * table.shape[0]
    shard, heads_width = wout.shape
    experts, _, hidden = wdown.shape
    size = lax.axis_size("fsdp")
    count = length // BLOCK
    hbm = pl.BlockSpec(memory_space=pl.ANY)
    vmem = pl.BlockSpec(memory_space=pltpu.VMEM)
    low_t, wide_t = jnp.bfloat16, jnp.float32
    dma = pltpu.SemaphoreType.DMA
    return pl.pallas_call(
        forward_kernel,
        in_specs=[vmem] * 15,
        out_specs=[hbm, vmem, vmem, hbm, hbm, vmem, hbm]
        + [vmem] * 4
        + [hbm, hbm],
        out_shape=[
            jax.ShapeDtypeStruct((size, shard, 4 * heads_width), low_t),
            jax.ShapeDtypeStruct((width, PAIR), low_t),
            jax.ShapeDtypeStruct((8, width), wide_t),
        ]
        + forward_results(length, width, heads_width, (experts, shard, 3 * hidden)),
        scratch_shapes=[
            pltpu.VMEM((size, shard, 4 * heads_width), low_t),
            pltpu.VMEM((length, width), low_t),
            pltpu.VMEM((length, 3 * heads_width), low_t),
            pltpu.VMEM((length, heads_width), low_t),
            pltpu.VMEM((length, width), low_t),
            pltpu.VMEM((length, width), low_t),
        ]
        + attend_scratch(length, width, heads_width)
        + [
            pltpu.VMEM((experts, shard, 3 * hidden), low_t),
            pltpu.VMEM((PAIR, PAIR), wide_t),
            pltpu.VMEM((size, 2, shard // 2, PAIR), wide_t),
            pltpu.VMEM((2, 32, own_rows), wide_t),
            dma((count,)),
            dma((count,)),
            dma((experts,)),
            dma((experts,)),
            dma((7,)),
            dma((7,)),
        ]
        + [dma((2, size // 4))] * 6
        + [dma((2, size // 2))] * 2
        + [dma((5,))],
        compiler_params=pltpu.CompilerParams(
            collective_id=3, has_side_effects=True, vmem_limit_bytes=60 << 20
        ),
    )(*operands)


def run_backward(wqkv, *operands):
    cot, mid, s1, qkv, mixed, blocks, own, egrads = (
        operands[index] for index in (4, 5, 6, 7, 9, 10, 14, 15)
    )
    length, width = cot.shape
    heads_width = mixed.shape[1]
    count = length // BLOCK
    own_rows = own.shape[0]
    parts, shard = blocks.shape[:2]
    columns = 4 * heads_width + PAIR
    vmem = pl.BlockSpec(memory_space=pltpu.VMEM)
    hbm = pl.BlockSpec(memory_space=pl.ANY)
    low_t, wide_t = jnp.bfloat16, jnp.float32
    dma = pltpu.SemaphoreType.DMA
    in_specs = [hbm] + [vmem] * 3 + [hbm] * 4 + [vmem] + [hbm] * 2 + [vmem] * 4 + [hbm]
    body = [
        pltpu.VMEM((count, BLOCK, width), low_t),
        pltpu.VMEM((count, BLOCK, width), low_t),
        pltpu.VMEM((count, 8, BLOCK), wide_t),
        pltpu.VMEM((count, 8, BLOCK), wide_t),
        pltpu.VMEM(mid.shape, wide_t),
        pltpu.VMEM(s1.shape, low_t),
        pltpu.VMEM(qkv.shape, low_t),
        pltpu.VMEM(mixed.shape, low_t),
        pltpu.VMEM(blocks.shape, low_t),
        pltpu.VMEM((2, BLOCK, width), low_t),
        pltpu.VMEM((2, BLOCK, width), low_t),
        pltpu.VMEM((length, width), wide_t),
        pltpu.VMEM((2, BLOCK, width), wide_t),
        pltpu.VMEM((heads_width, length), low_t),
        pltpu.VMEM((BLOCK, heads_width), low_t),
        pltpu.VMEM((length, heads_width), wide_t),
        pltpu.VMEM((length, heads_width), wide_t),
        pltpu.VMEM((length, 3 * heads_width), low_t),
        pltpu.VMEM((length, width), low_t),
        pltpu.VMEM((length, width), low_t),
        pltpu.VMEM((length, PAIR), low_t),
        pltpu.VMEM((length, PAIR), low_t),
        pltpu.VMEM((8, width), wide_t),
        dma((count,)),
        dma((count,)),
        dma((2,)),
        dma((2,)),
        dma((egrads.shape[0],)),
        dma((egrads.shape[0],)),
        dma((count,)),
        dma((count,)),
        dma((5,)),
        pltpu.VMEM(operands[0].shape, low_t),
        pltpu.VMEM(cot.shape, low_t),
        dma((2,)),
    ]
    own_wide = jax.ShapeDtypeStruct((own_rows, width), wide_t)
    own_low = jax.ShapeDtypeStruct((own_rows, width), low_t)
    arrived = jax.ShapeDtypeStruct(egrads.shape, low_t)
    params = pltpu.CompilerParams(
        collective_id=1, has_side_effects=True, vmem_limit_bytes=67043328
    )
    if wqkv is None:
        return pl.pallas_call(
            backward_plain_kernel,
            in_specs=in_specs,
            out_specs=[vmem] * 4 + [hbm],
            out_shape=[
                own_wide,
                own_wide,
                own_low,
                jax.ShapeDtypeStruct((parts, shard, columns), low_t),
                arrived,
            ],
            scratch_shapes=body,
            compiler_params=params,
        )(*operands)
    return pl.pallas_call(
        functools.partial(backward_kernel, len(body)),
        in_specs=in_specs + [vmem],
        out_specs=[vmem] * 2 + [hbm] + [vmem] * 3,
        out_shape=[
            own_wide,
            own_wide,
            arrived,
            own_low,
            jax.ShapeDtypeStruct((shard, columns - PAIR), wide_t),
            jax.ShapeDtypeStruct((shard // 2, PAIR), wide_t),
        ],
        scratch_shapes=[
            pltpu.VMEM((own_rows, width), low_t),
            pltpu.VMEM((parts, shard, columns), low_t),
        ]
        + body
        + sum_scratch(parts // 4, shard, columns),
        compiler_params=params,
    )(*operands, wqkv)


def shards(
    hidden,
    prev_logits,
    routes,
    slot_rank,
    dropped,
    cotangent,
    attn_norm,
    ffn_norm,
    w_qkv,
    w_attn_out,
    w_router,
    w_const_gate,
    w_const_value,
    w_expert_in,
    w_expert_out,
):
    own_rows, width = hidden.shape
    length = own_rows * lax.axis_size("tp")
    experts = w_expert_in.shape[0]
    route_count = w_router.shape[1]
    capacity = 9 * length // (4 * route_count)
    planned = lax.axis_size("fsdp") == 16
    table = jnp.asarray(rotary_table(length))
    gains = jnp.stack([wide(attn_norm), wide(ffn_norm)], axis=0)
    wqkv = w_qkv.transpose(1, 0, 2)
    operands = (
        hidden,
        cotangent,
        prev_logits.T,
        routes.T,
        slot_rank.T,
        dropped.T,
        gains,
        w_router.T,
        w_const_gate.T,
        w_const_value.T,
        wqkv,
        w_attn_out,
        w_expert_in,
        w_expert_out,
    )
    if planned:
        forward = run_forward(*operands, table)
    else:
        forward = forward_plain(operands, table)
    blocks, small, rows, s1, qkv, lse, mixed, mid, s2, tok, lines, gathered, cot = forward
    expert_weights = join_weights(gathered, experts)
    peers = 2 * experts
    half = capacity // 2
    block = half // 2
    place = jnp.arange(peers * block)
    owner = (lax.axis_index("fsdp") % peers) ^ (place // block)
    slot = wide(
        (owner // 2) * capacity
        + lax.axis_index("tp") * half
        + (owner % 2) * block
        + place % block
    )
    results, grad_rows, grads_exp = run_expert(
        s2, cot, lines, jnp.broadcast_to(slot[:, None], (slot.shape[0], PAIR)), expert_weights
    )
    backward = run_backward(
        wqkv if planned else None,
        results.reshape(-1, width),
        grad_rows.reshape(-1, width),
        jnp.broadcast_to(slot[None, :], (8, slot.shape[0])),
        tok,
        cot,
        mid,
        s1,
        qkv,
        lse,
        mixed,
        blocks,
        small,
        rows,
        table,
        hidden,
        split_grads(grads_exp),
    )
    if planned:
        grad_hidden, base, arrived, received, red, last = backward
    else:
        grad_hidden, base, for_other, big, arrived = backward
        received, red, last = finish_plain(big.reshape(width, -1), wqkv, for_other)
    output, grad_hidden, grad_qkv, grad_attn_out, gain_grads, grad_router, grad_mixing, grad_value, grad_in, grad_out = run_write(
        base, received, grad_hidden, red, last, gains, arrived
    )
    return (
        output,
        grad_hidden,
        gain_grads[0],
        gain_grads[1],
        grad_qkv.transpose(1, 0, 2),
        grad_attn_out,
        grad_router.T,
        grad_mixing.T,
        grad_value.T,
        grad_in,
        grad_out,
    )


def solution(mesh):
    in_specs = (
        P(("fsdp", "tp"), None),
        P(("fsdp", "tp"), None),
        P(("fsdp", "tp"), None),
        P(("fsdp", "tp"), None),
        P(("fsdp", "tp"), None),
        P(("fsdp", "tp"), None),
        P(("fsdp", "tp")),
        P(("fsdp", "tp")),
        P("fsdp", None, "tp"),
        P("fsdp", "tp"),
        P(("fsdp", "tp"), None),
        P(("fsdp", "tp"), None),
        P(("fsdp", "tp"), None),
        P(None, "fsdp", None, "tp"),
        P(None, "fsdp", "tp"),
    )
    out_specs = (
        P(("fsdp", "tp"), None),
        P(("fsdp", "tp"), None),
        P(("fsdp", "tp")),
        P(("fsdp", "tp")),
        P("fsdp", None, "tp"),
        P("fsdp", "tp"),
        P(("fsdp", "tp"), None),
        P(("fsdp", "tp"), None),
        P(("fsdp", "tp"), None),
        P(None, "fsdp", None, "tp"),
        P(None, "fsdp", "tp"),
    )
    return jax.shard_map(shards, mesh=mesh, in_specs=in_specs, out_specs=out_specs, check_vma=False)
```
